32 devices in a mesh: dp: 16 (over z, x, core), mod: 2 (over y).
Axes of the slice: x: 2, y: 2, z: 4, core: 2. Of those that a mesh axis runs over, the one named last changes fastest.
Arguments:
- x_in: bfloat16 [32768, 1152], P(('dp', 'mod')), may hold values from -6 to 6
- cond: bfloat16 [128, 1152], P('dp'), may hold values from -4 to 4
- segments: int32 [32768], P(('dp', 'mod')), may hold values from 0 to 3, as said below
- out_grad: bfloat16 [32768, 1152], P(('dp', 'mod')), may hold values from -6 to 6
- qkv_weight: float32 [1152, 3456], P('dp', 'mod'), may hold values from -0.11785113 to 0.11785113
- qkv_moment: float32 [1152, 3456], P('dp', 'mod'), may hold values from -448 to 448
- qkv_average: float32 [1152, 3456], P('dp', 'mod'), may hold values from -0.1875 to 0.1875
- proj_weight: float32 [1152, 1152], P('dp', 'mod'), may hold values from -0.375 to 0.375
- proj_moment: float32 [1152, 1152], P('dp', 'mod'), may hold values from -448 to 448
- proj_average: float32 [1152, 1152], P('dp', 'mod'), may hold values from -0.375 to 0.375
- fc1_weight: float32 [1152, 4608], P('dp', 'mod'), may hold values from -0.1875 to 0.1875
- fc1_moment: float32 [1152, 4608], P('dp', 'mod'), may hold values from -320 to 320
- fc1_average: float32 [1152, 4608], P('dp', 'mod'), may hold values from -0.1875 to 0.1875
- fc2_weight: float32 [4608, 1152], P('dp', 'mod'), may hold values from -0.09375 to 0.09375
- fc2_moment: float32 [4608, 1152], P('dp', 'mod'), may hold values from -384 to 384
- fc2_average: float32 [4608, 1152], P('dp', 'mod'), may hold values from -0.09375 to 0.09375
- bias_weight: float32 [9216], P(('dp', 'mod')), may hold values from -1.25 to 1.25
- bias_moment: float32 [9216], P(('dp', 'mod')), may hold values from -896 to 896
- bias_average: float32 [9216], P(('dp', 'mod')), may hold values from -1.25 to 1.25
- ada_weight: float32 [1152, 6912], P('dp', 'mod'), may hold values from -0.11785113 to 0.11785113
- ada_moment: float32 [1152, 6912], P('dp', 'mod'), may hold values from -512 to 512
- ada_average: float32 [1152, 6912], P('dp', 'mod'), may hold values from -0.1875 to 0.1875
- adab_weight: float32 [2, 3456], P('mod', 'dp'), may hold values from -0.8 to 0.8
- adab_moment: float32 [2, 3456], P('mod', 'dp'), may hold values from -768 to 768
- adab_average: float32 [2, 3456], P('mod', 'dp'), may hold values from -1.25 to 1.25
Outputs:
- block_out: bfloat16 [32768, 1152], P(('dp', 'mod'))
- x_grad: float32 [32768, 1152], P(('dp', 'mod'))
- cond_grad: float32 [128, 1152], P('dp')
- qkv_weight_next: float32 [1152, 3456], P('dp', 'mod')
- qkv_moment_next: float32 [1152, 3456], P('dp', 'mod')
- qkv_average_next: float32 [1152, 3456], P('dp', 'mod')
- proj_weight_next: float32 [1152, 1152], P('dp', 'mod')
- proj_moment_next: float32 [1152, 1152], P('dp', 'mod')
- proj_average_next: float32 [1152, 1152], P('dp', 'mod')
- fc1_weight_next: float32 [1152, 4608], P('dp', 'mod')
- fc1_moment_next: float32 [1152, 4608], P('dp', 'mod')
- fc1_average_next: float32 [1152, 4608], P('dp', 'mod')
- fc2_weight_next: float32 [4608, 1152], P('dp', 'mod')
- fc2_moment_next: float32 [4608, 1152], P('dp', 'mod')
- fc2_average_next: float32 [4608, 1152], P('dp', 'mod')
- bias_weight_next: float32 [9216], P(('dp', 'mod'))
- bias_moment_next: float32 [9216], P(('dp', 'mod'))
- bias_average_next: float32 [9216], P(('dp', 'mod'))
- ada_weight_next: float32 [1152, 6912], P('dp', 'mod')
- ada_moment_next: float32 [1152, 6912], P('dp', 'mod')
- ada_average_next: float32 [1152, 6912], P('dp', 'mod')
- adab_weight_next: float32 [2, 3456], P('mod', 'dp')
- adab_moment_next: float32 [2, 3456], P('mod', 'dp')
- adab_average_next: float32 [2, 3456], P('mod', 'dp')
The draws below stay inside these ranges and needn't reach their ends.
Inputs may be any that keep to these rules, and one draw needn't show every extreme that they name: `segments`: each aligned block of 1024 tokens of one device holds either one image, all of whose tokens carry the slot number of the block's first 256 tokens, or 4 images of 256 tokens, each token carrying its position within the device's tokens // 256. Both kinds occur in every draw.
All inputs are finite; a program needn't handle non-finite values.
Results may differ from the reference program's by a relative error of at most 0.013.
Values may be sent and summed in bfloat16 or wider, within the bound.
A program may use at most 384 MiB of HBM per device.

```python
import jax
import jax.numpy as jnp
from jax import lax

D = 1152
HEADS = 16
HEAD_DIM = 72
FF = 4608
LONG = 1024
SHORT = 256
TOK_DEV = 1024
SLOTS = 4
TOKENS = 32768
IMAGES = 128
ADA_HALF = 3456
BIAS = 9216
N_MOD = 2


def drawn_field(key, shape, spread):
    values = spread * jax.random.truncated_normal(key, -4.0, 4.0, shape, jnp.float32)
    return values


def draw_cond(key, part):
    return drawn_field(jax.random.fold_in(key, 11), (IMAGES, D), 1.0).astype(jnp.bfloat16)


def draw_qkv_weight(key, part):
    return drawn_field(jax.random.fold_in(key, 23), (D, 3 * D), D ** (-0.5))


def draw_ada_weight(key, part):
    return drawn_field(jax.random.fold_in(key, 37), (D, 6 * D), D ** (-0.5))


def draw_adab_weight(key, part):
    return drawn_field(jax.random.fold_in(key, 41), (N_MOD, ADA_HALF), 0.2)


def draw_segments(key, part):
    blocks_dev = TOK_DEV // LONG
    total_blocks = TOKENS // LONG
    block_kinds = jax.random.randint(key, (total_blocks,), 0, 2)
    block_number = jnp.arange(total_blocks, dtype=jnp.int32)
    block_kinds = jnp.where(block_number == 0, 1, block_kinds)
    block_kinds = jnp.where(block_number == 2 * blocks_dev - 1, 0, block_kinds)
    position = jnp.arange(TOKENS, dtype=jnp.int32) % TOK_DEV
    token_kind = jnp.repeat(block_kinds, LONG)
    first_slot = position // LONG * (LONG // SHORT)
    own_slot = position // SHORT
    return jnp.where(token_kind == 1, first_slot, own_slot).astype(jnp.int32)


def level_of(rng, extent, pieces, least, top_value):
    loudness = 1.0
    for axis_at, parts in pieces:
        heights = jax.random.uniform(jax.random.fold_in(jax.random.fold_in(rng, 6), axis_at), (parts,), jnp.float32, least / len(pieces), top_value / len(pieces))
        loudness = loudness * jnp.repeat(jnp.exp(heights), extent[axis_at] // parts).reshape((-1,) + (1,) * (len(extent) - 1 - axis_at))
    return loudness


def centred(key, shape, width, reach, cuts=(), kind=jnp.bfloat16):
    entries = jax.random.normal(key, shape, jnp.float32) * width
    if len(cuts) > 0:
        entries = level_of(key, shape, cuts, -0.22, 0.18) * entries
    return jnp.clip(entries, min=-reach, max=reach).astype(kind)


def setup_inputs(seed: int = 0) -> dict:
    keys = jax.random.split(jax.random.key(seed), 26)
    return {
        "x_in": centred(keys[0], (TOKENS, D), 1.0, 6.0, ((0, 32),)),
        "cond": draw_cond(jax.random.fold_in(keys[25], 71), 0),
        "segments": draw_segments(jax.random.fold_in(keys[25], 71), 0),
        "out_grad": centred(keys[3], (TOKENS, D), 1.0, 6.0, ((0, 32),)),
        "qkv_weight": draw_qkv_weight(jax.random.fold_in(keys[25], 71), 0),
        "qkv_moment": centred(keys[5], (D, 3 * D), (0.4 * TOKENS ** 0.5), 448.0, ((0, 16), (1, 2)), jnp.float32),
        "qkv_average": centred(keys[6], (D, 3 * D), D ** -0.5, 0.1875, ((0, 16), (1, 2)), jnp.float32),
        "proj_weight": centred(keys[7], (D, D), (D // 4) ** -0.5, 0.375, ((0, 16), (1, 2)), jnp.float32),
        "proj_moment": centred(keys[8], (D, D), (0.4 * TOKENS ** 0.5), 448.0, ((0, 16), (1, 2)), jnp.float32),
        "proj_average": centred(keys[9], (D, D), (D // 4) ** -0.5, 0.375, ((0, 16), (1, 2)), jnp.float32),
        "fc1_weight": centred(keys[10], (D, FF), D ** -0.5, 0.1875, ((0, 16), (1, 2)), jnp.float32),
        "fc1_moment": centred(keys[11], (D, FF), (0.3 * TOKENS ** 0.5), 320.0, ((0, 16), (1, 2)), jnp.float32),
        "fc1_average": centred(keys[12], (D, FF), D ** -0.5, 0.1875, ((0, 16), (1, 2)), jnp.float32),
        "fc2_weight": centred(keys[13], (FF, D), FF ** -0.5, 0.09375, ((0, 16), (1, 2)), jnp.float32),
        "fc2_moment": centred(keys[14], (FF, D), (0.36 * TOKENS ** 0.5), 384.0, ((0, 16), (1, 2)), jnp.float32),
        "fc2_average": centred(keys[15], (FF, D), FF ** -0.5, 0.09375, ((0, 16), (1, 2)), jnp.float32),
        "bias_weight": centred(keys[16], (BIAS,), 0.2, 1.25, ((0, 32),), jnp.float32),
        "bias_moment": centred(keys[17], (BIAS,), (0.8 * TOKENS ** 0.5), 896.0, ((0, 32),), jnp.float32),
        "bias_average": centred(keys[18], (BIAS,), 0.2, 1.25, ((0, 32),), jnp.float32),
        "ada_weight": draw_ada_weight(jax.random.fold_in(keys[25], 71), 0),
        "ada_moment": centred(keys[20], (D, 6 * D), (0.5 * TOKENS ** 0.5), 512.0, ((0, 16), (1, 2)), jnp.float32),
        "ada_average": centred(keys[21], (D, 6 * D), D ** -0.5, 0.1875, ((0, 16), (1, 2)), jnp.float32),
        "adab_weight": draw_adab_weight(jax.random.fold_in(keys[25], 71), 0),
        "adab_moment": centred(keys[23], (N_MOD, ADA_HALF), (0.7 * TOKENS ** 0.5), 768.0, ((0, 2), (1, 16)), jnp.float32),
        "adab_average": centred(keys[24], (N_MOD, ADA_HALF), 0.2, 1.25, ((0, 2), (1, 16)), jnp.float32),
    }


@jax.custom_vjp
def low(v):
    return lax.optimization_barrier(v.astype(jnp.bfloat16)).astype(jnp.float32)

@jax.custom_vjp
def low_back(v):
    return v

def low_keep(v):
    return (low(v), None)

def low_pass(kept, grad):
    return (grad,)

def back_keep(v):
    return (v, None)

def back_low(kept, grad):
    return (low(grad),)
low.defvjp(low_keep, low_pass)
low_back.defvjp(back_keep, back_low)
EPS = 1e-06
MOMENTUM = 0.9
DECAY = 0.5
HIGH = lax.Precision.HIGHEST

def normalize(values):
    centre = values - lax.optimization_barrier(jnp.mean(values, axis=-1, keepdims=True))
    return centre * lax.rsqrt(lax.optimization_barrier(jnp.mean(centre * centre, axis=-1, keepdims=True)) + EPS)

def matmul(left, right):
    return jnp.dot(left, right, precision=HIGH, preferred_element_type=jnp.float32)

def attend_pack(inputs):
    query_part, key_part, value_part, seg_part = inputs
    scaling = HEAD_DIM ** (-0.5)
    scores = low_back(jnp.einsum('qhd,khd->hqk', query_part, key_part, precision=HIGH) * scaling)
    allowed = seg_part[:, None] == seg_part[None, :]
    scores = jnp.where(allowed[None], scores, -1e+30)
    softmax = jax.nn.softmax(scores, axis=-1)
    return jnp.einsum('hqk,khd->qhd', low(softmax), value_part, precision=HIGH)

def forward(x_in, cond, segments, qkv_weight, proj_weight, fc1_weight, fc2_weight, bias_weight, ada_weight, ada_bias):
    qkv_weight = low(qkv_weight)
    proj_weight = low(proj_weight)
    fc1_weight = low(fc1_weight)
    fc2_weight = low(fc2_weight)
    bias_weight = low(bias_weight)
    ada_weight = low(ada_weight)
    ada_bias = low(ada_bias)
    cond_silu = low(jax.nn.silu(cond))
    modulation = low_back(low(matmul(cond_silu, ada_weight) + ada_bias))
    image_rows = jnp.arange(TOKENS, dtype=jnp.int32) // TOK_DEV * SLOTS + segments.astype(jnp.int32)
    per_token = jnp.take(modulation, image_rows, axis=0)
    shift_attn = per_token[:, 0:D]
    scale_attn = per_token[:, D:2 * D]
    gate_attn = per_token[:, 2 * D:3 * D]
    shift_mlp = per_token[:, 3 * D:4 * D]
    scale_mlp = per_token[:, 4 * D:5 * D]
    gate_mlp = per_token[:, 5 * D:6 * D]
    first_norm = normalize(x_in)
    attn_input = low(first_norm * (1.0 + scale_attn) + shift_attn)
    joint_proj = matmul(attn_input, qkv_weight)
    query_rows = low_back(low(joint_proj[:, 0:D] + bias_weight[0:D]))
    key_rows = low_back(low(joint_proj[:, D:2 * D]))
    value_rows = low_back(low(joint_proj[:, 2 * D:3 * D] + bias_weight[D:2 * D]))
    pack_count = TOKENS // TOK_DEV
    pack_shape = (pack_count, TOK_DEV, HEADS, HEAD_DIM)
    mixture = lax.map(jax.checkpoint(attend_pack), (query_rows.reshape(pack_shape), key_rows.reshape(pack_shape), value_rows.reshape(pack_shape), segments.reshape(pack_count, TOK_DEV)))
    mixture = low_back(low(mixture.reshape(TOKENS, D)))
    attn_out = low_back(matmul(mixture, proj_weight) + bias_weight[2 * D:3 * D])
    residual = x_in + gate_attn * attn_out
    second_norm = normalize(residual)
    mlp_input = low(second_norm * (1.0 + scale_mlp) + shift_mlp)
    pre_act = low_back(matmul(mlp_input, fc1_weight) + bias_weight[3 * D:3 * D + FF])
    hidden = low(jax.nn.gelu(pre_act, approximate=True))
    branch = low_back(matmul(hidden, fc2_weight) + bias_weight[3 * D + FF:])
    return residual + gate_mlp * branch

def step_rates(tokens_all):
    base_rate = tokens_all ** (-0.5)
    return (2.5 * D ** (-0.5) * base_rate, 3.0 * D ** (-0.5) * base_rate, 3.3 * D ** (-0.5) * base_rate, 2.8 * FF ** (-0.5) * base_rate, 0.5 * base_rate, 2.0 * D ** (-0.5) * base_rate, 0.3 * base_rate)

def nesterov(weight, moment, average, gradient, rate):
    moment = MOMENTUM * moment + gradient
    weight = weight - rate * (gradient + MOMENTUM * moment)
    average = DECAY * average + (1.0 - DECAY) * weight
    return (weight, moment, average)

def reference(x_in, cond, segments, out_grad, qkv_weight, qkv_moment, qkv_average, proj_weight, proj_moment, proj_average, fc1_weight, fc1_moment, fc1_average, fc2_weight, fc2_moment, fc2_average, bias_weight, bias_moment, bias_average, ada_weight, ada_moment, ada_average, adab_weight, adab_moment, adab_average):

    def wrapped(x_full, cond_full, qkv_full, proj_full, fc1_full, fc2_full, bias_full, ada_full, adab_full):
        return forward(x_full, cond_full, segments, qkv_full, proj_full, fc1_full, fc2_full, bias_full, ada_full, adab_full)
    block_out, pullback = jax.vjp(wrapped, x_in.astype(jnp.float32), cond.astype(jnp.float32), qkv_weight, proj_weight, fc1_weight, fc2_weight, bias_weight, ada_weight, adab_weight.reshape(-1))
    grads = pullback(out_grad.astype(jnp.float32))
    rates = step_rates(TOKENS)
    qkv_next = nesterov(qkv_weight, qkv_moment, qkv_average, grads[2], rates[0])
    proj_next = nesterov(proj_weight, proj_moment, proj_average, grads[3], rates[1])
    fc1_next = nesterov(fc1_weight, fc1_moment, fc1_average, grads[4], rates[2])
    fc2_next = nesterov(fc2_weight, fc2_moment, fc2_average, grads[5], rates[3])
    bias_next = nesterov(bias_weight, bias_moment, bias_average, grads[6], rates[4])
    ada_next = nesterov(ada_weight, ada_moment, ada_average, grads[7], rates[5])
    adab_flat = nesterov(adab_weight.reshape(-1), adab_moment.reshape(-1), adab_average.reshape(-1), grads[8], rates[6])
    adab_shape = (N_MOD, ADA_HALF)
    return (block_out.astype(jnp.bfloat16), grads[0], grads[1], qkv_next[0], qkv_next[1], qkv_next[2], proj_next[0], proj_next[1], proj_next[2], fc1_next[0], fc1_next[1], fc1_next[2], fc2_next[0], fc2_next[1], fc2_next[2], bias_next[0], bias_next[1], bias_next[2], ada_next[0], ada_next[1], ada_next[2], adab_flat[0].reshape(adab_shape), adab_flat[1].reshape(adab_shape), adab_flat[2].reshape(adab_shape))
```

```python
from functools import partial

import jax
import jax.numpy as jnp
from jax import lax
from jax.sharding import Mesh
from jax.sharding import PartitionSpec as P

D = 1152
HEADS = 16
FF = 4608


EPS = 1e-06
MOMENTUM = 0.9
DECAY = 0.5


def normalize(values):
    centre = values - jnp.mean(values, axis=-1, keepdims=True)
    inverse = lax.rsqrt(jnp.mean(centre * centre, axis=-1, keepdims=True) + EPS)
    return (centre * inverse, inverse)


def normalize_back(upstream, normed, inverse):
    return inverse * (
        upstream
        - jnp.mean(upstream, axis=-1, keepdims=True)
        - normed * jnp.mean(upstream * normed, axis=-1, keepdims=True)
    )


def step_rates(tokens_all):
    base_rate = tokens_all ** (-0.5)
    return (
        2.5 * D ** (-0.5) * base_rate,
        3.0 * D ** (-0.5) * base_rate,
        3.3 * D ** (-0.5) * base_rate,
        2.8 * FF ** (-0.5) * base_rate,
        0.5 * base_rate,
        2.0 * D ** (-0.5) * base_rate,
        0.3 * base_rate,
    )


def nesterov(weight, moment, average, gradient, rate):
    moment = MOMENTUM * moment + gradient
    weight = weight - rate * (gradient + MOMENTUM * moment)
    average = DECAY * average + (1.0 - DECAY) * weight
    return (weight, moment, average)


def masked_scores(query_part, seg_part, key_rows, segments, scaling):
    scores = (
        jnp.einsum("qhd,khd->hqk", query_part, key_rows, preferred_element_type=jnp.float32)
        * scaling
    )
    allowed = seg_part[:, None] == segments[None, :]
    return jnp.where(allowed[None], scores, -1e30)


def attend_forward(query_rows, key_rows, value_rows, segments, block_rows):
    tokens, head_count, head_width = query_rows.shape
    scaling = head_width ** (-0.5)
    blocks = tokens // block_rows

    def one_block(inputs):
        query_part, seg_part = inputs
        scores = masked_scores(query_part, seg_part, key_rows, segments, scaling)
        largest = jnp.max(scores, axis=-1, keepdims=True)
        weights = jnp.exp(scores - largest)
        totals = jnp.sum(weights, axis=-1, keepdims=True)
        softmax_low = (weights / totals).astype(jnp.bfloat16)
        mixture = jnp.einsum(
            "hqk,khd->qhd", softmax_low, value_rows, preferred_element_type=jnp.float32
        )
        return (mixture.astype(jnp.bfloat16), (largest + jnp.log(totals))[..., 0])

    mixture, log_totals = lax.map(
        one_block,
        (
            query_rows.reshape(blocks, block_rows, head_count, head_width),
            segments.reshape(blocks, block_rows),
        ),
    )
    return (mixture.reshape(tokens, head_count * head_width), log_totals)


def attend_backward(query_rows, key_rows, value_rows, segments, log_totals, upstream, block_rows):
    tokens, head_count, head_width = query_rows.shape
    scaling = head_width ** (-0.5)
    blocks = tokens // block_rows

    def one_block(carried, inputs):
        key_grad, value_grad = carried
        query_part, seg_part, log_part, up_part = inputs
        scores = masked_scores(query_part, seg_part, key_rows, segments, scaling)
        softmax = jnp.exp(scores - log_part[..., None])
        softmax_low = softmax.astype(jnp.bfloat16)
        value_grad = value_grad + jnp.einsum(
            "hqk,qhd->khd", softmax_low, up_part, preferred_element_type=jnp.float32
        )
        prob_grad = jnp.einsum(
            "qhd,khd->hqk", up_part, value_rows, preferred_element_type=jnp.float32
        )
        centred = prob_grad - jnp.sum(softmax * prob_grad, axis=-1, keepdims=True)
        score_grad = (softmax * centred).astype(jnp.bfloat16)
        query_grad = (
            jnp.einsum("hqk,khd->qhd", score_grad, key_rows, preferred_element_type=jnp.float32)
            * scaling
        )
        key_grad = (
            key_grad
            + jnp.einsum("hqk,qhd->khd", score_grad, query_part, preferred_element_type=jnp.float32)
            * scaling
        )
        return ((key_grad, value_grad), query_grad.astype(jnp.bfloat16))

    zeroes = jnp.zeros(key_rows.shape, jnp.float32)
    carried, query_grad = lax.scan(
        one_block,
        (zeroes, zeroes),
        (
            query_rows.reshape(blocks, block_rows, head_count, head_width),
            segments.reshape(blocks, block_rows),
            log_totals,
            upstream.reshape(blocks, block_rows, head_count, head_width),
        ),
    )
    full_width = head_count * head_width
    return (
        query_grad.reshape(tokens, full_width),
        carried[0].reshape(tokens, full_width).astype(jnp.bfloat16),
        carried[1].reshape(tokens, full_width).astype(jnp.bfloat16),
    )


ROWS = ("far", "near", "core")
ALL = ("far", "near", "core", "mod")
LOW = jnp.bfloat16
WIDE = jnp.float32


def swap(values, axis):
    return lax.ppermute(values, axis, [(0, 1), (1, 0)])


def shifted(values, distance, count):
    return lax.ppermute(values, "far", [(i, (i + distance) % count) for i in range(count)])


def collect_far(shard):
    count = lax.axis_size("far")
    if count > 4:
        return lax.all_gather(shard, "far", axis=0)
    here = lax.axis_index("far")
    held = jnp.zeros((count,) + shard.shape, shard.dtype)
    held = lax.dynamic_update_index_in_dim(held, shard, here, 0)
    for distance in range(1, count):
        came = shifted(shard, distance, count)
        held = lax.dynamic_update_index_in_dim(held, came, (here - distance) % count, 0)
    return held


def gather_weight(shard, first):
    near, core, half = lax.axis_index("near"), lax.axis_index("core"), lax.axis_index("mod")
    own = collect_far(shard)
    if first == "near":
        by_near = swap(own, "near")
        by_mod = swap(own, "mod")
        by_both = swap(by_near, "mod")
    else:
        by_mod = swap(own, "mod")
        by_near = swap(own, "near")
        by_both = swap(by_mod, "near")
    count, rows, columns = own.shape
    whole = jnp.zeros((2, count, 2, 2, rows, columns), shard.dtype)
    for piece, n, m in ((own, 0, 0), (by_near, 1, 0), (by_mod, 0, 1), (by_both, 1, 1)):
        other = swap(piece, "core")
        for part, k in ((piece, 0), (other, 1)):
            whole = lax.dynamic_update_slice(
                whole, part[None, :, None, None], (half ^ m, 0, near ^ n, core ^ k, 0, 0)
            )
    return whole.reshape(2, count * 4 * rows, columns)


def scatter_gradient(left, right, first):
    count = lax.axis_size("far")
    here = lax.axis_index("far")
    near, core, half = lax.axis_index("near"), lax.axis_index("core"), lax.axis_index("mod")
    tokens = left.shape[0]
    blocks = left.reshape(tokens, count, 2, 2, -1)

    def piece(n, k, m):
        rows = lax.dynamic_index_in_dim(blocks, near ^ n, 2, False)
        rows = lax.dynamic_index_in_dim(rows, core ^ k, 2, False)
        columns = lax.dynamic_index_in_dim(right, half ^ m, 0, False)
        product = jnp.dot(
            rows.reshape(tokens, -1).T, columns, preferred_element_type=WIDE
        )
        return product.reshape(count, -1, columns.shape[1])

    def chip_sum(n, m):
        came = swap(piece(n, 1, m).astype(LOW), "core")
        return (piece(n, 0, m) + came.astype(WIDE)).astype(LOW)

    def joined(kept, sent, axis):
        return (kept.astype(WIDE) + swap(sent, axis).astype(WIDE)).astype(LOW)

    if first == "mod":
        far_side = chip_sum(1, 1)
        near_side = chip_sum(0, 1)
        sent = joined(chip_sum(1, 0), far_side, "mod")
        kept = joined(chip_sum(0, 0), near_side, "mod")
        total = joined(kept, sent, "near")
    else:
        far_side = chip_sum(1, 1)
        near_side = chip_sum(1, 0)
        sent = joined(chip_sum(0, 1), far_side, "near")
        kept = joined(chip_sum(0, 0), near_side, "near")
        total = joined(kept, sent, "mod")
    if count > 4:
        return lax.psum_scatter(total.astype(WIDE), "far", scatter_dimension=0, tiled=False)
    result = lax.dynamic_index_in_dim(total, here, 0, False).astype(WIDE)
    for distance in range(1, count):
        block = lax.dynamic_index_in_dim(total, (here + distance) % count, 0, False)
        result = result + shifted(block, distance, count).astype(WIDE)
    return result


def times(left, right):
    return jnp.dot(left, right, preferred_element_type=WIDE)


def times_back(left, right):
    return lax.dot_general(left, right, (((1,), (1,)), ((), ())), preferred_element_type=WIDE)


def body(
    x_in,
    cond,
    segments,
    out_grad,
    qkv_weight,
    qkv_moment,
    qkv_average,
    proj_weight,
    proj_moment,
    proj_average,
    fc1_weight,
    fc1_moment,
    fc1_average,
    fc2_weight,
    fc2_moment,
    fc2_average,
    bias_weight,
    bias_moment,
    bias_average,
    ada_weight,
    ada_moment,
    ada_average,
    adab_weight,
    adab_moment,
    adab_average,
):
    tokens, width = x_in.shape
    row_devices = lax.axis_size(ROWS)
    devices = lax.axis_size(ALL)
    row_index = lax.axis_index(ROWS)
    images = cond.shape[0] // 2
    head_width = width // HEADS
    block_rows = min(512, tokens)

    cond_silu, silu_back = jax.vjp(jax.nn.silu, cond.astype(WIDE))
    silu_all = lax.all_gather(cond_silu.astype(LOW), ROWS, axis=0, tiled=True)
    ada_low = ada_weight.astype(LOW)
    ada_columns = lax.all_to_all(ada_low, ROWS, split_axis=1, concat_axis=0, tiled=True)
    adab_low = adab_weight.astype(LOW).astype(WIDE)
    mod_columns = (times(silu_all, ada_columns) + adab_low).astype(LOW)
    mod_rows = lax.all_to_all(mod_columns, ALL, split_axis=0, concat_axis=1, tiled=True)
    modulation = jnp.swapaxes(
        mod_rows.reshape(images, row_devices, 2, -1), 1, 2
    ).reshape(images, -1)

    bias_full = lax.all_gather(bias_weight.astype(LOW), ALL, axis=0, tiled=True).astype(WIDE)
    qkv_low = gather_weight(qkv_weight.astype(LOW), "near")
    proj_low = gather_weight(proj_weight.astype(LOW), "mod")
    fc1_low = gather_weight(fc1_weight.astype(LOW), "near")
    fc2_low = gather_weight(fc2_weight.astype(LOW), "mod")
    hidden_width = fc2_low.shape[1]

    chooser = segments[:, None] == jnp.arange(images, dtype=jnp.int32)[None, :]
    per_token = times(chooser.astype(LOW), modulation)
    shift_attn, scale_attn, gate_attn, shift_mlp, scale_mlp, gate_mlp = [
        per_token[:, group * width : (group + 1) * width] for group in range(6)
    ]
    residual = x_in.astype(WIDE)
    first_norm, first_inverse = normalize(residual)
    attn_input = (first_norm * (1.0 + scale_attn) + shift_attn).astype(LOW)
    joint_proj = jnp.concatenate([times(attn_input, qkv_low[0]), times(attn_input, qkv_low[1])], 1)
    query_rows = (joint_proj[:, 0:width] + bias_full[0:width]).astype(LOW)
    key_rows = joint_proj[:, width : 2 * width].astype(LOW)
    value_rows = (joint_proj[:, 2 * width :] + bias_full[width : 2 * width]).astype(LOW)
    head_shape = (tokens, HEADS, head_width)
    query_heads = query_rows.reshape(head_shape)
    key_heads = key_rows.reshape(head_shape)
    value_heads = value_rows.reshape(head_shape)
    mixture, log_totals = attend_forward(query_heads, key_heads, value_heads, segments, block_rows)
    attn_out = (
        jnp.concatenate([times(mixture, proj_low[0]), times(mixture, proj_low[1])], 1)
        + bias_full[2 * width : 3 * width]
    )
    residual_mid = residual + gate_attn * attn_out
    second_norm, second_inverse = normalize(residual_mid)
    mlp_input = (second_norm * (1.0 + scale_mlp) + shift_mlp).astype(LOW)
    pre_act = (
        jnp.concatenate([times(mlp_input, fc1_low[0]), times(mlp_input, fc1_low[1])], 1)
        + bias_full[3 * width : 3 * width + hidden_width]
    )
    hidden_full, gelu_back = jax.vjp(partial(jax.nn.gelu, approximate=True), pre_act)
    hidden = hidden_full.astype(LOW)
    branch = (
        jnp.concatenate([times(hidden, fc2_low[0]), times(hidden, fc2_low[1])], 1)
        + bias_full[3 * width + hidden_width :]
    )
    block_out = (residual_mid + gate_mlp * branch).astype(LOW)

    def halves(values):
        middle = values.shape[1] // 2
        return jnp.stack([values[:, :middle], values[:, middle:]])

    upstream = out_grad.astype(WIDE)
    branch_grad = (gate_mlp * upstream).astype(LOW)
    gate_mlp_grad = upstream * branch
    branch_halves = halves(branch_grad)
    fc2_shard = scatter_gradient(hidden, branch_halves, "mod")
    hidden_grad = times_back(branch_halves[0], fc2_low[0]) + times_back(branch_halves[1], fc2_low[1])
    pre_grad = gelu_back(hidden_grad)[0].astype(LOW)
    pre_halves = halves(pre_grad)
    fc1_shard = scatter_gradient(mlp_input, pre_halves, "near")
    mlp_grad = times_back(pre_halves[0], fc1_low[0]) + times_back(pre_halves[1], fc1_low[1])
    scale_mlp_grad = mlp_grad * second_norm
    middle_grad = upstream + normalize_back(
        mlp_grad * (1.0 + scale_mlp), second_norm, second_inverse
    )
    attn_grad = (gate_attn * middle_grad).astype(LOW)
    gate_attn_grad = middle_grad * attn_out
    attn_halves = halves(attn_grad)
    proj_shard = scatter_gradient(mixture, attn_halves, "mod")
    mixture_grad = (
        times_back(attn_halves[0], proj_low[0]) + times_back(attn_halves[1], proj_low[1])
    ).astype(LOW)
    query_grad, key_grad, value_grad = attend_backward(
        query_heads,
        key_heads,
        value_heads,
        segments,
        log_totals,
        mixture_grad.reshape(head_shape),
        block_rows,
    )
    joint_grad = jnp.concatenate([query_grad, key_grad, value_grad], axis=1)
    joint_halves = halves(joint_grad)
    qkv_shard = scatter_gradient(attn_input, joint_halves, "near")
    input_grad = times_back(joint_halves[0], qkv_low[0]) + times_back(joint_halves[1], qkv_low[1])
    scale_attn_grad = input_grad * first_norm
    x_grad = middle_grad + normalize_back(
        input_grad * (1.0 + scale_attn), first_norm, first_inverse
    )

    token_mod_grad = jnp.concatenate(
        [input_grad, scale_attn_grad, gate_attn_grad, mlp_grad, scale_mlp_grad, gate_mlp_grad],
        axis=1,
    )
    slot_mod_grad = jnp.einsum(
        "ts,tc->sc", chooser.astype(WIDE), token_mod_grad, precision=lax.Precision.HIGHEST
    ).astype(LOW)
    half_grad = lax.all_to_all(slot_mod_grad, "mod", split_axis=1, concat_axis=0, tiled=True)
    mod_grad_all = lax.all_gather(half_grad, ROWS, axis=0, tiled=True)
    own_rows = ada_weight.shape[0]
    own_silu = lax.dynamic_slice_in_dim(silu_all, row_index * own_rows, own_rows, 1)
    ada_shard = jnp.einsum("ic,io->co", own_silu, mod_grad_all, preferred_element_type=WIDE)
    own_columns = adab_weight.shape[1]
    adab_shard = jnp.sum(
        lax.dynamic_slice_in_dim(mod_grad_all, row_index * own_columns, own_columns, 1).astype(WIDE),
        axis=0,
    )
    silu_part = times_back(mod_grad_all, ada_low)
    silu_part = lax.all_to_all(silu_part, ROWS, split_axis=0, concat_axis=1, tiled=True)
    cond_grad = silu_back(silu_part + swap(silu_part, "mod"))[0]

    grad_bias = jnp.concatenate(
        [
            jnp.sum(part.astype(WIDE), axis=0)
            for part in (query_grad, value_grad, attn_grad, pre_grad, branch_grad)
        ]
    ).reshape(devices, -1)
    bias_shard = jnp.sum(
        lax.all_to_all(grad_bias, ALL, split_axis=0, concat_axis=0, tiled=True), axis=0
    )

    rates = step_rates(tokens * devices)
    states_out = []
    states_out.extend(nesterov(qkv_weight, qkv_moment, qkv_average, qkv_shard, rates[0]))
    states_out.extend(nesterov(proj_weight, proj_moment, proj_average, proj_shard, rates[1]))
    states_out.extend(nesterov(fc1_weight, fc1_moment, fc1_average, fc1_shard, rates[2]))
    states_out.extend(nesterov(fc2_weight, fc2_moment, fc2_average, fc2_shard, rates[3]))
    states_out.extend(nesterov(bias_weight, bias_moment, bias_average, bias_shard, rates[4]))
    states_out.extend(nesterov(ada_weight, ada_moment, ada_average, ada_shard, rates[5]))
    states_out.extend(
        nesterov(adab_weight, adab_moment, adab_average, adab_shard.reshape(1, -1), rates[6])
    )
    return (block_out, x_grad, cond_grad) + tuple(states_out)


def solution(mesh):
    far = mesh.shape["dp"] // 4
    fine = Mesh(mesh.devices.reshape(far, 2, 2, mesh.shape["mod"]), ALL)
    tokens = P(ALL, None)
    images = P(ROWS, None)
    trunk = P(ROWS, "mod")
    bias = P(ALL)
    adab = P("mod", ROWS)
    states = (trunk,) * 12 + (bias,) * 3 + (trunk,) * 3 + (adab,) * 3
    return jax.shard_map(
        body,
        mesh=fine,
        in_specs=(tokens, images, bias, tokens) + states,
        out_specs=(tokens, tokens, images) + states,
        check_vma=False,
    )
```

```python
from functools import partial

import jax
import jax.numpy as jnp
from jax import lax
from jax.experimental import pallas as pl
from jax.experimental.pallas import tpu as pltpu
from jax.sharding import Mesh
from jax.sharding import PartitionSpec as P

D = 1152
HEADS = 16
HEAD = 72
FF = 4608
LANES = 128
CHUNK = 256

ROWS = ("far", "near", "core")
ALL = ("far", "near", "core", "mod")
LOW = jnp.bfloat16
WIDE = jnp.float32
LOG2E = 1.4426950408889634
NEG = -1e30
MESH = pl.DeviceIdType.MESH
VMEM = pl.BlockSpec(memory_space=pltpu.VMEM)
ANY = pl.BlockSpec(memory_space=pl.ANY)

EPS = 1e-06
MOMENTUM = 0.9
DECAY = 0.5


def normalize(values):
    centre = values - jnp.mean(values, axis=-1, keepdims=True)
    inverse = lax.rsqrt(jnp.mean(centre * centre, axis=-1, keepdims=True) + EPS)
    return (centre * inverse, inverse)


def normalize_back(upstream, normed, inverse):
    return inverse * (
        upstream
        - jnp.mean(upstream, axis=-1, keepdims=True)
        - normed * jnp.mean(upstream * normed, axis=-1, keepdims=True)
    )


def step_rates(tokens_all):
    base_rate = tokens_all ** (-0.5)
    return (
        2.5 * D ** (-0.5) * base_rate,
        3.0 * D ** (-0.5) * base_rate,
        3.3 * D ** (-0.5) * base_rate,
        2.8 * FF ** (-0.5) * base_rate,
        0.5 * base_rate,
        2.0 * D ** (-0.5) * base_rate,
        0.3 * base_rate,
    )


def nesterov(weight, moment, average, gradient, rate):
    moment = MOMENTUM * moment + gradient
    weight = weight - rate * (gradient + MOMENTUM * moment)
    average = DECAY * average + (1.0 - DECAY) * weight
    return (weight, moment, average)


def places():
    return {name: lax.axis_index(name) for name in ALL}


def greet():
    here = places()
    count = lax.axis_size("far")
    others = [dict(far=lax.rem(here["far"] + d, count)) for d in range(1, count)]
    others += [{name: 1 - here[name]} for name in ("near", "core", "mod")]
    barrier = pltpu.get_barrier_semaphore()
    for other in others:
        pl.semaphore_signal(barrier, inc=1, device_id=other, device_id_type=MESH)
    pl.semaphore_wait(barrier, len(others))


def remote(source, target, sends, receives, slot, other):
    return pltpu.make_async_remote_copy(
        src_ref=source,
        dst_ref=target,
        send_sem=sends.at[slot],
        recv_sem=receives.at[slot],
        device_id=other,
        device_id_type=MESH,
    )


def messages(count):
    return count - 1 + 8


class Gather:
    def __init__(self, whole, sends, receives):
        self.whole, self.sends, self.receives = whole, sends, receives
        self.here = places()
        self.count = lax.axis_size("far")
        rows = whole.shape[4]
        self.rows = rows
        self.split = rows if rows % 16 else 8 * ((rows // 8 + 1) // 2)

    def _block(self, far):
        return self.whole.at[self.here["mod"], far, self.here["near"], self.here["core"]]

    def _far(self, shard, distance):
        far = self.here["far"]
        other = dict(far=lax.rem(far + distance, self.count))
        return remote(shard, self._block(far), self.sends, self.receives, distance - 1, other)

    def _far_came(self, shard, distance):
        origin = lax.rem(self.here["far"] + self.count - distance, self.count)
        return remote(
            shard, self._block(origin), self.sends, self.receives, distance - 1, dict(far=origin)
        )

    def start_far(self, shard, local):
        pltpu.make_async_copy(shard, self._block(self.here["far"]), local).start()
        for distance in range(1, self.count):
            self._far(shard, distance).start()

    def finish_far(self, shard, local):
        pltpu.make_async_copy(shard, self._block(self.here["far"]), local).wait()
        for distance in range(1, self.count):
            self._far(shard, distance).wait_send()
            self._far_came(shard, distance).wait_recv()

    def _quad(self, flips, first, size):
        near, core, mod = (
            1 - self.here[name] if name in flips else self.here[name] for name in ("near", "core", "mod")
        )
        return self.whole.at[mod, :, near, core, pl.ds(first, size)]

    def _step(self, name):
        head, rest = (0, self.split), (self.split, self.rows - self.split)
        full = (0, self.rows)
        return {
            "near": ((), "near", full, 0),
            "mod": ((), "mod", full, 1),
            "near_mod": (("near",), "mod", head, 2),
            "mod_near": (("mod",), "near", rest, 3),
            "core": ((), "core", full, 4),
            "near_core": (("near",), "core", full, 5),
            "mod_core": (("mod",), "core", full, 6),
            "both_core": (("near", "mod"), "core", full, 7),
        }[name]

    def _copy(self, name, incoming):
        flips, axis, span, slot = self._step(name)
        if span[1] == 0:
            return None
        quad = self._quad(flips + (axis,) if incoming else flips, *span)
        other = {axis: 1 - self.here[axis]}
        return remote(quad, quad, self.sends, self.receives, self.count - 1 + slot, other)

    def start(self, *names):
        for name in names:
            copy = self._copy(name, False)
            if copy is not None:
                copy.start()

    def receive(self, *names):
        for name in names:
            copy = self._copy(name, True)
            if copy is not None:
                copy.wait_recv()

    def spread(self):
        self.start("near", "mod", "core")

    def cross(self):
        self.receive("near")
        self.start("near_mod", "near_core")
        self.receive("mod")
        self.start("mod_near", "mod_core")

    def close(self):
        self.receive("near_mod", "mod_near")
        self.start("both_core")

    def end(self):
        self.receive("core", "near_core", "mod_core", "both_core")
        for name in (
            "near", "mod", "near_mod", "mod_near", "core", "near_core", "mod_core", "both_core",
        ):
            copy = self._copy(name, False)
            if copy is not None:
                copy.wait_send()


def gather_scratch(weights, locals_):
    count = lax.axis_size("far")
    shapes = [pltpu.SemaphoreType.DMA((messages(count),))] * (2 * weights)
    return shapes + [pltpu.SemaphoreType.DMA((locals_,))]


def whole_shape(shard):
    return jax.ShapeDtypeStruct((2, lax.axis_size("far"), 2, 2) + shard.shape, LOW)


def first_kernel(*refs):
    qkv_s, proj_s, fc1_s, qkv_w, proj_w, fc1_w = refs[:6]
    *sems, local = refs[6:]
    qkv, proj, fc1 = (
        Gather(w, s, r) for w, s, r in zip((qkv_w, proj_w, fc1_w), sems[0::2], sems[1::2])
    )
    greet()
    qkv.start_far(qkv_s, local.at[0])
    proj.start_far(proj_s, local.at[1])
    fc1.start_far(fc1_s, local.at[2])
    qkv.finish_far(qkv_s, local.at[0])
    qkv.spread()
    qkv.cross()
    qkv.close()
    qkv.end()
    proj.finish_far(proj_s, local.at[1])
    fc1.finish_far(fc1_s, local.at[2])


def first_gather(qkv_s, proj_s, fc1_s):
    shards = (qkv_s, proj_s, fc1_s)
    return pl.pallas_call(
        first_kernel,
        out_shape=tuple(whole_shape(shard) for shard in shards),
        in_specs=[VMEM] * 3,
        out_specs=(ANY,) * 3,
        scratch_shapes=gather_scratch(3, 3),
        compiler_params=pltpu.CompilerParams(collective_id=0, has_side_effects=True),
        name="first_gather",
    )(*shards)


def lanes(shape): return lax.broadcasted_iota(jnp.int32, shape, 1)

def seg_codes(seg, n):
    lane = lanes((n, LANES))
    code = lane - HEAD
    inside = jnp.logical_and(code >= 0, code < 4)
    same = code == seg
    q = jnp.where(jnp.logical_and(inside, same), 1.0, 0.0)
    k = jnp.where(jnp.logical_and(inside, jnp.logical_not(same)), NEG, 0.0)
    return q, k

def head_of(wide_rows, start):
    return wide_rows[:, start:start+HEAD]

def pad_head(part, aug):
    n = part.shape[0]
    full = jnp.concatenate([part, jnp.zeros((n, LANES-HEAD), part.dtype)], axis=1)
    return jnp.where(lanes((n,LANES)) < HEAD, full, aug)

def attend_kernel(*refs):
    qkv_ref, seg_ref, fc2_s = refs[:3]
    mixed_ref, lse_ref, proj_w, fc1_w, fc2_w = refs[5:10]
    qh, kh, vh = refs[10:13]
    *sems, local = refs[13:]
    proj, fc1, fc2 = (
        Gather(w, s, r) for w, s, r in zip((proj_w, fc1_w, fc2_w), sems[0::2], sems[1::2])
    )
    greet()
    fc2.start_far(fc2_s, local.at[0])
    proj.spread()
    fc1.spread()

    T = qkv_ref.shape[0]
    D = HEADS*HEAD
    def fill(i, carry):
        rows = pl.ds(pl.multiple_of(i*CHUNK, CHUNK), CHUNK)
        lane = lanes((CHUNK, LANES))
        qc, kc = seg_codes(seg_ref[rows, :], CHUNK)
        qc = qc.astype(LOW); kc = kc.astype(LOW)
        ones = jnp.where(jnp.logical_and(lane >= HEAD, lane < HEAD+3), 1.0, 0.0).astype(LOW)
        for h in range(HEADS):
            qh[h, rows, :] = pad_head(qkv_ref[rows, h*HEAD:(h+1)*HEAD], qc)
            kh[h, rows, :] = pad_head(qkv_ref[rows, D+h*HEAD:D+(h+1)*HEAD], kc)
            vh[h, rows, :] = pad_head(qkv_ref[rows, 2*D+h*HEAD:2*D+(h+1)*HEAD], ones)
        return carry
    lax.fori_loop(0, T//CHUNK, fill, 0)
    lse_ref[...] = jnp.zeros_like(lse_ref)
    def head(h, carry):
        k = kh[h]; v = vh[h]
        for i in range(T//CHUNK):
            rows = pl.ds(i*CHUNK, CHUNK)
            q = qh[h, rows, :]
            s = lax.dot_general(q, k, (((1,),(1,)),((),())), preferred_element_type=WIDE)
            m = jnp.max(s, axis=1, keepdims=True)
            p = jnp.exp2((s - m)*(HEAD**-0.5*LOG2E)).astype(LOW)
            o = jnp.dot(p, v, preferred_element_type=WIDE)
            l = o[:, HEAD:HEAD+1]
            qh[h, rows, :] = (o / l).astype(LOW)
            col = m*HEAD**-0.5 + jnp.log(l)
            lse_ref[rows, :] = jnp.where(lanes((CHUNK,LANES)) == h, col, lse_ref[rows, :])
        tasks = {
            2: proj.cross,
            5: proj.close,
            7: proj.end,
            9: lambda: fc2.finish_far(fc2_s, local.at[0]),
            10: fc2.spread,
            11: fc1.cross,
        }
        for at, task in tasks.items():
            pl.when(h == at)(task)
        return carry
    lax.fori_loop(0, HEADS, head, 0)
    def drain(i, carry):
        rows = pl.ds(pl.multiple_of(i*CHUNK, CHUNK), CHUNK)
        mixed_ref[rows, :] = jnp.concatenate([qh[h, rows, :][:, :HEAD] for h in range(HEADS)], axis=1)
        return carry
    lax.fori_loop(0, T//CHUNK, drain, 0)
    fc1.close()
    fc2.cross()
    fc1.end()
    fc2.close()
    fc2.end()


def attend(qkv, segments, fc2_s, proj_w, fc1_w):
    tokens = qkv.shape[0]
    return pl.pallas_call(
        attend_kernel,
        out_shape=(
            jax.ShapeDtypeStruct((tokens, HEADS * HEAD), LOW),
            jax.ShapeDtypeStruct((tokens, LANES), WIDE),
            jax.ShapeDtypeStruct(proj_w.shape, LOW),
            jax.ShapeDtypeStruct(fc1_w.shape, LOW),
            whole_shape(fc2_s),
        ),
        in_specs=[VMEM] * 3 + [ANY] * 2,
        out_specs=(VMEM,) * 2 + (ANY,) * 3,
        scratch_shapes=[pltpu.VMEM((HEADS, tokens, LANES), LOW)] * 3 + gather_scratch(3, 1),
        input_output_aliases={3: 2, 4: 3},
        compiler_params=pltpu.CompilerParams(
            collective_id=1, has_side_effects=True, vmem_limit_bytes=50 * 2**20
        ),
        name="attend",
    )(qkv, segments.reshape(tokens, 1), fc2_s, proj_w, fc1_w)


def split3(v):
    hi = v.astype(LOW).astype(WIDE)
    mid = (v-hi).astype(LOW).astype(WIDE)
    lo = (v-hi-mid)
    return hi, mid, lo

def attend_back_kernel(qkv_ref, seg_ref, mixed_ref, lse_ref, up_ref, out_ref, qh, kh, vh, uh):
    T = qkv_ref.shape[0]
    D = HEADS*HEAD
    def fill(i, carry):
        rows = pl.ds(pl.multiple_of(i*CHUNK, CHUNK), CHUNK)
        lane = lanes((CHUNK, LANES))
        qc, kc = seg_codes(seg_ref[rows, :], CHUNK)
        kc = jnp.where(jnp.logical_and(lane >= HEAD+4, lane < HEAD+7), 1.0, kc).astype(LOW)
        ones = jnp.where(jnp.logical_and(lane >= HEAD, lane < HEAD+3), 1.0, 0.0).astype(LOW)
        def spread(v, at, base):
            hi, mid, lo = split3(v)
            return jnp.where(lane == at, hi, jnp.where(lane == at+1, mid, jnp.where(lane == at+2, lo, base)))
        for h in range(HEADS):
            a, b = h*HEAD, (h+1)*HEAD
            qa = spread(-lse_ref[rows, h:h+1]*(1.0/HEAD**-0.5), HEAD+4, qc).astype(LOW)
            qh[h, rows, :] = pad_head(qkv_ref[rows, a:b], qa)
            kh[h, rows, :] = pad_head(qkv_ref[rows, D+a:D+b], kc)
            vh[h, rows, :] = pad_head(qkv_ref[rows, 2*D+a:2*D+b], ones)
            u = up_ref[rows, a:b]
            delta = jnp.sum(u.astype(WIDE)*mixed_ref[rows, a:b].astype(WIDE), axis=1, keepdims=True)
            ua = spread(-delta, HEAD, jnp.zeros((CHUNK,LANES),WIDE)).astype(LOW)
            uh[h, rows, :] = pad_head(u, ua)
        return carry
    lax.fori_loop(0, T//CHUNK, fill, 0)
    NT = (((1,),(1,)),((),()))
    def head(h, carry):
        k = kh[h]; v = vh[h]
        kt = k.T
        dk = jnp.zeros((T, LANES), WIDE); dv = jnp.zeros((T, LANES), WIDE)
        for i in range(T//CHUNK):
            rows = pl.ds(i*CHUNK, CHUNK)
            q = qh[h, rows, :]; u = uh[h, rows, :]
            s = lax.dot_general(k, q, NT, preferred_element_type=WIDE)
            p = jnp.exp2(s*(HEAD**-0.5*LOG2E))
            dp = lax.dot_general(v, u, NT, preferred_element_type=WIDE)
            ds = (p*dp).astype(LOW)
            dv = dv + jnp.dot(p.astype(LOW), u, preferred_element_type=WIDE)
            dk = dk + jnp.dot(ds, q, preferred_element_type=WIDE)
            dqt = jnp.dot(kt, ds, preferred_element_type=WIDE)
            qh[h, rows, :] = (dqt.T*HEAD**-0.5).astype(LOW)
        kh[h] = (dk*HEAD**-0.5).astype(LOW)
        vh[h] = dv.astype(LOW)
        return carry
    lax.fori_loop(0, HEADS, head, 0)
    def drain(i, carry):
        rows = pl.ds(pl.multiple_of(i*CHUNK, CHUNK), CHUNK)
        out_ref[rows, :] = jnp.concatenate([g[h, rows, :][:, :HEAD] for g in (qh,kh,vh) for h in range(HEADS)], axis=1)
        return carry
    lax.fori_loop(0, T//CHUNK, drain, 0)


def attend_back(qkv, segments, mixed, lse, upstream):
    tokens = qkv.shape[0]
    return pl.pallas_call(
        attend_back_kernel,
        out_shape=jax.ShapeDtypeStruct((tokens, 3 * HEADS * HEAD), LOW),
        in_specs=[VMEM] * 5,
        out_specs=VMEM,
        scratch_shapes=[pltpu.VMEM((HEADS, tokens, LANES), LOW)] * 4,
        compiler_params=pltpu.CompilerParams(vmem_limit_bytes=63 * 2**20),
        name="attend_back",
    )(qkv, segments.reshape(tokens, 1), mixed, lse, upstream)


def swap(values, axis):
    return lax.ppermute(values, axis, [(0, 1), (1, 0)])


def shifted(values, distance, count):
    return lax.ppermute(values, "far", [(i, (i + distance) % count) for i in range(count)])


def scatter_gradient(left, right, first):
    count = lax.axis_size("far")
    here = lax.axis_index("far")
    near, core, half = lax.axis_index("near"), lax.axis_index("core"), lax.axis_index("mod")
    tokens = left.shape[0]
    blocks = left.reshape(tokens, count, 2, 2, -1)

    def piece(n, k, m):
        rows = lax.dynamic_index_in_dim(blocks, near ^ n, 2, False)
        rows = lax.dynamic_index_in_dim(rows, core ^ k, 2, False)
        columns = lax.dynamic_index_in_dim(right, half ^ m, 0, False)
        product = jnp.dot(
            rows.reshape(tokens, -1).T, columns, preferred_element_type=WIDE
        )
        return product.reshape(count, -1, columns.shape[1])

    def chip_sum(n, m):
        came = swap(piece(n, 1, m).astype(LOW), "core")
        return (piece(n, 0, m) + came.astype(WIDE)).astype(LOW)

    def joined(kept, sent, axis):
        return (kept.astype(WIDE) + swap(sent, axis).astype(WIDE)).astype(LOW)

    if first == "mod":
        far_side = chip_sum(1, 1)
        near_side = chip_sum(0, 1)
        sent = joined(chip_sum(1, 0), far_side, "mod")
        kept = joined(chip_sum(0, 0), near_side, "mod")
        total = joined(kept, sent, "near")
    else:
        far_side = chip_sum(1, 1)
        near_side = chip_sum(1, 0)
        sent = joined(chip_sum(0, 1), far_side, "near")
        kept = joined(chip_sum(0, 0), near_side, "near")
        total = joined(kept, sent, "mod")
    if count > 4:
        return lax.psum_scatter(total.astype(WIDE), "far", scatter_dimension=0, tiled=False)
    result = lax.dynamic_index_in_dim(total, here, 0, False).astype(WIDE)
    for distance in range(1, count):
        block = lax.dynamic_index_in_dim(total, (here + distance) % count, 0, False)
        result = result + shifted(block, distance, count).astype(WIDE)
    return result


def times(left, right):
    return jnp.dot(left, right, preferred_element_type=WIDE)


def times_back(left, right):
    return lax.dot_general(left, right, (((1,), (1,)), ((), ())), preferred_element_type=WIDE)


def body(
    x_in,
    cond,
    segments,
    out_grad,
    qkv_weight,
    qkv_moment,
    qkv_average,
    proj_weight,
    proj_moment,
    proj_average,
    fc1_weight,
    fc1_moment,
    fc1_average,
    fc2_weight,
    fc2_moment,
    fc2_average,
    bias_weight,
    bias_moment,
    bias_average,
    ada_weight,
    ada_moment,
    ada_average,
    adab_weight,
    adab_moment,
    adab_average,
):
    tokens, width = x_in.shape
    row_devices = lax.axis_size(ROWS)
    devices = lax.axis_size(ALL)
    row_index = lax.axis_index(ROWS)
    images = cond.shape[0] // 2

    cond_silu, silu_back = jax.vjp(jax.nn.silu, cond.astype(WIDE))
    silu_all = lax.all_gather(cond_silu.astype(LOW), ROWS, axis=0, tiled=True)
    ada_low = ada_weight.astype(LOW)
    ada_columns = lax.all_to_all(ada_low, ROWS, split_axis=1, concat_axis=0, tiled=True)
    adab_low = adab_weight.astype(LOW).astype(WIDE)
    mod_columns = (times(silu_all, ada_columns) + adab_low).astype(LOW)
    mod_rows = lax.all_to_all(mod_columns, ALL, split_axis=0, concat_axis=1, tiled=True)
    modulation = jnp.swapaxes(
        mod_rows.reshape(images, row_devices, 2, -1), 1, 2
    ).reshape(images, -1)

    bias_full = lax.all_gather(bias_weight.astype(LOW), ALL, axis=0, tiled=True).astype(WIDE)
    qkv_w, proj_w, fc1_w = first_gather(
        qkv_weight.astype(LOW), proj_weight.astype(LOW), fc1_weight.astype(LOW)
    )

    def joined(whole):
        return whole.reshape(2, -1, whole.shape[-1])

    qkv_low = joined(qkv_w)

    chooser = segments[:, None] == jnp.arange(images, dtype=jnp.int32)[None, :]
    per_token = times(chooser.astype(LOW), modulation)
    shift_attn, scale_attn, gate_attn, shift_mlp, scale_mlp, gate_mlp = [
        per_token[:, group * width : (group + 1) * width] for group in range(6)
    ]
    residual = x_in.astype(WIDE)
    first_norm, first_inverse = normalize(residual)
    attn_input = (first_norm * (1.0 + scale_attn) + shift_attn).astype(LOW)
    joint_proj = jnp.concatenate([times(attn_input, qkv_low[0]), times(attn_input, qkv_low[1])], 1)
    joint_bias = jnp.concatenate(
        [bias_full[0:width], jnp.zeros((width,), WIDE), bias_full[width : 2 * width]]
    )
    joint_rows = (joint_proj + joint_bias).astype(LOW)
    mixture, log_totals, proj_w, fc1_w, fc2_w = attend(
        joint_rows, segments, fc2_weight.astype(LOW), proj_w, fc1_w
    )
    proj_low, fc1_low, fc2_low = joined(proj_w), joined(fc1_w), joined(fc2_w)
    hidden_width = fc2_low.shape[1]
    attn_out = (
        jnp.concatenate([times(mixture, proj_low[0]), times(mixture, proj_low[1])], 1)
        + bias_full[2 * width : 3 * width]
    )
    residual_mid = residual + gate_attn * attn_out
    second_norm, second_inverse = normalize(residual_mid)
    mlp_input = (second_norm * (1.0 + scale_mlp) + shift_mlp).astype(LOW)
    pre_act = (
        jnp.concatenate([times(mlp_input, fc1_low[0]), times(mlp_input, fc1_low[1])], 1)
        + bias_full[3 * width : 3 * width + hidden_width]
    )
    hidden_full, gelu_back = jax.vjp(partial(jax.nn.gelu, approximate=True), pre_act)
    hidden = hidden_full.astype(LOW)
    branch = (
        jnp.concatenate([times(hidden, fc2_low[0]), times(hidden, fc2_low[1])], 1)
        + bias_full[3 * width + hidden_width :]
    )
    block_out = (residual_mid + gate_mlp * branch).astype(LOW)

    def halves(values):
        middle = values.shape[1] // 2
        return jnp.stack([values[:, :middle], values[:, middle:]])

    upstream = out_grad.astype(WIDE)
    branch_grad = (gate_mlp * upstream).astype(LOW)
    gate_mlp_grad = upstream * branch
    branch_halves = halves(branch_grad)
    fc2_shard = scatter_gradient(hidden, branch_halves, "mod")
    hidden_grad = times_back(branch_halves[0], fc2_low[0]) + times_back(branch_halves[1], fc2_low[1])
    pre_grad = gelu_back(hidden_grad)[0].astype(LOW)
    pre_halves = halves(pre_grad)
    fc1_shard = scatter_gradient(mlp_input, pre_halves, "near")
    mlp_grad = times_back(pre_halves[0], fc1_low[0]) + times_back(pre_halves[1], fc1_low[1])
    scale_mlp_grad = mlp_grad * second_norm
    middle_grad = upstream + normalize_back(
        mlp_grad * (1.0 + scale_mlp), second_norm, second_inverse
    )
    attn_grad = (gate_attn * middle_grad).astype(LOW)
    gate_attn_grad = middle_grad * attn_out
    attn_halves = halves(attn_grad)
    proj_shard = scatter_gradient(mixture, attn_halves, "mod")
    mixture_grad = (
        times_back(attn_halves[0], proj_low[0]) + times_back(attn_halves[1], proj_low[1])
    ).astype(LOW)
    joint_grad = attend_back(joint_rows, segments, mixture, log_totals, mixture_grad)
    query_grad = joint_grad[:, 0:width]
    value_grad = joint_grad[:, 2 * width :]
    joint_halves = halves(joint_grad)
    qkv_shard = scatter_gradient(attn_input, joint_halves, "near")
    input_grad = times_back(joint_halves[0], qkv_low[0]) + times_back(joint_halves[1], qkv_low[1])
    scale_attn_grad = input_grad * first_norm
    x_grad = middle_grad + normalize_back(
        input_grad * (1.0 + scale_attn), first_norm, first_inverse
    )

    token_mod_grad = jnp.concatenate(
        [input_grad, scale_attn_grad, gate_attn_grad, mlp_grad, scale_mlp_grad, gate_mlp_grad],
        axis=1,
    )
    slot_mod_grad = jnp.einsum(
        "ts,tc->sc", chooser.astype(WIDE), token_mod_grad, precision=lax.Precision.HIGHEST
    ).astype(LOW)
    half_grad = lax.all_to_all(slot_mod_grad, "mod", split_axis=1, concat_axis=0, tiled=True)
    mod_grad_all = lax.all_gather(half_grad, ROWS, axis=0, tiled=True)
    own_rows = ada_weight.shape[0]
    own_silu = lax.dynamic_slice_in_dim(silu_all, row_index * own_rows, own_rows, 1)
    ada_shard = jnp.einsum("ic,io->co", own_silu, mod_grad_all, preferred_element_type=WIDE)
    own_columns = adab_weight.shape[1]
    adab_shard = jnp.sum(
        lax.dynamic_slice_in_dim(mod_grad_all, row_index * own_columns, own_columns, 1).astype(WIDE),
        axis=0,
    )
    silu_part = times_back(mod_grad_all, ada_low)
    silu_part = lax.all_to_all(silu_part, ROWS, split_axis=0, concat_axis=1, tiled=True)
    cond_grad = silu_back(silu_part + swap(silu_part, "mod"))[0]

    grad_bias = jnp.concatenate(
        [
            jnp.sum(part.astype(WIDE), axis=0)
            for part in (query_grad, value_grad, attn_grad, pre_grad, branch_grad)
        ]
    ).reshape(devices, -1)
    bias_shard = jnp.sum(
        lax.all_to_all(grad_bias, ALL, split_axis=0, concat_axis=0, tiled=True), axis=0
    )

    rates = step_rates(tokens * devices)
    states_out = []
    states_out.extend(nesterov(qkv_weight, qkv_moment, qkv_average, qkv_shard, rates[0]))
    states_out.extend(nesterov(proj_weight, proj_moment, proj_average, proj_shard, rates[1]))
    states_out.extend(nesterov(fc1_weight, fc1_moment, fc1_average, fc1_shard, rates[2]))
    states_out.extend(nesterov(fc2_weight, fc2_moment, fc2_average, fc2_shard, rates[3]))
    states_out.extend(nesterov(bias_weight, bias_moment, bias_average, bias_shard, rates[4]))
    states_out.extend(nesterov(ada_weight, ada_moment, ada_average, ada_shard, rates[5]))
    states_out.extend(
        nesterov(adab_weight, adab_moment, adab_average, adab_shard.reshape(1, -1), rates[6])
    )
    return (block_out, x_grad, cond_grad) + tuple(states_out)


def solution(mesh):
    far = mesh.shape["dp"] // 4
    fine = Mesh(mesh.devices.reshape(far, 2, 2, mesh.shape["mod"]), ALL)
    tokens = P(ALL, None)
    images = P(ROWS, None)
    trunk = P(ROWS, "mod")
    bias = P(ALL)
    adab = P("mod", ROWS)
    states = (trunk,) * 12 + (bias,) * 3 + (trunk,) * 3 + (adab,) * 3
    return jax.shard_map(
        body,
        mesh=fine,
        in_specs=(tokens, images, bias, tokens) + states,
        out_specs=(tokens, tokens, images) + states,
        check_vma=False,
    )
```

```python
from functools import partial

import jax
import jax.numpy as jnp
from jax import lax
from jax.experimental import pallas as pl
from jax.experimental.pallas import tpu as pltpu
from jax.sharding import Mesh
from jax.sharding import PartitionSpec as P

D = 1152
HEADS = 16
HEAD = 72
FF = 4608
LANES = 128
CHUNK = 256

ROWS = ("far", "near", "core")
ALL = ("far", "near", "core", "mod")
LOW = jnp.bfloat16
WIDE = jnp.float32
LOG2E = 1.4426950408889634
NEG = -1e30
MESH = pl.DeviceIdType.MESH
VMEM = pl.BlockSpec(memory_space=pltpu.VMEM)
ANY = pl.BlockSpec(memory_space=pl.ANY)

EPS = 1e-06
MOMENTUM = 0.9
DECAY = 0.5


def normalize(values):
    centre = values - jnp.mean(values, axis=-1, keepdims=True)
    inverse = lax.rsqrt(jnp.mean(centre * centre, axis=-1, keepdims=True) + EPS)
    return (centre * inverse, inverse)


def normalize_back(upstream, normed, inverse):
    return inverse * (
        upstream
        - jnp.mean(upstream, axis=-1, keepdims=True)
        - normed * jnp.mean(upstream * normed, axis=-1, keepdims=True)
    )


def step_rates(tokens_all):
    base_rate = tokens_all ** (-0.5)
    return (
        2.5 * D ** (-0.5) * base_rate,
        3.0 * D ** (-0.5) * base_rate,
        3.3 * D ** (-0.5) * base_rate,
        2.8 * FF ** (-0.5) * base_rate,
        0.5 * base_rate,
        2.0 * D ** (-0.5) * base_rate,
        0.3 * base_rate,
    )


def nesterov(weight, moment, average, gradient, rate):
    moment = MOMENTUM * moment + gradient
    weight = weight - rate * (gradient + MOMENTUM * moment)
    average = DECAY * average + (1.0 - DECAY) * weight
    return (weight, moment, average)


def places():
    return {name: lax.axis_index(name) for name in ALL}


def greet():
    here = places()
    count = lax.axis_size("far")
    others = [dict(far=lax.rem(here["far"] + d, count)) for d in range(1, count)]
    others += [{name: 1 - here[name]} for name in ("near", "core", "mod")]
    barrier = pltpu.get_barrier_semaphore()
    for other in others:
        pl.semaphore_signal(barrier, inc=1, device_id=other, device_id_type=MESH)
    pl.semaphore_wait(barrier, len(others))


def remote(source, target, sends, receives, slot, other):
    return pltpu.make_async_remote_copy(
        src_ref=source,
        dst_ref=target,
        send_sem=sends.at[slot],
        recv_sem=receives.at[slot],
        device_id=other,
        device_id_type=MESH,
    )


def messages(count):
    return count - 1 + 8


class Gather:
    def __init__(self, whole, sends, receives):
        self.whole, self.sends, self.receives = whole, sends, receives
        self.here = places()
        self.count = lax.axis_size("far")
        rows = whole.shape[4]
        self.rows = rows
        self.split = rows if rows % 16 else 8 * ((rows // 8 + 1) // 2)

    def _block(self, far):
        return self.whole.at[self.here["mod"], far, self.here["near"], self.here["core"]]

    def _far(self, shard, distance):
        far = self.here["far"]
        other = dict(far=lax.rem(far + distance, self.count))
        return remote(shard, self._block(far), self.sends, self.receives, distance - 1, other)

    def _far_came(self, shard, distance):
        origin = lax.rem(self.here["far"] + self.count - distance, self.count)
        return remote(
            shard, self._block(origin), self.sends, self.receives, distance - 1, dict(far=origin)
        )

    def start_far(self, shard, local):
        pltpu.make_async_copy(shard, self._block(self.here["far"]), local).start()
        for distance in range(1, self.count):
            self._far(shard, distance).start()

    def finish_far(self, shard, local):
        pltpu.make_async_copy(shard, self._block(self.here["far"]), local).wait()
        for distance in range(1, self.count):
            self._far(shard, distance).wait_send()
            self._far_came(shard, distance).wait_recv()

    def _quad(self, flips, first, size):
        near, core, mod = (
            1 - self.here[name] if name in flips else self.here[name] for name in ("near", "core", "mod")
        )
        return self.whole.at[mod, :, near, core, pl.ds(first, size)]

    def _step(self, name):
        head, rest = (0, self.split), (self.split, self.rows - self.split)
        full = (0, self.rows)
        return {
            "near": ((), "near", full, 0),
            "mod": ((), "mod", full, 1),
            "near_mod": (("near",), "mod", head, 2),
            "mod_near": (("mod",), "near", rest, 3),
            "core": ((), "core", full, 4),
            "near_core": (("near",), "core", full, 5),
            "mod_core": (("mod",), "core", full, 6),
            "both_core": (("near", "mod"), "core", full, 7),
        }[name]

    def _copy(self, name, incoming):
        flips, axis, span, slot = self._step(name)
        if span[1] == 0:
            return None
        quad = self._quad(flips + (axis,) if incoming else flips, *span)
        other = {axis: 1 - self.here[axis]}
        return remote(quad, quad, self.sends, self.receives, self.count - 1 + slot, other)

    def start(self, *names):
        for name in names:
            copy = self._copy(name, False)
            if copy is not None:
                copy.start()

    def receive(self, *names):
        for name in names:
            copy = self._copy(name, True)
            if copy is not None:
                copy.wait_recv()

    def spread(self):
        self.start("near", "mod", "core")

    def cross(self):
        self.receive("near")
        self.start("near_mod", "near_core")
        self.receive("mod")
        self.start("mod_near", "mod_core")

    def close(self):
        self.receive("near_mod", "mod_near")
        self.start("both_core")

    def end(self):
        self.receive("core", "near_core", "mod_core", "both_core")
        for name in (
            "near", "mod", "near_mod", "mod_near", "core", "near_core", "mod_core", "both_core",
        ):
            copy = self._copy(name, False)
            if copy is not None:
                copy.wait_send()


def gather_scratch(weights, locals_):
    count = lax.axis_size("far")
    shapes = [pltpu.SemaphoreType.DMA((messages(count),))] * (2 * weights)
    return shapes + [pltpu.SemaphoreType.DMA((locals_,))]


def whole_shape(shard):
    return jax.ShapeDtypeStruct((2, lax.axis_size("far"), 2, 2) + shard.shape, LOW)


def first_kernel(*refs):
    qkv_s, proj_s, fc1_s, qkv_w, proj_w, fc1_w = refs[:6]
    *sems, local = refs[6:]
    qkv, proj, fc1 = (
        Gather(w, s, r) for w, s, r in zip((qkv_w, proj_w, fc1_w), sems[0::2], sems[1::2])
    )
    greet()
    qkv.start_far(qkv_s, local.at[0])
    proj.start_far(proj_s, local.at[1])
    fc1.start_far(fc1_s, local.at[2])
    qkv.finish_far(qkv_s, local.at[0])
    qkv.spread()
    qkv.cross()
    qkv.close()
    qkv.end()
    proj.finish_far(proj_s, local.at[1])
    fc1.finish_far(fc1_s, local.at[2])


def first_gather(qkv_s, proj_s, fc1_s):
    shards = (qkv_s, proj_s, fc1_s)
    return pl.pallas_call(
        first_kernel,
        out_shape=tuple(whole_shape(shard) for shard in shards),
        in_specs=[VMEM] * 3,
        out_specs=(ANY,) * 3,
        scratch_shapes=gather_scratch(3, 3),
        compiler_params=pltpu.CompilerParams(collective_id=0, has_side_effects=True),
        name="first_gather",
    )(*shards)


def lanes(shape): return lax.broadcasted_iota(jnp.int32, shape, 1)

def seg_codes(seg, n):
    lane = lanes((n, LANES))
    code = lane - HEAD
    inside = jnp.logical_and(code >= 0, code < 4)
    same = code == seg
    q = jnp.where(jnp.logical_and(inside, same), 1.0, 0.0)
    k = jnp.where(jnp.logical_and(inside, jnp.logical_not(same)), NEG, 0.0)
    return q, k

def head_of(wide_rows, start):
    return wide_rows[:, start:start+HEAD]

def pad_head(part, aug):
    n = part.shape[0]
    full = jnp.concatenate([part, jnp.zeros((n, LANES-HEAD), part.dtype)], axis=1)
    return jnp.where(lanes((n,LANES)) < HEAD, full, aug)

def attend_kernel(*refs):
    qkv_ref, seg_ref, fc2_s = refs[:3]
    mixed_ref, lse_ref, proj_w, fc1_w, fc2_w = refs[5:10]
    qh, kh, vh = refs[10:13]
    *sems, local = refs[13:]
    proj, fc1, fc2 = (
        Gather(w, s, r) for w, s, r in zip((proj_w, fc1_w, fc2_w), sems[0::2], sems[1::2])
    )
    greet()
    fc2.start_far(fc2_s, local.at[0])
    proj.spread()
    fc1.spread()

    T = qkv_ref.shape[0]
    D = HEADS*HEAD
    def fill(i, carry):
        rows = pl.ds(pl.multiple_of(i*CHUNK, CHUNK), CHUNK)
        lane = lanes((CHUNK, LANES))
        qc, kc = seg_codes(seg_ref[rows, :], CHUNK)
        qc = qc.astype(LOW); kc = kc.astype(LOW)
        ones = jnp.where(jnp.logical_and(lane >= HEAD, lane < HEAD+3), 1.0, 0.0).astype(LOW)
        for h in range(HEADS):
            qh[h, rows, :] = pad_head(qkv_ref[rows, h*HEAD:(h+1)*HEAD], qc)
            kh[h, rows, :] = pad_head(qkv_ref[rows, D+h*HEAD:D+(h+1)*HEAD], kc)
            vh[h, rows, :] = pad_head(qkv_ref[rows, 2*D+h*HEAD:2*D+(h+1)*HEAD], ones)
        return carry
    lax.fori_loop(0, T//CHUNK, fill, 0)
    lse_ref[...] = jnp.zeros_like(lse_ref)
    def head(h, carry):
        k = kh[h]; v = vh[h]
        for i in range(T//CHUNK):
            rows = pl.ds(i*CHUNK, CHUNK)
            q = qh[h, rows, :]
            s = lax.dot_general(q, k, (((1,),(1,)),((),())), preferred_element_type=WIDE)
            m = jnp.max(s, axis=1, keepdims=True)
            p = jnp.exp2((s - m)*(HEAD**-0.5*LOG2E)).astype(LOW)
            o = jnp.dot(p, v, preferred_element_type=WIDE)
            l = o[:, HEAD:HEAD+1]
            qh[h, rows, :] = (o / l).astype(LOW)
            col = m*HEAD**-0.5 + jnp.log(l)
            lse_ref[rows, :] = jnp.where(lanes((CHUNK,LANES)) == h, col, lse_ref[rows, :])
        tasks = {
            2: proj.cross,
            5: proj.close,
            7: proj.end,
            9: lambda: fc2.finish_far(fc2_s, local.at[0]),
            10: fc2.spread,
            11: fc1.cross,
        }
        for at, task in tasks.items():
            pl.when(h == at)(task)
        return carry
    lax.fori_loop(0, HEADS, head, 0)
    def drain(i, carry):
        rows = pl.ds(pl.multiple_of(i*CHUNK, CHUNK), CHUNK)
        mixed_ref[rows, :] = jnp.concatenate([qh[h, rows, :][:, :HEAD] for h in range(HEADS)], axis=1)
        return carry
    lax.fori_loop(0, T//CHUNK, drain, 0)
    fc1.close()
    fc2.cross()
    fc1.end()
    fc2.close()
    fc2.end()


def attend(qkv, segments, fc2_s, proj_w, fc1_w):
    tokens = qkv.shape[0]
    return pl.pallas_call(
        attend_kernel,
        out_shape=(
            jax.ShapeDtypeStruct((tokens, HEADS * HEAD), LOW),
            jax.ShapeDtypeStruct((tokens, LANES), WIDE),
            jax.ShapeDtypeStruct(proj_w.shape, LOW),
            jax.ShapeDtypeStruct(fc1_w.shape, LOW),
            whole_shape(fc2_s),
        ),
        in_specs=[VMEM] * 3 + [ANY] * 2,
        out_specs=(VMEM,) * 2 + (ANY,) * 3,
        scratch_shapes=[pltpu.VMEM((HEADS, tokens, LANES), LOW)] * 3 + gather_scratch(3, 1),
        input_output_aliases={3: 2, 4: 3},
        compiler_params=pltpu.CompilerParams(
            collective_id=1, has_side_effects=True, vmem_limit_bytes=50 * 2**20
        ),
        name="attend",
    )(qkv, segments.reshape(tokens, 1), fc2_s, proj_w, fc1_w)


def row_spans(rows):
    first = rows if rows % 16 else 8 * ((rows // 8 + 1) // 2)
    return [(0, first)] + ([(first, rows - first)] if first < rows else [])


class Reduce:
    def __init__(self, quads, span, first, buffers, sems):
        self.quads, self.span, self.first = quads, span, first
        self.second = "near" if first == "mod" else "mod"
        self.came_both, self.came_first, self.came_second, self.joint, self.total_, self.came_far = buffers
        self.sends, self.receives, self.locals_ = sems
        self.here = places()
        self.count = lax.axis_size("far")

    @staticmethod
    def scratch(count, span, columns, own_total=True):
        block = (count, span[1], columns)
        buffers = [pltpu.VMEM(block, LOW)] * (5 if own_total else 4)
        buffers += [pltpu.VMEM((count - 1,) + block[1:], LOW)]
        return buffers + [pltpu.SemaphoreType.DMA((count + 2,))] * 2 + [pltpu.SemaphoreType.DMA((2,))]

    def _part(self, *flips):
        quad = self.quads["near" in flips, "mod" in flips]
        return quad.at[:, pl.ds(*self.span)]

    def _swap(self, source, target, slot, axis):
        return remote(source, target, self.sends, self.receives, slot, {axis: 1 - self.here[axis]})

    def _both(self):
        return self._swap(self._part("near", "mod"), self.came_both, 0, self.first)

    def _first(self):
        return self._swap(self._part(self.first), self.came_first, 1, self.first)

    def _second(self):
        return self._swap(self.joint, self.came_second, 2, self.second)

    def _local(self, source, target, slot):
        return pltpu.make_async_copy(source, target, self.locals_.at[slot])

    def _load(self, number):
        if number == 0:
            return self._local(self._part(self.second), self.joint, 0)
        return self._local(self._part(), self.total_, 1)

    def _far(self, distance):
        target = lax.rem(self.here["far"] + distance, self.count)
        return remote(
            self.total_.at[target],
            self.came_far.at[distance - 1],
            self.sends,
            self.receives,
            2 + distance,
            dict(far=target),
        )

    def start(self):
        self._both().start()
        self._first().start()
        self._load(0).start()
        self._load(1).start()

    def merge(self):
        self._load(0).wait()
        self._both().wait_recv()

        def add(at, carry):
            self.joint[at] = (self.joint[at].astype(WIDE) + self.came_both[at].astype(WIDE)).astype(LOW)
            return carry

        lax.fori_loop(0, self.count, add, 0)
        self._second().start()

    def total(self):
        self._load(1).wait()
        self._first().wait_recv()
        self._second().wait_recv()

        def add(at, carry):
            self.total_[at] = (
                self.total_[at].astype(WIDE)
                + self.came_first[at].astype(WIDE)
                + self.came_second[at].astype(WIDE)
            ).astype(LOW)
            return carry

        lax.fori_loop(0, self.count, add, 0)
        self._both().wait_send()
        self._first().wait_send()
        self._second().wait_send()

    def start_far(self):
        for distance in range(1, self.count):
            self._far(distance).start()

    def final(self, out):
        value = self.total_[self.here["far"]].astype(WIDE)
        for distance in range(1, self.count):
            self._far(distance).wait_recv()
            value = value + self.came_far[distance - 1].astype(WIDE)
        out[pl.ds(*self.span), :] = value
        for distance in range(1, self.count):
            self._far(distance).wait_send()


ORDERS = ("mod", "near")


def run(parts, *names):
    for part in parts:
        for name in names:
            getattr(part, name)()


def reduce_kernel_parts(quads, scratch, totals=None):
    by_flips = dict(zip(((False, False), (True, False), (False, True), (True, True)), quads))
    parts = []
    for number, span in enumerate(row_spans(quads[0].shape[1])):
        used = 6 if totals is None else 5
        buffers, scratch = list(scratch[:used]), scratch[used:]
        if totals is not None:
            buffers.insert(4, totals[number])
        sems, scratch = scratch[:3], scratch[3:]
        parts.append(Reduce(by_flips, span, ORDERS[number], buffers, sems))
    return parts, scratch


def reduce_scratch(shape, own_total=True):
    count, rows, columns = shape
    shapes = []
    for span in row_spans(rows):
        shapes += Reduce.scratch(count, span, columns, own_total)
    return shapes


def last_kernel(*refs, spans):
    quads, totals, refs = refs[:4], refs[4 : 4 + spans], refs[4 + spans :]
    qkv_out, fc1_out, *scratch = refs
    qkv, scratch = reduce_kernel_parts(quads, scratch)
    fc1 = []
    for total, span in zip(totals, row_spans(fc1_out.shape[0])):
        buffers = (None, None, None, None, total, scratch[0])
        fc1.append(Reduce(None, span, "mod", buffers, (scratch[1], scratch[2], None)))
        scratch = scratch[3:]
    greet()
    run(qkv, "start")
    run(fc1, "start_far")
    run(qkv, "merge")
    run(qkv, "total", "start_far")
    for part in fc1:
        part.final(fc1_out)
    for part in qkv:
        part.final(qkv_out)


def last_scatter(quads, totals):
    count, rows, columns = quads[0].shape
    fc1_columns = totals[0].shape[2]
    fc1_scratch = []
    for total in totals:
        fc1_scratch += [
            pltpu.VMEM((count - 1,) + total.shape[1:], LOW),
            pltpu.SemaphoreType.DMA((count + 2,)),
            pltpu.SemaphoreType.DMA((count + 2,)),
        ]
    return pl.pallas_call(
        partial(last_kernel, spans=len(totals)),
        out_shape=(
            jax.ShapeDtypeStruct((rows, columns), WIDE),
            jax.ShapeDtypeStruct((sum(total.shape[1] for total in totals), fc1_columns), WIDE),
        ),
        in_specs=[ANY] * 4 + [VMEM] * len(totals),
        out_specs=(VMEM,) * 2,
        scratch_shapes=reduce_scratch(quads[0].shape) + fc1_scratch,
        compiler_params=pltpu.CompilerParams(
            collective_id=3, has_side_effects=True, vmem_limit_bytes=50 * 2**20
        ),
        name="last_scatter",
    )(*quads, *totals)


def split3(v):
    hi = v.astype(LOW).astype(WIDE)
    mid = (v - hi).astype(LOW).astype(WIDE)
    lo = v - hi - mid
    return hi, mid, lo


def attend_back_kernel(*refs, spans):
    qkv_ref, seg_ref, mixed_ref, lse_ref, up_ref = refs[:5]
    fc2_q, fc1_q, proj_q = refs[5:9], refs[9:13], refs[13:17]
    out_ref, fc2_out, proj_out = refs[17:20]
    fc1_totals = refs[20 : 20 + spans]
    qh, kh, vh, uh, stage, stage_sems, leave, leave_sems, *scratch = refs[20 + spans :]
    fc2, scratch = reduce_kernel_parts(fc2_q, scratch)
    proj, scratch = reduce_kernel_parts(proj_q, scratch)
    fc1, scratch = reduce_kernel_parts(fc1_q, scratch, fc1_totals)
    T = mixed_ref.shape[0]
    chunks = T // CHUNK
    greet()
    run(fc2, "start")
    run(proj, "start")

    def load(i):
        rows = pl.ds(pl.multiple_of(i * CHUNK, CHUNK), CHUNK)
        slot = lax.rem(i, 2)
        return pltpu.make_async_copy(qkv_ref.at[rows], stage.at[slot], stage_sems.at[slot])

    load(0).start()

    def fill(i, carry):
        rows = pl.ds(pl.multiple_of(i * CHUNK, CHUNK), CHUNK)

        @pl.when(i + 1 < chunks)
        def _():
            load(i + 1).start()

        load(i).wait()
        qkv = stage.at[lax.rem(i, 2)]
        lane = lanes((CHUNK, LANES))
        qc, kc = seg_codes(seg_ref[rows, :], CHUNK)
        kc = jnp.where(jnp.logical_and(lane >= HEAD + 4, lane < HEAD + 7), 1.0, kc).astype(LOW)
        ones = jnp.where(jnp.logical_and(lane >= HEAD, lane < HEAD + 3), 1.0, 0.0).astype(LOW)

        def spread(v, at, base):
            hi, mid, lo = split3(v)
            return jnp.where(
                lane == at, hi, jnp.where(lane == at + 1, mid, jnp.where(lane == at + 2, lo, base))
            )

        for h in range(HEADS):
            a, b = h * HEAD, (h + 1) * HEAD
            qa = spread(-lse_ref[rows, h : h + 1] * HEAD**0.5, HEAD + 4, qc).astype(LOW)
            qh[h, rows, :] = pad_head(qkv[:, a:b], qa)
            kh[h, rows, :] = pad_head(qkv[:, D + a : D + b], kc)
            vh[h, rows, :] = pad_head(qkv[:, 2 * D + a : 2 * D + b], ones)
            u = up_ref[rows, a:b]
            delta = jnp.sum(u.astype(WIDE) * mixed_ref[rows, a:b].astype(WIDE), axis=1, keepdims=True)
            ua = spread(-delta, HEAD, jnp.zeros((CHUNK, LANES), WIDE)).astype(LOW)
            uh[h, rows, :] = pad_head(u, ua)
        return carry

    lax.fori_loop(0, chunks, fill, 0)
    across = (((1,), (1,)), ((), ()))
    tasks = {
        2: lambda: (run(fc2, "merge"), run(fc1, "start")),
        7: lambda: run(proj, "merge"),
        10: lambda: run(fc2, "total", "start_far"),
        12: lambda: run(proj, "total", "start_far"),
        13: lambda: run(fc1, "merge"),
    }

    def head(h, carry):
        k = kh[h]
        v = vh[h]
        kt = k.T
        dk = jnp.zeros((T, LANES), WIDE)
        dv = jnp.zeros((T, LANES), WIDE)
        for i in range(chunks):
            rows = pl.ds(i * CHUNK, CHUNK)
            q = qh[h, rows, :]
            u = uh[h, rows, :]
            s = lax.dot_general(k, q, across, preferred_element_type=WIDE)
            p = jnp.exp2(s * (HEAD**-0.5 * LOG2E))
            dp = lax.dot_general(v, u, across, preferred_element_type=WIDE)
            ds = (p * dp).astype(LOW)
            dv = dv + jnp.dot(p.astype(LOW), u, preferred_element_type=WIDE)
            dk = dk + jnp.dot(ds, q, preferred_element_type=WIDE)
            dqt = jnp.dot(kt, ds, preferred_element_type=WIDE)
            qh[h, rows, :] = (dqt.T * HEAD**-0.5).astype(LOW)
        kh[h] = (dk * HEAD**-0.5).astype(LOW)
        vh[h] = dv.astype(LOW)
        for at, task in tasks.items():

            @pl.when(h == at)
            def _(task=task):
                task()

        return carry

    lax.fori_loop(0, HEADS, head, 0)

    def store(i, side):
        rows = pl.ds(pl.multiple_of(i * CHUNK, CHUNK), CHUNK)
        return pltpu.make_async_copy(
            leave.at[side], out_ref.at[side, rows], leave_sems.at[side]
        )

    def drain(i, carry):
        rows = pl.ds(pl.multiple_of(i * CHUNK, CHUNK), CHUNK)
        parts = [g[h, rows, :][:, :HEAD] for g in (qh, kh, vh) for h in range(HEADS)]
        for side in range(2):

            @pl.when(i > 0)
            def _(side=side):
                store(i - 1, side).wait()

            own = parts[side * len(parts) // 2 : (side + 1) * len(parts) // 2]
            leave[side] = jnp.concatenate(own, axis=1)
            store(i, side).start()
        return carry

    lax.fori_loop(0, chunks, drain, 0)
    run(fc1, "total")
    for side in range(2):
        store(chunks - 1, side).wait()
    for part in fc2:
        part.final(fc2_out)
    for part in proj:
        part.final(proj_out)


def attend_back(qkv, segments, mixed, lse, upstream, fc2_q, fc1_q, proj_q):
    tokens = qkv.shape[0]
    spans = row_spans(fc1_q[0].shape[1])

    def shard(quads):
        return jax.ShapeDtypeStruct(quads[0].shape[1:], WIDE)

    out = pl.pallas_call(
        partial(attend_back_kernel, spans=len(spans)),
        out_shape=(
            jax.ShapeDtypeStruct((2, tokens, 3 * HEADS * HEAD // 2), LOW),
            shard(fc2_q),
            shard(proj_q),
        )
        + tuple(
            jax.ShapeDtypeStruct((fc1_q[0].shape[0], span[1], fc1_q[0].shape[2]), LOW)
            for span in spans
        ),
        in_specs=[ANY] + [VMEM] * 4 + [ANY] * 12,
        out_specs=(ANY, VMEM, VMEM) + (VMEM,) * len(spans),
        scratch_shapes=[pltpu.VMEM((HEADS, tokens, LANES), LOW)] * 4
        + [pltpu.VMEM((2, CHUNK, 3 * HEADS * HEAD), LOW), pltpu.SemaphoreType.DMA((2,))]
        + [pltpu.VMEM((2, CHUNK, 3 * HEADS * HEAD // 2), LOW), pltpu.SemaphoreType.DMA((2,))]
        + reduce_scratch(fc2_q[0].shape)
        + reduce_scratch(proj_q[0].shape)
        + reduce_scratch(fc1_q[0].shape, False),
        compiler_params=pltpu.CompilerParams(
            collective_id=2, has_side_effects=True, vmem_limit_bytes=63 * 2**20
        ),
        name="attend_back",
    )(qkv, segments.reshape(tokens, 1), mixed, lse, upstream, *fc2_q, *fc1_q, *proj_q)
    return out[0], out[1], out[2], out[3:]


def swap(values, axis):
    return lax.ppermute(values, axis, [(0, 1), (1, 0)])


def chip_quads(left, right):
    count = lax.axis_size("far")
    near, core, half = lax.axis_index("near"), lax.axis_index("core"), lax.axis_index("mod")
    tokens = left.shape[0]
    blocks = left.reshape(tokens, count, 2, 2, -1)

    def piece(n, k, m):
        rows = lax.dynamic_index_in_dim(blocks, near ^ n, 2, False)
        rows = lax.dynamic_index_in_dim(rows, core ^ k, 2, False)
        columns = lax.dynamic_index_in_dim(right, half ^ m, 0, False)
        product = times(rows.reshape(tokens, -1).T, columns)
        return product.reshape(count, -1, columns.shape[1])

    def chip_sum(n, m):
        came = swap(piece(n, 1, m).astype(LOW), "core")
        return (piece(n, 0, m) + came.astype(WIDE)).astype(LOW)

    return [chip_sum(n, m) for n, m in ((0, 0), (1, 0), (0, 1), (1, 1))]


def times(left, right):
    return jnp.dot(left, right, preferred_element_type=WIDE)


def times_back(left, right):
    return lax.dot_general(left, right, (((1,), (1,)), ((), ())), preferred_element_type=WIDE)


def body(
    x_in,
    cond,
    segments,
    out_grad,
    qkv_weight,
    qkv_moment,
    qkv_average,
    proj_weight,
    proj_moment,
    proj_average,
    fc1_weight,
    fc1_moment,
    fc1_average,
    fc2_weight,
    fc2_moment,
    fc2_average,
    bias_weight,
    bias_moment,
    bias_average,
    ada_weight,
    ada_moment,
    ada_average,
    adab_weight,
    adab_moment,
    adab_average,
):
    tokens, width = x_in.shape
    row_devices = lax.axis_size(ROWS)
    devices = lax.axis_size(ALL)
    row_index = lax.axis_index(ROWS)
    images = cond.shape[0] // 2

    cond_silu, silu_back = jax.vjp(jax.nn.silu, cond.astype(WIDE))
    silu_all = lax.all_gather(cond_silu.astype(LOW), ROWS, axis=0, tiled=True)
    ada_low = ada_weight.astype(LOW)
    ada_columns = lax.all_to_all(ada_low, ROWS, split_axis=1, concat_axis=0, tiled=True)
    adab_low = adab_weight.astype(LOW).astype(WIDE)
    mod_columns = (times(silu_all, ada_columns) + adab_low).astype(LOW)
    mod_rows = lax.all_to_all(mod_columns, ALL, split_axis=0, concat_axis=1, tiled=True)
    modulation = jnp.swapaxes(
        mod_rows.reshape(images, row_devices, 2, -1), 1, 2
    ).reshape(images, -1)

    bias_full = lax.all_gather(bias_weight.astype(LOW), ALL, axis=0, tiled=True).astype(WIDE)
    qkv_w, proj_w, fc1_w = first_gather(
        qkv_weight.astype(LOW), proj_weight.astype(LOW), fc1_weight.astype(LOW)
    )

    def joined(whole):
        return whole.reshape(2, -1, whole.shape[-1])

    qkv_low = joined(qkv_w)

    chooser = segments[:, None] == jnp.arange(images, dtype=jnp.int32)[None, :]
    per_token = times(chooser.astype(LOW), modulation)
    shift_attn, scale_attn, gate_attn, shift_mlp, scale_mlp, gate_mlp = [
        per_token[:, group * width : (group + 1) * width] for group in range(6)
    ]
    residual = x_in.astype(WIDE)
    first_norm, first_inverse = normalize(residual)
    attn_input = (first_norm * (1.0 + scale_attn) + shift_attn).astype(LOW)
    joint_proj = jnp.concatenate([times(attn_input, qkv_low[0]), times(attn_input, qkv_low[1])], 1)
    joint_bias = jnp.concatenate(
        [bias_full[0:width], jnp.zeros((width,), WIDE), bias_full[width : 2 * width]]
    )
    joint_rows = (joint_proj + joint_bias).astype(LOW)
    mixture, log_totals, proj_w, fc1_w, fc2_w = attend(
        joint_rows, segments, fc2_weight.astype(LOW), proj_w, fc1_w
    )
    proj_low, fc1_low, fc2_low = joined(proj_w), joined(fc1_w), joined(fc2_w)
    hidden_width = fc2_low.shape[1]
    attn_out = (
        jnp.concatenate([times(mixture, proj_low[0]), times(mixture, proj_low[1])], 1)
        + bias_full[2 * width : 3 * width]
    )
    residual_mid = residual + gate_attn * attn_out
    second_norm, second_inverse = normalize(residual_mid)
    mlp_input = (second_norm * (1.0 + scale_mlp) + shift_mlp).astype(LOW)
    pre_act = (
        jnp.concatenate([times(mlp_input, fc1_low[0]), times(mlp_input, fc1_low[1])], 1)
        + bias_full[3 * width : 3 * width + hidden_width]
    )
    hidden_full, gelu_back = jax.vjp(partial(jax.nn.gelu, approximate=True), pre_act)
    hidden = hidden_full.astype(LOW)
    branch = (
        jnp.concatenate([times(hidden, fc2_low[0]), times(hidden, fc2_low[1])], 1)
        + bias_full[3 * width + hidden_width :]
    )
    block_out = (residual_mid + gate_mlp * branch).astype(LOW)

    def halves(values):
        middle = values.shape[1] // 2
        return jnp.stack([values[:, :middle], values[:, middle:]])

    upstream = out_grad.astype(WIDE)
    branch_grad = (gate_mlp * upstream).astype(LOW)
    gate_mlp_grad = upstream * branch
    branch_halves = halves(branch_grad)
    fc2_quads = chip_quads(hidden, branch_halves)
    hidden_grad = times_back(branch_halves[0], fc2_low[0]) + times_back(branch_halves[1], fc2_low[1])
    pre_grad = gelu_back(hidden_grad)[0].astype(LOW)
    pre_halves = halves(pre_grad)
    fc1_quads = chip_quads(mlp_input, pre_halves)
    mlp_grad = times_back(pre_halves[0], fc1_low[0]) + times_back(pre_halves[1], fc1_low[1])
    scale_mlp_grad = mlp_grad * second_norm
    middle_grad = upstream + normalize_back(
        mlp_grad * (1.0 + scale_mlp), second_norm, second_inverse
    )
    attn_grad = (gate_attn * middle_grad).astype(LOW)
    gate_attn_grad = middle_grad * attn_out
    attn_halves = halves(attn_grad)
    proj_quads = chip_quads(mixture, attn_halves)
    mixture_grad = (
        times_back(attn_halves[0], proj_low[0]) + times_back(attn_halves[1], proj_low[1])
    ).astype(LOW)
    joint_halves, fc2_shard, proj_shard, fc1_totals = attend_back(
        joint_rows,
        segments,
        mixture,
        log_totals,
        mixture_grad,
        fc2_quads,
        fc1_quads,
        proj_quads,
    )
    query_grad = joint_halves[0, :, 0:width]
    value_grad = joint_halves[1, :, width // 2 :]
    qkv_quads = chip_quads(attn_input, joint_halves)
    qkv_shard, fc1_shard = last_scatter(qkv_quads, fc1_totals)
    input_grad = times_back(joint_halves[0], qkv_low[0]) + times_back(joint_halves[1], qkv_low[1])
    scale_attn_grad = input_grad * first_norm
    x_grad = middle_grad + normalize_back(
        input_grad * (1.0 + scale_attn), first_norm, first_inverse
    )

    token_mod_grad = jnp.concatenate(
        [input_grad, scale_attn_grad, gate_attn_grad, mlp_grad, scale_mlp_grad, gate_mlp_grad],
        axis=1,
    )
    slot_mod_grad = jnp.einsum(
        "ts,tc->sc", chooser.astype(WIDE), token_mod_grad, precision=lax.Precision.HIGHEST
    ).astype(LOW)
    half_grad = lax.all_to_all(slot_mod_grad, "mod", split_axis=1, concat_axis=0, tiled=True)
    mod_grad_all = lax.all_gather(half_grad, ROWS, axis=0, tiled=True)
    own_rows = ada_weight.shape[0]
    own_silu = lax.dynamic_slice_in_dim(silu_all, row_index * own_rows, own_rows, 1)
    ada_shard = jnp.einsum("ic,io->co", own_silu, mod_grad_all, preferred_element_type=WIDE)
    own_columns = adab_weight.shape[1]
    adab_shard = jnp.sum(
        lax.dynamic_slice_in_dim(mod_grad_all, row_index * own_columns, own_columns, 1).astype(WIDE),
        axis=0,
    )
    silu_part = times_back(mod_grad_all, ada_low)
    silu_part = lax.all_to_all(silu_part, ROWS, split_axis=0, concat_axis=1, tiled=True)
    cond_grad = silu_back(silu_part + swap(silu_part, "mod"))[0]

    grad_bias = jnp.concatenate(
        [
            jnp.sum(part.astype(WIDE), axis=0)
            for part in (query_grad, value_grad, attn_grad, pre_grad, branch_grad)
        ]
    ).reshape(devices, -1)
    bias_shard = jnp.sum(
        lax.all_to_all(grad_bias, ALL, split_axis=0, concat_axis=0, tiled=True), axis=0
    )

    rates = step_rates(tokens * devices)
    states_out = []
    states_out.extend(nesterov(qkv_weight, qkv_moment, qkv_average, qkv_shard, rates[0]))
    states_out.extend(nesterov(proj_weight, proj_moment, proj_average, proj_shard, rates[1]))
    states_out.extend(nesterov(fc1_weight, fc1_moment, fc1_average, fc1_shard, rates[2]))
    states_out.extend(nesterov(fc2_weight, fc2_moment, fc2_average, fc2_shard, rates[3]))
    states_out.extend(nesterov(bias_weight, bias_moment, bias_average, bias_shard, rates[4]))
    states_out.extend(nesterov(ada_weight, ada_moment, ada_average, ada_shard, rates[5]))
    states_out.extend(
        nesterov(adab_weight, adab_moment, adab_average, adab_shard.reshape(1, -1), rates[6])
    )
    return (block_out, x_grad, cond_grad) + tuple(states_out)


def solution(mesh):
    far = mesh.shape["dp"] // 4
    fine = Mesh(mesh.devices.reshape(far, 2, 2, mesh.shape["mod"]), ALL)
    tokens = P(ALL, None)
    images = P(ROWS, None)
    trunk = P(ROWS, "mod")
    bias = P(ALL)
    adab = P("mod", ROWS)
    states = (trunk,) * 12 + (bias,) * 3 + (trunk,) * 3 + (adab,) * 3
    return jax.shard_map(
        body,
        mesh=fine,
        in_specs=(tokens, images, bias, tokens) + states,
        out_specs=(tokens, tokens, images) + states,
        check_vma=False,
    )
```

```python
from functools import partial

import jax
import jax.numpy as jnp
from jax import lax
from jax.experimental import pallas as pl
from jax.experimental.pallas import tpu as pltpu
from jax.sharding import Mesh
from jax.sharding import PartitionSpec as P

D = 1152
HEADS = 16
HEAD = 72
FF = 4608
LANES = 128
CHUNK = 256

ROWS = ("far", "near", "core")
ALL = ("far", "near", "core", "mod")
LOW = jnp.bfloat16
WIDE = jnp.float32
LOG2E = 1.4426950408889634
NEG = -1e30
MESH = pl.DeviceIdType.MESH
VMEM = pl.BlockSpec(memory_space=pltpu.VMEM)
ANY = pl.BlockSpec(memory_space=pl.ANY)

EPS = 1e-06
MOMENTUM = 0.9
DECAY = 0.5


def step_rates(tokens_all):
    base_rate = tokens_all ** (-0.5)
    return (
        2.5 * D ** (-0.5) * base_rate,
        3.0 * D ** (-0.5) * base_rate,
        3.3 * D ** (-0.5) * base_rate,
        2.8 * FF ** (-0.5) * base_rate,
        0.5 * base_rate,
        2.0 * D ** (-0.5) * base_rate,
        0.3 * base_rate,
    )


def nesterov(weight, moment, average, gradient, rate):
    moment = MOMENTUM * moment + gradient
    weight = weight - rate * (gradient + MOMENTUM * moment)
    average = DECAY * average + (1.0 - DECAY) * weight
    return (weight, moment, average)


def places():
    return {name: lax.axis_index(name) for name in ALL}


def greet():
    here = places()
    count = lax.axis_size("far")
    others = [dict(far=lax.rem(here["far"] + d, count)) for d in range(1, count)]
    others += [{name: 1 - here[name]} for name in ("near", "core", "mod")]
    barrier = pltpu.get_barrier_semaphore()
    for other in others:
        pl.semaphore_signal(barrier, inc=1, device_id=other, device_id_type=MESH)
    pl.semaphore_wait(barrier, len(others))


def remote(source, target, sends, receives, slot, other):
    return pltpu.make_async_remote_copy(
        src_ref=source,
        dst_ref=target,
        send_sem=sends.at[slot],
        recv_sem=receives.at[slot],
        device_id=other,
        device_id_type=MESH,
    )


def messages(count):
    return count - 1 + 8


class Gather:
    def __init__(self, whole, sends, receives):
        self.whole, self.sends, self.receives = whole, sends, receives
        self.here = places()
        self.count = lax.axis_size("far")
        rows = whole.shape[4]
        self.rows = rows
        self.split = rows if rows % 16 else 8 * ((rows // 8 + 1) // 2)

    def _block(self, far):
        return self.whole.at[self.here["mod"], far, self.here["near"], self.here["core"]]

    def _far(self, shard, distance):
        far = self.here["far"]
        other = dict(far=lax.rem(far + distance, self.count))
        return remote(shard, self._block(far), self.sends, self.receives, distance - 1, other)

    def _far_came(self, shard, distance):
        origin = lax.rem(self.here["far"] + self.count - distance, self.count)
        return remote(
            shard, self._block(origin), self.sends, self.receives, distance - 1, dict(far=origin)
        )

    def start_far(self, shard, local):
        pltpu.make_async_copy(shard, self._block(self.here["far"]), local).start()
        for distance in range(1, self.count):
            self._far(shard, distance).start()

    def finish_far(self, shard, local):
        pltpu.make_async_copy(shard, self._block(self.here["far"]), local).wait()
        for distance in range(1, self.count):
            self._far(shard, distance).wait_send()
            self._far_came(shard, distance).wait_recv()

    def _quad(self, flips, first, size):
        near, core, mod = (
            1 - self.here[name] if name in flips else self.here[name] for name in ("near", "core", "mod")
        )
        return self.whole.at[mod, :, near, core, pl.ds(first, size)]

    def _step(self, name):
        head, rest = (0, self.split), (self.split, self.rows - self.split)
        full = (0, self.rows)
        return {
            "near": ((), "near", full, 0),
            "mod": ((), "mod", full, 1),
            "near_mod": (("near",), "mod", head, 2),
            "mod_near": (("mod",), "near", rest, 3),
            "core": ((), "core", full, 4),
            "near_core": (("near",), "core", full, 5),
            "mod_core": (("mod",), "core", full, 6),
            "both_core": (("near", "mod"), "core", full, 7),
        }[name]

    def _copy(self, name, incoming):
        flips, axis, span, slot = self._step(name)
        if span[1] == 0:
            return None
        quad = self._quad(flips + (axis,) if incoming else flips, *span)
        other = {axis: 1 - self.here[axis]}
        return remote(quad, quad, self.sends, self.receives, self.count - 1 + slot, other)

    def start(self, *names):
        for name in names:
            copy = self._copy(name, False)
            if copy is not None:
                copy.start()

    def receive(self, *names):
        for name in names:
            copy = self._copy(name, True)
            if copy is not None:
                copy.wait_recv()

    def spread(self):
        self.start("near", "mod", "core")

    def cross(self):
        self.receive("near")
        self.start("near_mod", "near_core")
        self.receive("mod")
        self.start("mod_near", "mod_core")

    def close(self):
        self.receive("near_mod", "mod_near")
        self.start("both_core")

    def end(self):
        self.receive("core", "near_core", "mod_core", "both_core")
        for name in (
            "near", "mod", "near_mod", "mod_near", "core", "near_core", "mod_core", "both_core",
        ):
            copy = self._copy(name, False)
            if copy is not None:
                copy.wait_send()


def gather_scratch(weights, locals_):
    count = lax.axis_size("far")
    shapes = [pltpu.SemaphoreType.DMA((messages(count),))] * (2 * weights)
    return shapes + [pltpu.SemaphoreType.DMA((locals_,))]


def whole_shape(shard):
    return jax.ShapeDtypeStruct((2, lax.axis_size("far"), 2, 2) + shard.shape, LOW)


def first_kernel(*refs):
    small_s, qkv_s, proj_s, fc1_s = refs[:4]
    *sems, local = refs[8:]
    small, qkv, proj, fc1 = (
        Gather(w, s, r) for w, s, r in zip(refs[4:8], sems[0::2], sems[1::2])
    )
    greet()
    small.start_far(small_s, local.at[3])
    qkv.start_far(qkv_s, local.at[0])
    proj.start_far(proj_s, local.at[1])
    fc1.start_far(fc1_s, local.at[2])
    small.finish_far(small_s, local.at[3])
    small.spread()
    small.cross()
    small.close()
    small.end()
    qkv.finish_far(qkv_s, local.at[0])
    qkv.spread()
    qkv.cross()
    qkv.close()
    qkv.end()
    proj.finish_far(proj_s, local.at[1])
    fc1.finish_far(fc1_s, local.at[2])


def first_gather(*shards):
    return pl.pallas_call(
        first_kernel,
        out_shape=tuple(whole_shape(shard) for shard in shards),
        in_specs=[VMEM] * 4,
        out_specs=(ANY,) * 4,
        scratch_shapes=gather_scratch(4, 4),
        compiler_params=pltpu.CompilerParams(collective_id=0, has_side_effects=True),
        name="first_gather",
    )(*shards)


def lanes(shape): return lax.broadcasted_iota(jnp.int32, shape, 1)

def seg_codes(seg, n):
    lane = lanes((n, LANES))
    code = lane - HEAD
    inside = jnp.logical_and(code >= 0, code < 4)
    same = code == seg
    q = jnp.where(jnp.logical_and(inside, same), 1.0, 0.0)
    k = jnp.where(jnp.logical_and(inside, jnp.logical_not(same)), NEG, 0.0)
    return q, k

def head_of(wide_rows, start):
    return wide_rows[:, start:start+HEAD]

def pad_head(part, aug):
    n = part.shape[0]
    full = jnp.concatenate([part, jnp.zeros((n, LANES-HEAD), part.dtype)], axis=1)
    return jnp.where(lanes((n,LANES)) < HEAD, full, aug)

def attend_kernel(*refs):
    qkv_ref, seg_ref, fc2_s = refs[:3]
    mixed_ref, lse_ref, proj_w, fc1_w, fc2_w = refs[5:10]
    qh, kh, vh = refs[10:13]
    *sems, local = refs[13:]
    proj, fc1, fc2 = (
        Gather(w, s, r) for w, s, r in zip((proj_w, fc1_w, fc2_w), sems[0::2], sems[1::2])
    )
    greet()
    fc2.start_far(fc2_s, local.at[0])
    proj.spread()
    fc1.spread()

    T = qkv_ref.shape[0]
    D = HEADS*HEAD
    def fill(i, carry):
        rows = pl.ds(pl.multiple_of(i*CHUNK, CHUNK), CHUNK)
        lane = lanes((CHUNK, LANES))
        qc, kc = seg_codes(seg_ref[rows, :], CHUNK)
        qc = qc.astype(LOW); kc = kc.astype(LOW)
        ones = jnp.where(jnp.logical_and(lane >= HEAD, lane < HEAD+3), 1.0, 0.0).astype(LOW)
        for h in range(HEADS):
            qh[h, rows, :] = pad_head(qkv_ref[rows, h*HEAD:(h+1)*HEAD], qc)
            kh[h, rows, :] = pad_head(qkv_ref[rows, D+h*HEAD:D+(h+1)*HEAD], kc)
            vh[h, rows, :] = pad_head(qkv_ref[rows, 2*D+h*HEAD:2*D+(h+1)*HEAD], ones)
        return carry
    lax.fori_loop(0, T//CHUNK, fill, 0)
    lse_ref[...] = jnp.zeros_like(lse_ref)
    def head(h, carry):
        k = kh[h]; v = vh[h]
        for i in range(T//CHUNK):
            rows = pl.ds(i*CHUNK, CHUNK)
            q = qh[h, rows, :]
            s = lax.dot_general(q, k, (((1,),(1,)),((),())), preferred_element_type=WIDE)
            m = jnp.max(s, axis=1, keepdims=True)
            p = jnp.exp2((s - m)*(HEAD**-0.5*LOG2E)).astype(LOW)
            o = jnp.dot(p, v, preferred_element_type=WIDE)
            l = o[:, HEAD:HEAD+1]
            qh[h, rows, :] = (o / l).astype(LOW)
            col = m*HEAD**-0.5 + jnp.log(l)
            lse_ref[rows, :] = jnp.where(lanes((CHUNK,LANES)) == h, col, lse_ref[rows, :])
        tasks = {
            2: proj.cross,
            5: proj.close,
            7: proj.end,
            9: lambda: fc2.finish_far(fc2_s, local.at[0]),
            10: fc2.spread,
            11: fc1.cross,
        }
        for at, task in tasks.items():
            pl.when(h == at)(task)
        return carry
    lax.fori_loop(0, HEADS, head, 0)
    def drain(i, carry):
        rows = pl.ds(pl.multiple_of(i*CHUNK, CHUNK), CHUNK)
        mixed_ref[rows, :] = jnp.concatenate([qh[h, rows, :][:, :HEAD] for h in range(HEADS)], axis=1)
        return carry
    lax.fori_loop(0, T//CHUNK, drain, 0)
    fc1.close()
    fc2.cross()
    fc1.end()
    fc2.close()
    fc2.end()


def attend(qkv, segments, fc2_s, proj_w, fc1_w):
    tokens = qkv.shape[0]
    return pl.pallas_call(
        attend_kernel,
        out_shape=(
            jax.ShapeDtypeStruct((tokens, HEADS * HEAD), LOW),
            jax.ShapeDtypeStruct((tokens, LANES), WIDE),
            jax.ShapeDtypeStruct(proj_w.shape, LOW),
            jax.ShapeDtypeStruct(fc1_w.shape, LOW),
            whole_shape(fc2_s),
        ),
        in_specs=[VMEM] * 3 + [ANY] * 2,
        out_specs=(VMEM,) * 2 + (ANY,) * 3,
        scratch_shapes=[pltpu.VMEM((HEADS, tokens, LANES), LOW)] * 3 + gather_scratch(3, 1),
        input_output_aliases={3: 2, 4: 3},
        compiler_params=pltpu.CompilerParams(
            collective_id=1, has_side_effects=True, vmem_limit_bytes=50 * 2**20
        ),
        name="attend",
    )(qkv, segments.reshape(tokens, 1), fc2_s, proj_w, fc1_w)


def row_spans(rows):
    first = rows if rows % 16 else 8 * ((rows // 8 + 1) // 2)
    return [(0, first)] + ([(first, rows - first)] if first < rows else [])


class Reduce:
    def __init__(self, quads, span, first, buffers, sems):
        self.quads, self.span, self.first = quads, span, first
        self.second = "near" if first == "mod" else "mod"
        self.came_both, self.came_first, self.came_second, self.joint, self.total_, self.came_far = buffers
        self.sends, self.receives, self.locals_ = sems
        self.here = places()
        self.count = lax.axis_size("far")

    @staticmethod
    def scratch(count, span, columns, own_total=True):
        block = (count, span[1], columns)
        buffers = [pltpu.VMEM(block, LOW)] * (5 if own_total else 4)
        buffers += [pltpu.VMEM((count - 1,) + block[1:], LOW)]
        return buffers + [pltpu.SemaphoreType.DMA((count + 2,))] * 2 + [pltpu.SemaphoreType.DMA((2,))]

    def _part(self, *flips):
        quad = self.quads["near" in flips, "mod" in flips]
        return quad.at[:, pl.ds(*self.span)]

    def _swap(self, source, target, slot, axis):
        return remote(source, target, self.sends, self.receives, slot, {axis: 1 - self.here[axis]})

    def _both(self):
        return self._swap(self._part("near", "mod"), self.came_both, 0, self.first)

    def _first(self):
        return self._swap(self._part(self.first), self.came_first, 1, self.first)

    def _second(self):
        return self._swap(self.joint, self.came_second, 2, self.second)

    def _local(self, source, target, slot):
        return pltpu.make_async_copy(source, target, self.locals_.at[slot])

    def _load(self, number):
        if number == 0:
            return self._local(self._part(self.second), self.joint, 0)
        return self._local(self._part(), self.total_, 1)

    def _far(self, distance):
        target = lax.rem(self.here["far"] + distance, self.count)
        return remote(
            self.total_.at[target],
            self.came_far.at[distance - 1],
            self.sends,
            self.receives,
            2 + distance,
            dict(far=target),
        )

    def start(self):
        self._both().start()
        self._first().start()
        self._load(0).start()
        self._load(1).start()

    def merge(self):
        self._load(0).wait()
        self._both().wait_recv()

        def add(at, carry):
            self.joint[at] = (self.joint[at].astype(WIDE) + self.came_both[at].astype(WIDE)).astype(LOW)
            return carry

        lax.fori_loop(0, self.count, add, 0)
        self._second().start()

    def total(self):
        self._load(1).wait()
        self._first().wait_recv()
        self._second().wait_recv()

        def add(at, carry):
            self.total_[at] = (
                self.total_[at].astype(WIDE)
                + self.came_first[at].astype(WIDE)
                + self.came_second[at].astype(WIDE)
            ).astype(LOW)
            return carry

        lax.fori_loop(0, self.count, add, 0)
        self._both().wait_send()
        self._first().wait_send()
        self._second().wait_send()

    def start_far(self):
        for distance in range(1, self.count):
            self._far(distance).start()

    def final(self, out):
        value = self.total_[self.here["far"]].astype(WIDE)
        for distance in range(1, self.count):
            self._far(distance).wait_recv()
            value = value + self.came_far[distance - 1].astype(WIDE)
        out[pl.ds(*self.span), :] = value
        for distance in range(1, self.count):
            self._far(distance).wait_send()


ORDERS = ("mod", "near")


def run(parts, *names):
    for part in parts:
        for name in names:
            getattr(part, name)()


def reduce_kernel_parts(quads, scratch, totals=None):
    by_flips = dict(zip(((False, False), (True, False), (False, True), (True, True)), quads))
    parts = []
    for number, span in enumerate(row_spans(quads[0].shape[1])):
        used = 6 if totals is None else 5
        buffers, scratch = list(scratch[:used]), scratch[used:]
        if totals is not None:
            buffers.insert(4, totals[number])
        sems, scratch = scratch[:3], scratch[3:]
        parts.append(Reduce(by_flips, span, ORDERS[number], buffers, sems))
    return parts, scratch


def reduce_scratch(shape, own_total=True):
    count, rows, columns = shape
    shapes = []
    for span in row_spans(rows):
        shapes += Reduce.scratch(count, span, columns, own_total)
    return shapes


def last_kernel(*refs, spans):
    quads, totals, refs = refs[:4], refs[4 : 4 + spans], refs[4 + spans :]
    qkv_out, fc1_out, *scratch = refs
    qkv, scratch = reduce_kernel_parts(quads, scratch)
    fc1 = []
    for total, span in zip(totals, row_spans(fc1_out.shape[0])):
        buffers = (None, None, None, None, total, scratch[0])
        fc1.append(Reduce(None, span, "mod", buffers, (scratch[1], scratch[2], None)))
        scratch = scratch[3:]
    greet()
    run(qkv, "start")
    run(fc1, "start_far")
    run(qkv, "merge")
    run(qkv, "total", "start_far")
    for part in fc1:
        part.final(fc1_out)
    for part in qkv:
        part.final(qkv_out)


def last_scatter(quads, totals):
    count, rows, columns = quads[0].shape
    fc1_columns = totals[0].shape[2]
    fc1_scratch = []
    for total in totals:
        fc1_scratch += [
            pltpu.VMEM((count - 1,) + total.shape[1:], LOW),
            pltpu.SemaphoreType.DMA((count + 2,)),
            pltpu.SemaphoreType.DMA((count + 2,)),
        ]
    return pl.pallas_call(
        partial(last_kernel, spans=len(totals)),
        out_shape=(
            jax.ShapeDtypeStruct((rows, columns), WIDE),
            jax.ShapeDtypeStruct((sum(total.shape[1] for total in totals), fc1_columns), WIDE),
        ),
        in_specs=[ANY] * 4 + [VMEM] * len(totals),
        out_specs=(VMEM,) * 2,
        scratch_shapes=reduce_scratch(quads[0].shape) + fc1_scratch,
        compiler_params=pltpu.CompilerParams(
            collective_id=3, has_side_effects=True, vmem_limit_bytes=50 * 2**20
        ),
        name="last_scatter",
    )(*quads, *totals)


def split3(v):
    hi = v.astype(LOW).astype(WIDE)
    mid = (v - hi).astype(LOW).astype(WIDE)
    lo = v - hi - mid
    return hi, mid, lo


def attend_back_kernel(*refs, spans):
    qkv_ref, seg_ref, mixed_ref, lse_ref, up_ref = refs[:5]
    fc2_q, fc1_q, proj_q = refs[5:9], refs[9:13], refs[13:17]
    out_ref, fc2_out, proj_out = refs[17:20]
    fc1_totals = refs[20 : 20 + spans]
    qh, kh, vh, uh, stage, stage_sems, leave, leave_sems, *scratch = refs[20 + spans :]
    fc2, scratch = reduce_kernel_parts(fc2_q, scratch)
    proj, scratch = reduce_kernel_parts(proj_q, scratch)
    fc1, scratch = reduce_kernel_parts(fc1_q, scratch, fc1_totals)
    T = mixed_ref.shape[0]
    chunks = T // CHUNK
    greet()
    run(fc2, "start")
    run(proj, "start")

    def load(i):
        rows = pl.ds(pl.multiple_of(i * CHUNK, CHUNK), CHUNK)
        slot = lax.rem(i, 2)
        return pltpu.make_async_copy(qkv_ref.at[rows], stage.at[slot], stage_sems.at[slot])

    load(0).start()

    def fill(i, carry):
        rows = pl.ds(pl.multiple_of(i * CHUNK, CHUNK), CHUNK)

        @pl.when(i + 1 < chunks)
        def _():
            load(i + 1).start()

        load(i).wait()
        qkv = stage.at[lax.rem(i, 2)]
        lane = lanes((CHUNK, LANES))
        qc, kc = seg_codes(seg_ref[rows, :], CHUNK)
        kc = jnp.where(jnp.logical_and(lane >= HEAD + 4, lane < HEAD + 7), 1.0, kc).astype(LOW)
        ones = jnp.where(jnp.logical_and(lane >= HEAD, lane < HEAD + 3), 1.0, 0.0).astype(LOW)

        def spread(v, at, base):
            hi, mid, lo = split3(v)
            return jnp.where(
                lane == at, hi, jnp.where(lane == at + 1, mid, jnp.where(lane == at + 2, lo, base))
            )

        for h in range(HEADS):
            a, b = h * HEAD, (h + 1) * HEAD
            qa = spread(-lse_ref[rows, h : h + 1] * HEAD**0.5, HEAD + 4, qc).astype(LOW)
            qh[h, rows, :] = pad_head(qkv[:, a:b], qa)
            kh[h, rows, :] = pad_head(qkv[:, D + a : D + b], kc)
            vh[h, rows, :] = pad_head(qkv[:, 2 * D + a : 2 * D + b], ones)
            u = up_ref[rows, a:b]
            delta = jnp.sum(u.astype(WIDE) * mixed_ref[rows, a:b].astype(WIDE), axis=1, keepdims=True)
            ua = spread(-delta, HEAD, jnp.zeros((CHUNK, LANES), WIDE)).astype(LOW)
            uh[h, rows, :] = pad_head(u, ua)
        return carry

    lax.fori_loop(0, chunks, fill, 0)
    across = (((1,), (1,)), ((), ()))
    tasks = {
        2: lambda: (run(fc2, "merge"), run(fc1, "start")),
        7: lambda: run(proj, "merge"),
        10: lambda: run(fc2, "total", "start_far"),
        12: lambda: run(proj, "total", "start_far"),
        13: lambda: run(fc1, "merge"),
    }

    def head(h, carry):
        k = kh[h]
        v = vh[h]
        kt = k.T
        dk = jnp.zeros((T, LANES), WIDE)
        dv = jnp.zeros((T, LANES), WIDE)
        for i in range(chunks):
            rows = pl.ds(i * CHUNK, CHUNK)
            q = qh[h, rows, :]
            u = uh[h, rows, :]
            s = lax.dot_general(k, q, across, preferred_element_type=WIDE)
            p = jnp.exp2(s * (HEAD**-0.5 * LOG2E))
            dp = lax.dot_general(v, u, across, preferred_element_type=WIDE)
            ds = (p * dp).astype(LOW)
            dv = dv + jnp.dot(p.astype(LOW), u, preferred_element_type=WIDE)
            dk = dk + jnp.dot(ds, q, preferred_element_type=WIDE)
            dqt = jnp.dot(kt, ds, preferred_element_type=WIDE)
            qh[h, rows, :] = (dqt.T * HEAD**-0.5).astype(LOW)
        kh[h] = (dk * HEAD**-0.5).astype(LOW)
        vh[h] = dv.astype(LOW)
        for at, task in tasks.items():

            @pl.when(h == at)
            def _(task=task):
                task()

        return carry

    lax.fori_loop(0, HEADS, head, 0)

    def store(i, side):
        rows = pl.ds(pl.multiple_of(i * CHUNK, CHUNK), CHUNK)
        return pltpu.make_async_copy(
            leave.at[side], out_ref.at[side, rows], leave_sems.at[side]
        )

    def drain(i, carry):
        rows = pl.ds(pl.multiple_of(i * CHUNK, CHUNK), CHUNK)
        parts = [g[h, rows, :][:, :HEAD] for g in (qh, kh, vh) for h in range(HEADS)]
        for side in range(2):

            @pl.when(i > 0)
            def _(side=side):
                store(i - 1, side).wait()

            own = parts[side * len(parts) // 2 : (side + 1) * len(parts) // 2]
            leave[side] = jnp.concatenate(own, axis=1)
            store(i, side).start()
        return carry

    lax.fori_loop(0, chunks, drain, 0)
    run(fc1, "total")
    for side in range(2):
        store(chunks - 1, side).wait()
    for part in fc2:
        part.final(fc2_out)
    for part in proj:
        part.final(proj_out)


def attend_back(qkv, segments, mixed, lse, upstream, fc2_q, fc1_q, proj_q):
    tokens = qkv.shape[0]
    spans = row_spans(fc1_q[0].shape[1])

    def shard(quads):
        return jax.ShapeDtypeStruct(quads[0].shape[1:], WIDE)

    out = pl.pallas_call(
        partial(attend_back_kernel, spans=len(spans)),
        out_shape=(
            jax.ShapeDtypeStruct((2, tokens, 3 * HEADS * HEAD // 2), LOW),
            shard(fc2_q),
            shard(proj_q),
        )
        + tuple(
            jax.ShapeDtypeStruct((fc1_q[0].shape[0], span[1], fc1_q[0].shape[2]), LOW)
            for span in spans
        ),
        in_specs=[ANY] + [VMEM] * 4 + [ANY] * 12,
        out_specs=(ANY, VMEM, VMEM) + (VMEM,) * len(spans),
        scratch_shapes=[pltpu.VMEM((HEADS, tokens, LANES), LOW)] * 4
        + [pltpu.VMEM((2, CHUNK, 3 * HEADS * HEAD), LOW), pltpu.SemaphoreType.DMA((2,))]
        + [pltpu.VMEM((2, CHUNK, 3 * HEADS * HEAD // 2), LOW), pltpu.SemaphoreType.DMA((2,))]
        + reduce_scratch(fc2_q[0].shape)
        + reduce_scratch(proj_q[0].shape)
        + reduce_scratch(fc1_q[0].shape, False),
        compiler_params=pltpu.CompilerParams(
            collective_id=2, has_side_effects=True, vmem_limit_bytes=63 * 2**20
        ),
        name="attend_back",
    )(qkv, segments.reshape(tokens, 1), mixed, lse, upstream, *fc2_q, *fc1_q, *proj_q)
    return out[0], out[1], out[2], out[3:]


def normed(values):
    centre = values - jnp.mean(values, axis=-1, keepdims=True)
    inverse = lax.rsqrt(jnp.mean(centre * centre, axis=-1, keepdims=True) + EPS)
    return centre * inverse, inverse


def row_of(table, slot, group):
    return table[pl.ds(slot, 1), group * D : (group + 1) * D]


def column_sums(values):
    return jnp.sum(values, axis=0, keepdims=True)


def times_across(left, right):
    return lax.dot_general(left, right, (((1,), (1,)), ((), ())), preferred_element_type=WIDE)


def tile(*shape):
    return pl.BlockSpec((CHUNK,) + shape, lambda i, slots: (i,) + (0,) * len(shape))


def half_tile(columns):
    return pl.BlockSpec((2, CHUNK, columns), lambda i, slots: (0, i, 0))


def fixed(*shape):
    return pl.BlockSpec(
        shape, lambda i, slots: (0,) * len(shape), pipeline_mode=pl.Buffered(1)
    )


def per_tile(rows, columns):
    return pl.BlockSpec((1, rows, columns), lambda i, slots: (i, 0, 0))


def tile_call(kernel, tokens, in_specs, out_specs, out_shapes, scratch, name, flops, traffic):
    return pl.pallas_call(
        kernel,
        out_shape=tuple(jax.ShapeDtypeStruct(shape, dtype) for shape, dtype in out_shapes),
        grid_spec=pltpu.PrefetchScalarGridSpec(
            num_scalar_prefetch=1,
            grid=(tokens // CHUNK,),
            in_specs=in_specs,
            out_specs=out_specs,
            scratch_shapes=scratch,
        ),
        compiler_params=pltpu.CompilerParams(
            dimension_semantics=("arbitrary",), vmem_limit_bytes=63 * 2**20
        ),
        cost_estimate=pl.CostEstimate(flops=flops, bytes_accessed=traffic, transcendentals=0),
        name=name,
    )


def qkv_forward_kernel(slots, x_ref, table, bias, weight, act_ref, joint_ref):
    slot = slots[pl.program_id(0)]
    h1, _ = normed(x_ref[...].astype(WIDE))
    act = (h1 * (1.0 + row_of(table, slot, 1)) + row_of(table, slot, 0)).astype(LOW)
    act_ref[...] = act
    joint = jnp.concatenate([times(act, weight[0]), times(act, weight[1])], axis=1)
    joint_ref[...] = (joint + bias[...]).astype(LOW)


def qkv_forward(slots, x_in, table, bias, weight):
    tokens = x_in.shape[0]
    wide = 3 * D
    return tile_call(
        qkv_forward_kernel,
        tokens,
        [tile(D), fixed(*table.shape), fixed(1, wide), fixed(*weight.shape)],
        (tile(D), tile(wide)),
        (((tokens, D), LOW), ((tokens, wide), LOW)),
        [],
        "qkv_forward",
        2 * tokens * D * wide,
        weight.size * 2 + tokens * D * 10,
    )(slots, x_in, table, bias, weight)


GELU = 0.7978845608028654
CUBIC = 0.044715
SPAN = 768


def middle_kernel(
    slots, x_ref, g_ref, mixed_ref, table, bias, proj, fc1, fc2,
    block_ref, mlp_ref, hidden_ref, dpre_ref, dbranch_ref, dattn_ref, dmixed_ref, dx1_ref, sums_ref, dpre_sums,
    slope,
):
    slot = slots[pl.program_id(0)]
    gate1, shift2, scale2, gate2 = (row_of(table, slot, group) for group in (2, 3, 4, 5))
    half = FF // 2
    mixed = mixed_ref[...]
    attn_out = jnp.concatenate([times(mixed, proj[0]), times(mixed, proj[1])], axis=1)
    attn_out = attn_out + bias[:, 2 * D : 3 * D]
    x1 = x_ref[...].astype(WIDE) + gate1 * attn_out
    h2, inverse = normed(x1)
    mlp_in = (h2 * (1.0 + scale2) + shift2).astype(LOW)
    mlp_ref[...] = mlp_in
    for side in range(2):
        for at in range(0, half, SPAN):
            column = side * half + at
            pre = times(mlp_in, fc1[side, :, at : at + SPAN])
            pre = pre + bias[:, 3 * D + column : 3 * D + column + SPAN]
            square = pre * pre
            bend = jnp.tanh(GELU * pre * (1.0 + CUBIC * square))
            rise = 0.5 * (1.0 + bend)
            hidden_ref[:, column : column + SPAN] = (pre * rise).astype(LOW)
            slope[:, column : column + SPAN] = rise + 0.5 * GELU * pre * (1.0 - bend * bend) * (
                1.0 + 3.0 * CUBIC * square
            )
    hidden = hidden_ref[...]
    branch = jnp.concatenate([times(hidden, fc2[0]), times(hidden, fc2[1])], axis=1)
    branch = branch + bias[:, 3 * D + FF :]
    block_ref[...] = (x1 + gate2 * branch).astype(LOW)
    g = g_ref[...].astype(WIDE)
    dbranch = (gate2 * g).astype(LOW)
    sums_ref[0, 3:4, :] = column_sums(g * branch)
    sums_ref[0, 5:6, :] = column_sums(dbranch.astype(WIDE))
    left, right = dbranch[:, : D // 2], dbranch[:, D // 2 :]
    dbranch_ref[0] = left
    dbranch_ref[1] = right
    for side in range(2):
        for at in range(0, half, SPAN):
            column = side * half + at
            rows = slice(column, column + SPAN)
            dhidden = times_across(left, fc2[0, rows]) + times_across(right, fc2[1, rows])
            dpre = (dhidden * slope[:, rows]).astype(LOW)
            dpre_ref[side, :, at : at + SPAN] = dpre
            dpre_sums[0, :, rows] = column_sums(dpre.astype(WIDE))
    dmlp = times_across(dpre_ref[0], fc1[0]) + times_across(dpre_ref[1], fc1[1])
    sums_ref[0, 1:2, :] = column_sums(dmlp)
    sums_ref[0, 2:3, :] = column_sums(dmlp * h2)
    dh2 = dmlp * (1.0 + scale2)
    dx1 = g + inverse * (
        dh2
        - jnp.mean(dh2, axis=-1, keepdims=True)
        - h2 * jnp.mean(dh2 * h2, axis=-1, keepdims=True)
    )
    dx1_ref[...] = dx1
    sums_ref[0, 0:1, :] = column_sums(dx1 * attn_out)
    dattn = (gate1 * dx1).astype(LOW)
    sums_ref[0, 4:5, :] = column_sums(dattn.astype(WIDE))
    left, right = dattn[:, : D // 2], dattn[:, D // 2 :]
    dattn_ref[0] = left
    dattn_ref[1] = right
    dmixed_ref[...] = (times_across(left, proj[0]) + times_across(right, proj[1])).astype(LOW)
    sums_ref[0, 6:8, :] = jnp.zeros((2, D), WIDE)


def middle(slots, x_in, out_grad, mixed, table, bias, proj, fc1, fc2):
    tokens = x_in.shape[0]
    tiles = tokens // CHUNK
    return tile_call(
        middle_kernel,
        tokens,
        [
            tile(D),
            tile(D),
            tile(D),
            fixed(*table.shape),
            fixed(*bias.shape),
            fixed(*proj.shape),
            fixed(*fc1.shape),
            fixed(*fc2.shape),
        ],
        (
            tile(D),
            tile(D),
            tile(FF),
            half_tile(FF // 2),
            half_tile(D // 2),
            half_tile(D // 2),
            tile(D),
            tile(D),
            per_tile(8, D),
            per_tile(1, FF),
        ),
        (
            ((tokens, D), LOW),
            ((tokens, D), LOW),
            ((tokens, FF), LOW),
            ((2, tokens, FF // 2), LOW),
            ((2, tokens, D // 2), LOW),
            ((2, tokens, D // 2), LOW),
            ((tokens, D), LOW),
            ((tokens, D), WIDE),
            ((tiles, 8, D), WIDE),
            ((tiles, 1, FF), WIDE),
        ),
        [pltpu.VMEM((CHUNK, FF), WIDE)],
        "middle",
        4 * tokens * (D * D + 2 * D * FF),
        (D * D + 2 * D * FF) * 2 + tokens * D * 40,
    )(slots, x_in, out_grad, mixed, table, bias, proj, fc1, fc2)


def qkv_backward_kernel(slots, joint_ref, x_ref, dx1_ref, table, weight, x_grad_ref, sums_ref, joint_sums):
    slot = slots[pl.program_id(0)]
    dact = times_across(joint_ref[0], weight[0]) + times_across(joint_ref[1], weight[1])
    h1, inverse = normed(x_ref[...].astype(WIDE))
    sums_ref[0, 0:1, :] = column_sums(dact)
    sums_ref[0, 1:2, :] = column_sums(dact * h1)
    sums_ref[0, 2:8, :] = jnp.zeros((6, D), WIDE)
    dh1 = dact * (1.0 + row_of(table, slot, 1))
    x_grad_ref[...] = dx1_ref[...] + inverse * (
        dh1
        - jnp.mean(dh1, axis=-1, keepdims=True)
        - h1 * jnp.mean(dh1 * h1, axis=-1, keepdims=True)
    )
    for side in range(2):
        joint_sums[0, side : side + 1, :] = column_sums(joint_ref[side].astype(WIDE))


def qkv_backward(slots, joint, x_in, dx1, table, weight):
    tokens = x_in.shape[0]
    tiles = tokens // CHUNK
    half = 3 * D // 2
    return tile_call(
        qkv_backward_kernel,
        tokens,
        [half_tile(half), tile(D), tile(D), fixed(*table.shape), fixed(*weight.shape)],
        (tile(D), per_tile(8, D), per_tile(2, half)),
        (((tokens, D), WIDE), ((tiles, 8, D), WIDE), ((tiles, 2, half), WIDE)),
        [],
        "qkv_backward",
        2 * tokens * D * 3 * D,
        weight.size * 2 + tokens * D * 18,
    )(slots, joint, x_in, dx1, table, weight)


def swap(values, axis):
    return lax.ppermute(values, axis, [(0, 1), (1, 0)])


def chip_quads(left, right):
    count = lax.axis_size("far")
    near, core, half = lax.axis_index("near"), lax.axis_index("core"), lax.axis_index("mod")
    tokens = left.shape[0]
    blocks = left.reshape(tokens, count, 2, 2, -1)

    def piece(n, k, m):
        rows = lax.dynamic_index_in_dim(blocks, near ^ n, 2, False)
        rows = lax.dynamic_index_in_dim(rows, core ^ k, 2, False)
        columns = lax.dynamic_index_in_dim(right, half ^ m, 0, False)
        product = times(rows.reshape(tokens, -1).T, columns)
        return product.reshape(count, -1, columns.shape[1])

    def chip_sum(n, m):
        came = swap(piece(n, 1, m).astype(LOW), "core")
        return (piece(n, 0, m) + came.astype(WIDE)).astype(LOW)

    return [chip_sum(n, m) for n, m in ((0, 0), (1, 0), (0, 1), (1, 1))]


def times(left, right):
    return jnp.dot(left, right, preferred_element_type=WIDE)


def times_back(left, right):
    return lax.dot_general(left, right, (((1,), (1,)), ((), ())), preferred_element_type=WIDE)


def body(
    x_in,
    cond,
    segments,
    out_grad,
    qkv_weight,
    qkv_moment,
    qkv_average,
    proj_weight,
    proj_moment,
    proj_average,
    fc1_weight,
    fc1_moment,
    fc1_average,
    fc2_weight,
    fc2_moment,
    fc2_average,
    bias_weight,
    bias_moment,
    bias_average,
    ada_weight,
    ada_moment,
    ada_average,
    adab_weight,
    adab_moment,
    adab_average,
):
    tokens, width = x_in.shape
    row_devices = lax.axis_size(ROWS)
    devices = lax.axis_size(ALL)
    row_index = lax.axis_index(ROWS)
    images = cond.shape[0] // 2

    cond_silu, silu_back = jax.vjp(jax.nn.silu, cond.astype(WIDE))
    half_silu = lax.dynamic_index_in_dim(
        cond_silu.astype(LOW).reshape(-1, 2, width // 2), lax.axis_index("mod"), 1, False
    )
    own_bias = bias_weight.shape[0]
    bias_block = jnp.pad(bias_weight.astype(LOW), (0, 8 * LANES - own_bias)).reshape(8, LANES)
    blank = jnp.zeros((8, LANES // 2), LOW)
    ada_low = ada_weight.astype(LOW)
    ada_columns = lax.all_to_all(ada_low, ROWS, split_axis=1, concat_axis=0, tiled=True)
    small_w, qkv_w, proj_w, fc1_w = first_gather(
        jnp.concatenate([half_silu, bias_block, blank], axis=1),
        qkv_weight.astype(LOW),
        proj_weight.astype(LOW),
        fc1_weight.astype(LOW),
    )
    small = small_w.reshape(2, row_devices * 8, -1)
    silu_all = jnp.concatenate([small[0, :, : width // 2], small[1, :, : width // 2]], axis=1)
    bias_all = small[:, :, width // 2 : width // 2 + LANES].reshape(2, row_devices, -1)
    bias_full = jnp.swapaxes(bias_all[:, :, :own_bias], 0, 1).reshape(1, -1).astype(WIDE)
    adab_low = adab_weight.astype(LOW).astype(WIDE)
    mod_columns = (times(silu_all, ada_columns) + adab_low).astype(LOW)
    mod_rows = lax.all_to_all(mod_columns, ALL, split_axis=0, concat_axis=1, tiled=True)
    table = jnp.swapaxes(mod_rows.reshape(images, row_devices, 2, -1), 1, 2).reshape(images, -1)
    table = table.astype(WIDE)

    def joined(whole):
        return whole.reshape(2, -1, whole.shape[-1])

    qkv_low = joined(qkv_w)
    slots = segments[::CHUNK]
    joint_bias = jnp.concatenate(
        [bias_full[:, 0:width], jnp.zeros((1, width), WIDE), bias_full[:, width : 2 * width]], axis=1
    )
    attn_input, joint_rows = qkv_forward(slots, x_in, table, joint_bias, qkv_low)
    mixture, log_totals, proj_w, fc1_w, fc2_w = attend(
        joint_rows, segments, fc2_weight.astype(LOW), proj_w, fc1_w
    )
    (
        block_out, mlp_input, hidden, pre_halves, branch_halves, attn_halves, mixture_grad, middle_grad, sums, pre_sums,
    ) = middle(
        slots, x_in, out_grad, mixture, table, bias_full, joined(proj_w), joined(fc1_w), joined(fc2_w)
    )
    fc2_quads = chip_quads(hidden, branch_halves)
    fc1_quads = chip_quads(mlp_input, pre_halves)
    proj_quads = chip_quads(mixture, attn_halves)
    joint_halves, fc2_shard, proj_shard, fc1_totals = attend_back(
        joint_rows,
        segments,
        mixture,
        log_totals,
        mixture_grad,
        fc2_quads,
        fc1_quads,
        proj_quads,
    )
    x_grad, first_sums, joint_sums = qkv_backward(
        slots, joint_halves, x_in, middle_grad, table, qkv_low
    )
    qkv_quads = chip_quads(attn_input, joint_halves)
    qkv_shard, fc1_shard = last_scatter(qkv_quads, fc1_totals)

    chooser = (slots[None, :] == jnp.arange(images, dtype=jnp.int32)[:, None]).astype(WIDE)
    tile_mod_grad = jnp.concatenate([first_sums[:, 0:2], sums[:, 0:4]], axis=1)
    slot_mod_grad = jnp.sum(chooser[:, :, None, None] * tile_mod_grad[None], axis=1)
    slot_mod_grad = slot_mod_grad.reshape(images, -1).astype(LOW)
    half_grad = lax.all_to_all(slot_mod_grad, "mod", split_axis=1, concat_axis=0, tiled=True)
    mod_grad_all = lax.all_gather(half_grad, ROWS, axis=0, tiled=True)
    own_rows = ada_weight.shape[0]
    own_silu = lax.dynamic_slice_in_dim(silu_all, row_index * own_rows, own_rows, 1)
    ada_shard = jnp.einsum("ic,io->co", own_silu, mod_grad_all, preferred_element_type=WIDE)
    own_columns = adab_weight.shape[1]
    adab_shard = jnp.sum(
        lax.dynamic_slice_in_dim(mod_grad_all, row_index * own_columns, own_columns, 1).astype(WIDE),
        axis=0,
    )
    silu_part = times_back(mod_grad_all, ada_low)
    silu_part = lax.all_to_all(silu_part, ROWS, split_axis=0, concat_axis=1, tiled=True)
    cond_grad = silu_back(silu_part + swap(silu_part, "mod"))[0]

    joint_sum = jnp.sum(joint_sums, axis=0).reshape(-1)
    sum_rows = jnp.sum(sums, axis=0)
    grad_bias = jnp.concatenate(
        [
            joint_sum[0:width],
            joint_sum[2 * width :],
            sum_rows[4],
            jnp.sum(pre_sums, axis=0).reshape(-1),
            sum_rows[5],
        ]
    ).reshape(devices, -1)
    bias_shard = jnp.sum(
        lax.all_to_all(grad_bias, ALL, split_axis=0, concat_axis=0, tiled=True), axis=0
    )

    rates = step_rates(tokens * devices)
    states_out = []
    states_out.extend(nesterov(qkv_weight, qkv_moment, qkv_average, qkv_shard, rates[0]))
    states_out.extend(nesterov(proj_weight, proj_moment, proj_average, proj_shard, rates[1]))
    states_out.extend(nesterov(fc1_weight, fc1_moment, fc1_average, fc1_shard, rates[2]))
    states_out.extend(nesterov(fc2_weight, fc2_moment, fc2_average, fc2_shard, rates[3]))
    states_out.extend(nesterov(bias_weight, bias_moment, bias_average, bias_shard, rates[4]))
    states_out.extend(nesterov(ada_weight, ada_moment, ada_average, ada_shard, rates[5]))
    states_out.extend(
        nesterov(adab_weight, adab_moment, adab_average, adab_shard.reshape(1, -1), rates[6])
    )
    return (block_out, x_grad, cond_grad) + tuple(states_out)


def solution(mesh):
    far = mesh.shape["dp"] // 4
    fine = Mesh(mesh.devices.reshape(far, 2, 2, mesh.shape["mod"]), ALL)
    tokens = P(ALL, None)
    images = P(ROWS, None)
    trunk = P(ROWS, "mod")
    bias = P(ALL)
    adab = P("mod", ROWS)
    states = (trunk,) * 12 + (bias,) * 3 + (trunk,) * 3 + (adab,) * 3
    return jax.shard_map(
        body,
        mesh=fine,
        in_specs=(tokens, images, bias, tokens) + states,
        out_specs=(tokens, tokens, images) + states,
        check_vma=False,
    )
```

```python
from functools import partial

import jax
import jax.numpy as jnp
from jax import lax
from jax.experimental import pallas as pl
from jax.experimental.pallas import tpu as pltpu
from jax.sharding import Mesh
from jax.sharding import PartitionSpec as P

D = 1152
HEADS = 16
HEAD = 72
FF = 4608
LANES = 128
CHUNK = 256

ROWS = ("far", "near", "core")
ALL = ("far", "near", "core", "mod")
LOW = jnp.bfloat16
WIDE = jnp.float32
LOG2E = 1.4426950408889634
NEG = -1e30
MESH = pl.DeviceIdType.MESH
VMEM = pl.BlockSpec(memory_space=pltpu.VMEM)
ANY = pl.BlockSpec(memory_space=pl.ANY)

EPS = 1e-06
MOMENTUM = 0.9
DECAY = 0.5


def step_rates(tokens_all):
    base_rate = tokens_all ** (-0.5)
    return (
        2.5 * D ** (-0.5) * base_rate,
        3.0 * D ** (-0.5) * base_rate,
        3.3 * D ** (-0.5) * base_rate,
        2.8 * FF ** (-0.5) * base_rate,
        0.5 * base_rate,
        2.0 * D ** (-0.5) * base_rate,
        0.3 * base_rate,
    )


def nesterov(weight, moment, average, gradient, rate):
    moment = MOMENTUM * moment + gradient
    weight = weight - rate * (gradient + MOMENTUM * moment)
    average = DECAY * average + (1.0 - DECAY) * weight
    return (weight, moment, average)


def places():
    return {name: lax.axis_index(name) for name in ALL}


def greet():
    here = places()
    count = lax.axis_size("far")
    others = [dict(far=lax.rem(here["far"] + d, count)) for d in range(1, count)]
    others += [{name: 1 - here[name]} for name in ("near", "core", "mod")]
    barrier = pltpu.get_barrier_semaphore()
    for other in others:
        pl.semaphore_signal(barrier, inc=1, device_id=other, device_id_type=MESH)
    pl.semaphore_wait(barrier, len(others))


def remote(source, target, sends, receives, slot, other):
    return pltpu.make_async_remote_copy(
        src_ref=source,
        dst_ref=target,
        send_sem=sends.at[slot],
        recv_sem=receives.at[slot],
        device_id=other,
        device_id_type=MESH,
    )


def messages(count):
    return count - 1 + 8


class Gather:
    def __init__(self, whole, sends, receives):
        self.whole, self.sends, self.receives = whole, sends, receives
        self.here = places()
        self.count = lax.axis_size("far")
        rows = whole.shape[4]
        self.rows = rows
        self.split = rows if rows % 8 else 8 * ((rows // 8 + 1) // 2)

    def _block(self, far):
        return self.whole.at[self.here["mod"], far, self.here["near"], self.here["core"]]

    def _far(self, shard, distance):
        far = self.here["far"]
        other = dict(far=lax.rem(far + distance, self.count))
        return remote(shard, self._block(far), self.sends, self.receives, distance - 1, other)

    def _far_came(self, shard, distance):
        origin = lax.rem(self.here["far"] + self.count - distance, self.count)
        return remote(
            shard, self._block(origin), self.sends, self.receives, distance - 1, dict(far=origin)
        )

    def start_far(self, shard, local):
        pltpu.make_async_copy(shard, self._block(self.here["far"]), local).start()
        for distance in range(1, self.count):
            self._far(shard, distance).start()

    def finish_far(self, shard, local):
        pltpu.make_async_copy(shard, self._block(self.here["far"]), local).wait()
        for distance in range(1, self.count):
            self._far(shard, distance).wait_send()
            self._far_came(shard, distance).wait_recv()

    def _quad(self, flips, first, size):
        near, core, mod = (
            1 - self.here[name] if name in flips else self.here[name] for name in ("near", "core", "mod")
        )
        return self.whole.at[mod, :, near, core, pl.ds(first, size)]

    def _step(self, name):
        head, rest = (0, self.split), (self.split, self.rows - self.split)
        full = (0, self.rows)
        return {
            "near": ((), "near", full, 0),
            "mod": ((), "mod", full, 1),
            "near_mod": (("near",), "mod", head, 2),
            "mod_near": (("mod",), "near", rest, 3),
            "core": ((), "core", full, 4),
            "near_core": (("near",), "core", full, 5),
            "mod_core": (("mod",), "core", full, 6),
            "both_core": (("near", "mod"), "core", full, 7),
        }[name]

    def _copy(self, name, incoming):
        flips, axis, span, slot = self._step(name)
        if span[1] == 0:
            return None
        quad = self._quad(flips + (axis,) if incoming else flips, *span)
        other = {axis: 1 - self.here[axis]}
        return remote(quad, quad, self.sends, self.receives, self.count - 1 + slot, other)

    def start(self, *names):
        for name in names:
            copy = self._copy(name, False)
            if copy is not None:
                copy.start()

    def receive(self, *names):
        for name in names:
            copy = self._copy(name, True)
            if copy is not None:
                copy.wait_recv()

    def spread(self):
        self.start("near", "mod", "core")

    def cross(self):
        self.receive("near")
        self.start("near_mod", "near_core")
        self.receive("mod")
        self.start("mod_near", "mod_core")

    def close(self):
        self.receive("near_mod", "mod_near")
        self.start("both_core")

    def end(self):
        self.receive("core", "near_core", "mod_core", "both_core")
        for name in (
            "near", "mod", "near_mod", "mod_near", "core", "near_core", "mod_core", "both_core",
        ):
            copy = self._copy(name, False)
            if copy is not None:
                copy.wait_send()


def gather_scratch(weights, locals_):
    count = lax.axis_size("far")
    shapes = [pltpu.SemaphoreType.DMA((messages(count),))] * (2 * weights)
    return shapes + [pltpu.SemaphoreType.DMA((locals_,))]


def whole_shape(shard):
    return jax.ShapeDtypeStruct((2, lax.axis_size("far"), 2, 2) + shard.shape, LOW)


def first_kernel(*refs):
    small_s, qkv_s, proj_s, fc1_s = refs[:4]
    *sems, local = refs[8:]
    small, qkv, proj, fc1 = (
        Gather(w, s, r) for w, s, r in zip(refs[4:8], sems[0::2], sems[1::2])
    )
    greet()
    small.start_far(small_s, local.at[3])
    qkv.start_far(qkv_s, local.at[0])
    proj.start_far(proj_s, local.at[1])
    fc1.start_far(fc1_s, local.at[2])
    small.finish_far(small_s, local.at[3])
    small.spread()
    small.cross()
    small.close()
    small.end()
    qkv.finish_far(qkv_s, local.at[0])
    qkv.spread()
    qkv.cross()
    qkv.close()
    qkv.end()
    proj.finish_far(proj_s, local.at[1])
    fc1.finish_far(fc1_s, local.at[2])


def first_gather(*shards):
    return pl.pallas_call(
        first_kernel,
        out_shape=tuple(whole_shape(shard) for shard in shards),
        in_specs=[VMEM] * 4,
        out_specs=(ANY,) * 4,
        scratch_shapes=gather_scratch(4, 4),
        compiler_params=pltpu.CompilerParams(collective_id=0, has_side_effects=True),
        name="first_gather",
    )(*shards)


def lanes(shape): return lax.broadcasted_iota(jnp.int32, shape, 1)

def seg_codes(seg, n):
    lane = lanes((n, LANES))
    code = lane - HEAD
    inside = jnp.logical_and(code >= 0, code < 4)
    same = code == seg
    q = jnp.where(jnp.logical_and(inside, same), 1.0, 0.0)
    k = jnp.where(jnp.logical_and(inside, jnp.logical_not(same)), NEG, 0.0)
    return q, k

def head_of(wide_rows, start):
    return wide_rows[:, start:start+HEAD]

def pad_head(part, aug):
    n = part.shape[0]
    full = jnp.concatenate([part, jnp.zeros((n, LANES-HEAD), part.dtype)], axis=1)
    return jnp.where(lanes((n,LANES)) < HEAD, full, aug)

def attend_kernel(*refs):
    qkv_ref, seg_ref, fc2_s = refs[:3]
    mixed_ref, turned_ref, lse_ref, proj_w, fc1_w, fc2_w = refs[5:11]
    qh, kh, vh = refs[11:14]
    *sems, local = refs[14:]
    proj, fc1, fc2 = (
        Gather(w, s, r) for w, s, r in zip((proj_w, fc1_w, fc2_w), sems[0::2], sems[1::2])
    )
    greet()
    fc2.start_far(fc2_s, local.at[0])
    proj.spread()
    fc1.spread()

    T = qkv_ref.shape[0]
    D = HEADS*HEAD
    def fill(i, carry):
        rows = pl.ds(pl.multiple_of(i*CHUNK, CHUNK), CHUNK)
        lane = lanes((CHUNK, LANES))
        qc, kc = seg_codes(seg_ref[rows, :], CHUNK)
        qc = qc.astype(LOW); kc = kc.astype(LOW)
        ones = jnp.where(jnp.logical_and(lane >= HEAD, lane < HEAD+3), 1.0, 0.0).astype(LOW)
        for h in range(HEADS):
            qh[h, rows, :] = pad_head(qkv_ref[rows, h*HEAD:(h+1)*HEAD], qc)
            kh[h, rows, :] = pad_head(qkv_ref[rows, D+h*HEAD:D+(h+1)*HEAD], kc)
            vh[h, rows, :] = pad_head(qkv_ref[rows, 2*D+h*HEAD:2*D+(h+1)*HEAD], ones)
        return carry
    lax.fori_loop(0, T//CHUNK, fill, 0)
    lse_ref[...] = jnp.zeros_like(lse_ref)
    def head(h, carry):
        k = kh[h]; v = vh[h]
        for i in range(T//CHUNK):
            rows = pl.ds(i*CHUNK, CHUNK)
            q = qh[h, rows, :]
            s = lax.dot_general(q, k, (((1,),(1,)),((),())), preferred_element_type=WIDE)
            m = jnp.max(s, axis=1, keepdims=True)
            p = jnp.exp2((s - m)*(HEAD**-0.5*LOG2E)).astype(LOW)
            o = jnp.dot(p, v, preferred_element_type=WIDE)
            l = o[:, HEAD:HEAD+1]
            qh[h, rows, :] = (o / l).astype(LOW)
            col = m*HEAD**-0.5 + jnp.log(l)
            lse_ref[rows, :] = jnp.where(lanes((CHUNK,LANES)) == h, col, lse_ref[rows, :])
        tasks = {
            2: proj.cross,
            5: proj.close,
            7: proj.end,
            9: lambda: fc2.finish_far(fc2_s, local.at[0]),
            10: fc2.spread,
            11: fc1.cross,
        }
        for at, task in tasks.items():
            pl.when(h == at)(task)
        return carry
    lax.fori_loop(0, HEADS, head, 0)
    def drain(i, carry):
        rows = pl.ds(pl.multiple_of(i*CHUNK, CHUNK), CHUNK)
        mixed = jnp.concatenate([qh[h, rows, :][:, :HEAD] for h in range(HEADS)], axis=1)
        mixed_ref[rows, :] = mixed
        turned_ref[:, rows] = mixed.T
        return carry
    lax.fori_loop(0, T//CHUNK, drain, 0)
    fc1.close()
    fc2.cross()
    fc1.end()
    fc2.close()
    fc2.end()


def attend(qkv, segments, fc2_s, proj_w, fc1_w):
    tokens = qkv.shape[0]
    return pl.pallas_call(
        attend_kernel,
        out_shape=(
            jax.ShapeDtypeStruct((tokens, HEADS * HEAD), LOW),
            jax.ShapeDtypeStruct((HEADS * HEAD, tokens), LOW),
            jax.ShapeDtypeStruct((tokens, LANES), WIDE),
            jax.ShapeDtypeStruct(proj_w.shape, LOW),
            jax.ShapeDtypeStruct(fc1_w.shape, LOW),
            whole_shape(fc2_s),
        ),
        in_specs=[VMEM] * 3 + [ANY] * 2,
        out_specs=(VMEM,) * 3 + (ANY,) * 3,
        scratch_shapes=[pltpu.VMEM((HEADS, tokens, LANES), LOW)] * 3 + gather_scratch(3, 1),
        input_output_aliases={3: 3, 4: 4},
        compiler_params=pltpu.CompilerParams(
            collective_id=1, has_side_effects=True, vmem_limit_bytes=50 * 2**20
        ),
        name="attend",
    )(qkv, segments.reshape(tokens, 1), fc2_s, proj_w, fc1_w)


def row_spans(rows):
    first = rows if rows % 8 else 8 * ((rows // 8 + 1) // 2)
    return [(0, first)] + ([(first, rows - first)] if first < rows else [])


class Reduce:
    def __init__(self, part, span, first, came, joint, total, base, sems, loads=False):
        self.part, self.span, self.first = part, span, first
        self.second = "near" if first == "mod" else "mod"
        self.came_both, self.came_first, self.came_second, self.came_far = came
        self.joint, self.total_, self.base = joint, total, base
        self.sends, self.receives, self.locals_ = sems
        self.loads = loads
        self.here = places()
        self.count = lax.axis_size("far")

    def _swap(self, source, target, slot, axis):
        return remote(source, target, self.sends, self.receives, slot, {axis: 1 - self.here[axis]})

    def _both(self):
        return self._swap(self.part("near", "mod"), self.came_both, 0, self.first)

    def _first(self):
        return self._swap(self.part(self.first), self.came_first, 1, self.first)

    def _second(self):
        return self._swap(self.joint, self.came_second, 2, self.second)

    def _load(self, number):
        source, target = ((self.part(self.second), self.joint), (self.part(), self.total_))[number]
        return pltpu.make_async_copy(source, target, self.locals_.at[number])

    def _far(self, distance):
        target = lax.rem(self.here["far"] + distance, self.count)
        return remote(
            self.total_.at[target],
            self.came_far.at[distance - 1],
            self.sends,
            self.receives,
            2 + distance,
            dict(far=target),
        )

    def start(self):
        self._both().start()
        self._first().start()
        if self.loads:
            self._load(0).start()
            self._load(1).start()

    def merge(self):
        if self.loads:
            self._load(0).wait()
        self._both().wait_recv()

        def add(at, carry):
            self.joint[at] = (self.joint[at].astype(WIDE) + self.came_both[at].astype(WIDE)).astype(LOW)
            return carry

        lax.fori_loop(0, self.count, add, 0)
        self._second().start()

    def total(self):
        if self.loads:
            self._load(1).wait()
        self._first().wait_recv()
        self._second().wait_recv()

        def add(at, carry):
            self.total_[at] = (
                self.base[at].astype(WIDE)
                + self.came_first[at].astype(WIDE)
                + self.came_second[at].astype(WIDE)
            ).astype(LOW)
            return carry

        lax.fori_loop(0, self.count, add, 0)
        self._both().wait_send()
        self._first().wait_send()
        self._second().wait_send()

    def start_far(self):
        for distance in range(1, self.count):
            self._far(distance).start()

    def final(self, out):
        value = self.total_[self.here["far"]].astype(WIDE)
        for distance in range(1, self.count):
            self._far(distance).wait_recv()
            value = value + self.came_far[distance - 1].astype(WIDE)
        out[pl.ds(*self.span), :] = value
        for distance in range(1, self.count):
            self._far(distance).wait_send()


ORDERS = ("mod", "near")


def run(parts, *names):
    for part in parts:
        for name in names:
            getattr(part, name)()


def span_part(sums, span):
    def part(*flips):
        near, mod = (
            1 - lax.axis_index(name) if name in flips else lax.axis_index(name) for name in ("near", "mod")
        )
        return sums.at[mod, near, :, pl.ds(*span)]

    return part


def take(scratch, number):
    return scratch[:number], scratch[number:]


def came_scratch(count, span, columns, far=True):
    block = (count, span[1], columns)
    shapes = [pltpu.VMEM(block, LOW)] * 3
    return shapes + ([pltpu.VMEM((count - 1,) + block[1:], LOW)] if far else [])


def sem_scratch(count):
    return [pltpu.SemaphoreType.DMA((count + 2,))] * 2 + [pltpu.SemaphoreType.DMA((2,))]


def loaded_scratch(shape, total=True):
    count, rows, columns = shape[2:]
    shapes = []
    for span in row_spans(rows):
        shapes += came_scratch(count, span, columns)
        shapes += [pltpu.VMEM((count, span[1], columns), LOW)] * (2 if total else 1)
        shapes += sem_scratch(count)
    return shapes


def loaded_reduces(sums, scratch, totals=None):
    reduces = []
    for number, span in enumerate(row_spans(sums.shape[3])):
        came, scratch = take(scratch, 4)
        (joint,), scratch = take(scratch, 1)
        if totals is None:
            (total,), scratch = take(scratch, 1)
        else:
            total = totals[number]
        sems, scratch = take(scratch, 3)
        reduces.append(
            Reduce(span_part(sums, span), span, ORDERS[number], came, joint, total, total, sems, True)
        )
    return reduces, scratch


def resident_scratch(shape, far=True):
    count, rows, columns = shape[2:]
    shapes = []
    for span in row_spans(rows):
        shapes += came_scratch(count, span, columns, far) + sem_scratch(count)
    return shapes


def resident_reduces(sums, scratch, totals=None):
    reduces = []
    for number, span in enumerate(row_spans(sums.shape[3])):
        came, scratch = take(scratch, 4 if totals is None else 3)
        sems, scratch = take(scratch, 3)
        part = span_part(sums, span)
        order = ORDERS[number]
        own = part()
        total = own if totals is None else totals[number]
        came = list(came) + [None] * (4 - len(came))
        joint = part("near" if order == "mod" else "mod")
        reduces.append(Reduce(part, span, order, came, joint, total, own, sems))
    return reduces, scratch


def far_scratch(totals):
    shapes = []
    for total in totals:
        count = total.shape[0]
        shapes += [pltpu.VMEM((count - 1,) + total.shape[1:], LOW)] + sem_scratch(count)[:2]
    return shapes


def far_reduces(totals, rows, scratch):
    reduces = []
    for total, span in zip(totals, row_spans(rows)):
        (came, sends, receives), scratch = take(scratch, 3)
        came = (None, None, None, came)
        reduces.append(Reduce(None, span, "mod", came, None, total, total, (sends, receives, None)))
    return reduces, scratch


class Product:
    def __init__(self, left, right, scratch):
        self.left, self.right = left, right
        self.rows_, self.sums, self.came, self.loads, self.sends, self.receives = scratch
        self.core = lax.axis_index("core")

    @staticmethod
    def scratch(count, rows, tokens, columns):
        sums = pltpu.VMEM((2, 2, count, rows, columns), LOW)
        sems = [pltpu.SemaphoreType.DMA((4,))] * 3
        return [pltpu.VMEM((4, count, rows, tokens), LOW), sums, sums] + sems

    def _load(self, near, own):
        core = self.core if own else 1 - self.core
        slot = 2 * own + near
        return pltpu.make_async_copy(
            self.left.at[:, near, core], self.rows_.at[slot], self.loads.at[slot]
        )

    def load(self):
        for own in (0, 1):
            for near in (0, 1):
                self._load(near, own).start()

    def _copy(self, mod, near):
        return remote(
            self.sums.at[mod, near],
            self.came.at[mod, near],
            self.sends,
            self.receives,
            2 * mod + near,
            dict(core=1 - self.core),
        )

    def _blocks(self, near, own, store):
        count, rows, tokens = self.rows_.shape[1:]
        columns = self.right.shape[2]
        self._load(near, own).wait()
        left = self.rows_[2 * own + near].reshape(count * rows, tokens)
        width = columns if columns <= 1024 else columns // 2
        width = width if width % LANES == 0 else columns
        for mod in (0, 1):
            for at in range(0, columns, width):
                product = times(left, self.right[mod, :, at : at + width])
                store(mod, at, width, product.reshape(count, rows, width))

    def send(self):
        for near in (0, 1):

            def store(mod, at, width, product, near=near):
                self.sums[mod, near, :, :, at : at + width] = product.astype(LOW)

            self._blocks(near, 0, store)
            for mod in (0, 1):
                self._copy(mod, near).start()

    def sum(self):
        for near in (0, 1):
            for mod in (0, 1):
                self._copy(mod, near).wait_send()
                self._copy(mod, near).wait_recv()

            def store(mod, at, width, product, near=near):
                came = self.came[mod, near, :, :, at : at + width]
                self.sums[mod, near, :, :, at : at + width] = (product + came.astype(WIDE)).astype(LOW)

            self._blocks(near, 1, store)


def total_shapes(count, rows, columns):
    return [jax.ShapeDtypeStruct((count, span[1], columns), LOW) for span in row_spans(rows)]


def weight_kernel(*refs, spans, stored):
    count = stored + (spans > 0)
    sides, refs = take(refs, 2 * count)
    outs, refs = take(refs, stored)
    totals, scratch = take(refs, spans)
    products = []
    for number in range(count):
        used, scratch = take(scratch, 6)
        products.append(Product(sides[2 * number], sides[2 * number + 1], used))
    reduces = []
    if spans:
        reduces, scratch = resident_reduces(products[0].sums, scratch, totals)
    (out_sems,) = scratch
    products[0].load()
    greet()
    copies = []
    for number, product in enumerate(products):
        product.send()
        if number + 1 < count:
            products[number + 1].load()
        product.sum()
        if spans and number == 0:
            run(reduces, "start")
            continue
        copy = pltpu.make_async_copy(product.sums, outs[len(copies)], out_sems.at[len(copies)])
        copy.start()
        copies.append(copy)
        if spans and number == 1:
            run(reduces, "merge")
    if spans and count == 1:
        run(reduces, "merge")
    run(reduces, "total")
    for copy in copies:
        copy.wait()


def weight_call(summed, stored, number):
    pairs = summed + stored
    count, _, _, rows, tokens = pairs[0][0].shape
    columns = pairs[0][1].shape[2]
    totals = total_shapes(count, rows, columns) if summed else []
    scratch = []
    for left, right in pairs:
        scratch += Product.scratch(count, left.shape[3], tokens, right.shape[2])
    if summed:
        scratch += resident_scratch((2, 2, count, rows, columns), False)
    out = pl.pallas_call(
        partial(weight_kernel, spans=len(totals), stored=len(stored)),
        out_shape=tuple(
            jax.ShapeDtypeStruct((2, 2, count, left.shape[3], right.shape[2]), LOW) for left, right in stored
        )
        + tuple(totals),
        in_specs=[ANY, VMEM] * len(pairs),
        out_specs=(ANY,) * len(stored) + (VMEM,) * len(totals),
        scratch_shapes=scratch + [pltpu.SemaphoreType.DMA((2,))],
        compiler_params=pltpu.CompilerParams(
            collective_id=number, has_side_effects=True, vmem_limit_bytes=63 * 2**20
        ),
        name="weight_grads",
    )(*[side for pair in pairs for side in pair])
    return out[: len(stored)], out[len(stored) :]


def weight_grads(hidden, branch, mlp, pre, mixed, attn):
    summed, stored = [(hidden, branch)], [(mlp, pre), (mixed, attn)]
    if mlp.shape[3] % 8 == 0:
        return weight_call(summed, stored, 4)
    _, totals = weight_call(summed, [], 4)
    sums, _ = weight_call([], stored, 5)
    return sums, totals


def last_kernel(*refs, spans):
    act, joint, small_s = refs[:3]
    totals, refs = take(refs[3:], spans)
    qkv_out, fc1_out, small_w, *scratch = refs
    qkv_scratch, scratch = take(scratch, 6)
    qkv = Product(act, joint, qkv_scratch)
    qkv_sum, scratch = resident_reduces(qkv.sums, scratch)
    fc1_sum, scratch = far_reduces(totals, fc1_out.shape[0], scratch)
    small_sends, small_receives, local = scratch
    small = Gather(small_w, small_sends, small_receives)
    qkv.load()
    greet()
    small.start_far(small_s, local.at[0])
    run(fc1_sum, "start_far")
    qkv.send()
    small.finish_far(small_s, local.at[0])
    small.spread()
    qkv.sum()
    small.cross()
    run(qkv_sum, "start")
    small.close()
    small.end()
    run(qkv_sum, "merge")
    run(qkv_sum, "total", "start_far")
    for part in fc1_sum:
        part.final(fc1_out)
    for part in qkv_sum:
        part.final(qkv_out)


def last_scatter(act, joint, totals, small_s):
    count, _, _, rows, tokens = act.shape
    fc1_columns = totals[0].shape[2]
    columns = joint.shape[2]
    return pl.pallas_call(
        partial(last_kernel, spans=len(totals)),
        out_shape=(
            jax.ShapeDtypeStruct((rows, columns), WIDE),
            jax.ShapeDtypeStruct((sum(total.shape[1] for total in totals), fc1_columns), WIDE),
            whole_shape(small_s),
        ),
        in_specs=[ANY, VMEM, VMEM] + [VMEM] * len(totals),
        out_specs=(VMEM, VMEM, ANY),
        scratch_shapes=Product.scratch(count, rows, tokens, columns)
        + resident_scratch((2, 2, count, rows, columns))
        + far_scratch(totals)
        + gather_scratch(1, 1),
        compiler_params=pltpu.CompilerParams(
            collective_id=3, has_side_effects=True, vmem_limit_bytes=60 * 2**20
        ),
        name="last_scatter",
    )(act, joint, small_s, *totals)


def split3(v):
    hi = v.astype(LOW).astype(WIDE)
    mid = (v - hi).astype(LOW).astype(WIDE)
    lo = v - hi - mid
    return hi, mid, lo


def attend_back_kernel(*refs, fc2_spans, spans):
    qkv_ref, seg_ref, mixed_ref, lse_ref, up_ref, fc1_sums, proj_sums = refs[:7]
    fc2_totals, refs = take(refs[7:], fc2_spans)
    out_ref, fc2_out, proj_out, *refs = refs
    fc1_totals, refs = take(refs, spans)
    qh, kh, vh, uh, stage, stage_sems, leave, leave_sems, *scratch = refs
    proj, scratch = loaded_reduces(proj_sums, scratch)
    fc1, scratch = loaded_reduces(fc1_sums, scratch, fc1_totals)
    fc2, scratch = far_reduces(fc2_totals, fc2_out.shape[0], scratch)
    T = mixed_ref.shape[0]
    chunks = T // CHUNK
    greet()
    run(fc2, "start_far")
    run(fc1, "start")

    def load(i):
        rows = pl.ds(pl.multiple_of(i * CHUNK, CHUNK), CHUNK)
        slot = lax.rem(i, 2)
        return pltpu.make_async_copy(qkv_ref.at[rows], stage.at[slot], stage_sems.at[slot])

    load(0).start()

    def fill(i, carry):
        rows = pl.ds(pl.multiple_of(i * CHUNK, CHUNK), CHUNK)

        @pl.when(i + 1 < chunks)
        def _():
            load(i + 1).start()

        load(i).wait()
        qkv = stage.at[lax.rem(i, 2)]
        lane = lanes((CHUNK, LANES))
        qc, kc = seg_codes(seg_ref[rows, :], CHUNK)
        kc = jnp.where(jnp.logical_and(lane >= HEAD + 4, lane < HEAD + 7), 1.0, kc).astype(LOW)
        ones = jnp.where(jnp.logical_and(lane >= HEAD, lane < HEAD + 3), 1.0, 0.0).astype(LOW)

        def spread(v, at, base):
            hi, mid, lo = split3(v)
            return jnp.where(
                lane == at, hi, jnp.where(lane == at + 1, mid, jnp.where(lane == at + 2, lo, base))
            )

        for h in range(HEADS):
            a, b = h * HEAD, (h + 1) * HEAD
            qa = spread(-lse_ref[rows, h : h + 1] * HEAD**0.5, HEAD + 4, qc).astype(LOW)
            qh[h, rows, :] = pad_head(qkv[:, a:b], qa)
            kh[h, rows, :] = pad_head(qkv[:, D + a : D + b], kc)
            vh[h, rows, :] = pad_head(qkv[:, 2 * D + a : 2 * D + b], ones)
            u = up_ref[rows, a:b]
            delta = jnp.sum(u.astype(WIDE) * mixed_ref[rows, a:b].astype(WIDE), axis=1, keepdims=True)
            ua = spread(-delta, HEAD, jnp.zeros((CHUNK, LANES), WIDE)).astype(LOW)
            uh[h, rows, :] = pad_head(u, ua)
        return carry

    lax.fori_loop(0, chunks, fill, 0)
    across = (((1,), (1,)), ((), ()))
    tasks = {
        4: lambda: (run(fc1, "merge"), run(proj, "start")),
        11: lambda: run(proj, "merge"),
        14: lambda: run(proj, "total", "start_far"),
    }

    def head(h, carry):
        k = kh[h]
        v = vh[h]
        kt = k.T
        dk = jnp.zeros((T, LANES), WIDE)
        dv = jnp.zeros((T, LANES), WIDE)
        for i in range(chunks):
            rows = pl.ds(i * CHUNK, CHUNK)
            q = qh[h, rows, :]
            u = uh[h, rows, :]
            s = lax.dot_general(k, q, across, preferred_element_type=WIDE)
            p = jnp.exp2(s * (HEAD**-0.5 * LOG2E))
            dp = lax.dot_general(v, u, across, preferred_element_type=WIDE)
            ds = (p * dp).astype(LOW)
            dv = dv + jnp.dot(p.astype(LOW), u, preferred_element_type=WIDE)
            dk = dk + jnp.dot(ds, q, preferred_element_type=WIDE)
            dqt = jnp.dot(kt, ds, preferred_element_type=WIDE)
            qh[h, rows, :] = (dqt.T * HEAD**-0.5).astype(LOW)
        kh[h] = (dk * HEAD**-0.5).astype(LOW)
        vh[h] = dv.astype(LOW)
        for at, task in tasks.items():

            @pl.when(h == at)
            def _(task=task):
                task()

        return carry

    lax.fori_loop(0, HEADS, head, 0)

    def store(i, side):
        rows = pl.ds(pl.multiple_of(i * CHUNK, CHUNK), CHUNK)
        return pltpu.make_async_copy(
            leave.at[side], out_ref.at[side, rows], leave_sems.at[side]
        )

    def drain(i, carry):
        rows = pl.ds(pl.multiple_of(i * CHUNK, CHUNK), CHUNK)
        parts = [g[h, rows, :][:, :HEAD] for g in (qh, kh, vh) for h in range(HEADS)]
        for side in range(2):

            @pl.when(i > 0)
            def _(side=side):
                store(i - 1, side).wait()

            own = parts[side * len(parts) // 2 : (side + 1) * len(parts) // 2]
            leave[side] = jnp.concatenate(own, axis=1)
            store(i, side).start()
        return carry

    lax.fori_loop(0, chunks, drain, 0)
    run(fc1, "total")
    for side in range(2):
        store(chunks - 1, side).wait()
    for part in fc2:
        part.final(fc2_out)
    for part in proj:
        part.final(proj_out)


def attend_back(qkv, segments, mixed, lse, upstream, fc1_sums, proj_sums, fc2_totals):
    tokens = qkv.shape[0]
    count, rows, columns = fc1_sums.shape[2:]
    totals = total_shapes(count, rows, columns)
    fc2_rows = sum(total.shape[1] for total in fc2_totals)
    out = pl.pallas_call(
        partial(attend_back_kernel, fc2_spans=len(fc2_totals), spans=len(totals)),
        out_shape=(
            jax.ShapeDtypeStruct((2, tokens, 3 * HEADS * HEAD // 2), LOW),
            jax.ShapeDtypeStruct((fc2_rows, fc2_totals[0].shape[2]), WIDE),
            jax.ShapeDtypeStruct(proj_sums.shape[3:], WIDE),
        )
        + tuple(totals),
        in_specs=[ANY] + [VMEM] * 4 + [ANY] * 2 + [VMEM] * len(fc2_totals),
        out_specs=(ANY, VMEM, VMEM) + (VMEM,) * len(totals),
        scratch_shapes=[pltpu.VMEM((HEADS, tokens, LANES), LOW)] * 4
        + [pltpu.VMEM((2, CHUNK, 3 * HEADS * HEAD), LOW), pltpu.SemaphoreType.DMA((2,))]
        + [pltpu.VMEM((2, CHUNK, 3 * HEADS * HEAD // 2), LOW), pltpu.SemaphoreType.DMA((2,))]
        + loaded_scratch(proj_sums.shape)
        + loaded_scratch(fc1_sums.shape, False)
        + far_scratch(fc2_totals),
        compiler_params=pltpu.CompilerParams(
            collective_id=2, has_side_effects=True, vmem_limit_bytes=63 * 2**20
        ),
        name="attend_back",
    )(qkv, segments.reshape(tokens, 1), mixed, lse, upstream, fc1_sums, proj_sums, *fc2_totals)
    return out[0], out[1], out[2], out[3:]


def normed(values):
    centre = values - jnp.mean(values, axis=-1, keepdims=True)
    inverse = lax.rsqrt(jnp.mean(centre * centre, axis=-1, keepdims=True) + EPS)
    return centre * inverse, inverse


def row_of(table, slot, group):
    return table[pl.ds(slot, 1), group * D : (group + 1) * D]


def column_sums(values):
    return jnp.sum(values, axis=0, keepdims=True)


def times_across(left, right):
    return lax.dot_general(left, right, (((1,), (1,)), ((), ())), preferred_element_type=WIDE)


def tile(*shape):
    return pl.BlockSpec((CHUNK,) + shape, lambda i, slots: (i,) + (0,) * len(shape))


def half_tile(columns):
    return pl.BlockSpec((2, CHUNK, columns), lambda i, slots: (0, i, 0))


def fixed(*shape):
    return pl.BlockSpec(
        shape, lambda i, slots: (0,) * len(shape), pipeline_mode=pl.Buffered(1)
    )


def turned_tile(rows):
    return pl.BlockSpec((rows, CHUNK), lambda i, slots: (0, i))


def per_tile(rows, columns):
    return pl.BlockSpec((1, rows, columns), lambda i, slots: (i, 0, 0))


def tile_call(kernel, tokens, in_specs, out_specs, out_shapes, scratch, name, flops, traffic):
    return pl.pallas_call(
        kernel,
        out_shape=tuple(jax.ShapeDtypeStruct(shape, dtype) for shape, dtype in out_shapes),
        grid_spec=pltpu.PrefetchScalarGridSpec(
            num_scalar_prefetch=1,
            grid=(tokens // CHUNK,),
            in_specs=in_specs,
            out_specs=out_specs,
            scratch_shapes=scratch,
        ),
        compiler_params=pltpu.CompilerParams(
            dimension_semantics=("arbitrary",), vmem_limit_bytes=63 * 2**20
        ),
        cost_estimate=pl.CostEstimate(flops=flops, bytes_accessed=traffic, transcendentals=0),
        name=name,
    )


def qkv_forward_kernel(slots, x_ref, table, bias, weight, act_ref, joint_ref):
    slot = slots[pl.program_id(0)]
    h1, _ = normed(x_ref[...].astype(WIDE))
    act = (h1 * (1.0 + row_of(table, slot, 1)) + row_of(table, slot, 0)).astype(LOW)
    act_ref[...] = act.T
    joint = jnp.concatenate([times(act, weight[0]), times(act, weight[1])], axis=1)
    joint_ref[...] = (joint + bias[...]).astype(LOW)


def qkv_forward(slots, x_in, table, bias, weight):
    tokens = x_in.shape[0]
    wide = 3 * D
    return tile_call(
        qkv_forward_kernel,
        tokens,
        [tile(D), fixed(*table.shape), fixed(1, wide), fixed(*weight.shape)],
        (turned_tile(D), tile(wide)),
        (((D, tokens), LOW), ((tokens, wide), LOW)),
        [],
        "qkv_forward",
        2 * tokens * D * wide,
        weight.size * 2 + tokens * D * 10,
    )(slots, x_in, table, bias, weight)


GELU = 0.7978845608028654
CUBIC = 0.044715
SPAN = 768


def middle_kernel(
    slots, x_ref, g_ref, mixed_ref, table, bias, proj, fc1, fc2,
    block_ref, mlp_ref, hidden_turned, dpre_ref, dbranch_ref, dattn_ref, dmixed_ref, dx1_ref, sums_ref, dpre_sums,
    slope,
):
    slot = slots[pl.program_id(0)]
    gate1, shift2, scale2, gate2 = (row_of(table, slot, group) for group in (2, 3, 4, 5))
    half = FF // 2
    mixed = mixed_ref[...]
    attn_out = jnp.concatenate([times(mixed, proj[0]), times(mixed, proj[1])], axis=1)
    attn_out = attn_out + bias[:, 2 * D : 3 * D]
    x1 = x_ref[...].astype(WIDE) + gate1 * attn_out
    h2, inverse = normed(x1)
    mlp_in = (h2 * (1.0 + scale2) + shift2).astype(LOW)
    mlp_ref[...] = mlp_in.T
    parts = [None, None]
    for side in range(2):
        for at in range(0, half, SPAN):
            column = side * half + at
            pre = times(mlp_in, fc1[side, :, at : at + SPAN])
            pre = pre + bias[:, 3 * D + column : 3 * D + column + SPAN]
            square = pre * pre
            bend = jnp.tanh(GELU * pre * (1.0 + CUBIC * square))
            rise = 0.5 * (1.0 + bend)
            hidden = (pre * rise).astype(LOW)
            for number in range(2):
                part = times(hidden, fc2[number, column : column + SPAN])
                parts[number] = part if column == 0 else parts[number] + part
            hidden_turned[column : column + SPAN, :] = hidden.T
            slope[:, column : column + SPAN] = rise + 0.5 * GELU * pre * (1.0 - bend * bend) * (
                1.0 + 3.0 * CUBIC * square
            )
    branch = jnp.concatenate(parts, axis=1) + bias[:, 3 * D + FF :]
    block_ref[...] = (x1 + gate2 * branch).astype(LOW)
    g = g_ref[...].astype(WIDE)
    dbranch = (gate2 * g).astype(LOW)
    sums_ref[0, 3:4, :] = column_sums(g * branch)
    sums_ref[0, 5:6, :] = column_sums(dbranch.astype(WIDE))
    left, right = dbranch[:, : D // 2], dbranch[:, D // 2 :]
    dbranch_ref[0] = left
    dbranch_ref[1] = right
    for side in range(2):
        for at in range(0, half, SPAN):
            column = side * half + at
            rows = slice(column, column + SPAN)
            dhidden = times_across(left, fc2[0, rows]) + times_across(right, fc2[1, rows])
            dpre = (dhidden * slope[:, rows]).astype(LOW)
            dpre_ref[side, :, at : at + SPAN] = dpre
            dpre_sums[0, :, rows] = column_sums(dpre.astype(WIDE))
    dmlp = times_across(dpre_ref[0], fc1[0]) + times_across(dpre_ref[1], fc1[1])
    sums_ref[0, 1:2, :] = column_sums(dmlp)
    sums_ref[0, 2:3, :] = column_sums(dmlp * h2)
    dh2 = dmlp * (1.0 + scale2)
    dx1 = g + inverse * (
        dh2
        - jnp.mean(dh2, axis=-1, keepdims=True)
        - h2 * jnp.mean(dh2 * h2, axis=-1, keepdims=True)
    )
    dx1_ref[...] = dx1
    sums_ref[0, 0:1, :] = column_sums(dx1 * attn_out)
    dattn = (gate1 * dx1).astype(LOW)
    sums_ref[0, 4:5, :] = column_sums(dattn.astype(WIDE))
    left, right = dattn[:, : D // 2], dattn[:, D // 2 :]
    dattn_ref[0] = left
    dattn_ref[1] = right
    dmixed_ref[...] = (times_across(left, proj[0]) + times_across(right, proj[1])).astype(LOW)
    sums_ref[0, 6:8, :] = jnp.zeros((2, D), WIDE)


def middle(slots, x_in, out_grad, mixed, table, bias, proj, fc1, fc2):
    tokens = x_in.shape[0]
    tiles = tokens // CHUNK
    return tile_call(
        middle_kernel,
        tokens,
        [
            tile(D),
            tile(D),
            tile(D),
            fixed(*table.shape),
            fixed(*bias.shape),
            fixed(*proj.shape),
            fixed(*fc1.shape),
            fixed(*fc2.shape),
        ],
        (
            tile(D),
            turned_tile(D),
            turned_tile(FF),
            half_tile(FF // 2),
            half_tile(D // 2),
            half_tile(D // 2),
            tile(D),
            tile(D),
            per_tile(8, D),
            per_tile(1, FF),
        ),
        (
            ((tokens, D), LOW),
            ((D, tokens), LOW),
            ((FF, tokens), LOW),
            ((2, tokens, FF // 2), LOW),
            ((2, tokens, D // 2), LOW),
            ((2, tokens, D // 2), LOW),
            ((tokens, D), LOW),
            ((tokens, D), WIDE),
            ((tiles, 8, D), WIDE),
            ((tiles, 1, FF), WIDE),
        ),
        [pltpu.VMEM((CHUNK, FF), WIDE)],
        "middle",
        4 * tokens * (D * D + 2 * D * FF),
        (D * D + 2 * D * FF) * 2 + tokens * D * 40,
    )(slots, x_in, out_grad, mixed, table, bias, proj, fc1, fc2)


def qkv_backward_kernel(slots, joint_ref, x_ref, dx1_ref, table, weight, x_grad_ref, sums_ref, joint_sums):
    slot = slots[pl.program_id(0)]
    dact = times_across(joint_ref[0], weight[0]) + times_across(joint_ref[1], weight[1])
    h1, inverse = normed(x_ref[...].astype(WIDE))
    sums_ref[0, 0:1, :] = column_sums(dact)
    sums_ref[0, 1:2, :] = column_sums(dact * h1)
    sums_ref[0, 2:8, :] = jnp.zeros((6, D), WIDE)
    dh1 = dact * (1.0 + row_of(table, slot, 1))
    x_grad_ref[...] = dx1_ref[...] + inverse * (
        dh1
        - jnp.mean(dh1, axis=-1, keepdims=True)
        - h1 * jnp.mean(dh1 * h1, axis=-1, keepdims=True)
    )
    for side in range(2):
        joint_sums[0, side : side + 1, :] = column_sums(joint_ref[side].astype(WIDE))


def qkv_backward(slots, joint, x_in, dx1, table, weight):
    tokens = x_in.shape[0]
    tiles = tokens // CHUNK
    half = 3 * D // 2
    return tile_call(
        qkv_backward_kernel,
        tokens,
        [half_tile(half), tile(D), tile(D), fixed(*table.shape), fixed(*weight.shape)],
        (tile(D), per_tile(8, D), per_tile(2, half)),
        (((tokens, D), WIDE), ((tiles, 8, D), WIDE), ((tiles, 2, half), WIDE)),
        [],
        "qkv_backward",
        2 * tokens * D * 3 * D,
        weight.size * 2 + tokens * D * 18,
    )(slots, joint, x_in, dx1, table, weight)


def swap(values, axis):
    return lax.ppermute(values, axis, [(0, 1), (1, 0)])


def times(left, right):
    return jnp.dot(left, right, preferred_element_type=WIDE)


def times_back(left, right):
    return lax.dot_general(left, right, (((1,), (1,)), ((), ())), preferred_element_type=WIDE)


def body(
    x_in,
    cond,
    segments,
    out_grad,
    qkv_weight,
    qkv_moment,
    qkv_average,
    proj_weight,
    proj_moment,
    proj_average,
    fc1_weight,
    fc1_moment,
    fc1_average,
    fc2_weight,
    fc2_moment,
    fc2_average,
    bias_weight,
    bias_moment,
    bias_average,
    ada_weight,
    ada_moment,
    ada_average,
    adab_weight,
    adab_moment,
    adab_average,
):
    tokens, width = x_in.shape
    row_devices = lax.axis_size(ROWS)
    devices = lax.axis_size(ALL)
    row_index = lax.axis_index(ROWS)
    images = cond.shape[0] // 2

    cond_silu, silu_back = jax.vjp(jax.nn.silu, cond.astype(WIDE))
    half_silu = lax.dynamic_index_in_dim(
        cond_silu.astype(LOW).reshape(-1, 2, width // 2), lax.axis_index("mod"), 1, False
    )
    own_bias = bias_weight.shape[0]
    bias_block = jnp.pad(bias_weight.astype(LOW), (0, 8 * LANES - own_bias)).reshape(8, LANES)
    blank = jnp.zeros((8, LANES // 2), LOW)
    ada_low = ada_weight.astype(LOW)
    ada_columns = lax.all_to_all(ada_low, ROWS, split_axis=1, concat_axis=0, tiled=True)
    small_w, qkv_w, proj_w, fc1_w = first_gather(
        jnp.concatenate([half_silu, bias_block, blank], axis=1),
        qkv_weight.astype(LOW),
        proj_weight.astype(LOW),
        fc1_weight.astype(LOW),
    )
    small = small_w.reshape(2, row_devices * 8, -1)
    silu_all = jnp.concatenate([small[0, :, : width // 2], small[1, :, : width // 2]], axis=1)
    bias_all = small[:, :, width // 2 : width // 2 + LANES].reshape(2, row_devices, -1)
    bias_full = jnp.swapaxes(bias_all[:, :, :own_bias], 0, 1).reshape(1, -1).astype(WIDE)
    adab_low = adab_weight.astype(LOW).astype(WIDE)
    mod_columns = (times(silu_all, ada_columns) + adab_low).astype(LOW)
    mod_rows = lax.all_to_all(mod_columns, ALL, split_axis=0, concat_axis=1, tiled=True)
    table = jnp.swapaxes(mod_rows.reshape(images, row_devices, 2, -1), 1, 2).reshape(images, -1)
    table = table.astype(WIDE)

    def joined(whole):
        return whole.reshape(2, -1, whole.shape[-1])

    qkv_low = joined(qkv_w)
    slots = segments[::CHUNK]
    joint_bias = jnp.concatenate(
        [bias_full[:, 0:width], jnp.zeros((1, width), WIDE), bias_full[:, width : 2 * width]], axis=1
    )
    def blocked(turned):
        return turned.reshape(row_devices // 4, 2, 2, -1, tokens)

    act_turned, joint_rows = qkv_forward(slots, x_in, table, joint_bias, qkv_low)
    mixture, mixture_turned, log_totals, proj_w, fc1_w, fc2_w = attend(
        joint_rows, segments, fc2_weight.astype(LOW), proj_w, fc1_w
    )
    (
        block_out, mlp_turned, hidden_turned, pre_halves, branch_halves, attn_halves, mixture_grad, middle_grad, sums, pre_sums,
    ) = middle(
        slots, x_in, out_grad, mixture, table, bias_full, joined(proj_w), joined(fc1_w), joined(fc2_w)
    )
    (fc1_sums, proj_sums), fc2_totals = weight_grads(
        blocked(hidden_turned),
        branch_halves,
        blocked(mlp_turned),
        pre_halves,
        blocked(mixture_turned),
        attn_halves,
    )
    joint_halves, fc2_shard, proj_shard, fc1_totals = attend_back(
        joint_rows,
        segments,
        mixture,
        log_totals,
        mixture_grad,
        fc1_sums,
        proj_sums,
        fc2_totals,
    )
    x_grad, first_sums, joint_sums = qkv_backward(
        slots, joint_halves, x_in, middle_grad, table, qkv_low
    )

    chooser = (slots[None, :] == jnp.arange(images, dtype=jnp.int32)[:, None]).astype(WIDE)
    tile_mod_grad = jnp.concatenate([first_sums[:, 0:2], sums[:, 0:4]], axis=1)
    slot_mod_grad = jnp.sum(chooser[:, :, None, None] * tile_mod_grad[None], axis=1)
    slot_mod_grad = slot_mod_grad.reshape(images, -1).astype(LOW)
    by_half = jnp.swapaxes(slot_mod_grad.reshape(images, 2, -1), 0, 1).reshape(2 * images, -1)
    qkv_shard, fc1_shard, mod_grad_w = last_scatter(
        blocked(act_turned), joint_halves, fc1_totals, by_half
    )
    mod_grads = mod_grad_w.reshape(2, row_devices, 2, images, -1)
    mod_grads = lax.dynamic_index_in_dim(mod_grads, lax.axis_index("mod"), 2, False)
    mod_grad_all = jnp.swapaxes(mod_grads, 0, 1).reshape(2 * row_devices * images, -1)
    own_rows = ada_weight.shape[0]
    own_silu = lax.dynamic_slice_in_dim(silu_all, row_index * own_rows, own_rows, 1)
    ada_shard = jnp.einsum("ic,io->co", own_silu, mod_grad_all, preferred_element_type=WIDE)
    own_columns = adab_weight.shape[1]
    adab_shard = jnp.sum(
        lax.dynamic_slice_in_dim(mod_grad_all, row_index * own_columns, own_columns, 1).astype(WIDE),
        axis=0,
    )
    silu_part = times_back(mod_grad_all, ada_low)
    silu_part = lax.all_to_all(silu_part, ROWS, split_axis=0, concat_axis=1, tiled=True)
    cond_grad = silu_back(silu_part + swap(silu_part, "mod"))[0]

    joint_sum = jnp.sum(joint_sums, axis=0).reshape(-1)
    sum_rows = jnp.sum(sums, axis=0)
    grad_bias = jnp.concatenate(
        [
            joint_sum[0:width],
            joint_sum[2 * width :],
            sum_rows[4],
            jnp.sum(pre_sums, axis=0).reshape(-1),
            sum_rows[5],
        ]
    ).reshape(devices, -1)
    bias_shard = jnp.sum(
        lax.all_to_all(grad_bias, ALL, split_axis=0, concat_axis=0, tiled=True), axis=0
    )

    rates = step_rates(tokens * devices)
    states_out = []
    states_out.extend(nesterov(qkv_weight, qkv_moment, qkv_average, qkv_shard, rates[0]))
    states_out.extend(nesterov(proj_weight, proj_moment, proj_average, proj_shard, rates[1]))
    states_out.extend(nesterov(fc1_weight, fc1_moment, fc1_average, fc1_shard, rates[2]))
    states_out.extend(nesterov(fc2_weight, fc2_moment, fc2_average, fc2_shard, rates[3]))
    states_out.extend(nesterov(bias_weight, bias_moment, bias_average, bias_shard, rates[4]))
    states_out.extend(nesterov(ada_weight, ada_moment, ada_average, ada_shard, rates[5]))
    states_out.extend(
        nesterov(adab_weight, adab_moment, adab_average, adab_shard.reshape(1, -1), rates[6])
    )
    return (block_out, x_grad, cond_grad) + tuple(states_out)


def solution(mesh):
    far = mesh.shape["dp"] // 4
    fine = Mesh(mesh.devices.reshape(far, 2, 2, mesh.shape["mod"]), ALL)
    tokens = P(ALL, None)
    images = P(ROWS, None)
    trunk = P(ROWS, "mod")
    bias = P(ALL)
    adab = P("mod", ROWS)
    states = (trunk,) * 12 + (bias,) * 3 + (trunk,) * 3 + (adab,) * 3
    return jax.shard_map(
        body,
        mesh=fine,
        in_specs=(tokens, images, bias, tokens) + states,
        out_specs=(tokens, tokens, images) + states,
        check_vma=False,
    )
```

```python
from functools import partial

import jax
import jax.numpy as jnp
from jax import lax
from jax.experimental import pallas as pl
from jax.experimental.pallas import tpu as pltpu
from jax.sharding import Mesh
from jax.sharding import PartitionSpec as P

D = 1152
HEADS = 16
HEAD = 72
FF = 4608
LANES = 128
CHUNK = 256

ROWS = ("far", "near", "core")
ALL = ("far", "near", "core", "mod")
LOW = jnp.bfloat16
WIDE = jnp.float32
LOG2E = 1.4426950408889634
NEG = -1e30
MESH = pl.DeviceIdType.MESH
VMEM = pl.BlockSpec(memory_space=pltpu.VMEM)
ANY = pl.BlockSpec(memory_space=pl.ANY)

EPS = 1e-06
MOMENTUM = 0.9
DECAY = 0.5


def step_rates(tokens_all):
    base_rate = tokens_all ** (-0.5)
    return (
        2.5 * D ** (-0.5) * base_rate,
        3.0 * D ** (-0.5) * base_rate,
        3.3 * D ** (-0.5) * base_rate,
        2.8 * FF ** (-0.5) * base_rate,
        0.5 * base_rate,
        2.0 * D ** (-0.5) * base_rate,
        0.3 * base_rate,
    )


def nesterov(weight, moment, average, gradient, rate):
    moment = MOMENTUM * moment + gradient
    weight = weight - rate * (gradient + MOMENTUM * moment)
    average = DECAY * average + (1.0 - DECAY) * weight
    return (weight, moment, average)


def places():
    return {name: lax.axis_index(name) for name in ALL}


def greet():
    here = places()
    count = lax.axis_size("far")
    others = [dict(far=lax.rem(here["far"] + d, count)) for d in range(1, count)]
    others += [{name: 1 - here[name]} for name in ("near", "core", "mod")]
    barrier = pltpu.get_barrier_semaphore()
    for other in others:
        pl.semaphore_signal(barrier, inc=1, device_id=other, device_id_type=MESH)
    pl.semaphore_wait(barrier, len(others))


def remote(source, target, sends, receives, slot, other):
    return pltpu.make_async_remote_copy(
        src_ref=source,
        dst_ref=target,
        send_sem=sends.at[slot],
        recv_sem=receives.at[slot],
        device_id=other,
        device_id_type=MESH,
    )


def messages(count):
    return count - 1 + 8


class Gather:
    def __init__(self, whole, sends, receives):
        self.whole, self.sends, self.receives = whole, sends, receives
        self.here = places()
        self.count = lax.axis_size("far")
        rows = whole.shape[4]
        self.rows = rows
        self.split = rows if rows % 8 else 8 * ((rows // 8 + 1) // 2)

    def _block(self, far):
        return self.whole.at[self.here["mod"], far, self.here["near"], self.here["core"]]

    def _far(self, shard, distance):
        far = self.here["far"]
        other = dict(far=lax.rem(far + distance, self.count))
        return remote(shard, self._block(far), self.sends, self.receives, distance - 1, other)

    def _far_came(self, shard, distance):
        origin = lax.rem(self.here["far"] + self.count - distance, self.count)
        return remote(
            shard, self._block(origin), self.sends, self.receives, distance - 1, dict(far=origin)
        )

    def start_far(self, shard, local):
        pltpu.make_async_copy(shard, self._block(self.here["far"]), local).start()
        for distance in range(1, self.count):
            self._far(shard, distance).start()

    def finish_far(self, shard, local):
        pltpu.make_async_copy(shard, self._block(self.here["far"]), local).wait()
        for distance in range(1, self.count):
            self._far(shard, distance).wait_send()
            self._far_came(shard, distance).wait_recv()

    def _quad(self, flips, first, size):
        near, core, mod = (
            1 - self.here[name] if name in flips else self.here[name] for name in ("near", "core", "mod")
        )
        return self.whole.at[mod, :, near, core, pl.ds(first, size)]

    def _step(self, name):
        head, rest = (0, self.split), (self.split, self.rows - self.split)
        full = (0, self.rows)
        return {
            "near": ((), "near", full, 0),
            "mod": ((), "mod", full, 1),
            "near_mod": (("near",), "mod", head, 2),
            "mod_near": (("mod",), "near", rest, 3),
            "core": ((), "core", full, 4),
            "near_core": (("near",), "core", full, 5),
            "mod_core": (("mod",), "core", full, 6),
            "both_core": (("near", "mod"), "core", full, 7),
        }[name]

    def _copy(self, name, incoming):
        flips, axis, span, slot = self._step(name)
        if span[1] == 0:
            return None
        quad = self._quad(flips + (axis,) if incoming else flips, *span)
        other = {axis: 1 - self.here[axis]}
        return remote(quad, quad, self.sends, self.receives, self.count - 1 + slot, other)

    def start(self, *names):
        for name in names:
            copy = self._copy(name, False)
            if copy is not None:
                copy.start()

    def receive(self, *names):
        for name in names:
            copy = self._copy(name, True)
            if copy is not None:
                copy.wait_recv()

    def spread(self):
        self.start("near", "mod", "core")

    def cross(self):
        self.receive("near")
        self.start("near_mod", "near_core")
        self.receive("mod")
        self.start("mod_near", "mod_core")

    def close(self):
        self.receive("near_mod", "mod_near")
        self.start("both_core")

    def end(self):
        self.receive("core", "near_core", "mod_core", "both_core")
        for name in (
            "near", "mod", "near_mod", "mod_near", "core", "near_core", "mod_core", "both_core",
        ):
            copy = self._copy(name, False)
            if copy is not None:
                copy.wait_send()


def gather_scratch(weights, locals_):
    count = lax.axis_size("far")
    shapes = [pltpu.SemaphoreType.DMA((messages(count),))] * (2 * weights)
    return shapes + [pltpu.SemaphoreType.DMA((locals_,))]


def whole_shape(shard):
    return jax.ShapeDtypeStruct((2, lax.axis_size("far"), 2, 2) + shard.shape, LOW)


def modulate(small_w, ada, table, local, small, partials, came_core, came_near, came_far, own, sends, receives):
    here = places()
    count = lax.axis_size("far")
    far, near, core, mod = (here[name] for name in ALL)
    row_devices = 4 * count
    rows = D // row_devices
    fetch = pltpu.make_async_copy(small_w, small, local)
    fetch.start()
    fetch.wait()
    device = (far * 2 + near) * 2 + core
    half = lax.div(device, row_devices // 2)
    first = lax.rem(device, row_devices // 2) * rows
    width = small.shape[-1]
    images = small.shape[-2]
    row = lax.broadcasted_iota(jnp.int32, (width, LANES), 0)
    column = lax.broadcasted_iota(jnp.int32, (width, LANES), 1)
    select = jnp.where(jnp.logical_and(row == first + column, column < rows), 1.0, 0.0).astype(LOW)
    for at in range(count):
        silu = small[half, at].reshape(4 * images, width).astype(WIDE).astype(LOW)
        mine = times(silu, select)
        mine = jnp.where(lanes(mine.shape) == rows, 1.0, mine).astype(LOW)
        partials[at] = times(mine, ada[...]).reshape(2, 2, images, -1)

    def move(source, target, slot, other):
        return remote(source, target, sends, receives, slot, other)

    to_core = move(partials.at[:, :, 1 - core], came_core, 0, dict(core=1 - core))
    to_core.start()
    to_core.wait()
    for at in range(count):
        partials[at, :, core] = partials[at, :, core] + came_core[at]
    to_near = move(partials.at[:, 1 - near, core], came_near, 1, dict(near=1 - near))
    to_near.start()
    to_near.wait()
    for at in range(count):
        partials[at, near, core] = partials[at, near, core] + came_near[at]
    copies = []
    for distance in range(1, count):
        target = lax.rem(far + distance, count)
        copies.append(
            move(partials.at[target, near, core], came_far.at[distance - 1], 2 + distance, dict(far=target))
        )
        copies[-1].start()
    total = partials[far, near, core]
    for distance, copy in enumerate(copies):
        copy.wait()
        total = total + came_far[distance]
    own[...] = total.astype(LOW).astype(WIDE)
    keep = pltpu.make_async_copy(own, table.at[mod], local)
    keep.start()
    to_mod = move(own, table.at[mod], 2, dict(mod=1 - mod))
    to_mod.start()
    keep.wait()
    to_mod.wait_send()
    move(own, table.at[1 - mod], 2, dict(mod=1 - mod)).wait_recv()


def first_kernel(*refs):
    small_s, qkv_s, proj_s, fc1_s, ada = refs[:5]
    table = refs[9]
    gather_sems, (local, *parts) = refs[10:18], refs[18:]
    small, qkv, proj, fc1 = (
        Gather(w, s, r) for w, s, r in zip(refs[5:9], gather_sems[0::2], gather_sems[1::2])
    )
    greet()
    small.start_far(small_s, local.at[3])
    qkv.start_far(qkv_s, local.at[0])
    proj.start_far(proj_s, local.at[1])
    fc1.start_far(fc1_s, local.at[2])
    small.finish_far(small_s, local.at[3])
    small.spread()
    small.cross()
    small.close()
    small.end()
    modulate(small.whole, ada, table, local.at[3], *parts)
    qkv.finish_far(qkv_s, local.at[0])
    qkv.spread()
    qkv.cross()
    qkv.close()
    qkv.end()
    proj.finish_far(proj_s, local.at[1])
    fc1.finish_far(fc1_s, local.at[2])


def first_gather(ada, *shards):
    count = lax.axis_size("far")
    small = whole_shape(shards[0])
    images = small.shape[4]
    columns = ada.shape[1]
    return pl.pallas_call(
        first_kernel,
        out_shape=tuple(whole_shape(shard) for shard in shards)
        + (jax.ShapeDtypeStruct((2, images, columns), WIDE),),
        in_specs=[VMEM] * 5,
        out_specs=(ANY,) * 5,
        scratch_shapes=gather_scratch(4, 4)
        + [
            pltpu.VMEM(small.shape, LOW),
            pltpu.VMEM((count, 2, 2, images, columns), WIDE),
            pltpu.VMEM((count, 2, images, columns), WIDE),
            pltpu.VMEM((count, images, columns), WIDE),
            pltpu.VMEM((count - 1, images, columns), WIDE),
            pltpu.VMEM((images, columns), WIDE),
            pltpu.SemaphoreType.DMA((count + 2,)),
            pltpu.SemaphoreType.DMA((count + 2,)),
        ],
        compiler_params=pltpu.CompilerParams(
            collective_id=0, has_side_effects=True, vmem_limit_bytes=60 * 2**20
        ),
        name="first_gather",
    )(*shards, ada)


def lanes(shape): return lax.broadcasted_iota(jnp.int32, shape, 1)

def seg_codes(seg, n):
    lane = lanes((n, LANES))
    code = lane - HEAD
    inside = jnp.logical_and(code >= 0, code < 4)
    same = code == seg
    q = jnp.where(jnp.logical_and(inside, same), 1.0, 0.0)
    k = jnp.where(jnp.logical_and(inside, jnp.logical_not(same)), NEG, 0.0)
    return q, k

def head_of(wide_rows, start):
    return wide_rows[:, start:start+HEAD]

def pad_head(part, aug):
    n = part.shape[0]
    full = jnp.concatenate([part, jnp.zeros((n, LANES-HEAD), part.dtype)], axis=1)
    return jnp.where(lanes((n,LANES)) < HEAD, full, aug)

def attend_kernel(*refs):
    slots, x_ref, table, bias, weight, seg_ref, fc2_s = refs[:7]
    act_turned, joint_ref, mixed_ref, turned_ref, lse_ref, proj_w, fc1_w, fc2_w = refs[9:17]
    qh, kh, vh = refs[17:20]
    *sems, local = refs[20:]
    proj, fc1, fc2 = (
        Gather(w, s, r) for w, s, r in zip((proj_w, fc1_w, fc2_w), sems[0::2], sems[1::2])
    )
    greet()
    fc2.start_far(fc2_s, local.at[0])
    proj.spread()
    fc1.spread()

    T = x_ref.shape[0]

    def fill(i, carry):
        rows = pl.ds(pl.multiple_of(i * CHUNK, CHUNK), CHUNK)
        slot = slots[i]
        h1, _ = normed(x_ref[rows, :].astype(WIDE))
        act = (h1 * (1.0 + row_of(table, slot, 1)) + row_of(table, slot, 0)).astype(LOW)
        act_turned[:, rows] = act.T
        joint = jnp.concatenate([times(act, weight[0]), times(act, weight[1])], axis=1)
        joint_ref[rows, :] = (joint + bias[...]).astype(LOW)
        lane = lanes((CHUNK, LANES))
        qc, kc = seg_codes(seg_ref[rows, :], CHUNK)
        qc = qc.astype(LOW); kc = kc.astype(LOW)
        ones = jnp.where(jnp.logical_and(lane >= HEAD, lane < HEAD+3), 1.0, 0.0).astype(LOW)
        for h in range(HEADS):
            qh[h, rows, :] = pad_head(joint_ref[rows, h*HEAD:(h+1)*HEAD], qc)
            kh[h, rows, :] = pad_head(joint_ref[rows, D+h*HEAD:D+(h+1)*HEAD], kc)
            vh[h, rows, :] = pad_head(joint_ref[rows, 2*D+h*HEAD:2*D+(h+1)*HEAD], ones)
        return carry
    lax.fori_loop(0, T//CHUNK, fill, 0)
    lse_ref[...] = jnp.zeros_like(lse_ref)
    def head(h, carry):
        k = kh[h]; v = vh[h]
        for i in range(T//CHUNK):
            rows = pl.ds(i*CHUNK, CHUNK)
            q = qh[h, rows, :]
            s = lax.dot_general(q, k, (((1,),(1,)),((),())), preferred_element_type=WIDE)
            m = jnp.max(s, axis=1, keepdims=True)
            p = jnp.exp2((s - m)*(HEAD**-0.5*LOG2E)).astype(LOW)
            o = jnp.dot(p, v, preferred_element_type=WIDE)
            l = o[:, HEAD:HEAD+1]
            qh[h, rows, :] = (o / l).astype(LOW)
            col = m*HEAD**-0.5 + jnp.log(l)
            lse_ref[rows, :] = jnp.where(lanes((CHUNK,LANES)) == h, col, lse_ref[rows, :])
        tasks = {
            2: proj.cross,
            5: proj.close,
            7: proj.end,
            9: lambda: fc2.finish_far(fc2_s, local.at[0]),
            10: fc2.spread,
            11: fc1.cross,
        }
        for at, task in tasks.items():
            pl.when(h == at)(task)
        return carry
    lax.fori_loop(0, HEADS, head, 0)
    def drain(i, carry):
        rows = pl.ds(pl.multiple_of(i*CHUNK, CHUNK), CHUNK)
        mixed = jnp.concatenate([qh[h, rows, :][:, :HEAD] for h in range(HEADS)], axis=1)
        mixed_ref[rows, :] = mixed
        turned_ref[:, rows] = mixed.T
        return carry
    lax.fori_loop(0, T//CHUNK, drain, 0)
    fc1.close()
    fc2.cross()
    fc1.end()
    fc2.close()
    fc2.end()


def attend(slots, x_in, table, bias, weight, segments, fc2_s, proj_w, fc1_w):
    tokens = x_in.shape[0]
    wide = HEADS * HEAD
    return pl.pallas_call(
        attend_kernel,
        out_shape=(
            jax.ShapeDtypeStruct((wide, tokens), LOW),
            jax.ShapeDtypeStruct((tokens, 3 * wide), LOW),
            jax.ShapeDtypeStruct((tokens, wide), LOW),
            jax.ShapeDtypeStruct((wide, tokens), LOW),
            jax.ShapeDtypeStruct((tokens, LANES), WIDE),
            jax.ShapeDtypeStruct(proj_w.shape, LOW),
            jax.ShapeDtypeStruct(fc1_w.shape, LOW),
            whole_shape(fc2_s),
        ),
        in_specs=[pl.BlockSpec(memory_space=pltpu.SMEM)] + [VMEM] * 6 + [ANY] * 2,
        out_specs=(VMEM,) * 5 + (ANY,) * 3,
        scratch_shapes=[pltpu.VMEM((HEADS, tokens, LANES), LOW)] * 3 + gather_scratch(3, 1),
        input_output_aliases={7: 5, 8: 6},
        compiler_params=pltpu.CompilerParams(
            collective_id=1, has_side_effects=True, vmem_limit_bytes=60 * 2**20
        ),
        name="attend",
    )(slots, x_in, table, bias, weight, segments.reshape(tokens, 1), fc2_s, proj_w, fc1_w)


def row_spans(rows):
    first = rows if rows % 8 else 8 * ((rows // 8 + 1) // 2)
    return [(0, first)] + ([(first, rows - first)] if first < rows else [])


class Reduce:
    def __init__(self, part, span, first, came, joint, total, base, sems, loads=False):
        self.part, self.span, self.first = part, span, first
        self.second = "near" if first == "mod" else "mod"
        self.came_both, self.came_first, self.came_second, self.came_far = came
        self.joint, self.total_, self.base = joint, total, base
        self.sends, self.receives, self.locals_ = sems
        self.loads = loads
        self.here = places()
        self.count = lax.axis_size("far")

    def _swap(self, source, target, slot, axis):
        return remote(source, target, self.sends, self.receives, slot, {axis: 1 - self.here[axis]})

    def _both(self):
        return self._swap(self.part("near", "mod"), self.came_both, 0, self.first)

    def _first(self):
        return self._swap(self.part(self.first), self.came_first, 1, self.first)

    def _second(self):
        return self._swap(self.joint, self.came_second, 2, self.second)

    def _load(self, number):
        source, target = ((self.part(self.second), self.joint), (self.part(), self.total_))[number]
        return pltpu.make_async_copy(source, target, self.locals_.at[number])

    def _far(self, distance):
        target = lax.rem(self.here["far"] + distance, self.count)
        return remote(
            self.total_.at[target],
            self.came_far.at[distance - 1],
            self.sends,
            self.receives,
            2 + distance,
            dict(far=target),
        )

    def start(self):
        self._both().start()
        self._first().start()
        if self.loads:
            self._load(0).start()
            self._load(1).start()

    def merge(self):
        if self.loads:
            self._load(0).wait()
        self._both().wait_recv()

        def add(at, carry):
            self.joint[at] = (self.joint[at].astype(WIDE) + self.came_both[at].astype(WIDE)).astype(LOW)
            return carry

        lax.fori_loop(0, self.count, add, 0)
        self._second().start()

    def total(self):
        if self.loads:
            self._load(1).wait()
        self._first().wait_recv()
        self._second().wait_recv()

        def add(at, carry):
            self.total_[at] = (
                self.base[at].astype(WIDE)
                + self.came_first[at].astype(WIDE)
                + self.came_second[at].astype(WIDE)
            ).astype(LOW)
            return carry

        lax.fori_loop(0, self.count, add, 0)
        self._both().wait_send()
        self._first().wait_send()
        self._second().wait_send()

    def start_far(self):
        for distance in range(1, self.count):
            self._far(distance).start()

    def final(self, out):
        value = self.total_[self.here["far"]].astype(WIDE)
        for distance in range(1, self.count):
            self._far(distance).wait_recv()
            value = value + self.came_far[distance - 1].astype(WIDE)
        out[pl.ds(*self.span), :] = value
        for distance in range(1, self.count):
            self._far(distance).wait_send()


ORDERS = ("mod", "near")


def run(parts, *names):
    for part in parts:
        for name in names:
            getattr(part, name)()


def span_part(sums, span):
    def part(*flips):
        near, mod = (
            1 - lax.axis_index(name) if name in flips else lax.axis_index(name) for name in ("near", "mod")
        )
        return sums.at[mod, near, :, pl.ds(*span)]

    return part


def take(scratch, number):
    return scratch[:number], scratch[number:]


def came_scratch(count, span, columns, far=True):
    block = (count, span[1], columns)
    shapes = [pltpu.VMEM(block, LOW)] * 3
    return shapes + ([pltpu.VMEM((count - 1,) + block[1:], LOW)] if far else [])


def sem_scratch(count):
    return [pltpu.SemaphoreType.DMA((count + 2,))] * 2 + [pltpu.SemaphoreType.DMA((2,))]


def loaded_scratch(shape, total=True):
    count, rows, columns = shape[2:]
    shapes = []
    for span in row_spans(rows):
        shapes += came_scratch(count, span, columns)
        shapes += [pltpu.VMEM((count, span[1], columns), LOW)] * (2 if total else 1)
        shapes += sem_scratch(count)
    return shapes


def loaded_reduces(sums, scratch, totals=None):
    reduces = []
    for number, span in enumerate(row_spans(sums.shape[3])):
        came, scratch = take(scratch, 4)
        (joint,), scratch = take(scratch, 1)
        if totals is None:
            (total,), scratch = take(scratch, 1)
        else:
            total = totals[number]
        sems, scratch = take(scratch, 3)
        reduces.append(
            Reduce(span_part(sums, span), span, ORDERS[number], came, joint, total, total, sems, True)
        )
    return reduces, scratch


def resident_scratch(shape, far=True):
    count, rows, columns = shape[2:]
    shapes = []
    for span in row_spans(rows):
        shapes += came_scratch(count, span, columns, far) + sem_scratch(count)
    return shapes


def resident_reduces(sums, scratch, totals=None):
    reduces = []
    for number, span in enumerate(row_spans(sums.shape[3])):
        came, scratch = take(scratch, 4 if totals is None else 3)
        sems, scratch = take(scratch, 3)
        part = span_part(sums, span)
        order = ORDERS[number]
        own = part()
        total = own if totals is None else totals[number]
        came = list(came) + [None] * (4 - len(came))
        joint = part("near" if order == "mod" else "mod")
        reduces.append(Reduce(part, span, order, came, joint, total, own, sems))
    return reduces, scratch


def far_scratch(totals):
    shapes = []
    for total in totals:
        count = total.shape[0]
        shapes += [pltpu.VMEM((count - 1,) + total.shape[1:], LOW)] + sem_scratch(count)[:2]
    return shapes


def far_reduces(totals, rows, scratch):
    reduces = []
    for total, span in zip(totals, row_spans(rows)):
        (came, sends, receives), scratch = take(scratch, 3)
        came = (None, None, None, came)
        reduces.append(Reduce(None, span, "mod", came, None, total, total, (sends, receives, None)))
    return reduces, scratch


class Product:
    def __init__(self, left, right, scratch):
        self.left, self.right = left, right
        self.rows_, self.sums, self.came, self.loads, self.sends, self.receives = scratch
        self.core = lax.axis_index("core")

    @staticmethod
    def scratch(count, rows, tokens, columns):
        sums = pltpu.VMEM((2, 2, count, rows, columns), LOW)
        sems = [pltpu.SemaphoreType.DMA((4,))] * 3
        return [pltpu.VMEM((4, count, rows, tokens), LOW), sums, sums] + sems

    def _load(self, near, own):
        core = self.core if own else 1 - self.core
        slot = 2 * own + near
        return pltpu.make_async_copy(
            self.left.at[:, near, core], self.rows_.at[slot], self.loads.at[slot]
        )

    def load(self):
        for own in (0, 1):
            for near in (0, 1):
                self._load(near, own).start()

    def _copy(self, mod, near):
        return remote(
            self.sums.at[mod, near],
            self.came.at[mod, near],
            self.sends,
            self.receives,
            2 * mod + near,
            dict(core=1 - self.core),
        )

    def _blocks(self, near, own, store):
        count, rows, tokens = self.rows_.shape[1:]
        columns = self.right.shape[2]
        self._load(near, own).wait()
        left = self.rows_[2 * own + near].reshape(count * rows, tokens)
        width = columns if columns <= 1024 else columns // 2
        width = width if width % LANES == 0 else columns
        for mod in (0, 1):
            for at in range(0, columns, width):
                product = times(left, self.right[mod, :, at : at + width])
                store(mod, at, width, product.reshape(count, rows, width))

    def send(self):
        for near in (0, 1):

            def store(mod, at, width, product, near=near):
                self.sums[mod, near, :, :, at : at + width] = product.astype(LOW)

            self._blocks(near, 0, store)
            for mod in (0, 1):
                self._copy(mod, near).start()

    def sum(self):
        for near in (0, 1):
            for mod in (0, 1):
                self._copy(mod, near).wait_send()
                self._copy(mod, near).wait_recv()

            def store(mod, at, width, product, near=near):
                came = self.came[mod, near, :, :, at : at + width]
                self.sums[mod, near, :, :, at : at + width] = (product + came.astype(WIDE)).astype(LOW)

            self._blocks(near, 1, store)


def total_shapes(count, rows, columns):
    return [jax.ShapeDtypeStruct((count, span[1], columns), LOW) for span in row_spans(rows)]


def weight_kernel(*refs, spans, stored):
    count = stored + (spans > 0)
    sides, refs = take(refs, 2 * count)
    outs, refs = take(refs, stored)
    totals, scratch = take(refs, spans)
    products = []
    for number in range(count):
        used, scratch = take(scratch, 6)
        products.append(Product(sides[2 * number], sides[2 * number + 1], used))
    reduces = []
    if spans:
        reduces, scratch = resident_reduces(products[0].sums, scratch, totals)
    (out_sems,) = scratch
    products[0].load()
    greet()
    copies = []
    for number, product in enumerate(products):
        product.send()
        if number + 1 < count:
            products[number + 1].load()
        product.sum()
        if spans and number == 0:
            run(reduces, "start")
            continue
        copy = pltpu.make_async_copy(product.sums, outs[len(copies)], out_sems.at[len(copies)])
        copy.start()
        copies.append(copy)
        if spans and number == 1:
            run(reduces, "merge")
    if spans and count == 1:
        run(reduces, "merge")
    run(reduces, "total")
    for copy in copies:
        copy.wait()


def weight_call(summed, stored, number):
    pairs = summed + stored
    count, _, _, rows, tokens = pairs[0][0].shape
    columns = pairs[0][1].shape[2]
    totals = total_shapes(count, rows, columns) if summed else []
    scratch = []
    for left, right in pairs:
        scratch += Product.scratch(count, left.shape[3], tokens, right.shape[2])
    if summed:
        scratch += resident_scratch((2, 2, count, rows, columns), False)
    out = pl.pallas_call(
        partial(weight_kernel, spans=len(totals), stored=len(stored)),
        out_shape=tuple(
            jax.ShapeDtypeStruct((2, 2, count, left.shape[3], right.shape[2]), LOW) for left, right in stored
        )
        + tuple(totals),
        in_specs=[ANY, VMEM] * len(pairs),
        out_specs=(ANY,) * len(stored) + (VMEM,) * len(totals),
        scratch_shapes=scratch + [pltpu.SemaphoreType.DMA((2,))],
        compiler_params=pltpu.CompilerParams(
            collective_id=number, has_side_effects=True, vmem_limit_bytes=63 * 2**20
        ),
        name="weight_grads",
    )(*[side for pair in pairs for side in pair])
    return out[: len(stored)], out[len(stored) :]


def weight_grads(hidden, branch, mlp, pre, mixed, attn):
    summed, stored = [(hidden, branch)], [(mlp, pre), (mixed, attn)]
    if mlp.shape[3] % 8 == 0:
        return weight_call(summed, stored, 4)
    _, totals = weight_call(summed, [], 4)
    sums, _ = weight_call([], stored, 5)
    return sums, totals


def tile_sums_by_slot(chooser, sums):
    total = None
    for at, row in enumerate(sums):
        part = chooser[:, at : at + 1] * row
        total = part if total is None else total + part
    return total


def last_kernel(*refs, spans):
    slots, act, joint, x_ref, dx1_ref, table, weight, mid_sums, chooser = refs[:9]
    totals, refs = take(refs[9:], spans)
    qkv_out, fc1_out, small_w, x_grad_ref, joint_sums, *scratch = refs
    qkv_scratch, scratch = take(scratch, 6)
    qkv = Product(act, joint, qkv_scratch)
    qkv_sum, scratch = resident_reduces(qkv.sums, scratch)
    fc1_sum, scratch = far_reduces(totals, fc1_out.shape[0], scratch)
    small_sends, small_receives, local, first_sums, small_s = scratch
    small = Gather(small_w, small_sends, small_receives)
    tiles = x_ref.shape[0] // CHUNK
    qkv.load()
    greet()
    run(fc1_sum, "start_far")
    qkv.send()
    qkv.sum()
    run(qkv_sum, "start")

    def back(at, carry):
        rows = pl.ds(pl.multiple_of(at * CHUNK, CHUNK), CHUNK)
        dact = times_across(joint[0, rows, :], weight[0]) + times_across(joint[1, rows, :], weight[1])
        h1, inverse = normed(x_ref[rows, :].astype(WIDE))
        first_sums[at, 0:1, :] = column_sums(dact)
        first_sums[at, 1:2, :] = column_sums(dact * h1)
        dh1 = dact * (1.0 + row_of(table, slots[at], 1))
        x_grad_ref[rows, :] = dx1_ref[rows, :] + inverse * (
            dh1
            - jnp.mean(dh1, axis=-1, keepdims=True)
            - h1 * jnp.mean(dh1 * h1, axis=-1, keepdims=True)
        )
        for side in range(2):
            joint_sums[side : side + 1, :] += column_sums(joint[side, rows, :].astype(WIDE))

        @pl.when(at == tiles // 2 - 1)
        def _():
            run(qkv_sum, "merge")

        return carry

    joint_sums[...] = jnp.zeros_like(joint_sums)
    lax.fori_loop(0, tiles, back, 0)
    choose = chooser[...]
    upper = lax.broadcasted_iota(jnp.int32, (choose.shape[0], D), 0) < choose.shape[0] // 2
    groups = (
        [first_sums[at, 0:1, :] for at in range(tiles)],
        [first_sums[at, 1:2, :] for at in range(tiles)],
    ) + tuple([mid_sums[at, row : row + 1, :] for at in range(tiles)] for row in range(4))
    for group in range(3):
        value = jnp.where(
            upper, tile_sums_by_slot(choose, groups[group]), tile_sums_by_slot(choose, groups[group + 3])
        )
        small_s[:, group * D : (group + 1) * D] = value.astype(LOW)
    small.start_far(small_s, local.at[0])
    small.finish_far(small_s, local.at[0])
    small.spread()
    small.cross()
    small.close()
    small.end()
    run(qkv_sum, "total", "start_far")
    for part in fc1_sum:
        part.final(fc1_out)
    for part in qkv_sum:
        part.final(qkv_out)


def last_scatter(slots, act, joint, x_in, dx1, table, weight, mid_sums, chooser, totals):
    count, _, _, rows, tokens = act.shape
    fc1_columns = totals[0].shape[2]
    columns = joint.shape[2]
    small_s = jax.ShapeDtypeStruct((chooser.shape[0], 3 * D), LOW)
    return pl.pallas_call(
        partial(last_kernel, spans=len(totals)),
        out_shape=(
            jax.ShapeDtypeStruct((rows, columns), WIDE),
            jax.ShapeDtypeStruct((sum(total.shape[1] for total in totals), fc1_columns), WIDE),
            whole_shape(small_s),
            jax.ShapeDtypeStruct((tokens, D), WIDE),
            jax.ShapeDtypeStruct((2, columns), WIDE),
        ),
        in_specs=[pl.BlockSpec(memory_space=pltpu.SMEM), ANY] + [VMEM] * (7 + len(totals)),
        out_specs=(VMEM, VMEM, ANY, VMEM, VMEM),
        scratch_shapes=Product.scratch(count, rows, tokens, columns)
        + resident_scratch((2, 2, count, rows, columns))
        + far_scratch(totals)
        + gather_scratch(1, 1)
        + [pltpu.VMEM((tokens // CHUNK, 8, D), WIDE), pltpu.VMEM(small_s.shape, LOW)],
        compiler_params=pltpu.CompilerParams(
            collective_id=3, has_side_effects=True, vmem_limit_bytes=63 * 2**20
        ),
        name="last_scatter",
    )(slots, act, joint, x_in, dx1, table, weight, mid_sums, chooser, *totals)


def split3(v):
    hi = v.astype(LOW).astype(WIDE)
    mid = (v - hi).astype(LOW).astype(WIDE)
    lo = v - hi - mid
    return hi, mid, lo


def attend_back_kernel(*refs, fc2_spans, spans):
    qkv_ref, seg_ref, mixed_ref, lse_ref, up_ref, fc1_sums, proj_sums = refs[:7]
    fc2_totals, refs = take(refs[7:], fc2_spans)
    out_ref, fc2_out, proj_out, *refs = refs
    fc1_totals, refs = take(refs, spans)
    qh, kh, vh, uh, stage, stage_sems, leave, leave_sems, *scratch = refs
    proj, scratch = loaded_reduces(proj_sums, scratch)
    fc1, scratch = loaded_reduces(fc1_sums, scratch, fc1_totals)
    fc2, scratch = far_reduces(fc2_totals, fc2_out.shape[0], scratch)
    T = mixed_ref.shape[0]
    chunks = T // CHUNK
    greet()
    run(fc2, "start_far")
    run(fc1, "start")

    def load(i):
        rows = pl.ds(pl.multiple_of(i * CHUNK, CHUNK), CHUNK)
        slot = lax.rem(i, 2)
        return pltpu.make_async_copy(qkv_ref.at[rows], stage.at[slot], stage_sems.at[slot])

    load(0).start()

    def fill(i, carry):
        rows = pl.ds(pl.multiple_of(i * CHUNK, CHUNK), CHUNK)

        @pl.when(i + 1 < chunks)
        def _():
            load(i + 1).start()

        load(i).wait()
        qkv = stage.at[lax.rem(i, 2)]
        lane = lanes((CHUNK, LANES))
        qc, kc = seg_codes(seg_ref[rows, :], CHUNK)
        kc = jnp.where(jnp.logical_and(lane >= HEAD + 4, lane < HEAD + 7), 1.0, kc).astype(LOW)
        ones = jnp.where(jnp.logical_and(lane >= HEAD, lane < HEAD + 3), 1.0, 0.0).astype(LOW)

        def spread(v, at, base):
            hi, mid, lo = split3(v)
            return jnp.where(
                lane == at, hi, jnp.where(lane == at + 1, mid, jnp.where(lane == at + 2, lo, base))
            )

        for h in range(HEADS):
            a, b = h * HEAD, (h + 1) * HEAD
            qa = spread(-lse_ref[rows, h : h + 1] * HEAD**0.5, HEAD + 4, qc).astype(LOW)
            qh[h, rows, :] = pad_head(qkv[:, a:b], qa)
            kh[h, rows, :] = pad_head(qkv[:, D + a : D + b], kc)
            vh[h, rows, :] = pad_head(qkv[:, 2 * D + a : 2 * D + b], ones)
            u = up_ref[rows, a:b]
            delta = jnp.sum(u.astype(WIDE) * mixed_ref[rows, a:b].astype(WIDE), axis=1, keepdims=True)
            ua = spread(-delta, HEAD, jnp.zeros((CHUNK, LANES), WIDE)).astype(LOW)
            uh[h, rows, :] = pad_head(u, ua)
        return carry

    lax.fori_loop(0, chunks, fill, 0)
    across = (((1,), (1,)), ((), ()))
    tasks = {
        4: lambda: (run(fc1, "merge"), run(proj, "start")),
        11: lambda: run(proj, "merge"),
        14: lambda: run(proj, "total", "start_far"),
    }

    def head(h, carry):
        k = kh[h]
        v = vh[h]
        kt = k.T
        dk = jnp.zeros((T, LANES), WIDE)
        dv = jnp.zeros((T, LANES), WIDE)
        for i in range(chunks):
            rows = pl.ds(i * CHUNK, CHUNK)
            q = qh[h, rows, :]
            u = uh[h, rows, :]
            s = lax.dot_general(k, q, across, preferred_element_type=WIDE)
            p = jnp.exp2(s * (HEAD**-0.5 * LOG2E))
            dp = lax.dot_general(v, u, across, preferred_element_type=WIDE)
            ds = (p * dp).astype(LOW)
            dv = dv + jnp.dot(p.astype(LOW), u, preferred_element_type=WIDE)
            dk = dk + jnp.dot(ds, q, preferred_element_type=WIDE)
            dqt = jnp.dot(kt, ds, preferred_element_type=WIDE)
            qh[h, rows, :] = (dqt.T * HEAD**-0.5).astype(LOW)
        kh[h] = (dk * HEAD**-0.5).astype(LOW)
        vh[h] = dv.astype(LOW)
        for at, task in tasks.items():

            @pl.when(h == at)
            def _(task=task):
                task()

        return carry

    lax.fori_loop(0, HEADS, head, 0)

    def store(i, side):
        rows = pl.ds(pl.multiple_of(i * CHUNK, CHUNK), CHUNK)
        return pltpu.make_async_copy(
            leave.at[side], out_ref.at[side, rows], leave_sems.at[side]
        )

    def drain(i, carry):
        rows = pl.ds(pl.multiple_of(i * CHUNK, CHUNK), CHUNK)
        parts = [g[h, rows, :][:, :HEAD] for g in (qh, kh, vh) for h in range(HEADS)]
        for side in range(2):

            @pl.when(i > 0)
            def _(side=side):
                store(i - 1, side).wait()

            own = parts[side * len(parts) // 2 : (side + 1) * len(parts) // 2]
            leave[side] = jnp.concatenate(own, axis=1)
            store(i, side).start()
        return carry

    lax.fori_loop(0, chunks, drain, 0)
    run(fc1, "total")
    for side in range(2):
        store(chunks - 1, side).wait()
    for part in fc2:
        part.final(fc2_out)
    for part in proj:
        part.final(proj_out)


def attend_back(qkv, segments, mixed, lse, upstream, fc1_sums, proj_sums, fc2_totals):
    tokens = qkv.shape[0]
    count, rows, columns = fc1_sums.shape[2:]
    totals = total_shapes(count, rows, columns)
    fc2_rows = sum(total.shape[1] for total in fc2_totals)
    out = pl.pallas_call(
        partial(attend_back_kernel, fc2_spans=len(fc2_totals), spans=len(totals)),
        out_shape=(
            jax.ShapeDtypeStruct((2, tokens, 3 * HEADS * HEAD // 2), LOW),
            jax.ShapeDtypeStruct((fc2_rows, fc2_totals[0].shape[2]), WIDE),
            jax.ShapeDtypeStruct(proj_sums.shape[3:], WIDE),
        )
        + tuple(totals),
        in_specs=[ANY] + [VMEM] * 4 + [ANY] * 2 + [VMEM] * len(fc2_totals),
        out_specs=(ANY, VMEM, VMEM) + (VMEM,) * len(totals),
        scratch_shapes=[pltpu.VMEM((HEADS, tokens, LANES), LOW)] * 4
        + [pltpu.VMEM((2, CHUNK, 3 * HEADS * HEAD), LOW), pltpu.SemaphoreType.DMA((2,))]
        + [pltpu.VMEM((2, CHUNK, 3 * HEADS * HEAD // 2), LOW), pltpu.SemaphoreType.DMA((2,))]
        + loaded_scratch(proj_sums.shape)
        + loaded_scratch(fc1_sums.shape, False)
        + far_scratch(fc2_totals),
        compiler_params=pltpu.CompilerParams(
            collective_id=2, has_side_effects=True, vmem_limit_bytes=63 * 2**20
        ),
        name="attend_back",
    )(qkv, segments.reshape(tokens, 1), mixed, lse, upstream, fc1_sums, proj_sums, *fc2_totals)
    return out[0], out[1], out[2], out[3:]


def normed(values):
    centre = values - jnp.mean(values, axis=-1, keepdims=True)
    inverse = lax.rsqrt(jnp.mean(centre * centre, axis=-1, keepdims=True) + EPS)
    return centre * inverse, inverse


def row_of(table, slot, group):
    return table[pl.ds(slot, 1), group * D : (group + 1) * D]


def column_sums(values):
    return jnp.sum(values, axis=0, keepdims=True)


def times_across(left, right):
    return lax.dot_general(left, right, (((1,), (1,)), ((), ())), preferred_element_type=WIDE)


def fixed(*shape):
    return pl.BlockSpec(
        shape, lambda i, slots: (0,) * len(shape), pipeline_mode=pl.Buffered(1)
    )


GELU = 0.7978845608028654
CUBIC = 0.044715
SPAN = 768
BLOCK = 512


def middle_kernel(
    slots, x_ref, g_ref, mixed_ref, table, bias, bias1, proj, fc1, fc2,
    block_ref, mlp_turned, hidden_turned, dpre_ref, dbranch_ref, dattn_ref, dmixed_ref, dx1_ref, sums_ref, dpre_sums,
    attn_out, mlp, branch,
):
    step = pl.program_id(0)
    tokens = x_ref.shape[0]

    @pl.when(step == 0)
    def _():
        def enter(tile_at, carry):
            rows = pl.ds(pl.multiple_of(tile_at * CHUNK, CHUNK), CHUNK)
            slot = slots[tile_at]
            gate1, shift2, scale2, gate2 = (row_of(table, slot, group) for group in (2, 3, 4, 5))
            mixed = mixed_ref[rows, :]
            out = jnp.concatenate([times(mixed, proj[0]), times(mixed, proj[1])], axis=1)
            out = out + bias[:, 2 * D : 3 * D]
            attn_out[rows, :] = out
            h2, _ = normed(x_ref[rows, :].astype(WIDE) + gate1 * out)
            mlp_in = (h2 * (1.0 + scale2) + shift2).astype(LOW)
            mlp[rows, :] = mlp_in
            mlp_turned[:, rows] = mlp_in.T
            dbranch = (gate2 * g_ref[rows, :].astype(WIDE)).astype(LOW)
            sums_ref[tile_at, 5:6, :] = column_sums(dbranch.astype(WIDE))
            dbranch_ref[0, rows, :] = dbranch[:, : D // 2]
            dbranch_ref[1, rows, :] = dbranch[:, D // 2 :]
            return carry

        lax.fori_loop(0, tokens // CHUNK, enter, 0)
        branch[...] = jnp.zeros_like(branch)
        dx1_ref[...] = jnp.zeros_like(dx1_ref)

    total = None
    for first in range(0, tokens, BLOCK):
        rows = slice(first, first + BLOCK)
        pre = times(mlp[rows, :], fc1[0]) + bias1[0]
        square = pre * pre
        bend = jnp.tanh(GELU * pre * (1.0 + CUBIC * square))
        rise = 0.5 * (1.0 + bend)
        hidden = (pre * rise).astype(LOW)
        hidden_turned[:, rows] = hidden.T
        for side in range(2):
            branch[side, rows] += times(hidden, fc2[side])
        slope = rise + 0.5 * GELU * pre * (1.0 - bend * bend) * (1.0 + 3.0 * CUBIC * square)
        dhidden = times_across(dbranch_ref[0, rows], fc2[0]) + times_across(dbranch_ref[1, rows], fc2[1])
        dpre = (dhidden * slope).astype(LOW)
        dpre_ref[0, rows] = dpre
        part = column_sums(dpre.astype(WIDE))
        total = part if total is None else total + part
        dx1_ref[rows, :] += times_across(dpre, fc1[0])
    dpre_sums[...] = total

    @pl.when(step == pl.num_programs(0) - 1)
    def _():
        def leave(tile_at, carry):
            rows = pl.ds(pl.multiple_of(tile_at * CHUNK, CHUNK), CHUNK)
            slot = slots[tile_at]
            gate1, scale2, gate2 = (row_of(table, slot, group) for group in (2, 4, 5))
            out = attn_out[rows, :]
            x1 = x_ref[rows, :].astype(WIDE) + gate1 * out
            h2, inverse = normed(x1)
            whole = jnp.concatenate([branch[0, rows, :], branch[1, rows, :]], axis=1) + bias[:, 3 * D + FF :]
            block_ref[rows, :] = (x1 + gate2 * whole).astype(LOW)
            g = g_ref[rows, :].astype(WIDE)
            sums_ref[tile_at, 3:4, :] = column_sums(g * whole)
            dmlp = dx1_ref[rows, :]
            sums_ref[tile_at, 1:2, :] = column_sums(dmlp)
            sums_ref[tile_at, 2:3, :] = column_sums(dmlp * h2)
            dh2 = dmlp * (1.0 + scale2)
            dx1 = g + inverse * (
                dh2
                - jnp.mean(dh2, axis=-1, keepdims=True)
                - h2 * jnp.mean(dh2 * h2, axis=-1, keepdims=True)
            )
            dx1_ref[rows, :] = dx1
            sums_ref[tile_at, 0:1, :] = column_sums(dx1 * out)
            dattn = (gate1 * dx1).astype(LOW)
            sums_ref[tile_at, 4:5, :] = column_sums(dattn.astype(WIDE))
            sums_ref[tile_at, 6:8, :] = jnp.zeros((2, D), WIDE)
            left, right = dattn[:, : D // 2], dattn[:, D // 2 :]
            dattn_ref[0, rows, :] = left
            dattn_ref[1, rows, :] = right
            dmixed_ref[rows, :] = (times_across(left, proj[0]) + times_across(right, proj[1])).astype(LOW)
            return carry

        lax.fori_loop(0, tokens // CHUNK, leave, 0)


def middle(slots, x_in, out_grad, mixed, table, bias, proj, fc1, fc2):
    tokens = x_in.shape[0]
    tiles = tokens // CHUNK
    steps = FF // SPAN
    per_side = steps // 2
    bias1 = bias[:, 3 * D : 3 * D + FF].reshape(steps, 1, SPAN)

    def by_unit(shape, place):
        return pl.BlockSpec(shape, lambda j, slots: place(j))

    outs = (
        ((tokens, D), LOW),
        ((D, tokens), LOW),
        ((FF, tokens), LOW),
        ((2, tokens, FF // 2), LOW),
        ((2, tokens, D // 2), LOW),
        ((2, tokens, D // 2), LOW),
        ((tokens, D), LOW),
        ((tokens, D), WIDE),
        ((tiles, 8, D), WIDE),
        ((1, FF), WIDE),
    )
    out_specs = [fixed(*shape) for shape, _ in outs]
    out_specs[2] = by_unit((SPAN, tokens), lambda j: (j, 0))
    out_specs[3] = by_unit((1, tokens, SPAN), lambda j: (j // per_side, 0, j % per_side))
    out_specs[9] = by_unit((1, SPAN), lambda j: (0, j))
    return pl.pallas_call(
        middle_kernel,
        out_shape=tuple(jax.ShapeDtypeStruct(shape, dtype) for shape, dtype in outs),
        grid_spec=pltpu.PrefetchScalarGridSpec(
            num_scalar_prefetch=1,
            grid=(steps,),
            in_specs=[
                fixed(tokens, D),
                fixed(tokens, D),
                fixed(tokens, D),
                fixed(*table.shape),
                fixed(*bias.shape),
                by_unit((1, 1, SPAN), lambda j: (j, 0, 0)),
                fixed(*proj.shape),
                by_unit((1, D, SPAN), lambda j: (j // per_side, 0, j % per_side)),
                by_unit((2, SPAN, D // 2), lambda j: (0, j, 0)),
            ],
            out_specs=tuple(out_specs),
            scratch_shapes=[
                pltpu.VMEM((tokens, D), WIDE),
                pltpu.VMEM((tokens, D), LOW),
                pltpu.VMEM((2, tokens, D // 2), WIDE),
            ],
        ),
        compiler_params=pltpu.CompilerParams(
            dimension_semantics=("arbitrary",), vmem_limit_bytes=63 * 2**20
        ),
        cost_estimate=pl.CostEstimate(
            flops=4 * tokens * (D * D + 2 * D * FF),
            bytes_accessed=(D * D + 2 * D * FF) * 2 + tokens * D * 40,
            transcendentals=0,
        ),
        name="middle",
    )(slots, x_in, out_grad, mixed, table, bias, bias1, proj, fc1, fc2)


def swap(values, axis):
    return lax.ppermute(values, axis, [(0, 1), (1, 0)])


def times(left, right):
    return jnp.dot(left, right, preferred_element_type=WIDE)


def times_back(left, right):
    return lax.dot_general(left, right, (((1,), (1,)), ((), ())), preferred_element_type=WIDE)


def body(
    x_in,
    cond,
    segments,
    out_grad,
    qkv_weight,
    qkv_moment,
    qkv_average,
    proj_weight,
    proj_moment,
    proj_average,
    fc1_weight,
    fc1_moment,
    fc1_average,
    fc2_weight,
    fc2_moment,
    fc2_average,
    bias_weight,
    bias_moment,
    bias_average,
    ada_weight,
    ada_moment,
    ada_average,
    adab_weight,
    adab_moment,
    adab_average,
):
    tokens, width = x_in.shape
    row_devices = lax.axis_size(ROWS)
    devices = lax.axis_size(ALL)
    row_index = lax.axis_index(ROWS)
    images = cond.shape[0] // 2

    cond_silu, silu_back = jax.vjp(jax.nn.silu, cond.astype(WIDE))
    half_silu = lax.dynamic_index_in_dim(
        cond_silu.astype(LOW).reshape(-1, 2, width // 2), lax.axis_index("mod"), 1, False
    )
    own_bias = bias_weight.shape[0]
    bias_block = jnp.pad(bias_weight.astype(LOW), (0, 8 * LANES - own_bias)).reshape(8, LANES)
    blank = jnp.zeros((8, LANES // 2), LOW)
    ada_low = ada_weight.astype(LOW)
    adab_row = lax.dynamic_update_slice_in_dim(
        jnp.zeros((1, ada_weight.shape[1]), LOW),
        adab_weight.astype(LOW),
        row_index * adab_weight.shape[1],
        1,
    )
    ada_rows = jnp.concatenate([ada_low, adab_row])
    small_w, qkv_w, proj_w, fc1_w, table = first_gather(
        jnp.pad(ada_rows, ((0, LANES - ada_rows.shape[0]), (0, 0))),
        jnp.concatenate([half_silu, bias_block, blank], axis=1),
        qkv_weight.astype(LOW),
        proj_weight.astype(LOW),
        fc1_weight.astype(LOW),
    )
    small = small_w.reshape(2, row_devices * 8, -1)
    silu_all = jnp.concatenate([small[0, :, : width // 2], small[1, :, : width // 2]], axis=1)
    bias_all = small[:, :, width // 2 : width // 2 + LANES].reshape(2, row_devices, -1)
    bias_full = jnp.swapaxes(bias_all[:, :, :own_bias], 0, 1).reshape(1, -1).astype(WIDE)
    table = lax.dynamic_slice_in_dim(table, lax.axis_index("mod") * images, images, 1)
    table = jnp.swapaxes(table, 0, 1).reshape(images, -1)

    def joined(whole):
        return whole.reshape(2, -1, whole.shape[-1])

    qkv_low = joined(qkv_w)
    slots = segments[::CHUNK]
    joint_bias = jnp.concatenate(
        [bias_full[:, 0:width], jnp.zeros((1, width), WIDE), bias_full[:, width : 2 * width]], axis=1
    )
    def blocked(turned):
        return turned.reshape(row_devices // 4, 2, 2, -1, tokens)

    act_turned, joint_rows, mixture, mixture_turned, log_totals, proj_w, fc1_w, fc2_w = attend(
        slots,
        x_in,
        table,
        joint_bias,
        qkv_low,
        segments,
        fc2_weight.astype(LOW),
        proj_w,
        fc1_w,
    )
    (
        block_out, mlp_turned, hidden_turned, pre_halves, branch_halves, attn_halves, mixture_grad, middle_grad, sums, pre_sums,
    ) = middle(
        slots, x_in, out_grad, mixture, table, bias_full, joined(proj_w), joined(fc1_w), joined(fc2_w)
    )
    (fc1_sums, proj_sums), fc2_totals = weight_grads(
        blocked(hidden_turned),
        branch_halves,
        blocked(mlp_turned),
        pre_halves,
        blocked(mixture_turned),
        attn_halves,
    )
    joint_halves, fc2_shard, proj_shard, fc1_totals = attend_back(
        joint_rows,
        segments,
        mixture,
        log_totals,
        mixture_grad,
        fc1_sums,
        proj_sums,
        fc2_totals,
    )
    chooser = (slots[None, :] == (jnp.arange(2 * images, dtype=jnp.int32) % images)[:, None]).astype(WIDE)
    qkv_shard, fc1_shard, mod_grad_w, x_grad, joint_sums = last_scatter(
        slots,
        blocked(act_turned),
        joint_halves,
        x_in,
        middle_grad,
        table,
        qkv_low,
        sums,
        chooser,
        fc1_totals,
    )
    mod_grads = mod_grad_w.reshape(2, row_devices, 2, images, -1)
    mod_grads = lax.dynamic_index_in_dim(mod_grads, lax.axis_index("mod"), 2, False)
    mod_grad_all = jnp.swapaxes(mod_grads, 0, 1).reshape(2 * row_devices * images, -1)
    own_rows = ada_weight.shape[0]
    own_silu = lax.dynamic_slice_in_dim(silu_all, row_index * own_rows, own_rows, 1)
    ada_shard = jnp.einsum("ic,io->co", own_silu, mod_grad_all, preferred_element_type=WIDE)
    own_columns = adab_weight.shape[1]
    adab_shard = jnp.sum(
        lax.dynamic_slice_in_dim(mod_grad_all, row_index * own_columns, own_columns, 1).astype(WIDE),
        axis=0,
    )
    silu_part = times_back(mod_grad_all, ada_low)
    silu_part = lax.all_to_all(silu_part, ROWS, split_axis=0, concat_axis=1, tiled=True)
    cond_grad = silu_back(silu_part + swap(silu_part, "mod"))[0]

    joint_sum = joint_sums.reshape(-1)
    sum_rows = jnp.sum(sums, axis=0)
    grad_bias = jnp.concatenate(
        [
            joint_sum[0:width],
            joint_sum[2 * width :],
            sum_rows[4],
            pre_sums.reshape(-1),
            sum_rows[5],
        ]
    ).reshape(devices, -1)
    bias_shard = jnp.sum(
        lax.all_to_all(grad_bias, ALL, split_axis=0, concat_axis=0, tiled=True), axis=0
    )

    rates = step_rates(tokens * devices)
    states_out = []
    states_out.extend(nesterov(qkv_weight, qkv_moment, qkv_average, qkv_shard, rates[0]))
    states_out.extend(nesterov(proj_weight, proj_moment, proj_average, proj_shard, rates[1]))
    states_out.extend(nesterov(fc1_weight, fc1_moment, fc1_average, fc1_shard, rates[2]))
    states_out.extend(nesterov(fc2_weight, fc2_moment, fc2_average, fc2_shard, rates[3]))
    states_out.extend(nesterov(bias_weight, bias_moment, bias_average, bias_shard, rates[4]))
    states_out.extend(nesterov(ada_weight, ada_moment, ada_average, ada_shard, rates[5]))
    states_out.extend(
        nesterov(adab_weight, adab_moment, adab_average, adab_shard.reshape(1, -1), rates[6])
    )
    return (block_out, x_grad, cond_grad) + tuple(states_out)


def solution(mesh):
    far = mesh.shape["dp"] // 4
    fine = Mesh(mesh.devices.reshape(far, 2, 2, mesh.shape["mod"]), ALL)
    tokens = P(ALL, None)
    images = P(ROWS, None)
    trunk = P(ROWS, "mod")
    bias = P(ALL)
    adab = P("mod", ROWS)
    states = (trunk,) * 12 + (bias,) * 3 + (trunk,) * 3 + (adab,) * 3
    return jax.shard_map(
        body,
        mesh=fine,
        in_specs=(tokens, images, bias, tokens) + states,
        out_specs=(tokens, tokens, images) + states,
        check_vma=False,
    )
```

```python
from functools import partial

import jax
import jax.numpy as jnp
from jax import lax
from jax.experimental import pallas as pl
from jax.experimental.pallas import tpu as pltpu
from jax.sharding import Mesh
from jax.sharding import PartitionSpec as P

D = 1152
HEADS = 16
HEAD = 72
FF = 4608
LANES = 128
CHUNK = 256

ROWS = ("far", "near", "core")
ALL = ("far", "near", "core", "mod")
LOW = jnp.bfloat16
WIDE = jnp.float32
LOG2E = 1.4426950408889634
NEG = -1e30
MESH = pl.DeviceIdType.MESH
VMEM = pl.BlockSpec(memory_space=pltpu.VMEM)
ANY = pl.BlockSpec(memory_space=pl.ANY)

EPS = 1e-06
MOMENTUM = 0.9
DECAY = 0.5


def step_rates(tokens_all):
    base_rate = tokens_all ** (-0.5)
    return (
        2.5 * D ** (-0.5) * base_rate,
        3.0 * D ** (-0.5) * base_rate,
        3.3 * D ** (-0.5) * base_rate,
        2.8 * FF ** (-0.5) * base_rate,
        0.5 * base_rate,
        2.0 * D ** (-0.5) * base_rate,
        0.3 * base_rate,
    )


def nesterov(weight, moment, average, gradient, rate):
    moment = MOMENTUM * moment + gradient
    weight = weight - rate * (gradient + MOMENTUM * moment)
    average = DECAY * average + (1.0 - DECAY) * weight
    return (weight, moment, average)


def places():
    return {name: lax.axis_index(name) for name in ALL}


def greet():
    here = places()
    count = lax.axis_size("far")
    others = [dict(far=lax.rem(here["far"] + d, count)) for d in range(1, count)]
    others += [{name: 1 - here[name]} for name in ("near", "core", "mod")]
    barrier = pltpu.get_barrier_semaphore()
    for other in others:
        pl.semaphore_signal(barrier, inc=1, device_id=other, device_id_type=MESH)
    pl.semaphore_wait(barrier, len(others))


def remote(source, target, sends, receives, slot, other):
    return pltpu.make_async_remote_copy(
        src_ref=source,
        dst_ref=target,
        send_sem=sends.at[slot],
        recv_sem=receives.at[slot],
        device_id=other,
        device_id_type=MESH,
    )


def messages(count):
    return count - 1 + 8


class Gather:
    def __init__(self, whole, sends, receives):
        self.whole, self.sends, self.receives = whole, sends, receives
        self.here = places()
        self.count = lax.axis_size("far")
        rows = whole.shape[4]
        self.rows = rows
        self.split = rows if rows % 8 else 8 * ((rows // 8 + 1) // 2)

    def _block(self, far):
        return self.whole.at[self.here["mod"], far, self.here["near"], self.here["core"]]

    def _far(self, shard, distance):
        far = self.here["far"]
        other = dict(far=lax.rem(far + distance, self.count))
        return remote(shard, self._block(far), self.sends, self.receives, distance - 1, other)

    def _far_came(self, shard, distance):
        origin = lax.rem(self.here["far"] + self.count - distance, self.count)
        return remote(
            shard, self._block(origin), self.sends, self.receives, distance - 1, dict(far=origin)
        )

    def start_far(self, shard, local):
        pltpu.make_async_copy(shard, self._block(self.here["far"]), local).start()
        for distance in range(1, self.count):
            self._far(shard, distance).start()

    def finish_far(self, shard, local):
        pltpu.make_async_copy(shard, self._block(self.here["far"]), local).wait()
        for distance in range(1, self.count):
            self._far(shard, distance).wait_send()
            self._far_came(shard, distance).wait_recv()

    def _quad(self, flips, first, size):
        near, core, mod = (
            1 - self.here[name] if name in flips else self.here[name] for name in ("near", "core", "mod")
        )
        return self.whole.at[mod, :, near, core, pl.ds(first, size)]

    def _step(self, name):
        head, rest = (0, self.split), (self.split, self.rows - self.split)
        full = (0, self.rows)
        return {
            "near": ((), "near", full, 0),
            "mod": ((), "mod", full, 1),
            "near_mod": (("near",), "mod", head, 2),
            "mod_near": (("mod",), "near", rest, 3),
            "core": ((), "core", full, 4),
            "near_core": (("near",), "core", full, 5),
            "mod_core": (("mod",), "core", full, 6),
            "both_core": (("near", "mod"), "core", full, 7),
        }[name]

    def _copy(self, name, incoming):
        flips, axis, span, slot = self._step(name)
        if span[1] == 0:
            return None
        quad = self._quad(flips + (axis,) if incoming else flips, *span)
        other = {axis: 1 - self.here[axis]}
        return remote(quad, quad, self.sends, self.receives, self.count - 1 + slot, other)

    def start(self, *names):
        for name in names:
            copy = self._copy(name, False)
            if copy is not None:
                copy.start()

    def receive(self, *names):
        for name in names:
            copy = self._copy(name, True)
            if copy is not None:
                copy.wait_recv()

    def spread(self):
        self.start("near", "mod", "core")

    def cross(self):
        self.receive("near")
        self.start("near_mod", "near_core")
        self.receive("mod")
        self.start("mod_near", "mod_core")

    def close(self):
        self.receive("near_mod", "mod_near")
        self.start("both_core")

    def end(self):
        self.receive("core", "near_core", "mod_core", "both_core")
        for name in (
            "near", "mod", "near_mod", "mod_near", "core", "near_core", "mod_core", "both_core",
        ):
            copy = self._copy(name, False)
            if copy is not None:
                copy.wait_send()


def gather_scratch(weights, locals_):
    count = lax.axis_size("far")
    shapes = [pltpu.SemaphoreType.DMA((messages(count),))] * (2 * weights)
    return shapes + [pltpu.SemaphoreType.DMA((locals_,))]


def whole_shape(shard):
    return jax.ShapeDtypeStruct((2, lax.axis_size("far"), 2, 2) + shard.shape, LOW)


def modulate(small_w, ada, table, local, small, partials, came_core, came_near, came_far, own, sends, receives):
    here = places()
    count = lax.axis_size("far")
    far, near, core, mod = (here[name] for name in ALL)
    row_devices = 4 * count
    rows = D // row_devices
    fetch = pltpu.make_async_copy(small_w, small, local)
    fetch.start()
    fetch.wait()
    device = (far * 2 + near) * 2 + core
    half = lax.div(device, row_devices // 2)
    first = lax.rem(device, row_devices // 2) * rows
    width = small.shape[-1]
    images = small.shape[-2]
    row = lax.broadcasted_iota(jnp.int32, (width, LANES), 0)
    column = lax.broadcasted_iota(jnp.int32, (width, LANES), 1)
    select = jnp.where(jnp.logical_and(row == first + column, column < rows), 1.0, 0.0).astype(LOW)
    for at in range(count):
        silu = small[half, at].reshape(4 * images, width).astype(WIDE).astype(LOW)
        mine = times(silu, select)
        mine = jnp.where(lanes(mine.shape) == rows, 1.0, mine).astype(LOW)
        partials[at] = times(mine, ada[...]).reshape(2, 2, images, -1)

    def move(source, target, slot, other):
        return remote(source, target, sends, receives, slot, other)

    to_core = move(partials.at[:, :, 1 - core], came_core, 0, dict(core=1 - core))
    to_core.start()
    to_core.wait()
    for at in range(count):
        partials[at, :, core] = partials[at, :, core] + came_core[at]
    to_near = move(partials.at[:, 1 - near, core], came_near, 1, dict(near=1 - near))
    to_near.start()
    yield
    to_near.wait()
    for at in range(count):
        partials[at, near, core] = partials[at, near, core] + came_near[at]
    copies = []
    for distance in range(1, count):
        target = lax.rem(far + distance, count)
        copies.append(
            move(partials.at[target, near, core], came_far.at[distance - 1], 2 + distance, dict(far=target))
        )
        copies[-1].start()
    yield
    total = partials[far, near, core]
    for distance, copy in enumerate(copies):
        copy.wait()
        total = total + came_far[distance]
    own[...] = total.astype(LOW).astype(WIDE)
    keep = pltpu.make_async_copy(own, table.at[mod], local)
    keep.start()
    to_mod = move(own, table.at[mod], 2, dict(mod=1 - mod))
    to_mod.start()
    yield
    keep.wait()
    to_mod.wait_send()
    move(own, table.at[1 - mod], 2, dict(mod=1 - mod)).wait_recv()


def first_kernel(*refs):
    small_s, qkv_s, proj_s, fc1_s, ada = refs[:5]
    table = refs[9]
    gather_sems, (local, *parts) = refs[10:18], refs[18:]
    small, qkv, proj, fc1 = (
        Gather(w, s, r) for w, s, r in zip(refs[5:9], gather_sems[0::2], gather_sems[1::2])
    )
    greet()
    small.start_far(small_s, local.at[3])
    qkv.start_far(qkv_s, local.at[0])
    small.finish_far(small_s, local.at[3])
    small.spread()
    small.cross()
    small.close()
    small.end()
    stages = modulate(small.whole, ada, table, local.at[3], *parts)
    next(stages)
    qkv.finish_far(qkv_s, local.at[0])
    qkv.spread()
    next(stages)
    proj.start_far(proj_s, local.at[1])
    fc1.start_far(fc1_s, local.at[2])
    next(stages)
    qkv.cross()
    qkv.close()
    qkv.end()
    next(stages, None)
    proj.finish_far(proj_s, local.at[1])
    fc1.finish_far(fc1_s, local.at[2])


def first_gather(ada, *shards):
    count = lax.axis_size("far")
    small = whole_shape(shards[0])
    images = small.shape[4]
    columns = ada.shape[1]
    return pl.pallas_call(
        first_kernel,
        out_shape=tuple(whole_shape(shard) for shard in shards)
        + (jax.ShapeDtypeStruct((2, images, columns), WIDE),),
        in_specs=[VMEM] * 5,
        out_specs=(ANY,) * 5,
        scratch_shapes=gather_scratch(4, 4)
        + [
            pltpu.VMEM(small.shape, LOW),
            pltpu.VMEM((count, 2, 2, images, columns), WIDE),
            pltpu.VMEM((count, 2, images, columns), WIDE),
            pltpu.VMEM((count, images, columns), WIDE),
            pltpu.VMEM((count - 1, images, columns), WIDE),
            pltpu.VMEM((images, columns), WIDE),
            pltpu.SemaphoreType.DMA((count + 2,)),
            pltpu.SemaphoreType.DMA((count + 2,)),
        ],
        compiler_params=pltpu.CompilerParams(
            collective_id=0, has_side_effects=True, vmem_limit_bytes=60 * 2**20
        ),
        name="first_gather",
    )(*shards, ada)


def lanes(shape): return lax.broadcasted_iota(jnp.int32, shape, 1)

def seg_codes(seg, n):
    lane = lanes((n, LANES))
    code = lane - HEAD
    inside = jnp.logical_and(code >= 0, code < 4)
    same = code == seg
    q = jnp.where(jnp.logical_and(inside, same), 1.0, 0.0)
    k = jnp.where(jnp.logical_and(inside, jnp.logical_not(same)), NEG, 0.0)
    return q, k

def head_of(wide_rows, start):
    return wide_rows[:, start:start+HEAD]

def pad_head(part, aug):
    n = part.shape[0]
    full = jnp.concatenate([part, jnp.zeros((n, LANES-HEAD), part.dtype)], axis=1)
    return jnp.where(lanes((n,LANES)) < HEAD, full, aug)

def attend_kernel(*refs):
    slots, x_ref, table, bias, weight, seg_ref, fc2_s = refs[:7]
    act_turned, joint_ref, mixed_ref, turned_ref, lse_ref, proj_w, fc1_w, fc2_w = refs[9:17]
    qh, kh, vh = refs[17:20]
    *sems, local = refs[20:]
    proj, fc1, fc2 = (
        Gather(w, s, r) for w, s, r in zip((proj_w, fc1_w, fc2_w), sems[0::2], sems[1::2])
    )
    greet()
    fc2.start_far(fc2_s, local.at[0])
    proj.spread()
    fc1.spread()

    T = x_ref.shape[0]

    def fill(i, carry):
        rows = pl.ds(pl.multiple_of(i * CHUNK, CHUNK), CHUNK)
        slot = slots[i]
        h1, _ = normed(x_ref[rows, :].astype(WIDE))
        act = (h1 * (1.0 + row_of(table, slot, 1)) + row_of(table, slot, 0)).astype(LOW)
        act_turned[:, rows] = act.T
        joint = jnp.concatenate([times(act, weight[0]), times(act, weight[1])], axis=1)
        joint_ref[rows, :] = (joint + bias[...]).astype(LOW)
        lane = lanes((CHUNK, LANES))
        qc, kc = seg_codes(seg_ref[rows, :], CHUNK)
        qc = qc.astype(LOW); kc = kc.astype(LOW)
        ones = jnp.where(jnp.logical_and(lane >= HEAD, lane < HEAD+3), 1.0, 0.0).astype(LOW)
        for h in range(HEADS):
            qh[h, rows, :] = pad_head(joint_ref[rows, h*HEAD:(h+1)*HEAD], qc)
            kh[h, rows, :] = pad_head(joint_ref[rows, D+h*HEAD:D+(h+1)*HEAD], kc)
            vh[h, rows, :] = pad_head(joint_ref[rows, 2*D+h*HEAD:2*D+(h+1)*HEAD], ones)
        pl.when(i == 2)(proj.cross)
        return carry
    lax.fori_loop(0, T//CHUNK, fill, 0)
    lse_ref[...] = jnp.zeros_like(lse_ref)
    def head(h, carry):
        k = kh[h]; v = vh[h]
        for i in range(T//CHUNK):
            rows = pl.ds(i*CHUNK, CHUNK)
            q = qh[h, rows, :]
            s = lax.dot_general(q, k, (((1,),(1,)),((),())), preferred_element_type=WIDE)
            m = jnp.max(s, axis=1, keepdims=True)
            p = jnp.exp2((s - m)*(HEAD**-0.5*LOG2E)).astype(LOW)
            o = jnp.dot(p, v, preferred_element_type=WIDE)
            l = o[:, HEAD:HEAD+1]
            qh[h, rows, :] = (o / l).astype(LOW)
            col = m*HEAD**-0.5 + jnp.log(l)
            lse_ref[rows, :] = jnp.where(lanes((CHUNK,LANES)) == h, col, lse_ref[rows, :])
        tasks = {
            3: lambda: (fc2.finish_far(fc2_s, local.at[0]), fc2.spread()),
            6: fc1.cross,
            8: proj.close,
            10: proj.end,
        }
        for at, task in tasks.items():

            @pl.when(h == at)
            def _(task=task):
                task()

        return carry
    lax.fori_loop(0, HEADS, head, 0)
    def drain(i, carry):
        rows = pl.ds(pl.multiple_of(i*CHUNK, CHUNK), CHUNK)
        mixed = jnp.concatenate([qh[h, rows, :][:, :HEAD] for h in range(HEADS)], axis=1)
        mixed_ref[rows, :] = mixed
        turned_ref[:, rows] = mixed.T
        return carry
    lax.fori_loop(0, T//CHUNK, drain, 0)
    fc2.cross()
    fc1.close()
    fc1.end()
    fc2.close()
    fc2.end()


def attend(slots, x_in, table, bias, weight, segments, fc2_s, proj_w, fc1_w):
    tokens = x_in.shape[0]
    wide = HEADS * HEAD
    return pl.pallas_call(
        attend_kernel,
        out_shape=(
            jax.ShapeDtypeStruct((wide, tokens), LOW),
            jax.ShapeDtypeStruct((tokens, 3 * wide), LOW),
            jax.ShapeDtypeStruct((tokens, wide), LOW),
            jax.ShapeDtypeStruct((wide, tokens), LOW),
            jax.ShapeDtypeStruct((tokens, LANES), WIDE),
            jax.ShapeDtypeStruct(proj_w.shape, LOW),
            jax.ShapeDtypeStruct(fc1_w.shape, LOW),
            whole_shape(fc2_s),
        ),
        in_specs=[pl.BlockSpec(memory_space=pltpu.SMEM)] + [VMEM] * 6 + [ANY] * 2,
        out_specs=(VMEM,) * 5 + (ANY,) * 3,
        scratch_shapes=[pltpu.VMEM((HEADS, tokens, LANES), LOW)] * 3 + gather_scratch(3, 1),
        input_output_aliases={7: 5, 8: 6},
        compiler_params=pltpu.CompilerParams(
            collective_id=1, has_side_effects=True, vmem_limit_bytes=60 * 2**20
        ),
        name="attend",
    )(slots, x_in, table, bias, weight, segments.reshape(tokens, 1), fc2_s, proj_w, fc1_w)


def row_spans(rows):
    first = rows if rows % 8 else 8 * ((rows // 8 + 1) // 2)
    return [(0, first)] + ([(first, rows - first)] if first < rows else [])


class Reduce:
    def __init__(self, part, span, first, came, joint, total, base, sems, loads=False):
        self.part, self.span, self.first = part, span, first
        self.second = "near" if first == "mod" else "mod"
        self.came_both, self.came_first, self.came_second, self.came_far = came
        self.joint, self.total_, self.base = joint, total, base
        self.sends, self.receives, self.locals_ = sems
        self.loads = loads
        self.here = places()
        self.count = lax.axis_size("far")

    def _swap(self, source, target, slot, axis):
        return remote(source, target, self.sends, self.receives, slot, {axis: 1 - self.here[axis]})

    def _both(self):
        return self._swap(self.part("near", "mod"), self.came_both, 0, self.first)

    def _first(self):
        return self._swap(self.part(self.first), self.came_first, 1, self.first)

    def _second(self):
        return self._swap(self.joint, self.came_second, 2, self.second)

    def _load(self, number):
        source, target = ((self.part(self.second), self.joint), (self.part(), self.total_))[number]
        return pltpu.make_async_copy(source, target, self.locals_.at[number])

    def _far(self, distance):
        target = lax.rem(self.here["far"] + distance, self.count)
        return remote(
            self.total_.at[target],
            self.came_far.at[distance - 1],
            self.sends,
            self.receives,
            2 + distance,
            dict(far=target),
        )

    def start(self):
        self._both().start()
        self._first().start()
        if self.loads:
            self._load(0).start()
            self._load(1).start()

    def merge(self):
        if self.loads:
            self._load(0).wait()
        self._both().wait_recv()

        def add(at, carry):
            self.joint[at] = (self.joint[at].astype(WIDE) + self.came_both[at].astype(WIDE)).astype(LOW)
            return carry

        lax.fori_loop(0, self.count, add, 0)
        self._second().start()

    def total(self):
        if self.loads:
            self._load(1).wait()
        self._first().wait_recv()
        self._second().wait_recv()

        def add(at, carry):
            self.total_[at] = (
                self.base[at].astype(WIDE)
                + self.came_first[at].astype(WIDE)
                + self.came_second[at].astype(WIDE)
            ).astype(LOW)
            return carry

        lax.fori_loop(0, self.count, add, 0)
        self._both().wait_send()
        self._first().wait_send()
        self._second().wait_send()

    def start_far(self):
        for distance in range(1, self.count):
            self._far(distance).start()

    def final(self, out):
        value = self.total_[self.here["far"]].astype(WIDE)
        for distance in range(1, self.count):
            self._far(distance).wait_recv()
            value = value + self.came_far[distance - 1].astype(WIDE)
        out[pl.ds(*self.span), :] = value
        for distance in range(1, self.count):
            self._far(distance).wait_send()


ORDERS = ("mod", "near")


def run(parts, *names):
    for part in parts:
        for name in names:
            getattr(part, name)()


def span_part(sums, span):
    def part(*flips):
        near, mod = (
            1 - lax.axis_index(name) if name in flips else lax.axis_index(name) for name in ("near", "mod")
        )
        return sums.at[mod, near, :, pl.ds(*span)]

    return part


def take(scratch, number):
    return scratch[:number], scratch[number:]


def came_scratch(count, span, columns, far=True):
    block = (count, span[1], columns)
    shapes = [pltpu.VMEM(block, LOW)] * 3
    return shapes + ([pltpu.VMEM((count - 1,) + block[1:], LOW)] if far else [])


def sem_scratch(count):
    return [pltpu.SemaphoreType.DMA((count + 2,))] * 2 + [pltpu.SemaphoreType.DMA((2,))]


def loaded_scratch(shape, total=True):
    count, rows, columns = shape[2:]
    shapes = []
    for span in row_spans(rows):
        shapes += came_scratch(count, span, columns)
        shapes += [pltpu.VMEM((count, span[1], columns), LOW)] * (2 if total else 1)
        shapes += sem_scratch(count)
    return shapes


def loaded_reduces(sums, scratch, totals=None):
    reduces = []
    for number, span in enumerate(row_spans(sums.shape[3])):
        came, scratch = take(scratch, 4)
        (joint,), scratch = take(scratch, 1)
        if totals is None:
            (total,), scratch = take(scratch, 1)
        else:
            total = totals[number]
        sems, scratch = take(scratch, 3)
        reduces.append(
            Reduce(span_part(sums, span), span, ORDERS[number], came, joint, total, total, sems, True)
        )
    return reduces, scratch


def resident_scratch(shape, far=True):
    count, rows, columns = shape[2:]
    shapes = []
    for span in row_spans(rows):
        shapes += came_scratch(count, span, columns, far) + sem_scratch(count)
    return shapes


def resident_reduces(sums, scratch, totals=None):
    reduces = []
    for number, span in enumerate(row_spans(sums.shape[3])):
        came, scratch = take(scratch, 4 if totals is None else 3)
        sems, scratch = take(scratch, 3)
        part = span_part(sums, span)
        order = ORDERS[number]
        own = part()
        total = own if totals is None else totals[number]
        came = list(came) + [None] * (4 - len(came))
        joint = part("near" if order == "mod" else "mod")
        reduces.append(Reduce(part, span, order, came, joint, total, own, sems))
    return reduces, scratch


def far_scratch(totals):
    shapes = []
    for total in totals:
        count = total.shape[0]
        shapes += [pltpu.VMEM((count - 1,) + total.shape[1:], LOW)] + sem_scratch(count)[:2]
    return shapes


def far_reduces(totals, rows, scratch):
    reduces = []
    for total, span in zip(totals, row_spans(rows)):
        (came, sends, receives), scratch = take(scratch, 3)
        came = (None, None, None, came)
        reduces.append(Reduce(None, span, "mod", came, None, total, total, (sends, receives, None)))
    return reduces, scratch


class Product:
    def __init__(self, left, right, scratch):
        self.left, self.right = left, right
        self.rows_, self.sums, self.came, self.loads, self.sends, self.receives = scratch
        self.core = lax.axis_index("core")

    @staticmethod
    def scratch(count, rows, tokens, columns):
        sums = pltpu.VMEM((2, 2, count, rows, columns), LOW)
        sems = [pltpu.SemaphoreType.DMA((4,))] * 3
        return [pltpu.VMEM((4, count, rows, tokens), LOW), sums, sums] + sems

    def _load(self, near, own):
        core = self.core if own else 1 - self.core
        slot = 2 * own + near
        return pltpu.make_async_copy(
            self.left.at[:, near, core], self.rows_.at[slot], self.loads.at[slot]
        )

    def load(self):
        for own in (0, 1):
            for near in (0, 1):
                self._load(near, own).start()

    def _copy(self, mod, near):
        return remote(
            self.sums.at[mod, near],
            self.came.at[mod, near],
            self.sends,
            self.receives,
            2 * mod + near,
            dict(core=1 - self.core),
        )

    def _blocks(self, near, own, store):
        count, rows, tokens = self.rows_.shape[1:]
        columns = self.right.shape[2]
        self._load(near, own).wait()
        left = self.rows_[2 * own + near].reshape(count * rows, tokens)
        width = columns if columns <= 1024 else columns // 2
        width = width if width % LANES == 0 else columns
        for mod in (0, 1):
            for at in range(0, columns, width):
                product = times(left, self.right[mod, :, at : at + width])
                store(mod, at, width, product.reshape(count, rows, width))

    def send(self):
        for near in (0, 1):

            def store(mod, at, width, product, near=near):
                self.sums[mod, near, :, :, at : at + width] = product.astype(LOW)

            self._blocks(near, 0, store)
            for mod in (0, 1):
                self._copy(mod, near).start()

    def sum(self):
        for near in (0, 1):
            for mod in (0, 1):
                self._copy(mod, near).wait_send()
                self._copy(mod, near).wait_recv()

            def store(mod, at, width, product, near=near):
                came = self.came[mod, near, :, :, at : at + width]
                self.sums[mod, near, :, :, at : at + width] = (product + came.astype(WIDE)).astype(LOW)

            self._blocks(near, 1, store)


def total_shapes(count, rows, columns):
    return [jax.ShapeDtypeStruct((count, span[1], columns), LOW) for span in row_spans(rows)]


def weight_kernel(*refs, spans, stored):
    count = stored + (spans > 0)
    sides, refs = take(refs, 2 * count)
    outs, refs = take(refs, stored)
    totals, scratch = take(refs, spans)
    products = []
    for number in range(count):
        used, scratch = take(scratch, 6)
        products.append(Product(sides[2 * number], sides[2 * number + 1], used))
    reduces = []
    if spans:
        reduces, scratch = resident_reduces(products[0].sums, scratch, totals)
    (out_sems,) = scratch
    products[0].load()
    greet()
    copies = []
    for number, product in enumerate(products):
        product.send()
        if number + 1 < count:
            products[number + 1].load()
        product.sum()
        if spans and number == 0:
            run(reduces, "start")
            continue
        copy = pltpu.make_async_copy(product.sums, outs[len(copies)], out_sems.at[len(copies)])
        copy.start()
        copies.append(copy)
        if spans and number == 1:
            run(reduces, "merge")
    if spans and count == 1:
        run(reduces, "merge")
    run(reduces, "total")
    for copy in copies:
        copy.wait()


def weight_call(summed, stored, number):
    pairs = summed + stored
    count, _, _, rows, tokens = pairs[0][0].shape
    columns = pairs[0][1].shape[2]
    totals = total_shapes(count, rows, columns) if summed else []
    scratch = []
    for left, right in pairs:
        scratch += Product.scratch(count, left.shape[3], tokens, right.shape[2])
    if summed:
        scratch += resident_scratch((2, 2, count, rows, columns), False)
    out = pl.pallas_call(
        partial(weight_kernel, spans=len(totals), stored=len(stored)),
        out_shape=tuple(
            jax.ShapeDtypeStruct((2, 2, count, left.shape[3], right.shape[2]), LOW) for left, right in stored
        )
        + tuple(totals),
        in_specs=[ANY, VMEM] * len(pairs),
        out_specs=(ANY,) * len(stored) + (VMEM,) * len(totals),
        scratch_shapes=scratch + [pltpu.SemaphoreType.DMA((2,))],
        compiler_params=pltpu.CompilerParams(
            collective_id=number, has_side_effects=True, vmem_limit_bytes=63 * 2**20
        ),
        name="weight_grads",
    )(*[side for pair in pairs for side in pair])
    return out[: len(stored)], out[len(stored) :]


def weight_grads(hidden, branch, mlp, pre, mixed, attn):
    summed, stored = [(hidden, branch)], [(mlp, pre), (mixed, attn)]
    if mlp.shape[3] % 8 == 0:
        return weight_call(summed, stored, 4)
    _, totals = weight_call(summed, [], 4)
    sums, _ = weight_call([], stored, 5)
    return sums, totals


def tile_sums_by_slot(chooser, sums):
    total = None
    for at, row in enumerate(sums):
        part = chooser[:, at : at + 1] * row
        total = part if total is None else total + part
    return total


def last_kernel(*refs, spans):
    slots, act, joint, x_ref, dx1_ref, table, weight, mid_sums, pre_sums, chooser = refs[:10]
    totals, refs = take(refs[10:], spans)
    qkv_out, fc1_out, small_w, x_grad_ref, *scratch = refs
    qkv_scratch, scratch = take(scratch, 6)
    qkv = Product(act, joint, qkv_scratch)
    qkv_sum, scratch = resident_reduces(qkv.sums, scratch)
    fc1_sum, scratch = far_reduces(totals, fc1_out.shape[0], scratch)
    small_sends, small_receives, local, first_sums, joint_sums, small_s = scratch
    small = Gather(small_w, small_sends, small_receives)
    tiles = x_ref.shape[0] // CHUNK
    qkv.load()
    greet()
    run(fc1_sum, "start_far")
    qkv.send()
    qkv.sum()
    run(qkv_sum, "start")

    def back(at, carry):
        rows = pl.ds(pl.multiple_of(at * CHUNK, CHUNK), CHUNK)
        dact = times_across(joint[0, rows, :], weight[0]) + times_across(joint[1, rows, :], weight[1])
        h1, inverse = normed(x_ref[rows, :].astype(WIDE))
        first_sums[at, 0:1, :] = column_sums(dact)
        first_sums[at, 1:2, :] = column_sums(dact * h1)
        dh1 = dact * (1.0 + row_of(table, slots[at], 1))
        x_grad_ref[rows, :] = dx1_ref[rows, :] + inverse * (
            dh1
            - jnp.mean(dh1, axis=-1, keepdims=True)
            - h1 * jnp.mean(dh1 * h1, axis=-1, keepdims=True)
        )
        for side in range(2):
            joint_sums[side : side + 1, :] += column_sums(joint[side, rows, :].astype(WIDE))

        @pl.when(at == tiles // 2 - 1)
        def _():
            run(qkv_sum, "merge")

        return carry

    joint_sums[...] = jnp.zeros_like(joint_sums)
    lax.fori_loop(0, tiles, back, 0)
    choose = chooser[...]
    upper = lax.broadcasted_iota(jnp.int32, (choose.shape[0], D), 0) < choose.shape[0] // 2
    groups = (
        [first_sums[at, 0:1, :] for at in range(tiles)],
        [first_sums[at, 1:2, :] for at in range(tiles)],
    ) + tuple([mid_sums[at, row : row + 1, :] for at in range(tiles)] for row in range(4))
    for group in range(3):
        value = jnp.where(
            upper, tile_sums_by_slot(choose, groups[group]), tile_sums_by_slot(choose, groups[group + 3])
        )
        small_s[0:8, group * D : (group + 1) * D] = value.astype(LOW)
    pre = pre_sums[...]
    tile_rows = [column_sums(mid_sums[:, row, :]) for row in (4, 5)]
    biases = (
        (joint_sums[0:1, :D], joint_sums[1:2, D // 2 :], tile_rows[0]),
        tuple(pre[:, at * D : (at + 1) * D] for at in range(3)),
        (pre[:, 3 * D :], tile_rows[1], jnp.zeros((1, D), WIDE)),
    )
    blank = jnp.zeros((5, D), WIDE)
    for group in range(3):
        rows = jnp.concatenate([biases[row][group] for row in range(3)] + [blank], axis=0)
        small_s[8:16, group * D : (group + 1) * D] = rows.astype(LOW)
    small.start_far(small_s, local.at[0])
    small.finish_far(small_s, local.at[0])
    small.spread()
    run(qkv_sum, "total", "start_far")
    small.cross()
    small.close()
    small.end()
    for part in fc1_sum:
        part.final(fc1_out)
    for part in qkv_sum:
        part.final(qkv_out)


def last_scatter(slots, act, joint, x_in, dx1, table, weight, mid_sums, pre_sums, chooser, totals):
    count, _, _, rows, tokens = act.shape
    fc1_columns = totals[0].shape[2]
    columns = joint.shape[2]
    small_s = jax.ShapeDtypeStruct((16, 3 * D), LOW)
    return pl.pallas_call(
        partial(last_kernel, spans=len(totals)),
        out_shape=(
            jax.ShapeDtypeStruct((rows, columns), WIDE),
            jax.ShapeDtypeStruct((sum(total.shape[1] for total in totals), fc1_columns), WIDE),
            whole_shape(small_s),
            jax.ShapeDtypeStruct((tokens, D), WIDE),
        ),
        in_specs=[pl.BlockSpec(memory_space=pltpu.SMEM), ANY] + [VMEM] * (8 + len(totals)),
        out_specs=(VMEM, VMEM, ANY, VMEM),
        scratch_shapes=Product.scratch(count, rows, tokens, columns)
        + resident_scratch((2, 2, count, rows, columns))
        + far_scratch(totals)
        + gather_scratch(1, 1)
        + [
            pltpu.VMEM((tokens // CHUNK, 8, D), WIDE),
            pltpu.VMEM((2, columns), WIDE),
            pltpu.VMEM(small_s.shape, LOW),
        ],
        compiler_params=pltpu.CompilerParams(
            collective_id=3, has_side_effects=True, vmem_limit_bytes=63 * 2**20
        ),
        name="last_scatter",
    )(slots, act, joint, x_in, dx1, table, weight, mid_sums, pre_sums, chooser, *totals)


def split3(v):
    hi = v.astype(LOW).astype(WIDE)
    mid = (v - hi).astype(LOW).astype(WIDE)
    lo = v - hi - mid
    return hi, mid, lo


def attend_back_kernel(*refs, fc2_spans, spans):
    qkv_ref, seg_ref, mixed_ref, lse_ref, up_ref, fc1_sums, proj_sums = refs[:7]
    fc2_totals, refs = take(refs[7:], fc2_spans)
    out_ref, fc2_out, proj_out, *refs = refs
    fc1_totals, refs = take(refs, spans)
    qh, kh, vh, uh, stage, stage_sems, leave, leave_sems, *scratch = refs
    proj, scratch = loaded_reduces(proj_sums, scratch)
    fc1, scratch = loaded_reduces(fc1_sums, scratch, fc1_totals)
    fc2, scratch = far_reduces(fc2_totals, fc2_out.shape[0], scratch)
    T = mixed_ref.shape[0]
    chunks = T // CHUNK
    greet()
    run(fc2, "start_far")
    run(fc1, "start")

    def load(i):
        rows = pl.ds(pl.multiple_of(i * CHUNK, CHUNK), CHUNK)
        slot = lax.rem(i, 2)
        return pltpu.make_async_copy(qkv_ref.at[rows], stage.at[slot], stage_sems.at[slot])

    load(0).start()

    def fill(i, carry):
        rows = pl.ds(pl.multiple_of(i * CHUNK, CHUNK), CHUNK)

        @pl.when(i + 1 < chunks)
        def _():
            load(i + 1).start()

        load(i).wait()
        qkv = stage.at[lax.rem(i, 2)]
        lane = lanes((CHUNK, LANES))
        qc, kc = seg_codes(seg_ref[rows, :], CHUNK)
        kc = jnp.where(jnp.logical_and(lane >= HEAD + 4, lane < HEAD + 7), 1.0, kc).astype(LOW)
        ones = jnp.where(jnp.logical_and(lane >= HEAD, lane < HEAD + 3), 1.0, 0.0).astype(LOW)

        def spread(v, at, base):
            hi, mid, lo = split3(v)
            return jnp.where(
                lane == at, hi, jnp.where(lane == at + 1, mid, jnp.where(lane == at + 2, lo, base))
            )

        for h in range(HEADS):
            a, b = h * HEAD, (h + 1) * HEAD
            qa = spread(-lse_ref[rows, h : h + 1] * HEAD**0.5, HEAD + 4, qc).astype(LOW)
            qh[h, rows, :] = pad_head(qkv[:, a:b], qa)
            kh[h, rows, :] = pad_head(qkv[:, D + a : D + b], kc)
            vh[h, rows, :] = pad_head(qkv[:, 2 * D + a : 2 * D + b], ones)
            u = up_ref[rows, a:b]
            delta = jnp.sum(u.astype(WIDE) * mixed_ref[rows, a:b].astype(WIDE), axis=1, keepdims=True)
            ua = spread(-delta, HEAD, jnp.zeros((CHUNK, LANES), WIDE)).astype(LOW)
            uh[h, rows, :] = pad_head(u, ua)
        return carry

    lax.fori_loop(0, chunks, fill, 0)
    across = (((1,), (1,)), ((), ()))
    tasks = {
        4: lambda: (run(fc1, "merge"), run(proj, "start")),
        11: lambda: run(proj, "merge"),
        14: lambda: run(proj, "total", "start_far"),
    }

    def head(h, carry):
        k = kh[h]
        v = vh[h]
        kt = k.T
        dk = jnp.zeros((T, LANES), WIDE)
        dv = jnp.zeros((T, LANES), WIDE)
        for i in range(chunks):
            rows = pl.ds(i * CHUNK, CHUNK)
            q = qh[h, rows, :]
            u = uh[h, rows, :]
            s = lax.dot_general(k, q, across, preferred_element_type=WIDE)
            p = jnp.exp2(s * (HEAD**-0.5 * LOG2E))
            dp = lax.dot_general(v, u, across, preferred_element_type=WIDE)
            ds = (p * dp).astype(LOW)
            dv = dv + jnp.dot(p.astype(LOW), u, preferred_element_type=WIDE)
            dk = dk + jnp.dot(ds, q, preferred_element_type=WIDE)
            dqt = jnp.dot(kt, ds, preferred_element_type=WIDE)
            qh[h, rows, :] = (dqt.T * HEAD**-0.5).astype(LOW)
        kh[h] = (dk * HEAD**-0.5).astype(LOW)
        vh[h] = dv.astype(LOW)
        for at, task in tasks.items():

            @pl.when(h == at)
            def _(task=task):
                task()

        return carry

    lax.fori_loop(0, HEADS, head, 0)

    def store(i, side):
        rows = pl.ds(pl.multiple_of(i * CHUNK, CHUNK), CHUNK)
        return pltpu.make_async_copy(
            leave.at[side], out_ref.at[side, rows], leave_sems.at[side]
        )

    def drain(i, carry):
        rows = pl.ds(pl.multiple_of(i * CHUNK, CHUNK), CHUNK)
        parts = [g[h, rows, :][:, :HEAD] for g in (qh, kh, vh) for h in range(HEADS)]
        for side in range(2):

            @pl.when(i > 0)
            def _(side=side):
                store(i - 1, side).wait()

            own = parts[side * len(parts) // 2 : (side + 1) * len(parts) // 2]
            leave[side] = jnp.concatenate(own, axis=1)
            store(i, side).start()
        return carry

    lax.fori_loop(0, chunks, drain, 0)
    run(fc1, "total")
    for side in range(2):
        store(chunks - 1, side).wait()
    for part in fc2:
        part.final(fc2_out)
    for part in proj:
        part.final(proj_out)


def attend_back(qkv, segments, mixed, lse, upstream, fc1_sums, proj_sums, fc2_totals):
    tokens = qkv.shape[0]
    count, rows, columns = fc1_sums.shape[2:]
    totals = total_shapes(count, rows, columns)
    fc2_rows = sum(total.shape[1] for total in fc2_totals)
    out = pl.pallas_call(
        partial(attend_back_kernel, fc2_spans=len(fc2_totals), spans=len(totals)),
        out_shape=(
            jax.ShapeDtypeStruct((2, tokens, 3 * HEADS * HEAD // 2), LOW),
            jax.ShapeDtypeStruct((fc2_rows, fc2_totals[0].shape[2]), WIDE),
            jax.ShapeDtypeStruct(proj_sums.shape[3:], WIDE),
        )
        + tuple(totals),
        in_specs=[ANY] + [VMEM] * 4 + [ANY] * 2 + [VMEM] * len(fc2_totals),
        out_specs=(ANY, VMEM, VMEM) + (VMEM,) * len(totals),
        scratch_shapes=[pltpu.VMEM((HEADS, tokens, LANES), LOW)] * 4
        + [pltpu.VMEM((2, CHUNK, 3 * HEADS * HEAD), LOW), pltpu.SemaphoreType.DMA((2,))]
        + [pltpu.VMEM((2, CHUNK, 3 * HEADS * HEAD // 2), LOW), pltpu.SemaphoreType.DMA((2,))]
        + loaded_scratch(proj_sums.shape)
        + loaded_scratch(fc1_sums.shape, False)
        + far_scratch(fc2_totals),
        compiler_params=pltpu.CompilerParams(
            collective_id=2, has_side_effects=True, vmem_limit_bytes=63 * 2**20
        ),
        name="attend_back",
    )(qkv, segments.reshape(tokens, 1), mixed, lse, upstream, fc1_sums, proj_sums, *fc2_totals)
    return out[0], out[1], out[2], out[3:]


def normed(values):
    centre = values - jnp.mean(values, axis=-1, keepdims=True)
    inverse = lax.rsqrt(jnp.mean(centre * centre, axis=-1, keepdims=True) + EPS)
    return centre * inverse, inverse


def row_of(table, slot, group):
    return table[pl.ds(slot, 1), group * D : (group + 1) * D]


def column_sums(values):
    return jnp.sum(values, axis=0, keepdims=True)


def times_across(left, right):
    return lax.dot_general(left, right, (((1,), (1,)), ((), ())), preferred_element_type=WIDE)


def fixed(*shape):
    return pl.BlockSpec(
        shape, lambda i, slots: (0,) * len(shape), pipeline_mode=pl.Buffered(1)
    )


GELU = 0.7978845608028654
CUBIC = 0.044715
SPAN = 768
BLOCK = 512


def middle_kernel(
    slots, x_ref, g_ref, mixed_ref, table, bias, bias1, proj, fc1, fc2,
    block_ref, mlp_turned, hidden_turned, dpre_ref, dbranch_ref, dattn_ref, dmixed_ref, dx1_ref, sums_ref, dpre_sums,
    attn_out, mlp, branch,
):
    step = pl.program_id(0)
    tokens = x_ref.shape[0]

    @pl.when(step == 0)
    def _():
        def enter(tile_at, carry):
            rows = pl.ds(pl.multiple_of(tile_at * CHUNK, CHUNK), CHUNK)
            slot = slots[tile_at]
            gate1, shift2, scale2, gate2 = (row_of(table, slot, group) for group in (2, 3, 4, 5))
            mixed = mixed_ref[rows, :]
            out = jnp.concatenate([times(mixed, proj[0]), times(mixed, proj[1])], axis=1)
            out = out + bias[:, 2 * D : 3 * D]
            attn_out[rows, :] = out
            h2, _ = normed(x_ref[rows, :].astype(WIDE) + gate1 * out)
            mlp_in = (h2 * (1.0 + scale2) + shift2).astype(LOW)
            mlp[rows, :] = mlp_in
            mlp_turned[:, rows] = mlp_in.T
            dbranch = (gate2 * g_ref[rows, :].astype(WIDE)).astype(LOW)
            sums_ref[tile_at, 5:6, :] = column_sums(dbranch.astype(WIDE))
            dbranch_ref[0, rows, :] = dbranch[:, : D // 2]
            dbranch_ref[1, rows, :] = dbranch[:, D // 2 :]
            return carry

        lax.fori_loop(0, tokens // CHUNK, enter, 0)
        branch[...] = jnp.zeros_like(branch)
        dx1_ref[...] = jnp.zeros_like(dx1_ref)

    total = None
    for first in range(0, tokens, BLOCK):
        rows = slice(first, first + BLOCK)
        pre = times(mlp[rows, :], fc1[0]) + bias1[0]
        square = pre * pre
        bend = jnp.tanh(GELU * pre * (1.0 + CUBIC * square))
        rise = 0.5 * (1.0 + bend)
        hidden = (pre * rise).astype(LOW)
        hidden_turned[:, rows] = hidden.T
        for side in range(2):
            branch[side, rows] += times(hidden, fc2[side])
        slope = rise + 0.5 * GELU * pre * (1.0 - bend * bend) * (1.0 + 3.0 * CUBIC * square)
        dhidden = times_across(dbranch_ref[0, rows], fc2[0]) + times_across(dbranch_ref[1, rows], fc2[1])
        dpre = (dhidden * slope).astype(LOW)
        dpre_ref[0, rows] = dpre
        part = column_sums(dpre.astype(WIDE))
        total = part if total is None else total + part
        dx1_ref[rows, :] += times_across(dpre, fc1[0])
    dpre_sums[...] = total

    @pl.when(step == pl.num_programs(0) - 1)
    def _():
        def leave(tile_at, carry):
            rows = pl.ds(pl.multiple_of(tile_at * CHUNK, CHUNK), CHUNK)
            slot = slots[tile_at]
            gate1, scale2, gate2 = (row_of(table, slot, group) for group in (2, 4, 5))
            out = attn_out[rows, :]
            x1 = x_ref[rows, :].astype(WIDE) + gate1 * out
            h2, inverse = normed(x1)
            whole = jnp.concatenate([branch[0, rows, :], branch[1, rows, :]], axis=1) + bias[:, 3 * D + FF :]
            block_ref[rows, :] = (x1 + gate2 * whole).astype(LOW)
            g = g_ref[rows, :].astype(WIDE)
            sums_ref[tile_at, 3:4, :] = column_sums(g * whole)
            dmlp = dx1_ref[rows, :]
            sums_ref[tile_at, 1:2, :] = column_sums(dmlp)
            sums_ref[tile_at, 2:3, :] = column_sums(dmlp * h2)
            dh2 = dmlp * (1.0 + scale2)
            dx1 = g + inverse * (
                dh2
                - jnp.mean(dh2, axis=-1, keepdims=True)
                - h2 * jnp.mean(dh2 * h2, axis=-1, keepdims=True)
            )
            dx1_ref[rows, :] = dx1
            sums_ref[tile_at, 0:1, :] = column_sums(dx1 * out)
            dattn = (gate1 * dx1).astype(LOW)
            sums_ref[tile_at, 4:5, :] = column_sums(dattn.astype(WIDE))
            sums_ref[tile_at, 6:8, :] = jnp.zeros((2, D), WIDE)
            left, right = dattn[:, : D // 2], dattn[:, D // 2 :]
            dattn_ref[0, rows, :] = left
            dattn_ref[1, rows, :] = right
            dmixed_ref[rows, :] = (times_across(left, proj[0]) + times_across(right, proj[1])).astype(LOW)
            return carry

        lax.fori_loop(0, tokens // CHUNK, leave, 0)


def middle(slots, x_in, out_grad, mixed, table, bias, proj, fc1, fc2):
    tokens = x_in.shape[0]
    tiles = tokens // CHUNK
    steps = FF // SPAN
    per_side = steps // 2
    bias1 = bias[:, 3 * D : 3 * D + FF].reshape(steps, 1, SPAN)

    def by_unit(shape, place):
        return pl.BlockSpec(shape, lambda j, slots: place(j))

    outs = (
        ((tokens, D), LOW),
        ((D, tokens), LOW),
        ((FF, tokens), LOW),
        ((2, tokens, FF // 2), LOW),
        ((2, tokens, D // 2), LOW),
        ((2, tokens, D // 2), LOW),
        ((tokens, D), LOW),
        ((tokens, D), WIDE),
        ((tiles, 8, D), WIDE),
        ((1, FF), WIDE),
    )
    out_specs = [fixed(*shape) for shape, _ in outs]
    out_specs[2] = by_unit((SPAN, tokens), lambda j: (j, 0))
    out_specs[3] = by_unit((1, tokens, SPAN), lambda j: (j // per_side, 0, j % per_side))
    out_specs[9] = by_unit((1, SPAN), lambda j: (0, j))
    return pl.pallas_call(
        middle_kernel,
        out_shape=tuple(jax.ShapeDtypeStruct(shape, dtype) for shape, dtype in outs),
        grid_spec=pltpu.PrefetchScalarGridSpec(
            num_scalar_prefetch=1,
            grid=(steps,),
            in_specs=[
                fixed(tokens, D),
                fixed(tokens, D),
                fixed(tokens, D),
                fixed(*table.shape),
                fixed(*bias.shape),
                by_unit((1, 1, SPAN), lambda j: (j, 0, 0)),
                fixed(*proj.shape),
                by_unit((1, D, SPAN), lambda j: (j // per_side, 0, j % per_side)),
                by_unit((2, SPAN, D // 2), lambda j: (0, j, 0)),
            ],
            out_specs=tuple(out_specs),
            scratch_shapes=[
                pltpu.VMEM((tokens, D), WIDE),
                pltpu.VMEM((tokens, D), LOW),
                pltpu.VMEM((2, tokens, D // 2), WIDE),
            ],
        ),
        compiler_params=pltpu.CompilerParams(
            dimension_semantics=("arbitrary",), vmem_limit_bytes=63 * 2**20
        ),
        cost_estimate=pl.CostEstimate(
            flops=4 * tokens * (D * D + 2 * D * FF),
            bytes_accessed=(D * D + 2 * D * FF) * 2 + tokens * D * 40,
            transcendentals=0,
        ),
        name="middle",
    )(slots, x_in, out_grad, mixed, table, bias, bias1, proj, fc1, fc2)


def times(left, right):
    return jnp.dot(left, right, preferred_element_type=WIDE)


def times_back(left, right):
    return lax.dot_general(left, right, (((1,), (1,)), ((), ())), preferred_element_type=WIDE)


def body(
    x_in,
    cond,
    segments,
    out_grad,
    qkv_weight,
    qkv_moment,
    qkv_average,
    proj_weight,
    proj_moment,
    proj_average,
    fc1_weight,
    fc1_moment,
    fc1_average,
    fc2_weight,
    fc2_moment,
    fc2_average,
    bias_weight,
    bias_moment,
    bias_average,
    ada_weight,
    ada_moment,
    ada_average,
    adab_weight,
    adab_moment,
    adab_average,
):
    tokens, width = x_in.shape
    row_devices = lax.axis_size(ROWS)
    devices = lax.axis_size(ALL)
    row_index = lax.axis_index(ROWS)
    images = cond.shape[0] // 2

    cond_silu, silu_back = jax.vjp(jax.nn.silu, cond.astype(WIDE))
    half_silu = lax.dynamic_index_in_dim(
        cond_silu.astype(LOW).reshape(-1, 2, width // 2), lax.axis_index("mod"), 1, False
    )
    own_bias = bias_weight.shape[0]
    bias_block = jnp.pad(bias_weight.astype(LOW), (0, 8 * LANES - own_bias)).reshape(8, LANES)
    blank = jnp.zeros((8, LANES // 2), LOW)
    ada_low = ada_weight.astype(LOW)
    adab_row = lax.dynamic_update_slice_in_dim(
        jnp.zeros((1, ada_weight.shape[1]), LOW),
        adab_weight.astype(LOW),
        row_index * adab_weight.shape[1],
        1,
    )
    ada_rows = jnp.concatenate([ada_low, adab_row])
    small_w, qkv_w, proj_w, fc1_w, table = first_gather(
        jnp.pad(ada_rows, ((0, LANES - ada_rows.shape[0]), (0, 0))),
        jnp.concatenate([half_silu, bias_block, blank], axis=1),
        qkv_weight.astype(LOW),
        proj_weight.astype(LOW),
        fc1_weight.astype(LOW),
    )
    small = small_w.reshape(2, row_devices * 8, -1)
    silu_all = jnp.concatenate([small[0, :, : width // 2], small[1, :, : width // 2]], axis=1)
    bias_all = small[:, :, width // 2 : width // 2 + LANES].reshape(2, row_devices, -1)
    bias_full = jnp.swapaxes(bias_all[:, :, :own_bias], 0, 1).reshape(1, -1).astype(WIDE)
    table = lax.dynamic_slice_in_dim(table, lax.axis_index("mod") * images, images, 1)
    table = jnp.swapaxes(table, 0, 1).reshape(images, -1)

    def joined(whole):
        return whole.reshape(2, -1, whole.shape[-1])

    qkv_low = joined(qkv_w)
    slots = segments[::CHUNK]
    joint_bias = jnp.concatenate(
        [bias_full[:, 0:width], jnp.zeros((1, width), WIDE), bias_full[:, width : 2 * width]], axis=1
    )
    def blocked(turned):
        return turned.reshape(row_devices // 4, 2, 2, -1, tokens)

    act_turned, joint_rows, mixture, mixture_turned, log_totals, proj_w, fc1_w, fc2_w = attend(
        slots,
        x_in,
        table,
        joint_bias,
        qkv_low,
        segments,
        fc2_weight.astype(LOW),
        proj_w,
        fc1_w,
    )
    (
        block_out, mlp_turned, hidden_turned, pre_halves, branch_halves, attn_halves, mixture_grad, middle_grad, sums, pre_sums,
    ) = middle(
        slots, x_in, out_grad, mixture, table, bias_full, joined(proj_w), joined(fc1_w), joined(fc2_w)
    )
    (fc1_sums, proj_sums), fc2_totals = weight_grads(
        blocked(hidden_turned),
        branch_halves,
        blocked(mlp_turned),
        pre_halves,
        blocked(mixture_turned),
        attn_halves,
    )
    joint_halves, fc2_shard, proj_shard, fc1_totals = attend_back(
        joint_rows,
        segments,
        mixture,
        log_totals,
        mixture_grad,
        fc1_sums,
        proj_sums,
        fc2_totals,
    )
    chooser = (slots[None, :] == (jnp.arange(2 * images, dtype=jnp.int32) % images)[:, None]).astype(WIDE)
    qkv_shard, fc1_shard, small_grads, x_grad = last_scatter(
        slots,
        blocked(act_turned),
        joint_halves,
        x_in,
        middle_grad,
        table,
        qkv_low,
        sums,
        pre_sums,
        chooser,
        fc1_totals,
    )
    small_grads = small_grads.reshape(2, row_devices, 16, -1)
    mod_grads = lax.dynamic_slice_in_dim(small_grads, lax.axis_index("mod") * images, images, 2)
    mod_grad_all = jnp.swapaxes(mod_grads, 0, 1).reshape(2 * row_devices * images, -1)
    bias_grads = small_grads[:, :, 8:11].reshape(devices, -1)
    own_biases = lax.dynamic_slice_in_dim(bias_grads, lax.axis_index(ALL) * own_bias, own_bias, 1)
    bias_shard = jnp.sum(own_biases.astype(WIDE), axis=0)
    own_rows = ada_weight.shape[0]
    own_silu = lax.dynamic_slice_in_dim(silu_all, row_index * own_rows, own_rows, 1)
    ada_shard = jnp.einsum("ic,io->co", own_silu, mod_grad_all, preferred_element_type=WIDE)
    own_columns = adab_weight.shape[1]
    adab_shard = jnp.sum(
        lax.dynamic_slice_in_dim(mod_grad_all, row_index * own_columns, own_columns, 1).astype(WIDE),
        axis=0,
    )
    silu_part = times_back(mod_grad_all, ada_low)
    row_images = 2 * images
    silu_part = jnp.broadcast_to(
        silu_part.reshape(row_devices, 1, row_images, -1), (row_devices, 2, row_images, own_rows)
    ).reshape(devices * row_images, own_rows)
    silu_part = lax.all_to_all(silu_part, ALL, split_axis=0, concat_axis=1, tiled=True)
    silu_grad = jnp.sum(silu_part.reshape(row_images, row_devices, 2, own_rows), axis=2)
    cond_grad = silu_back(silu_grad.reshape(row_images, -1))[0]

    rates = step_rates(tokens * devices)
    states_out = []
    states_out.extend(nesterov(qkv_weight, qkv_moment, qkv_average, qkv_shard, rates[0]))
    states_out.extend(nesterov(proj_weight, proj_moment, proj_average, proj_shard, rates[1]))
    states_out.extend(nesterov(fc1_weight, fc1_moment, fc1_average, fc1_shard, rates[2]))
    states_out.extend(nesterov(fc2_weight, fc2_moment, fc2_average, fc2_shard, rates[3]))
    states_out.extend(nesterov(bias_weight, bias_moment, bias_average, bias_shard, rates[4]))
    states_out.extend(nesterov(ada_weight, ada_moment, ada_average, ada_shard, rates[5]))
    states_out.extend(
        nesterov(adab_weight, adab_moment, adab_average, adab_shard.reshape(1, -1), rates[6])
    )
    return (block_out, x_grad, cond_grad) + tuple(states_out)


def solution(mesh):
    far = mesh.shape["dp"] // 4
    fine = Mesh(mesh.devices.reshape(far, 2, 2, mesh.shape["mod"]), ALL)
    tokens = P(ALL, None)
    images = P(ROWS, None)
    trunk = P(ROWS, "mod")
    bias = P(ALL)
    adab = P("mod", ROWS)
    states = (trunk,) * 12 + (bias,) * 3 + (trunk,) * 3 + (adab,) * 3
    return jax.shard_map(
        body,
        mesh=fine,
        in_specs=(tokens, images, bias, tokens) + states,
        out_specs=(tokens, tokens, images) + states,
        check_vma=False,
    )
```

```python
from functools import partial

import jax
import jax.numpy as jnp
from jax import lax
from jax.experimental import pallas as pl
from jax.experimental.pallas import tpu as pltpu
from jax.sharding import Mesh
from jax.sharding import PartitionSpec as P

D = 1152
HEADS = 16
HEAD = 72
FF = 4608
LANES = 128
CHUNK = 256

ROWS = ("far", "near", "core")
ALL = ("far", "near", "core", "mod")
LOW = jnp.bfloat16
WIDE = jnp.float32
LOG2E = 1.4426950408889634
NEG = -1e30
MESH = pl.DeviceIdType.MESH
VMEM = pl.BlockSpec(memory_space=pltpu.VMEM)
ANY = pl.BlockSpec(memory_space=pl.ANY)

EPS = 1e-06
MOMENTUM = 0.9
DECAY = 0.5


def step_rates(tokens_all):
    base_rate = tokens_all ** (-0.5)
    return (
        2.5 * D ** (-0.5) * base_rate,
        3.0 * D ** (-0.5) * base_rate,
        3.3 * D ** (-0.5) * base_rate,
        2.8 * FF ** (-0.5) * base_rate,
        0.5 * base_rate,
        2.0 * D ** (-0.5) * base_rate,
        0.3 * base_rate,
    )


def nesterov(weight, moment, average, gradient, rate):
    moment = MOMENTUM * moment + gradient
    weight = weight - rate * (gradient + MOMENTUM * moment)
    average = DECAY * average + (1.0 - DECAY) * weight
    return (weight, moment, average)


def places():
    return {name: lax.axis_index(name) for name in ALL}


def greet():
    here = places()
    count = lax.axis_size("far")
    others = [dict(far=lax.rem(here["far"] + d, count)) for d in range(1, count)]
    others += [{name: 1 - here[name]} for name in ("near", "core", "mod")]
    barrier = pltpu.get_barrier_semaphore()
    for other in others:
        pl.semaphore_signal(barrier, inc=1, device_id=other, device_id_type=MESH)
    pl.semaphore_wait(barrier, len(others))


def remote(source, target, sends, receives, slot, other):
    return pltpu.make_async_remote_copy(
        src_ref=source,
        dst_ref=target,
        send_sem=sends.at[slot],
        recv_sem=receives.at[slot],
        device_id=other,
        device_id_type=MESH,
    )


def messages(count):
    return count - 1 + 8


class Gather:
    def __init__(self, whole, sends, receives):
        self.whole, self.sends, self.receives = whole, sends, receives
        self.here = places()
        self.count = lax.axis_size("far")
        rows = whole.shape[4]
        self.rows = rows
        self.split = rows if rows % 8 else 8 * ((rows // 8 + 1) // 2)

    def _block(self, far):
        return self.whole.at[self.here["mod"], far, self.here["near"], self.here["core"]]

    def _far(self, shard, distance):
        far = self.here["far"]
        other = dict(far=lax.rem(far + distance, self.count))
        return remote(shard, self._block(far), self.sends, self.receives, distance - 1, other)

    def _far_came(self, shard, distance):
        origin = lax.rem(self.here["far"] + self.count - distance, self.count)
        return remote(
            shard, self._block(origin), self.sends, self.receives, distance - 1, dict(far=origin)
        )

    def start_far(self, shard, local):
        pltpu.make_async_copy(shard, self._block(self.here["far"]), local).start()
        for distance in range(1, self.count):
            self._far(shard, distance).start()

    def finish_far(self, shard, local):
        pltpu.make_async_copy(shard, self._block(self.here["far"]), local).wait()
        for distance in range(1, self.count):
            self._far(shard, distance).wait_send()
            self._far_came(shard, distance).wait_recv()

    def _quad(self, flips, first, size):
        near, core, mod = (
            1 - self.here[name] if name in flips else self.here[name] for name in ("near", "core", "mod")
        )
        return self.whole.at[mod, :, near, core, pl.ds(first, size)]

    def _step(self, name):
        head, rest = (0, self.split), (self.split, self.rows - self.split)
        full = (0, self.rows)
        return {
            "near": ((), "near", full, 0),
            "mod": ((), "mod", full, 1),
            "near_mod": (("near",), "mod", head, 2),
            "mod_near": (("mod",), "near", rest, 3),
            "core": ((), "core", full, 4),
            "near_core": (("near",), "core", full, 5),
            "mod_core": (("mod",), "core", full, 6),
            "both_core": (("near", "mod"), "core", full, 7),
        }[name]

    def _copy(self, name, incoming):
        flips, axis, span, slot = self._step(name)
        if span[1] == 0:
            return None
        quad = self._quad(flips + (axis,) if incoming else flips, *span)
        other = {axis: 1 - self.here[axis]}
        return remote(quad, quad, self.sends, self.receives, self.count - 1 + slot, other)

    def start(self, *names):
        for name in names:
            copy = self._copy(name, False)
            if copy is not None:
                copy.start()

    def receive(self, *names):
        for name in names:
            copy = self._copy(name, True)
            if copy is not None:
                copy.wait_recv()

    def spread(self):
        self.start("near", "mod", "core")

    def cross(self):
        self.receive("near")
        self.start("near_mod", "near_core")
        self.receive("mod")
        self.start("mod_near", "mod_core")

    def close(self):
        self.receive("near_mod", "mod_near")
        self.start("both_core")

    def end(self):
        self.receive("core", "near_core", "mod_core", "both_core")
        for name in (
            "near", "mod", "near_mod", "mod_near", "core", "near_core", "mod_core", "both_core",
        ):
            copy = self._copy(name, False)
            if copy is not None:
                copy.wait_send()


def gather_scratch(weights, locals_):
    count = lax.axis_size("far")
    shapes = [pltpu.SemaphoreType.DMA((messages(count),))] * (2 * weights)
    return shapes + [pltpu.SemaphoreType.DMA((locals_,))]


def whole_shape(shard):
    return jax.ShapeDtypeStruct((2, lax.axis_size("far"), 2, 2) + shard.shape, LOW)


def modulate(small_w, ada, table, local, small, partials, came_core, came_near, came_far, own, sends, receives):
    here = places()
    count = lax.axis_size("far")
    far, near, core, mod = (here[name] for name in ALL)
    row_devices = 4 * count
    rows = D // row_devices
    fetch = pltpu.make_async_copy(small_w, small, local)
    fetch.start()
    fetch.wait()
    device = (far * 2 + near) * 2 + core
    half = lax.div(device, row_devices // 2)
    first = lax.rem(device, row_devices // 2) * rows
    width = small.shape[-1]
    images = small.shape[-2]
    row = lax.broadcasted_iota(jnp.int32, (width, LANES), 0)
    column = lax.broadcasted_iota(jnp.int32, (width, LANES), 1)
    select = jnp.where(jnp.logical_and(row == first + column, column < rows), 1.0, 0.0).astype(LOW)
    for at in range(count):
        silu = small[half, at].reshape(4 * images, width).astype(WIDE).astype(LOW)
        mine = times(silu, select)
        mine = jnp.where(lanes(mine.shape) == rows, 1.0, mine).astype(LOW)
        partials[at] = times(mine, ada[...]).reshape(2, 2, images, -1)

    def move(source, target, slot, other):
        return remote(source, target, sends, receives, slot, other)

    to_core = move(partials.at[:, :, 1 - core], came_core, 0, dict(core=1 - core))
    to_core.start()
    to_core.wait()
    for at in range(count):
        partials[at, :, core] = partials[at, :, core] + came_core[at]
    to_near = move(partials.at[:, 1 - near, core], came_near, 1, dict(near=1 - near))
    to_near.start()
    yield
    to_near.wait()
    for at in range(count):
        partials[at, near, core] = partials[at, near, core] + came_near[at]
    copies = []
    for distance in range(1, count):
        target = lax.rem(far + distance, count)
        copies.append(
            move(partials.at[target, near, core], came_far.at[distance - 1], 2 + distance, dict(far=target))
        )
        copies[-1].start()
    yield
    total = partials[far, near, core]
    for distance, copy in enumerate(copies):
        copy.wait()
        total = total + came_far[distance]
    own[...] = total.astype(LOW).astype(WIDE)
    keep = pltpu.make_async_copy(own, table.at[mod], local)
    keep.start()
    to_mod = move(own, table.at[mod], 2, dict(mod=1 - mod))
    to_mod.start()
    yield
    keep.wait()
    to_mod.wait_send()
    move(own, table.at[1 - mod], 2, dict(mod=1 - mod)).wait_recv()


def first_kernel(*refs):
    small_s, qkv_s, proj_s, fc1_s, ada = refs[:5]
    table = refs[9]
    gather_sems, (local, *parts) = refs[10:18], refs[18:]
    small, qkv, proj, fc1 = (
        Gather(w, s, r) for w, s, r in zip(refs[5:9], gather_sems[0::2], gather_sems[1::2])
    )
    greet()
    small.start_far(small_s, local.at[3])
    qkv.start_far(qkv_s, local.at[0])
    small.finish_far(small_s, local.at[3])
    small.spread()
    small.cross()
    small.close()
    small.end()
    stages = modulate(small.whole, ada, table, local.at[3], *parts)
    next(stages)
    qkv.finish_far(qkv_s, local.at[0])
    qkv.spread()
    next(stages)
    proj.start_far(proj_s, local.at[1])
    fc1.start_far(fc1_s, local.at[2])
    next(stages)
    qkv.cross()
    qkv.close()
    qkv.end()
    next(stages, None)
    proj.finish_far(proj_s, local.at[1])
    fc1.finish_far(fc1_s, local.at[2])


def first_gather(ada, *shards):
    count = lax.axis_size("far")
    small = whole_shape(shards[0])
    images = small.shape[4]
    columns = ada.shape[1]
    return pl.pallas_call(
        first_kernel,
        out_shape=tuple(whole_shape(shard) for shard in shards)
        + (jax.ShapeDtypeStruct((2, images, columns), WIDE),),
        in_specs=[VMEM] * 5,
        out_specs=(ANY,) * 5,
        scratch_shapes=gather_scratch(4, 4)
        + [
            pltpu.VMEM(small.shape, LOW),
            pltpu.VMEM((count, 2, 2, images, columns), WIDE),
            pltpu.VMEM((count, 2, images, columns), WIDE),
            pltpu.VMEM((count, images, columns), WIDE),
            pltpu.VMEM((count - 1, images, columns), WIDE),
            pltpu.VMEM((images, columns), WIDE),
            pltpu.SemaphoreType.DMA((count + 2,)),
            pltpu.SemaphoreType.DMA((count + 2,)),
        ],
        compiler_params=pltpu.CompilerParams(
            collective_id=0, has_side_effects=True, vmem_limit_bytes=60 * 2**20
        ),
        name="first_gather",
    )(*shards, ada)


def lanes(shape): return lax.broadcasted_iota(jnp.int32, shape, 1)

def seg_codes(seg, n):
    lane = lanes((n, LANES))
    code = lane - HEAD
    inside = jnp.logical_and(code >= 0, code < 4)
    same = code == seg
    q = jnp.where(jnp.logical_and(inside, same), 1.0, 0.0)
    k = jnp.where(jnp.logical_and(inside, jnp.logical_not(same)), NEG, 0.0)
    return q, k

def head_of(wide_rows, start):
    return wide_rows[:, start:start+HEAD]

def pad_head(part, aug):
    n = part.shape[0]
    full = jnp.concatenate([part, jnp.zeros((n, LANES-HEAD), part.dtype)], axis=1)
    return jnp.where(lanes((n,LANES)) < HEAD, full, aug)

def split3(v):
    hi = v.astype(LOW).astype(WIDE)
    mid = (v - hi).astype(LOW).astype(WIDE)
    lo = v - hi - mid
    return hi, mid, lo


def attend_kernel(*refs):
    slots, x_ref, table, bias, weight, seg_ref, fc2_s = refs[:7]
    act_turned, mixed_ref, turned_ref = refs[9:12]
    saved, (proj_w, fc1_w, fc2_w) = refs[12:16], refs[16:19]
    heads, (*sems, local, save_sems) = refs[19:23], refs[23:]
    qh, kh, vh, oh = heads
    proj, fc1, fc2 = (
        Gather(w, s, r) for w, s, r in zip((proj_w, fc1_w, fc2_w), sems[0::2], sems[1::2])
    )
    greet()
    fc2.start_far(fc2_s, local.at[0])
    proj.spread()
    fc1.spread()

    T = x_ref.shape[0]

    def fill(i, carry):
        rows = pl.ds(pl.multiple_of(i * CHUNK, CHUNK), CHUNK)
        slot = slots[i]
        h1, _ = normed(x_ref[rows, :].astype(WIDE))
        act = (h1 * (1.0 + row_of(table, slot, 1)) + row_of(table, slot, 0)).astype(LOW)
        act_turned[:, rows] = act.T
        joint = jnp.concatenate([times(act, weight[0]), times(act, weight[1])], axis=1)
        joint = (joint + bias[...]).astype(LOW)
        lane = lanes((CHUNK, LANES))
        qc, kc = seg_codes(seg_ref[rows, :], CHUNK)
        qc = qc.astype(LOW)
        kc = jnp.where(jnp.logical_and(lane >= HEAD + 4, lane < HEAD + 7), 1.0, kc).astype(LOW)
        ones = jnp.where(jnp.logical_and(lane >= HEAD, lane < HEAD+3), 1.0, 0.0).astype(LOW)
        for h in range(HEADS):
            qh[h, rows, :] = pad_head(joint[:, h*HEAD:(h+1)*HEAD], qc)
            kh[h, rows, :] = pad_head(joint[:, D+h*HEAD:D+(h+1)*HEAD], kc)
            vh[h, rows, :] = pad_head(joint[:, 2*D+h*HEAD:2*D+(h+1)*HEAD], ones)
        pl.when(i == 2)(proj.cross)
        return carry
    lax.fori_loop(0, T//CHUNK, fill, 0)

    def save(number):
        return pltpu.make_async_copy(heads[number], saved[number], save_sems.at[number])

    save(1).start()
    save(2).start()
    def head(h, carry):
        k = kh[h]; v = vh[h]
        for i in range(T//CHUNK):
            rows = pl.ds(i*CHUNK, CHUNK)
            q = qh[h, rows, :]
            s = lax.dot_general(q, k, (((1,),(1,)),((),())), preferred_element_type=WIDE)
            m = jnp.max(s, axis=1, keepdims=True)
            p = jnp.exp2((s - m)*(HEAD**-0.5*LOG2E)).astype(LOW)
            o = jnp.dot(p, v, preferred_element_type=WIDE)
            l = o[:, HEAD:HEAD+1]
            oh[h, rows, :] = (o / l).astype(LOW)
            hi, mid, lo = split3(-(m + jnp.log(l) * HEAD**0.5))
            lane = lanes((CHUNK, LANES))
            q = jnp.where(lane == HEAD + 4, hi.astype(LOW), q)
            q = jnp.where(lane == HEAD + 5, mid.astype(LOW), q)
            qh[h, rows, :] = jnp.where(lane == HEAD + 6, lo.astype(LOW), q)
        tasks = {
            3: lambda: (fc2.finish_far(fc2_s, local.at[0]), fc2.spread()),
            6: fc1.cross,
            8: proj.close,
            10: proj.end,
        }
        for at, task in tasks.items():

            @pl.when(h == at)
            def _(task=task):
                task()

        return carry
    lax.fori_loop(0, HEADS, head, 0)
    save(0).start()
    save(3).start()

    def drain(i, carry):
        rows = pl.ds(pl.multiple_of(i*CHUNK, CHUNK), CHUNK)
        mixed = jnp.concatenate([oh[h, rows, :][:, :HEAD] for h in range(HEADS)], axis=1)
        mixed_ref[rows, :] = mixed
        turned_ref[:, rows] = mixed.T
        return carry
    lax.fori_loop(0, T//CHUNK, drain, 0)
    fc2.cross()
    fc1.close()
    fc1.end()
    fc2.close()
    fc2.end()
    for number in range(4):
        save(number).wait()


def attend(slots, x_in, table, bias, weight, segments, fc2_s, proj_w, fc1_w):
    tokens = x_in.shape[0]
    wide = HEADS * HEAD
    heads = (HEADS, tokens, LANES)
    out = pl.pallas_call(
        attend_kernel,
        out_shape=(
            jax.ShapeDtypeStruct((wide, tokens), LOW),
            jax.ShapeDtypeStruct((tokens, wide), LOW),
            jax.ShapeDtypeStruct((wide, tokens), LOW),
        )
        + (jax.ShapeDtypeStruct(heads, LOW),) * 4
        + (
            jax.ShapeDtypeStruct(proj_w.shape, LOW),
            jax.ShapeDtypeStruct(fc1_w.shape, LOW),
            whole_shape(fc2_s),
        ),
        in_specs=[pl.BlockSpec(memory_space=pltpu.SMEM)] + [VMEM] * 6 + [ANY] * 2,
        out_specs=(VMEM,) * 3 + (ANY,) * 7,
        scratch_shapes=[pltpu.VMEM(heads, LOW)] * 4
        + gather_scratch(3, 1)
        + [pltpu.SemaphoreType.DMA((4,))],
        input_output_aliases={7: 7, 8: 8},
        compiler_params=pltpu.CompilerParams(
            collective_id=1, has_side_effects=True, vmem_limit_bytes=60 * 2**20
        ),
        name="attend",
    )(slots, x_in, table, bias, weight, segments.reshape(tokens, 1), fc2_s, proj_w, fc1_w)
    return out[0], out[1], out[2], out[3:7], out[7:]


def row_spans(rows):
    first = rows if rows % 8 else 8 * ((rows // 8 + 1) // 2)
    return [(0, first)] + ([(first, rows - first)] if first < rows else [])


class Reduce:
    def __init__(self, part, span, first, came, joint, total, base, sems, loads=False):
        self.part, self.span, self.first = part, span, first
        self.second = "near" if first == "mod" else "mod"
        self.came_both, self.came_first, self.came_second, self.came_far = came
        self.joint, self.total_, self.base = joint, total, base
        self.sends, self.receives, self.locals_ = sems
        self.loads = loads
        self.here = places()
        self.count = lax.axis_size("far")

    def _swap(self, source, target, slot, axis):
        return remote(source, target, self.sends, self.receives, slot, {axis: 1 - self.here[axis]})

    def _both(self):
        return self._swap(self.part("near", "mod"), self.came_both, 0, self.first)

    def _first(self):
        return self._swap(self.part(self.first), self.came_first, 1, self.first)

    def _second(self):
        return self._swap(self.joint, self.came_second, 2, self.second)

    def _load(self, number):
        source, target = ((self.part(self.second), self.joint), (self.part(), self.total_))[number]
        return pltpu.make_async_copy(source, target, self.locals_.at[number])

    def _far(self, distance):
        target = lax.rem(self.here["far"] + distance, self.count)
        return remote(
            self.total_.at[target],
            self.came_far.at[distance - 1],
            self.sends,
            self.receives,
            2 + distance,
            dict(far=target),
        )

    def start(self):
        self._both().start()
        self._first().start()
        if self.loads:
            self._load(0).start()
            self._load(1).start()

    def merge(self):
        if self.loads:
            self._load(0).wait()
        self._both().wait_recv()

        def add(at, carry):
            self.joint[at] = (self.joint[at].astype(WIDE) + self.came_both[at].astype(WIDE)).astype(LOW)
            return carry

        lax.fori_loop(0, self.count, add, 0)
        self._second().start()

    def total(self):
        if self.loads:
            self._load(1).wait()
        self._first().wait_recv()
        self._second().wait_recv()

        def add(at, carry):
            self.total_[at] = (
                self.base[at].astype(WIDE)
                + self.came_first[at].astype(WIDE)
                + self.came_second[at].astype(WIDE)
            ).astype(LOW)
            return carry

        lax.fori_loop(0, self.count, add, 0)
        self._both().wait_send()
        self._first().wait_send()
        self._second().wait_send()

    def early(self):
        second = self.part(self.second)
        self._both().wait_recv()
        self._first().wait_recv()

        def add(at, carry):
            self.joint[at] = (second[at].astype(WIDE) + self.came_both[at].astype(WIDE)).astype(LOW)
            self.total_[at] = (self.base[at].astype(WIDE) + self.came_first[at].astype(WIDE)).astype(LOW)
            return carry

        lax.fori_loop(0, self.count, add, 0)
        self._both().wait_send()
        self._first().wait_send()

    def _load_base(self):
        return pltpu.make_async_copy(self.base, self.total_, self.locals_.at[1])

    def late_start(self):
        self._load_base().start()
        self._second().start()

    def late_total(self):
        self._load_base().wait()
        self._second().wait_recv()

        def add(at, carry):
            self.total_[at] = (self.total_[at].astype(WIDE) + self.came_second[at].astype(WIDE)).astype(LOW)
            return carry

        lax.fori_loop(0, self.count, add, 0)
        self._second().wait_send()

    def start_far(self):
        for distance in range(1, self.count):
            self._far(distance).start()

    def final(self, out):
        value = self.total_[self.here["far"]].astype(WIDE)
        for distance in range(1, self.count):
            self._far(distance).wait_recv()
            value = value + self.came_far[distance - 1].astype(WIDE)
        out[pl.ds(*self.span), :] = value
        for distance in range(1, self.count):
            self._far(distance).wait_send()


ORDERS = ("mod", "near")


def run(parts, *names):
    for part in parts:
        for name in names:
            getattr(part, name)()


def span_part(sums, span):
    def part(*flips):
        near, mod = (
            1 - lax.axis_index(name) if name in flips else lax.axis_index(name) for name in ("near", "mod")
        )
        return sums.at[mod, near, :, pl.ds(*span)]

    return part


def take(scratch, number):
    return scratch[:number], scratch[number:]


def came_scratch(count, span, columns, far=True):
    block = (count, span[1], columns)
    shapes = [pltpu.VMEM(block, LOW)] * 3
    return shapes + ([pltpu.VMEM((count - 1,) + block[1:], LOW)] if far else [])


def sem_scratch(count):
    return [pltpu.SemaphoreType.DMA((count + 2,))] * 2 + [pltpu.SemaphoreType.DMA((2,))]


def loaded_scratch(shape, total=True):
    count, rows, columns = shape[2:]
    shapes = []
    for span in row_spans(rows):
        shapes += came_scratch(count, span, columns, total)
        shapes += [pltpu.VMEM((count, span[1], columns), LOW)] * (2 if total else 1)
        shapes += sem_scratch(count)
    return shapes


def loaded_reduces(sums, scratch, totals=None):
    reduces = []
    for number, span in enumerate(row_spans(sums.shape[3])):
        came, scratch = take(scratch, 4 if totals is None else 3)
        came = list(came) + [None] * (4 - len(came))
        (joint,), scratch = take(scratch, 1)
        if totals is None:
            (total,), scratch = take(scratch, 1)
        else:
            total = totals[number]
        sems, scratch = take(scratch, 3)
        reduces.append(
            Reduce(span_part(sums, span), span, ORDERS[number], came, joint, total, total, sems, True)
        )
    return reduces, scratch


def resident_scratch(shape, far=True):
    count, rows, columns = shape[2:]
    shapes = []
    for span in row_spans(rows):
        shapes += came_scratch(count, span, columns, far) + sem_scratch(count)
    return shapes


def resident_reduces(sums, scratch, totals=None, joints=None):
    reduces = []
    for number, span in enumerate(row_spans(sums.shape[3])):
        came, scratch = take(scratch, 4 if totals is None else 3 if joints is None else 2)
        sems, scratch = take(scratch, 3)
        part = span_part(sums, span)
        order = ORDERS[number]
        own = part()
        total = own if totals is None else totals[number]
        came = list(came) + [None] * (4 - len(came))
        joint = part("near" if order == "mod" else "mod") if joints is None else joints[number]
        reduces.append(Reduce(part, span, order, came, joint, total, own, sems))
    return reduces, scratch


def early_scratch(shape):
    count, rows, columns = shape[2:]
    shapes = []
    for span in row_spans(rows):
        shapes += [pltpu.VMEM((count, span[1], columns), LOW)] * 2 + sem_scratch(count)
    return shapes


def late_scratch(bases):
    shapes = []
    for base in bases:
        far = pltpu.VMEM((base.shape[0] - 1,) + base.shape[1:], LOW)
        shapes += [pltpu.VMEM(base.shape, LOW)] * 2 + [far] + sem_scratch(base.shape[0])
    return shapes


def late_reduces(joints, bases, rows, scratch):
    reduces = []
    for number, span in enumerate(row_spans(rows)):
        (came, total, came_far), scratch = take(scratch, 3)
        sems, scratch = take(scratch, 3)
        came = (None, None, came, came_far)
        reduces.append(
            Reduce(None, span, ORDERS[number], came, joints[number], total, bases[number], sems)
        )
    return reduces, scratch


def far_scratch(totals):
    shapes = []
    for total in totals:
        count = total.shape[0]
        shapes += [pltpu.VMEM((count - 1,) + total.shape[1:], LOW)] + sem_scratch(count)[:2]
    return shapes


def far_reduces(totals, rows, scratch):
    reduces = []
    for total, span in zip(totals, row_spans(rows)):
        (came, sends, receives), scratch = take(scratch, 3)
        came = (None, None, None, came)
        reduces.append(Reduce(None, span, "mod", came, None, total, total, (sends, receives, None)))
    return reduces, scratch


class Product:
    def __init__(self, left, right, scratch):
        self.left, self.right = left, right
        self.rows_, self.sums, self.came, self.loads, self.sends, self.receives = scratch
        self.core = lax.axis_index("core")

    @staticmethod
    def scratch(count, rows, tokens, columns):
        sums = pltpu.VMEM((2, 2, count, rows, columns), LOW)
        sems = [pltpu.SemaphoreType.DMA((4,))] * 3
        return [pltpu.VMEM((2, count, rows, tokens), LOW), sums, sums] + sems

    def _load(self, near, own):
        core = self.core if own else 1 - self.core
        return pltpu.make_async_copy(
            self.left.at[:, near, core], self.rows_.at[near], self.loads.at[2 * own + near]
        )

    def load(self):
        for near in (0, 1):
            self._load(near, 0).start()

    def _copy(self, mod, near):
        return remote(
            self.sums.at[mod, near],
            self.came.at[mod, near],
            self.sends,
            self.receives,
            2 * mod + near,
            dict(core=1 - self.core),
        )

    def _blocks(self, near, own, store):
        count, rows, tokens = self.rows_.shape[1:]
        columns = self.right.shape[2]
        self._load(near, own).wait()
        left = self.rows_[near].reshape(count * rows, tokens)
        width = columns if columns <= 1024 else columns // 2
        width = width if width % LANES == 0 else columns
        for mod in (0, 1):
            for at in range(0, columns, width):
                product = times(left, self.right[mod, :, at : at + width])
                store(mod, at, width, product.reshape(count, rows, width))

    def send(self):
        for near in (0, 1):

            def store(mod, at, width, product, near=near):
                self.sums[mod, near, :, :, at : at + width] = product.astype(LOW)

            self._blocks(near, 0, store)
            self._load(near, 1).start()
            for mod in (0, 1):
                self._copy(mod, near).start()

    def sum(self):
        for near in (0, 1):
            for mod in (0, 1):
                self._copy(mod, near).wait_send()
                self._copy(mod, near).wait_recv()

            def store(mod, at, width, product, near=near):
                came = self.came[mod, near, :, :, at : at + width]
                self.sums[mod, near, :, :, at : at + width] = (product + came.astype(WIDE)).astype(LOW)

            self._blocks(near, 1, store)


def total_shapes(count, rows, columns):
    return [jax.ShapeDtypeStruct((count, span[1], columns), LOW) for span in row_spans(rows)]


def weight_kernel(*refs, modes, spans):
    sides, refs = take(refs, 2 * len(modes))
    outs = []
    for mode, count in zip(modes, spans):
        used, refs = take(refs, {"whole": count, "early": 2 * count, "chip": 1}[mode])
        outs.append(used)
    scratch = refs
    products, reduces = [], []
    for number in range(len(modes)):
        used, scratch = take(scratch, 6)
        products.append(Product(sides[2 * number], sides[2 * number + 1], used))
    for mode, count, product, out in zip(modes, spans, products, outs):
        parts = []
        if mode == "whole":
            parts, scratch = resident_reduces(product.sums, scratch, out)
        elif mode == "early":
            parts, scratch = resident_reduces(product.sums, scratch, out[count:], out[:count])
        reduces.append(parts)
    (out_sem,) = scratch
    products[0].load()
    greet()
    copies = []
    for number, product in enumerate(products):
        before = number and modes[number - 1] == "whole"
        product.send()
        if before:
            run(reduces[number - 1], "merge")
        if number + 1 < len(products):
            products[number + 1].load()
        product.sum()
        run(reduces[number], "start") if reduces[number] else None
        if before:
            run(reduces[number - 1], "total")
        if modes[number] == "chip":
            copies.append(pltpu.make_async_copy(product.sums, outs[number][0], out_sem.at[0]))
            copies[-1].start()
    for number, mode in enumerate(modes):
        if mode == "early":
            run(reduces[number], "early")
    for copy in copies:
        copy.wait()


def weight_call(pairs, modes, number):
    count = pairs[0][0].shape[0]
    tokens = pairs[0][0].shape[4]
    products, sums, shapes, specs, spans = [], [], [], [], []
    for (left, right), mode in zip(pairs, modes):
        rows, columns = left.shape[3], right.shape[2]
        shape = (2, 2, count, rows, columns)
        products += Product.scratch(count, rows, tokens, columns)
        totals = total_shapes(count, rows, columns)
        spans.append(len(totals))
        if mode == "chip":
            shapes.append(jax.ShapeDtypeStruct(shape, LOW))
            specs.append(ANY)
        else:
            sums += resident_scratch(shape, False) if mode == "whole" else early_scratch(shape)
            outs = totals * (1 if mode == "whole" else 2)
            shapes += outs
            specs += [VMEM] * len(outs)
    out = pl.pallas_call(
        partial(weight_kernel, modes=modes, spans=tuple(spans)),
        out_shape=tuple(shapes),
        in_specs=[ANY, VMEM] * len(pairs),
        out_specs=tuple(specs),
        scratch_shapes=products + sums + [pltpu.SemaphoreType.DMA((1,))],
        compiler_params=pltpu.CompilerParams(
            collective_id=number, has_side_effects=True, vmem_limit_bytes=63 * 2**20
        ),
        name="weight_grads",
    )(*[side for pair in pairs for side in pair])
    return out, spans


def weight_grads(hidden, branch, mlp, pre, mixed, attn):
    proj, fc2, fc1 = (mixed, attn), (hidden, branch), (mlp, pre)
    if mlp.shape[3] % 8 == 0:
        out, spans = weight_call([proj, fc2, fc1], ("whole", "early", "chip"), 4)
        first, second = spans[0], spans[0] + spans[1]
        return out[:first], out[first:second], out[second:-1], out[-1]
    early, spans = weight_call([fc2], ("early",), 4)
    rest, _ = weight_call([proj, fc1], ("whole", "chip"), 5)
    return rest[:-1], early[: spans[0]], early[spans[0] :], rest[-1]


def tile_sums_by_slot(chooser, sums):
    total = None
    for at, row in enumerate(sums):
        part = chooser[:, at : at + 1] * row
        total = part if total is None else total + part
    return total


def last_kernel(*refs, spans):
    slots, act, joint, x_ref, dx1_ref, table, weight, mid_sums, pre_sums, chooser = refs[:10]
    totals, refs = take(refs[10:], spans)
    qkv_out, fc1_out, small_w, x_grad_ref, *scratch = refs
    qkv_scratch, scratch = take(scratch, 6)
    qkv = Product(act, joint, qkv_scratch)
    qkv_sum, scratch = resident_reduces(qkv.sums, scratch)
    fc1_sum, scratch = far_reduces(totals, fc1_out.shape[0], scratch)
    small_sends, small_receives, local, first_sums, joint_sums, small_s = scratch
    small = Gather(small_w, small_sends, small_receives)
    tiles = x_ref.shape[0] // CHUNK
    qkv.load()
    greet()
    run(fc1_sum, "start_far")
    qkv.send()
    qkv.sum()
    run(qkv_sum, "start")

    def back(at, carry):
        rows = pl.ds(pl.multiple_of(at * CHUNK, CHUNK), CHUNK)
        dact = times_across(joint[0, rows, :], weight[0]) + times_across(joint[1, rows, :], weight[1])
        h1, inverse = normed(x_ref[rows, :].astype(WIDE))
        first_sums[at, 0:1, :] = column_sums(dact)
        first_sums[at, 1:2, :] = column_sums(dact * h1)
        dh1 = dact * (1.0 + row_of(table, slots[at], 1))
        x_grad_ref[rows, :] = dx1_ref[rows, :] + inverse * (
            dh1
            - jnp.mean(dh1, axis=-1, keepdims=True)
            - h1 * jnp.mean(dh1 * h1, axis=-1, keepdims=True)
        )
        for side in range(2):
            joint_sums[side : side + 1, :] += column_sums(joint[side, rows, :].astype(WIDE))

        @pl.when(at == tiles // 2 - 1)
        def _():
            run(qkv_sum, "merge")

        return carry

    joint_sums[...] = jnp.zeros_like(joint_sums)
    lax.fori_loop(0, tiles, back, 0)
    choose = chooser[...]
    upper = lax.broadcasted_iota(jnp.int32, (choose.shape[0], D), 0) < choose.shape[0] // 2
    groups = (
        [first_sums[at, 0:1, :] for at in range(tiles)],
        [first_sums[at, 1:2, :] for at in range(tiles)],
    ) + tuple([mid_sums[at, row : row + 1, :] for at in range(tiles)] for row in range(4))
    for group in range(3):
        value = jnp.where(
            upper, tile_sums_by_slot(choose, groups[group]), tile_sums_by_slot(choose, groups[group + 3])
        )
        small_s[0:8, group * D : (group + 1) * D] = value.astype(LOW)
    pre = pre_sums[...]
    tile_rows = [column_sums(mid_sums[:, row, :]) for row in (4, 5)]
    biases = (
        (joint_sums[0:1, :D], joint_sums[1:2, D // 2 :], tile_rows[0]),
        tuple(pre[:, at * D : (at + 1) * D] for at in range(3)),
        (pre[:, 3 * D :], tile_rows[1], jnp.zeros((1, D), WIDE)),
    )
    blank = jnp.zeros((5, D), WIDE)
    for group in range(3):
        rows = jnp.concatenate([biases[row][group] for row in range(3)] + [blank], axis=0)
        small_s[8:16, group * D : (group + 1) * D] = rows.astype(LOW)
    small.start_far(small_s, local.at[0])
    small.finish_far(small_s, local.at[0])
    small.spread()
    run(qkv_sum, "total", "start_far")
    small.cross()
    small.close()
    small.end()
    for part in fc1_sum:
        part.final(fc1_out)
    for part in qkv_sum:
        part.final(qkv_out)


def last_scatter(slots, act, joint, x_in, dx1, table, weight, mid_sums, pre_sums, chooser, totals):
    count, _, _, rows, tokens = act.shape
    fc1_columns = totals[0].shape[2]
    columns = joint.shape[2]
    small_s = jax.ShapeDtypeStruct((16, 3 * D), LOW)
    return pl.pallas_call(
        partial(last_kernel, spans=len(totals)),
        out_shape=(
            jax.ShapeDtypeStruct((rows, columns), WIDE),
            jax.ShapeDtypeStruct((sum(total.shape[1] for total in totals), fc1_columns), WIDE),
            whole_shape(small_s),
            jax.ShapeDtypeStruct((tokens, D), WIDE),
        ),
        in_specs=[pl.BlockSpec(memory_space=pltpu.SMEM), ANY] + [VMEM] * (8 + len(totals)),
        out_specs=(VMEM, VMEM, ANY, VMEM),
        scratch_shapes=Product.scratch(count, rows, tokens, columns)
        + resident_scratch((2, 2, count, rows, columns))
        + far_scratch(totals)
        + gather_scratch(1, 1)
        + [
            pltpu.VMEM((tokens // CHUNK, 8, D), WIDE),
            pltpu.VMEM((2, columns), WIDE),
            pltpu.VMEM(small_s.shape, LOW),
        ],
        compiler_params=pltpu.CompilerParams(
            collective_id=3, has_side_effects=True, vmem_limit_bytes=63 * 2**20
        ),
        name="last_scatter",
    )(slots, act, joint, x_in, dx1, table, weight, mid_sums, pre_sums, chooser, *totals)


def attend_back_kernel(*refs, counts):
    up_ref, heads, fc1_sums = refs[0], refs[1:5], refs[5]
    proj_totals, refs = take(refs[6:], counts[0])
    joints, refs = take(refs, counts[1])
    bases, refs = take(refs, counts[1])
    out_ref, fc2_out, proj_out, *refs = refs
    fc1_totals, refs = take(refs, counts[2])
    qh, kh, vh, uh, oh, load_sems, leave, leave_sems, *scratch = refs
    fc1, scratch = loaded_reduces(fc1_sums, scratch, fc1_totals)
    proj, scratch = far_reduces(proj_totals, proj_out.shape[0], scratch)
    fc2, scratch = late_reduces(joints, bases, fc2_out.shape[0], scratch)
    T = up_ref.shape[0]
    chunks = T // CHUNK

    def load(number):
        return pltpu.make_async_copy(heads[number], (qh, kh, vh, oh)[number], load_sems.at[number])

    for number in (3, 0, 1, 2):
        load(number).start()
    greet()
    run(fc2, "late_start")
    run(proj, "start_far")
    run(fc1, "start")
    load(3).wait()

    def fill(i, carry):
        rows = pl.ds(pl.multiple_of(i * CHUNK, CHUNK), CHUNK)
        lane = lanes((CHUNK, LANES))
        for h in range(HEADS):
            u = pad_head(up_ref[rows, h * HEAD : (h + 1) * HEAD], jnp.zeros((CHUNK, LANES), LOW))
            delta = jnp.sum(u.astype(WIDE) * oh[h, rows, :].astype(WIDE), axis=1, keepdims=True)
            hi, mid, lo = split3(-delta)
            u = jnp.where(lane == HEAD, hi.astype(LOW), u)
            u = jnp.where(lane == HEAD + 1, mid.astype(LOW), u)
            uh[h, rows, :] = jnp.where(lane == HEAD + 2, lo.astype(LOW), u)
        return carry

    lax.fori_loop(0, chunks, fill, 0)
    for number in range(3):
        load(number).wait()
    across = (((1,), (1,)), ((), ()))
    tasks = {
        4: lambda: run(fc2, "late_total", "start_far"),
        9: lambda: run(fc1, "merge"),
    }

    def head(h, carry):
        k = kh[h]
        v = vh[h]
        kt = k.T
        dk = jnp.zeros((T, LANES), WIDE)
        dv = jnp.zeros((T, LANES), WIDE)
        for i in range(chunks):
            rows = pl.ds(i * CHUNK, CHUNK)
            q = qh[h, rows, :]
            u = uh[h, rows, :]
            s = lax.dot_general(k, q, across, preferred_element_type=WIDE)
            p = jnp.exp2(s * (HEAD**-0.5 * LOG2E))
            dp = lax.dot_general(v, u, across, preferred_element_type=WIDE)
            ds = (p * dp).astype(LOW)
            dv = dv + jnp.dot(p.astype(LOW), u, preferred_element_type=WIDE)
            dk = dk + jnp.dot(ds, q, preferred_element_type=WIDE)
            dqt = jnp.dot(kt, ds, preferred_element_type=WIDE)
            qh[h, rows, :] = (dqt.T * HEAD**-0.5).astype(LOW)
        kh[h] = (dk * HEAD**-0.5).astype(LOW)
        vh[h] = dv.astype(LOW)
        for at, task in tasks.items():

            @pl.when(h == at)
            def _(task=task):
                task()

        return carry

    lax.fori_loop(0, HEADS, head, 0)

    def store(i, side):
        rows = pl.ds(pl.multiple_of(i * CHUNK, CHUNK), CHUNK)
        return pltpu.make_async_copy(
            leave.at[side], out_ref.at[side, rows], leave_sems.at[side]
        )

    def drain(i, carry):
        rows = pl.ds(pl.multiple_of(i * CHUNK, CHUNK), CHUNK)
        parts = [g[h, rows, :][:, :HEAD] for g in (qh, kh, vh) for h in range(HEADS)]
        for side in range(2):

            @pl.when(i > 0)
            def _(side=side):
                store(i - 1, side).wait()

            own = parts[side * len(parts) // 2 : (side + 1) * len(parts) // 2]
            leave[side] = jnp.concatenate(own, axis=1)
            store(i, side).start()
        return carry

    lax.fori_loop(0, chunks, drain, 0)
    run(fc1, "total")
    for side in range(2):
        store(chunks - 1, side).wait()
    for part in fc2:
        part.final(fc2_out)
    for part in proj:
        part.final(proj_out)


def attend_back(upstream, heads, fc1_sums, proj_totals, joints, bases):
    tokens = upstream.shape[0]
    count, rows, columns = fc1_sums.shape[2:]
    totals = total_shapes(count, rows, columns)

    def shard(parts):
        return jax.ShapeDtypeStruct((sum(part.shape[1] for part in parts), parts[0].shape[2]), WIDE)

    out = pl.pallas_call(
        partial(attend_back_kernel, counts=(len(proj_totals), len(joints), len(totals))),
        out_shape=(
            jax.ShapeDtypeStruct((2, tokens, 3 * HEADS * HEAD // 2), LOW),
            shard(bases),
            shard(proj_totals),
        )
        + tuple(totals),
        in_specs=[VMEM] + [ANY] * 5 + [VMEM] * len(proj_totals) + [ANY] * (2 * len(joints)),
        out_specs=(ANY, VMEM, VMEM) + (VMEM,) * len(totals),
        scratch_shapes=[pltpu.VMEM((HEADS, tokens, LANES), LOW)] * 5
        + [pltpu.SemaphoreType.DMA((4,))]
        + [pltpu.VMEM((2, CHUNK, 3 * HEADS * HEAD // 2), LOW), pltpu.SemaphoreType.DMA((2,))]
        + loaded_scratch(fc1_sums.shape, False)
        + far_scratch(proj_totals)
        + late_scratch(bases),
        compiler_params=pltpu.CompilerParams(
            collective_id=2, has_side_effects=True, vmem_limit_bytes=63 * 2**20
        ),
        name="attend_back",
    )(upstream, *heads, fc1_sums, *proj_totals, *joints, *bases)
    return out[0], out[1], out[2], out[3:]


def normed(values):
    centre = values - jnp.mean(values, axis=-1, keepdims=True)
    inverse = lax.rsqrt(jnp.mean(centre * centre, axis=-1, keepdims=True) + EPS)
    return centre * inverse, inverse


def row_of(table, slot, group):
    return table[pl.ds(slot, 1), group * D : (group + 1) * D]


def column_sums(values):
    return jnp.sum(values, axis=0, keepdims=True)


def times_across(left, right):
    return lax.dot_general(left, right, (((1,), (1,)), ((), ())), preferred_element_type=WIDE)


def fixed(*shape):
    return pl.BlockSpec(
        shape, lambda i, slots: (0,) * len(shape), pipeline_mode=pl.Buffered(1)
    )


GELU = 0.7978845608028654
CUBIC = 0.044715
SPAN = 768
BLOCK = 512


def middle_kernel(
    slots, x_ref, g_ref, mixed_ref, table, bias, bias1, proj, fc1, fc2,
    block_ref, mlp_turned, hidden_turned, dpre_ref, dbranch_ref, dattn_ref, dmixed_ref, dx1_ref, sums_ref, dpre_sums,
    attn_out, mlp, branch,
):
    step = pl.program_id(0)
    tokens = x_ref.shape[0]

    @pl.when(step == 0)
    def _():
        def enter(tile_at, carry):
            rows = pl.ds(pl.multiple_of(tile_at * CHUNK, CHUNK), CHUNK)
            slot = slots[tile_at]
            gate1, shift2, scale2, gate2 = (row_of(table, slot, group) for group in (2, 3, 4, 5))
            mixed = mixed_ref[rows, :]
            out = jnp.concatenate([times(mixed, proj[0]), times(mixed, proj[1])], axis=1)
            out = out + bias[:, 2 * D : 3 * D]
            attn_out[rows, :] = out
            h2, _ = normed(x_ref[rows, :].astype(WIDE) + gate1 * out)
            mlp_in = (h2 * (1.0 + scale2) + shift2).astype(LOW)
            mlp[rows, :] = mlp_in
            mlp_turned[:, rows] = mlp_in.T
            dbranch = (gate2 * g_ref[rows, :].astype(WIDE)).astype(LOW)
            sums_ref[tile_at, 5:6, :] = column_sums(dbranch.astype(WIDE))
            dbranch_ref[0, rows, :] = dbranch[:, : D // 2]
            dbranch_ref[1, rows, :] = dbranch[:, D // 2 :]
            return carry

        lax.fori_loop(0, tokens // CHUNK, enter, 0)
        branch[...] = jnp.zeros_like(branch)
        dx1_ref[...] = jnp.zeros_like(dx1_ref)

    total = None
    for first in range(0, tokens, BLOCK):
        rows = slice(first, first + BLOCK)
        pre = times(mlp[rows, :], fc1[0]) + bias1[0]
        square = pre * pre
        bend = jnp.tanh(GELU * pre * (1.0 + CUBIC * square))
        rise = 0.5 * (1.0 + bend)
        hidden = (pre * rise).astype(LOW)
        hidden_turned[:, rows] = hidden.T
        for side in range(2):
            branch[side, rows] += times(hidden, fc2[side])
        slope = rise + 0.5 * GELU * pre * (1.0 - bend * bend) * (1.0 + 3.0 * CUBIC * square)
        dhidden = times_across(dbranch_ref[0, rows], fc2[0]) + times_across(dbranch_ref[1, rows], fc2[1])
        dpre = (dhidden * slope).astype(LOW)
        dpre_ref[0, rows] = dpre
        part = column_sums(dpre.astype(WIDE))
        total = part if total is None else total + part
        dx1_ref[rows, :] += times_across(dpre, fc1[0])
    dpre_sums[...] = total

    @pl.when(step == pl.num_programs(0) - 1)
    def _():
        def leave(tile_at, carry):
            rows = pl.ds(pl.multiple_of(tile_at * CHUNK, CHUNK), CHUNK)
            slot = slots[tile_at]
            gate1, scale2, gate2 = (row_of(table, slot, group) for group in (2, 4, 5))
            out = attn_out[rows, :]
            x1 = x_ref[rows, :].astype(WIDE) + gate1 * out
            h2, inverse = normed(x1)
            whole = jnp.concatenate([branch[0, rows, :], branch[1, rows, :]], axis=1) + bias[:, 3 * D + FF :]
            block_ref[rows, :] = (x1 + gate2 * whole).astype(LOW)
            g = g_ref[rows, :].astype(WIDE)
            sums_ref[tile_at, 3:4, :] = column_sums(g * whole)
            dmlp = dx1_ref[rows, :]
            sums_ref[tile_at, 1:2, :] = column_sums(dmlp)
            sums_ref[tile_at, 2:3, :] = column_sums(dmlp * h2)
            dh2 = dmlp * (1.0 + scale2)
            dx1 = g + inverse * (
                dh2
                - jnp.mean(dh2, axis=-1, keepdims=True)
                - h2 * jnp.mean(dh2 * h2, axis=-1, keepdims=True)
            )
            dx1_ref[rows, :] = dx1
            sums_ref[tile_at, 0:1, :] = column_sums(dx1 * out)
            dattn = (gate1 * dx1).astype(LOW)
            sums_ref[tile_at, 4:5, :] = column_sums(dattn.astype(WIDE))
            sums_ref[tile_at, 6:8, :] = jnp.zeros((2, D), WIDE)
            left, right = dattn[:, : D // 2], dattn[:, D // 2 :]
            dattn_ref[0, rows, :] = left
            dattn_ref[1, rows, :] = right
            dmixed_ref[rows, :] = (times_across(left, proj[0]) + times_across(right, proj[1])).astype(LOW)
            return carry

        lax.fori_loop(0, tokens // CHUNK, leave, 0)


def middle(slots, x_in, out_grad, mixed, table, bias, proj, fc1, fc2):
    tokens = x_in.shape[0]
    tiles = tokens // CHUNK
    steps = FF // SPAN
    per_side = steps // 2
    bias1 = bias[:, 3 * D : 3 * D + FF].reshape(steps, 1, SPAN)

    def by_unit(shape, place):
        return pl.BlockSpec(shape, lambda j, slots: place(j))

    outs = (
        ((tokens, D), LOW),
        ((D, tokens), LOW),
        ((FF, tokens), LOW),
        ((2, tokens, FF // 2), LOW),
        ((2, tokens, D // 2), LOW),
        ((2, tokens, D // 2), LOW),
        ((tokens, D), LOW),
        ((tokens, D), WIDE),
        ((tiles, 8, D), WIDE),
        ((1, FF), WIDE),
    )
    out_specs = [fixed(*shape) for shape, _ in outs]
    out_specs[2] = by_unit((SPAN, tokens), lambda j: (j, 0))
    out_specs[3] = by_unit((1, tokens, SPAN), lambda j: (j // per_side, 0, j % per_side))
    out_specs[9] = by_unit((1, SPAN), lambda j: (0, j))
    return pl.pallas_call(
        middle_kernel,
        out_shape=tuple(jax.ShapeDtypeStruct(shape, dtype) for shape, dtype in outs),
        grid_spec=pltpu.PrefetchScalarGridSpec(
            num_scalar_prefetch=1,
            grid=(steps,),
            in_specs=[
                fixed(tokens, D),
                fixed(tokens, D),
                fixed(tokens, D),
                fixed(*table.shape),
                fixed(*bias.shape),
                by_unit((1, 1, SPAN), lambda j: (j, 0, 0)),
                fixed(*proj.shape),
                by_unit((1, D, SPAN), lambda j: (j // per_side, 0, j % per_side)),
                by_unit((2, SPAN, D // 2), lambda j: (0, j, 0)),
            ],
            out_specs=tuple(out_specs),
            scratch_shapes=[
                pltpu.VMEM((tokens, D), WIDE),
                pltpu.VMEM((tokens, D), LOW),
                pltpu.VMEM((2, tokens, D // 2), WIDE),
            ],
        ),
        compiler_params=pltpu.CompilerParams(
            dimension_semantics=("arbitrary",), vmem_limit_bytes=63 * 2**20
        ),
        cost_estimate=pl.CostEstimate(
            flops=4 * tokens * (D * D + 2 * D * FF),
            bytes_accessed=(D * D + 2 * D * FF) * 2 + tokens * D * 40,
            transcendentals=0,
        ),
        name="middle",
    )(slots, x_in, out_grad, mixed, table, bias, bias1, proj, fc1, fc2)


def times(left, right):
    return jnp.dot(left, right, preferred_element_type=WIDE)


def times_back(left, right):
    return lax.dot_general(left, right, (((1,), (1,)), ((), ())), preferred_element_type=WIDE)


def body(
    x_in,
    cond,
    segments,
    out_grad,
    qkv_weight,
    qkv_moment,
    qkv_average,
    proj_weight,
    proj_moment,
    proj_average,
    fc1_weight,
    fc1_moment,
    fc1_average,
    fc2_weight,
    fc2_moment,
    fc2_average,
    bias_weight,
    bias_moment,
    bias_average,
    ada_weight,
    ada_moment,
    ada_average,
    adab_weight,
    adab_moment,
    adab_average,
):
    tokens, width = x_in.shape
    row_devices = lax.axis_size(ROWS)
    devices = lax.axis_size(ALL)
    row_index = lax.axis_index(ROWS)
    images = cond.shape[0] // 2

    cond_silu, silu_back = jax.vjp(jax.nn.silu, cond.astype(WIDE))
    half_silu = lax.dynamic_index_in_dim(
        cond_silu.astype(LOW).reshape(-1, 2, width // 2), lax.axis_index("mod"), 1, False
    )
    own_bias = bias_weight.shape[0]
    bias_block = jnp.pad(bias_weight.astype(LOW), (0, 8 * LANES - own_bias)).reshape(8, LANES)
    blank = jnp.zeros((8, LANES // 2), LOW)
    ada_low = ada_weight.astype(LOW)
    adab_row = lax.dynamic_update_slice_in_dim(
        jnp.zeros((1, ada_weight.shape[1]), LOW),
        adab_weight.astype(LOW),
        row_index * adab_weight.shape[1],
        1,
    )
    ada_rows = jnp.concatenate([ada_low, adab_row])
    small_w, qkv_w, proj_w, fc1_w, table = first_gather(
        jnp.pad(ada_rows, ((0, LANES - ada_rows.shape[0]), (0, 0))),
        jnp.concatenate([half_silu, bias_block, blank], axis=1),
        qkv_weight.astype(LOW),
        proj_weight.astype(LOW),
        fc1_weight.astype(LOW),
    )
    small = small_w.reshape(2, row_devices * 8, -1)
    silu_all = jnp.concatenate([small[0, :, : width // 2], small[1, :, : width // 2]], axis=1)
    bias_all = small[:, :, width // 2 : width // 2 + LANES].reshape(2, row_devices, -1)
    bias_full = jnp.swapaxes(bias_all[:, :, :own_bias], 0, 1).reshape(1, -1).astype(WIDE)
    table = lax.dynamic_slice_in_dim(table, lax.axis_index("mod") * images, images, 1)
    table = jnp.swapaxes(table, 0, 1).reshape(images, -1)

    def joined(whole):
        return whole.reshape(2, -1, whole.shape[-1])

    qkv_low = joined(qkv_w)
    slots = segments[::CHUNK]
    joint_bias = jnp.concatenate(
        [bias_full[:, 0:width], jnp.zeros((1, width), WIDE), bias_full[:, width : 2 * width]], axis=1
    )
    def blocked(turned):
        return turned.reshape(row_devices // 4, 2, 2, -1, tokens)

    act_turned, mixture, mixture_turned, heads, (proj_w, fc1_w, fc2_w) = attend(
        slots,
        x_in,
        table,
        joint_bias,
        qkv_low,
        segments,
        fc2_weight.astype(LOW),
        proj_w,
        fc1_w,
    )
    (
        block_out, mlp_turned, hidden_turned, pre_halves, branch_halves, attn_halves, mixture_grad, middle_grad, sums, pre_sums,
    ) = middle(
        slots, x_in, out_grad, mixture, table, bias_full, joined(proj_w), joined(fc1_w), joined(fc2_w)
    )
    proj_totals, fc2_joints, fc2_bases, fc1_sums = weight_grads(
        blocked(hidden_turned),
        branch_halves,
        blocked(mlp_turned),
        pre_halves,
        blocked(mixture_turned),
        attn_halves,
    )
    joint_halves, fc2_shard, proj_shard, fc1_totals = attend_back(
        mixture_grad, heads, fc1_sums, proj_totals, fc2_joints, fc2_bases
    )
    chooser = (slots[None, :] == (jnp.arange(2 * images, dtype=jnp.int32) % images)[:, None]).astype(WIDE)
    qkv_shard, fc1_shard, small_grads, x_grad = last_scatter(
        slots,
        blocked(act_turned),
        joint_halves,
        x_in,
        middle_grad,
        table,
        qkv_low,
        sums,
        pre_sums,
        chooser,
        fc1_totals,
    )
    small_grads = small_grads.reshape(2, row_devices, 16, -1)
    mod_grads = lax.dynamic_slice_in_dim(small_grads, lax.axis_index("mod") * images, images, 2)
    mod_grad_all = jnp.swapaxes(mod_grads, 0, 1).reshape(2 * row_devices * images, -1)
    bias_grads = small_grads[:, :, 8:11].reshape(devices, -1)
    own_biases = lax.dynamic_slice_in_dim(bias_grads, lax.axis_index(ALL) * own_bias, own_bias, 1)
    bias_shard = jnp.sum(own_biases.astype(WIDE), axis=0)
    own_rows = ada_weight.shape[0]
    own_silu = lax.dynamic_slice_in_dim(silu_all, row_index * own_rows, own_rows, 1)
    ada_shard = jnp.einsum("ic,io->co", own_silu, mod_grad_all, preferred_element_type=WIDE)
    own_columns = adab_weight.shape[1]
    adab_shard = jnp.sum(
        lax.dynamic_slice_in_dim(mod_grad_all, row_index * own_columns, own_columns, 1).astype(WIDE),
        axis=0,
    )
    silu_part = times_back(mod_grad_all, ada_low)
    row_images = 2 * images
    silu_part = jnp.broadcast_to(
        silu_part.reshape(row_devices, 1, row_images, -1), (row_devices, 2, row_images, own_rows)
    ).reshape(devices * row_images, own_rows)
    silu_part = lax.all_to_all(silu_part, ALL, split_axis=0, concat_axis=1, tiled=True)
    silu_grad = jnp.sum(silu_part.reshape(row_images, row_devices, 2, own_rows), axis=2)
    cond_grad = silu_back(silu_grad.reshape(row_images, -1))[0]

    rates = step_rates(tokens * devices)
    states_out = []
    states_out.extend(nesterov(qkv_weight, qkv_moment, qkv_average, qkv_shard, rates[0]))
    states_out.extend(nesterov(proj_weight, proj_moment, proj_average, proj_shard, rates[1]))
    states_out.extend(nesterov(fc1_weight, fc1_moment, fc1_average, fc1_shard, rates[2]))
    states_out.extend(nesterov(fc2_weight, fc2_moment, fc2_average, fc2_shard, rates[3]))
    states_out.extend(nesterov(bias_weight, bias_moment, bias_average, bias_shard, rates[4]))
    states_out.extend(nesterov(ada_weight, ada_moment, ada_average, ada_shard, rates[5]))
    states_out.extend(
        nesterov(adab_weight, adab_moment, adab_average, adab_shard.reshape(1, -1), rates[6])
    )
    return (block_out, x_grad, cond_grad) + tuple(states_out)


def solution(mesh):
    far = mesh.shape["dp"] // 4
    fine = Mesh(mesh.devices.reshape(far, 2, 2, mesh.shape["mod"]), ALL)
    tokens = P(ALL, None)
    images = P(ROWS, None)
    trunk = P(ROWS, "mod")
    bias = P(ALL)
    adab = P("mod", ROWS)
    states = (trunk,) * 12 + (bias,) * 3 + (trunk,) * 3 + (adab,) * 3
    return jax.shard_map(
        body,
        mesh=fine,
        in_specs=(tokens, images, bias, tokens) + states,
        out_specs=(tokens, tokens, images) + states,
        check_vma=False,
    )
```

```python
from functools import partial

import jax
import jax.numpy as jnp
from jax import lax
from jax.experimental import pallas as pl
from jax.experimental.pallas import tpu as pltpu
from jax.sharding import Mesh
from jax.sharding import PartitionSpec as P

D = 1152
HEADS = 16
HEAD = 72
FF = 4608
LANES = 128
CHUNK = 256

ROWS = ("far", "near", "core")
ALL = ("far", "near", "core", "mod")
LOW = jnp.bfloat16
WIDE = jnp.float32
LOG2E = 1.4426950408889634
NEG = -1e30
MESH = pl.DeviceIdType.MESH
VMEM = pl.BlockSpec(memory_space=pltpu.VMEM)
ANY = pl.BlockSpec(memory_space=pl.ANY)

EPS = 1e-06
MOMENTUM = 0.9
DECAY = 0.5


def step_rates(tokens_all):
    base_rate = tokens_all ** (-0.5)
    return (
        2.5 * D ** (-0.5) * base_rate,
        3.0 * D ** (-0.5) * base_rate,
        3.3 * D ** (-0.5) * base_rate,
        2.8 * FF ** (-0.5) * base_rate,
        0.5 * base_rate,
        2.0 * D ** (-0.5) * base_rate,
        0.3 * base_rate,
    )


def nesterov(weight, moment, average, gradient, rate):
    moment = MOMENTUM * moment + gradient
    weight = weight - rate * (gradient + MOMENTUM * moment)
    average = DECAY * average + (1.0 - DECAY) * weight
    return (weight, moment, average)


def places():
    return {name: lax.axis_index(name) for name in ALL}


def greet():
    here = places()
    count = lax.axis_size("far")
    others = [dict(far=lax.rem(here["far"] + d, count)) for d in range(1, count)]
    others += [{name: 1 - here[name]} for name in ("near", "core", "mod")]
    barrier = pltpu.get_barrier_semaphore()
    for other in others:
        pl.semaphore_signal(barrier, inc=1, device_id=other, device_id_type=MESH)
    pl.semaphore_wait(barrier, len(others))


def fetches(pairs, sems):
    return [
        pltpu.make_async_copy(source, target, sems.at[number])
        for number, (source, target) in enumerate(pairs)
    ]


def remote(source, target, sends, receives, slot, other):
    return pltpu.make_async_remote_copy(
        src_ref=source,
        dst_ref=target,
        send_sem=sends.at[slot],
        recv_sem=receives.at[slot],
        device_id=other,
        device_id_type=MESH,
    )


def messages(count):
    return count - 1 + 8


class Gather:
    def __init__(self, whole, sends, receives):
        self.whole, self.sends, self.receives = whole, sends, receives
        self.here = places()
        self.count = lax.axis_size("far")
        rows = whole.shape[4]
        self.rows = rows
        self.split = rows if rows % 8 else 8 * ((rows // 8 + 1) // 2)

    def _block(self, far):
        return self.whole.at[self.here["mod"], far, self.here["near"], self.here["core"]]

    def _far(self, shard, distance):
        far = self.here["far"]
        other = dict(far=lax.rem(far + distance, self.count))
        return remote(shard, self._block(far), self.sends, self.receives, distance - 1, other)

    def _far_came(self, shard, distance):
        origin = lax.rem(self.here["far"] + self.count - distance, self.count)
        return remote(
            shard, self._block(origin), self.sends, self.receives, distance - 1, dict(far=origin)
        )

    def start_far(self, shard, local):
        pltpu.make_async_copy(shard, self._block(self.here["far"]), local).start()
        for distance in range(1, self.count):
            self._far(shard, distance).start()

    def finish_far(self, shard, local):
        pltpu.make_async_copy(shard, self._block(self.here["far"]), local).wait()
        for distance in range(1, self.count):
            self._far(shard, distance).wait_send()
            self._far_came(shard, distance).wait_recv()

    def _quad(self, flips, first, size):
        near, core, mod = (
            1 - self.here[name] if name in flips else self.here[name] for name in ("near", "core", "mod")
        )
        return self.whole.at[mod, :, near, core, pl.ds(first, size)]

    def _step(self, name):
        head, rest = (0, self.split), (self.split, self.rows - self.split)
        full = (0, self.rows)
        return {
            "near": ((), "near", full, 0),
            "mod": ((), "mod", full, 1),
            "near_mod": (("near",), "mod", head, 2),
            "mod_near": (("mod",), "near", rest, 3),
            "core": ((), "core", full, 4),
            "near_core": (("near",), "core", full, 5),
            "mod_core": (("mod",), "core", full, 6),
            "both_core": (("near", "mod"), "core", full, 7),
        }[name]

    def _copy(self, name, incoming):
        flips, axis, span, slot = self._step(name)
        if span[1] == 0:
            return None
        quad = self._quad(flips + (axis,) if incoming else flips, *span)
        other = {axis: 1 - self.here[axis]}
        return remote(quad, quad, self.sends, self.receives, self.count - 1 + slot, other)

    def start(self, *names):
        for name in names:
            copy = self._copy(name, False)
            if copy is not None:
                copy.start()

    def receive(self, *names):
        for name in names:
            copy = self._copy(name, True)
            if copy is not None:
                copy.wait_recv()

    def spread(self):
        self.start("near", "mod", "core")

    def cross(self):
        self.receive("near")
        self.start("near_mod", "near_core")
        self.receive("mod")
        self.start("mod_near", "mod_core")

    def close(self):
        self.receive("near_mod", "mod_near")
        self.start("both_core")

    def end(self):
        self.receive("core", "near_core", "mod_core", "both_core")
        for name in (
            "near", "mod", "near_mod", "mod_near", "core", "near_core", "mod_core", "both_core",
        ):
            copy = self._copy(name, False)
            if copy is not None:
                copy.wait_send()


def gather_scratch(weights, locals_):
    count = lax.axis_size("far")
    shapes = [pltpu.SemaphoreType.DMA((messages(count),))] * (2 * weights)
    return shapes + [pltpu.SemaphoreType.DMA((locals_,))]


def whole_shape(shard):
    return jax.ShapeDtypeStruct((2, lax.axis_size("far"), 2, 2) + shard.shape, LOW)


def modulate(small_w, ada, table, local, small, partials, came_core, came_near, came_far, own, sends, receives):
    here = places()
    count = lax.axis_size("far")
    far, near, core, mod = (here[name] for name in ALL)
    row_devices = 4 * count
    rows = D // row_devices
    fetch = pltpu.make_async_copy(small_w, small, local)
    fetch.start()
    fetch.wait()
    device = (far * 2 + near) * 2 + core
    half = lax.div(device, row_devices // 2)
    first = lax.rem(device, row_devices // 2) * rows
    width = small.shape[-1]
    images = small.shape[-2]
    row = lax.broadcasted_iota(jnp.int32, (width, LANES), 0)
    column = lax.broadcasted_iota(jnp.int32, (width, LANES), 1)
    select = jnp.where(jnp.logical_and(row == first + column, column < rows), 1.0, 0.0).astype(LOW)
    for at in range(count):
        silu = small[half, at].reshape(4 * images, width).astype(WIDE).astype(LOW)
        mine = times(silu, select)
        mine = jnp.where(lanes(mine.shape) == rows, 1.0, mine).astype(LOW)
        partials[at] = times(mine, ada[...]).reshape(2, 2, images, -1)

    def move(source, target, slot, other):
        return remote(source, target, sends, receives, slot, other)

    to_core = move(partials.at[:, :, 1 - core], came_core, 0, dict(core=1 - core))
    to_core.start()
    to_core.wait()
    for at in range(count):
        partials[at, :, core] = partials[at, :, core] + came_core[at]
    to_near = move(partials.at[:, 1 - near, core], came_near, 1, dict(near=1 - near))
    to_near.start()
    yield
    to_near.wait()
    for at in range(count):
        partials[at, near, core] = partials[at, near, core] + came_near[at]
    copies = []
    for distance in range(1, count):
        target = lax.rem(far + distance, count)
        copies.append(
            move(partials.at[target, near, core], came_far.at[distance - 1], 2 + distance, dict(far=target))
        )
        copies[-1].start()
    yield
    total = partials[far, near, core]
    for distance, copy in enumerate(copies):
        copy.wait()
        total = total + came_far[distance]
    own[...] = total.astype(LOW).astype(WIDE)
    keep = pltpu.make_async_copy(own, table.at[mod], local)
    keep.start()
    to_mod = move(own, table.at[mod], 2, dict(mod=1 - mod))
    to_mod.start()
    yield
    keep.wait()
    to_mod.wait_send()
    move(own, table.at[1 - mod], 2, dict(mod=1 - mod)).wait_recv()


def first_kernel(*refs):
    small_s, qkv_s, proj_s, fc1_s, ada = refs[:5]
    table = refs[9]
    gather_sems, (local, *parts) = refs[10:18], refs[18:]
    small, qkv, proj, fc1 = (
        Gather(w, s, r) for w, s, r in zip(refs[5:9], gather_sems[0::2], gather_sems[1::2])
    )
    greet()
    small.start_far(small_s, local.at[3])
    qkv.start_far(qkv_s, local.at[0])
    proj.start_far(proj_s, local.at[1])
    small.finish_far(small_s, local.at[3])
    small.spread()
    small.cross()
    small.close()
    small.end()
    stages = modulate(small.whole, ada, table, local.at[3], *parts)
    next(stages)
    qkv.finish_far(qkv_s, local.at[0])
    qkv.spread()
    next(stages)
    fc1.start_far(fc1_s, local.at[2])
    next(stages)
    qkv.cross()
    qkv.close()
    qkv.end()
    next(stages, None)
    proj.finish_far(proj_s, local.at[1])
    fc1.finish_far(fc1_s, local.at[2])


def first_gather(ada, *shards):
    count = lax.axis_size("far")
    small = whole_shape(shards[0])
    images = small.shape[4]
    columns = ada.shape[1]
    return pl.pallas_call(
        first_kernel,
        out_shape=tuple(whole_shape(shard) for shard in shards)
        + (jax.ShapeDtypeStruct((2, images, columns), WIDE),),
        in_specs=[VMEM] * 5,
        out_specs=(ANY,) * 5,
        scratch_shapes=gather_scratch(4, 4)
        + [
            pltpu.VMEM(small.shape, LOW),
            pltpu.VMEM((count, 2, 2, images, columns), WIDE),
            pltpu.VMEM((count, 2, images, columns), WIDE),
            pltpu.VMEM((count, images, columns), WIDE),
            pltpu.VMEM((count - 1, images, columns), WIDE),
            pltpu.VMEM((images, columns), WIDE),
            pltpu.SemaphoreType.DMA((count + 2,)),
            pltpu.SemaphoreType.DMA((count + 2,)),
        ],
        compiler_params=pltpu.CompilerParams(
            collective_id=0, has_side_effects=True, vmem_limit_bytes=60 * 2**20
        ),
        name="first_gather",
    )(*shards, ada)


def lanes(shape): return lax.broadcasted_iota(jnp.int32, shape, 1)

def seg_codes(seg, n):
    lane = lanes((n, LANES))
    code = lane - HEAD
    inside = jnp.logical_and(code >= 0, code < 4)
    same = code == seg
    q = jnp.where(jnp.logical_and(inside, same), 1.0, 0.0)
    k = jnp.where(jnp.logical_and(inside, jnp.logical_not(same)), NEG, 0.0)
    return q, k

def head_of(wide_rows, start):
    return wide_rows[:, start:start+HEAD]

def pad_head(part, aug):
    n = part.shape[0]
    full = jnp.concatenate([part, jnp.zeros((n, LANES-HEAD), part.dtype)], axis=1)
    return jnp.where(lanes((n,LANES)) < HEAD, full, aug)

def split3(v):
    hi = v.astype(LOW).astype(WIDE)
    mid = (v - hi).astype(LOW).astype(WIDE)
    lo = v - hi - mid
    return hi, mid, lo


def attend_kernel(*refs):
    slots, x_hbm, table, bias, weight_hbm, seg_ref, fc2_s = refs[:7]
    act_turned, mixed_ref, turned_ref = refs[9:12]
    saved, (proj_w, fc1_w, fc2_w) = refs[12:16], refs[16:19]
    heads, (x_ref, weight, fetch_sems, *sems, local, save_sems) = refs[19:23], refs[23:]
    qh, kh, vh, oh = heads
    proj, fc1, fc2 = (
        Gather(w, s, r) for w, s, r in zip((proj_w, fc1_w, fc2_w), sems[0::2], sems[1::2])
    )
    greet()
    fc2.start_far(fc2_s, local.at[0])
    proj.spread()
    fc1.spread()
    loads = fetches(((x_hbm, x_ref), (weight_hbm, weight)), fetch_sems)
    for load in loads:
        load.start()
    for load in loads:
        load.wait()

    T = x_ref.shape[0]

    def fill(i, carry):
        rows = pl.ds(pl.multiple_of(i * CHUNK, CHUNK), CHUNK)
        slot = slots[i]
        h1, _ = normed(x_ref[rows, :].astype(WIDE))
        act = (h1 * (1.0 + row_of(table, slot, 1)) + row_of(table, slot, 0)).astype(LOW)
        act_turned[:, rows] = act.T
        joint = jnp.concatenate([times(act, weight[0]), times(act, weight[1])], axis=1)
        joint = (joint + bias[...]).astype(LOW)
        lane = lanes((CHUNK, LANES))
        qc, kc = seg_codes(seg_ref[rows, :], CHUNK)
        qc = qc.astype(LOW)
        kc = jnp.where(jnp.logical_and(lane >= HEAD + 4, lane < HEAD + 7), 1.0, kc).astype(LOW)
        ones = jnp.where(jnp.logical_and(lane >= HEAD, lane < HEAD+3), 1.0, 0.0).astype(LOW)
        for h in range(HEADS):
            qh[h, rows, :] = pad_head(joint[:, h*HEAD:(h+1)*HEAD], qc)
            kh[h, rows, :] = pad_head(joint[:, D+h*HEAD:D+(h+1)*HEAD], kc)
            vh[h, rows, :] = pad_head(joint[:, 2*D+h*HEAD:2*D+(h+1)*HEAD], ones)
        pl.when(i == 2)(proj.cross)
        return carry
    lax.fori_loop(0, T//CHUNK, fill, 0)

    def save(number):
        return pltpu.make_async_copy(heads[number], saved[number], save_sems.at[number])

    save(1).start()
    save(2).start()
    def head(h, carry):
        k = kh[h]; v = vh[h]
        for i in range(T//CHUNK):
            rows = pl.ds(i*CHUNK, CHUNK)
            q = qh[h, rows, :]
            s = lax.dot_general(q, k, (((1,),(1,)),((),())), preferred_element_type=WIDE)
            m = jnp.max(s, axis=1, keepdims=True)
            p = jnp.exp2((s - m)*(HEAD**-0.5*LOG2E)).astype(LOW)
            o = jnp.dot(p, v, preferred_element_type=WIDE)
            l = o[:, HEAD:HEAD+1]
            oh[h, rows, :] = (o / l).astype(LOW)
            hi, mid, lo = split3(-(m + jnp.log(l) * HEAD**0.5))
            lane = lanes((CHUNK, LANES))
            q = jnp.where(lane == HEAD + 4, hi.astype(LOW), q)
            q = jnp.where(lane == HEAD + 5, mid.astype(LOW), q)
            qh[h, rows, :] = jnp.where(lane == HEAD + 6, lo.astype(LOW), q)
        tasks = {
            3: lambda: (fc2.finish_far(fc2_s, local.at[0]), fc2.spread()),
            6: fc1.cross,
            8: proj.close,
            10: proj.end,
        }
        for at, task in tasks.items():

            @pl.when(h == at)
            def _(task=task):
                task()

        return carry
    lax.fori_loop(0, HEADS, head, 0)
    save(0).start()
    save(3).start()

    def drain(i, carry):
        rows = pl.ds(pl.multiple_of(i*CHUNK, CHUNK), CHUNK)
        mixed = jnp.concatenate([oh[h, rows, :][:, :HEAD] for h in range(HEADS)], axis=1)
        mixed_ref[rows, :] = mixed
        turned_ref[:, rows] = mixed.T
        return carry
    lax.fori_loop(0, T//CHUNK, drain, 0)
    fc2.cross()
    fc1.close()
    fc1.end()
    fc2.close()
    fc2.end()
    for number in range(4):
        save(number).wait()


def attend(slots, x_in, table, bias, weight, segments, fc2_s, proj_w, fc1_w):
    tokens = x_in.shape[0]
    wide = HEADS * HEAD
    heads = (HEADS, tokens, LANES)
    out = pl.pallas_call(
        attend_kernel,
        out_shape=(
            jax.ShapeDtypeStruct((wide, tokens), LOW),
            jax.ShapeDtypeStruct((tokens, wide), LOW),
            jax.ShapeDtypeStruct((wide, tokens), LOW),
        )
        + (jax.ShapeDtypeStruct(heads, LOW),) * 4
        + (
            jax.ShapeDtypeStruct(proj_w.shape, LOW),
            jax.ShapeDtypeStruct(fc1_w.shape, LOW),
            whole_shape(fc2_s),
        ),
        in_specs=[pl.BlockSpec(memory_space=pltpu.SMEM), ANY, VMEM, VMEM, ANY, VMEM, VMEM, ANY, ANY],
        out_specs=(VMEM,) * 3 + (ANY,) * 7,
        scratch_shapes=[pltpu.VMEM(heads, LOW)] * 4
        + [pltpu.VMEM(x_in.shape, LOW), pltpu.VMEM(weight.shape, LOW), pltpu.SemaphoreType.DMA((2,))]
        + gather_scratch(3, 1)
        + [pltpu.SemaphoreType.DMA((4,))],
        input_output_aliases={7: 7, 8: 8},
        compiler_params=pltpu.CompilerParams(
            collective_id=1, has_side_effects=True, vmem_limit_bytes=60 * 2**20
        ),
        name="attend",
    )(slots, x_in, table, bias, weight, segments.reshape(tokens, 1), fc2_s, proj_w, fc1_w)
    return out[0], out[1], out[2], out[3:7], out[7:]


def row_spans(rows):
    first = rows if rows % 8 else 8 * ((rows // 8 + 1) // 2)
    return [(0, first)] + ([(first, rows - first)] if first < rows else [])


class Reduce:
    def __init__(self, part, span, first, came, joint, total, base, sems, loads=False):
        self.part, self.span, self.first = part, span, first
        self.second = "near" if first == "mod" else "mod"
        self.came_both, self.came_first, self.came_second, self.came_far = came
        self.joint, self.total_, self.base = joint, total, base
        self.sends, self.receives, self.locals_ = sems
        self.loads = loads
        self.here = places()
        self.count = lax.axis_size("far")

    def _swap(self, source, target, slot, axis):
        return remote(source, target, self.sends, self.receives, slot, {axis: 1 - self.here[axis]})

    def _both(self):
        return self._swap(self.part("near", "mod"), self.came_both, 0, self.first)

    def _first(self):
        return self._swap(self.part(self.first), self.came_first, 1, self.first)

    def _second(self):
        return self._swap(self.joint, self.came_second, 2, self.second)

    def _load(self, number):
        source, target = ((self.part(self.second), self.joint), (self.part(), self.total_))[number]
        return pltpu.make_async_copy(source, target, self.locals_.at[number])

    def _far(self, distance):
        target = lax.rem(self.here["far"] + distance, self.count)
        return remote(
            self.total_.at[target],
            self.came_far.at[distance - 1],
            self.sends,
            self.receives,
            2 + distance,
            dict(far=target),
        )

    def start(self):
        self._both().start()
        self._first().start()
        if self.loads:
            self._load(0).start()
            self._load(1).start()

    def merge(self):
        if self.loads:
            self._load(0).wait()
        self._both().wait_recv()

        def add(at, carry):
            self.joint[at] = (self.joint[at].astype(WIDE) + self.came_both[at].astype(WIDE)).astype(LOW)
            return carry

        lax.fori_loop(0, self.count, add, 0)
        self._second().start()

    def total(self):
        if self.loads:
            self._load(1).wait()
        self._first().wait_recv()
        self._second().wait_recv()

        def add(at, carry):
            self.total_[at] = (
                self.base[at].astype(WIDE)
                + self.came_first[at].astype(WIDE)
                + self.came_second[at].astype(WIDE)
            ).astype(LOW)
            return carry

        lax.fori_loop(0, self.count, add, 0)
        self._both().wait_send()
        self._first().wait_send()
        self._second().wait_send()

    def early(self):
        second = self.part(self.second)
        self._both().wait_recv()
        self._first().wait_recv()

        def add(at, carry):
            self.joint[at] = (second[at].astype(WIDE) + self.came_both[at].astype(WIDE)).astype(LOW)
            self.total_[at] = (self.base[at].astype(WIDE) + self.came_first[at].astype(WIDE)).astype(LOW)
            return carry

        lax.fori_loop(0, self.count, add, 0)
        self._both().wait_send()
        self._first().wait_send()

    def _load_base(self):
        return pltpu.make_async_copy(self.base, self.total_, self.locals_.at[1])

    def late_start(self):
        self._load_base().start()
        self._second().start()

    def late_total(self):
        self._load_base().wait()
        self._second().wait_recv()

        def add(at, carry):
            self.total_[at] = (self.total_[at].astype(WIDE) + self.came_second[at].astype(WIDE)).astype(LOW)
            return carry

        lax.fori_loop(0, self.count, add, 0)
        self._second().wait_send()

    def start_far(self):
        for distance in range(1, self.count):
            self._far(distance).start()

    def final(self, out):
        value = self.total_[self.here["far"]].astype(WIDE)
        for distance in range(1, self.count):
            self._far(distance).wait_recv()
            value = value + self.came_far[distance - 1].astype(WIDE)
        out[pl.ds(*self.span), :] = value
        for distance in range(1, self.count):
            self._far(distance).wait_send()


ORDERS = ("mod", "near")


def run(parts, *names):
    for part in parts:
        for name in names:
            getattr(part, name)()


def span_part(sums, span):
    def part(*flips):
        near, mod = (
            1 - lax.axis_index(name) if name in flips else lax.axis_index(name) for name in ("near", "mod")
        )
        return sums.at[mod, near, :, pl.ds(*span)]

    return part


def take(scratch, number):
    return scratch[:number], scratch[number:]


def came_scratch(count, span, columns, far=True):
    block = (count, span[1], columns)
    shapes = [pltpu.VMEM(block, LOW)] * 3
    return shapes + ([pltpu.VMEM((count - 1,) + block[1:], LOW)] if far else [])


def sem_scratch(count):
    return [pltpu.SemaphoreType.DMA((count + 2,))] * 2 + [pltpu.SemaphoreType.DMA((2,))]


def loaded_scratch(shape, total=True):
    count, rows, columns = shape[2:]
    shapes = []
    for span in row_spans(rows):
        shapes += came_scratch(count, span, columns, total)
        shapes += [pltpu.VMEM((count, span[1], columns), LOW)] * (2 if total else 1)
        shapes += sem_scratch(count)
    return shapes


def loaded_reduces(sums, scratch, totals=None):
    reduces = []
    for number, span in enumerate(row_spans(sums.shape[3])):
        came, scratch = take(scratch, 4 if totals is None else 3)
        came = list(came) + [None] * (4 - len(came))
        (joint,), scratch = take(scratch, 1)
        if totals is None:
            (total,), scratch = take(scratch, 1)
        else:
            total = totals[number]
        sems, scratch = take(scratch, 3)
        reduces.append(
            Reduce(span_part(sums, span), span, ORDERS[number], came, joint, total, total, sems, True)
        )
    return reduces, scratch


def resident_scratch(shape, far=True):
    count, rows, columns = shape[2:]
    shapes = []
    for span in row_spans(rows):
        shapes += came_scratch(count, span, columns, far) + sem_scratch(count)
    return shapes


def resident_reduces(sums, scratch, totals=None, joints=None):
    reduces = []
    for number, span in enumerate(row_spans(sums.shape[3])):
        came, scratch = take(scratch, 4 if totals is None else 3 if joints is None else 2)
        sems, scratch = take(scratch, 3)
        part = span_part(sums, span)
        order = ORDERS[number]
        own = part()
        total = own if totals is None else totals[number]
        came = list(came) + [None] * (4 - len(came))
        joint = part("near" if order == "mod" else "mod") if joints is None else joints[number]
        reduces.append(Reduce(part, span, order, came, joint, total, own, sems))
    return reduces, scratch


def early_scratch(shape):
    count, rows, columns = shape[2:]
    shapes = []
    for span in row_spans(rows):
        shapes += [pltpu.VMEM((count, span[1], columns), LOW)] * 2 + sem_scratch(count)
    return shapes


def late_scratch(bases):
    shapes = []
    for base in bases:
        far = pltpu.VMEM((base.shape[0] - 1,) + base.shape[1:], LOW)
        shapes += [pltpu.VMEM(base.shape, LOW)] * 2 + [far] + sem_scratch(base.shape[0])
    return shapes


def late_reduces(joints, bases, rows, scratch):
    reduces = []
    for number, span in enumerate(row_spans(rows)):
        (came, total, came_far), scratch = take(scratch, 3)
        sems, scratch = take(scratch, 3)
        came = (None, None, came, came_far)
        reduces.append(
            Reduce(None, span, ORDERS[number], came, joints[number], total, bases[number], sems)
        )
    return reduces, scratch


def far_scratch(totals):
    shapes = []
    for total in totals:
        count = total.shape[0]
        shapes += [pltpu.VMEM((count - 1,) + total.shape[1:], LOW)] + sem_scratch(count)[:2]
    return shapes


def far_reduces(totals, rows, scratch):
    reduces = []
    for total, span in zip(totals, row_spans(rows)):
        (came, sends, receives), scratch = take(scratch, 3)
        came = (None, None, None, came)
        reduces.append(Reduce(None, span, "mod", came, None, total, total, (sends, receives, None)))
    return reduces, scratch


class Product:
    def __init__(self, left, right, scratch):
        self.left, self.right = left, right
        self.rows_, self.sums, self.came, self.loads, self.sends, self.receives = scratch
        self.core = lax.axis_index("core")

    @staticmethod
    def scratch(count, rows, tokens, columns):
        sums = pltpu.VMEM((2, 2, count, rows, columns), LOW)
        sems = [pltpu.SemaphoreType.DMA((4,))] * 3
        return [pltpu.VMEM((2, count, rows, tokens), LOW), sums, sums] + sems

    def _load(self, near, own):
        core = self.core if own else 1 - self.core
        return pltpu.make_async_copy(
            self.left.at[:, near, core], self.rows_.at[near], self.loads.at[2 * own + near]
        )

    def load(self):
        for near in (0, 1):
            self._load(near, 0).start()

    def _copy(self, mod, near):
        return remote(
            self.sums.at[mod, near],
            self.came.at[mod, near],
            self.sends,
            self.receives,
            2 * mod + near,
            dict(core=1 - self.core),
        )

    def _blocks(self, near, own, store):
        count, rows, tokens = self.rows_.shape[1:]
        columns = self.right.shape[2]
        self._load(near, own).wait()
        left = self.rows_[near].reshape(count * rows, tokens)
        width = columns if columns <= 1024 else columns // 2
        width = width if width % LANES == 0 else columns
        for mod in (0, 1):
            for at in range(0, columns, width):
                product = times(left, self.right[mod, :, at : at + width])
                store(mod, at, width, product.reshape(count, rows, width))

    def send(self):
        for near in (0, 1):

            def store(mod, at, width, product, near=near):
                self.sums[mod, near, :, :, at : at + width] = product.astype(LOW)

            self._blocks(near, 0, store)
            self._load(near, 1).start()
            for mod in (0, 1):
                self._copy(mod, near).start()

    def sum(self):
        for near in (0, 1):
            for mod in (0, 1):
                self._copy(mod, near).wait_send()
                self._copy(mod, near).wait_recv()

            def store(mod, at, width, product, near=near):
                came = self.came[mod, near, :, :, at : at + width]
                self.sums[mod, near, :, :, at : at + width] = (product + came.astype(WIDE)).astype(LOW)

            self._blocks(near, 1, store)


def total_shapes(count, rows, columns):
    return [jax.ShapeDtypeStruct((count, span[1], columns), LOW) for span in row_spans(rows)]


def weight_kernel(*refs, modes, spans):
    sides, refs = take(refs, 2 * len(modes))
    outs = []
    for mode, count in zip(modes, spans):
        used, refs = take(refs, {"whole": count, "early": 2 * count, "chip": 1}[mode])
        outs.append(used)
    fetch_sems, *scratch = refs
    rights, scratch = take(scratch, len(modes) - 1)
    products, reduces = [], []
    for number in range(len(modes)):
        used, scratch = take(scratch, 6)
        right = rights[number - 1] if number else sides[1]
        products.append(Product(sides[2 * number], right, used))
    loads = fetches(list(zip(sides[3::2], rights)), fetch_sems)
    for mode, count, product, out in zip(modes, spans, products, outs):
        parts = []
        if mode == "whole":
            parts, scratch = resident_reduces(product.sums, scratch, out)
        elif mode == "early":
            parts, scratch = resident_reduces(product.sums, scratch, out[count:], out[:count])
        reduces.append(parts)
    (out_sem,) = scratch
    products[0].load()
    for load in loads:
        load.start()
    greet()
    copies = []
    for number, product in enumerate(products):
        before = number and modes[number - 1] == "whole"
        if number:
            loads[number - 1].wait()
        product.send()
        if before:
            run(reduces[number - 1], "merge")
        if number + 1 < len(products):
            products[number + 1].load()
        product.sum()
        run(reduces[number], "start") if reduces[number] else None
        if before:
            run(reduces[number - 1], "total")
        if modes[number] == "chip":
            copies.append(pltpu.make_async_copy(product.sums, outs[number][0], out_sem.at[0]))
            copies[-1].start()
    for number, mode in enumerate(modes):
        if mode == "early":
            run(reduces[number], "early")
    for copy in copies:
        copy.wait()


def weight_call(pairs, modes, number):
    count = pairs[0][0].shape[0]
    tokens = pairs[0][0].shape[4]
    products, sums, shapes, specs, spans = [], [], [], [], []
    for (left, right), mode in zip(pairs, modes):
        rows, columns = left.shape[3], right.shape[2]
        shape = (2, 2, count, rows, columns)
        products += Product.scratch(count, rows, tokens, columns)
        totals = total_shapes(count, rows, columns)
        spans.append(len(totals))
        if mode == "chip":
            shapes.append(jax.ShapeDtypeStruct(shape, LOW))
            specs.append(ANY)
        else:
            sums += resident_scratch(shape, False) if mode == "whole" else early_scratch(shape)
            outs = totals * (1 if mode == "whole" else 2)
            shapes += outs
            specs += [VMEM] * len(outs)
    out = pl.pallas_call(
        partial(weight_kernel, modes=modes, spans=tuple(spans)),
        out_shape=tuple(shapes),
        in_specs=[ANY, VMEM] + [ANY, ANY] * (len(pairs) - 1),
        out_specs=tuple(specs),
        scratch_shapes=[pltpu.SemaphoreType.DMA((len(pairs),))]
        + [pltpu.VMEM(right.shape, LOW) for _, right in pairs[1:]]
        + products
        + sums
        + [pltpu.SemaphoreType.DMA((1,))],
        compiler_params=pltpu.CompilerParams(
            collective_id=number, has_side_effects=True, vmem_limit_bytes=63 * 2**20
        ),
        name="weight_grads",
    )(*[side for pair in pairs for side in pair])
    return out, spans


def weight_grads(hidden, branch, mlp, pre, mixed, attn):
    proj, fc2, fc1 = (mixed, attn), (hidden, branch), (mlp, pre)
    if mlp.shape[3] % 8 == 0:
        out, spans = weight_call([proj, fc2, fc1], ("whole", "early", "chip"), 4)
        first, second = spans[0], spans[0] + spans[1]
        return out[:first], out[first:second], out[second:-1], out[-1]
    early, spans = weight_call([fc2], ("early",), 4)
    rest, _ = weight_call([proj, fc1], ("whole", "chip"), 5)
    return rest[:-1], early[: spans[0]], early[spans[0] :], rest[-1]


def tile_sums_by_slot(chooser, sums):
    total = None
    for at, row in enumerate(sums):
        part = chooser[:, at : at + 1] * row
        total = part if total is None else total + part
    return total


def last_kernel(*refs, spans):
    slots, act, joint, x_hbm, dx1_hbm, weight_hbm, table, mid_sums, pre_sums, chooser = refs[:10]
    totals, refs = take(refs[10:], spans)
    qkv_out, fc1_out, small_w, x_grad_ref, *scratch = refs
    qkv_scratch, scratch = take(scratch, 6)
    qkv = Product(act, joint, qkv_scratch)
    qkv_sum, scratch = resident_reduces(qkv.sums, scratch)
    fc1_sum, scratch = far_reduces(totals, fc1_out.shape[0], scratch)
    small_sends, small_receives, local, first_sums, joint_sums, small_s, *scratch = scratch
    x_ref, dx1_ref, weight, fetch_sems = scratch
    loads = fetches(((x_hbm, x_ref), (dx1_hbm, dx1_ref), (weight_hbm, weight)), fetch_sems)
    small = Gather(small_w, small_sends, small_receives)
    tiles = x_ref.shape[0] // CHUNK
    qkv.load()
    greet()
    run(fc1_sum, "start_far")
    for load in loads:
        load.start()
    qkv.send()
    qkv.sum()
    run(qkv_sum, "start")
    for load in loads:
        load.wait()

    def back(at, carry):
        rows = pl.ds(pl.multiple_of(at * CHUNK, CHUNK), CHUNK)
        dact = times_across(joint[0, rows, :], weight[0]) + times_across(joint[1, rows, :], weight[1])
        h1, inverse = normed(x_ref[rows, :].astype(WIDE))
        first_sums[at, 0:1, :] = column_sums(dact)
        first_sums[at, 1:2, :] = column_sums(dact * h1)
        dh1 = dact * (1.0 + row_of(table, slots[at], 1))
        x_grad_ref[rows, :] = dx1_ref[rows, :] + inverse * (
            dh1
            - jnp.mean(dh1, axis=-1, keepdims=True)
            - h1 * jnp.mean(dh1 * h1, axis=-1, keepdims=True)
        )
        for side in range(2):
            joint_sums[side : side + 1, :] += column_sums(joint[side, rows, :].astype(WIDE))

        @pl.when(at == tiles // 2 - 1)
        def _():
            run(qkv_sum, "merge")

        return carry

    joint_sums[...] = jnp.zeros_like(joint_sums)
    lax.fori_loop(0, tiles, back, 0)
    choose = chooser[...]
    upper = lax.broadcasted_iota(jnp.int32, (choose.shape[0], D), 0) < choose.shape[0] // 2
    groups = (
        [first_sums[at, 0:1, :] for at in range(tiles)],
        [first_sums[at, 1:2, :] for at in range(tiles)],
    ) + tuple([mid_sums[at, row : row + 1, :] for at in range(tiles)] for row in range(4))
    for group in range(3):
        value = jnp.where(
            upper, tile_sums_by_slot(choose, groups[group]), tile_sums_by_slot(choose, groups[group + 3])
        )
        small_s[0:8, group * D : (group + 1) * D] = value.astype(LOW)
    pre = pre_sums[...]
    tile_rows = [column_sums(mid_sums[:, row, :]) for row in (4, 5)]
    biases = (
        (joint_sums[0:1, :D], joint_sums[1:2, D // 2 :], tile_rows[0]),
        tuple(pre[:, at * D : (at + 1) * D] for at in range(3)),
        (pre[:, 3 * D :], tile_rows[1], jnp.zeros((1, D), WIDE)),
    )
    blank = jnp.zeros((5, D), WIDE)
    for group in range(3):
        rows = jnp.concatenate([biases[row][group] for row in range(3)] + [blank], axis=0)
        small_s[8:16, group * D : (group + 1) * D] = rows.astype(LOW)
    small.start_far(small_s, local.at[0])
    small.finish_far(small_s, local.at[0])
    small.spread()
    run(qkv_sum, "total", "start_far")
    small.cross()
    small.close()
    small.end()
    for part in fc1_sum:
        part.final(fc1_out)
    for part in qkv_sum:
        part.final(qkv_out)


def last_scatter(slots, act, joint, x_in, dx1, table, weight, mid_sums, pre_sums, chooser, totals):
    count, _, _, rows, tokens = act.shape
    fc1_columns = totals[0].shape[2]
    columns = joint.shape[2]
    small_s = jax.ShapeDtypeStruct((16, 3 * D), LOW)
    return pl.pallas_call(
        partial(last_kernel, spans=len(totals)),
        out_shape=(
            jax.ShapeDtypeStruct((rows, columns), WIDE),
            jax.ShapeDtypeStruct((sum(total.shape[1] for total in totals), fc1_columns), WIDE),
            whole_shape(small_s),
            jax.ShapeDtypeStruct((tokens, D), WIDE),
        ),
        in_specs=[pl.BlockSpec(memory_space=pltpu.SMEM), ANY, VMEM, ANY, ANY, ANY]
        + [VMEM] * (4 + len(totals)),
        out_specs=(VMEM, VMEM, ANY, VMEM),
        scratch_shapes=Product.scratch(count, rows, tokens, columns)
        + resident_scratch((2, 2, count, rows, columns))
        + far_scratch(totals)
        + gather_scratch(1, 1)
        + [
            pltpu.VMEM((tokens // CHUNK, 8, D), WIDE),
            pltpu.VMEM((2, columns), WIDE),
            pltpu.VMEM(small_s.shape, LOW),
            pltpu.VMEM(x_in.shape, LOW),
            pltpu.VMEM(dx1.shape, WIDE),
            pltpu.VMEM(weight.shape, LOW),
            pltpu.SemaphoreType.DMA((3,)),
        ],
        compiler_params=pltpu.CompilerParams(
            collective_id=3, has_side_effects=True, vmem_limit_bytes=63 * 2**20
        ),
        name="last_scatter",
    )(slots, act, joint, x_in, dx1, weight, table, mid_sums, pre_sums, chooser, *totals)


def attend_back_kernel(*refs, counts):
    up_ref, heads, fc1_sums = refs[0], refs[1:5], refs[5]
    proj_totals, refs = take(refs[6:], counts[0])
    joints, refs = take(refs, counts[1])
    bases, refs = take(refs, counts[1])
    out_ref, fc2_out, proj_out, *refs = refs
    fc1_totals, refs = take(refs, counts[2])
    qh, kh, vh, uh, oh, load_sems, leave, leave_sems, *scratch = refs
    fc1, scratch = loaded_reduces(fc1_sums, scratch, fc1_totals)
    proj, scratch = far_reduces(proj_totals, proj_out.shape[0], scratch)
    fc2, scratch = late_reduces(joints, bases, fc2_out.shape[0], scratch)
    T = up_ref.shape[0]
    chunks = T // CHUNK

    def load(number):
        return pltpu.make_async_copy(heads[number], (qh, kh, vh, oh)[number], load_sems.at[number])

    for number in (3, 0, 1, 2):
        load(number).start()
    greet()
    run(fc2, "late_start")
    run(proj, "start_far")
    run(fc1, "start")
    load(3).wait()

    def fill(i, carry):
        rows = pl.ds(pl.multiple_of(i * CHUNK, CHUNK), CHUNK)
        lane = lanes((CHUNK, LANES))
        for h in range(HEADS):
            u = pad_head(up_ref[rows, h * HEAD : (h + 1) * HEAD], jnp.zeros((CHUNK, LANES), LOW))
            delta = jnp.sum(u.astype(WIDE) * oh[h, rows, :].astype(WIDE), axis=1, keepdims=True)
            hi, mid, lo = split3(-delta)
            u = jnp.where(lane == HEAD, hi.astype(LOW), u)
            u = jnp.where(lane == HEAD + 1, mid.astype(LOW), u)
            uh[h, rows, :] = jnp.where(lane == HEAD + 2, lo.astype(LOW), u)
        return carry

    lax.fori_loop(0, chunks, fill, 0)
    for number in range(3):
        load(number).wait()
    across = (((1,), (1,)), ((), ()))
    tasks = {
        4: lambda: run(fc2, "late_total", "start_far"),
        9: lambda: run(fc1, "merge"),
    }

    def head(h, carry):
        k = kh[h]
        v = vh[h]
        kt = k.T
        dk = jnp.zeros((T, LANES), WIDE)
        dv = jnp.zeros((T, LANES), WIDE)
        for i in range(chunks):
            rows = pl.ds(i * CHUNK, CHUNK)
            q = qh[h, rows, :]
            u = uh[h, rows, :]
            s = lax.dot_general(k, q, across, preferred_element_type=WIDE)
            p = jnp.exp2(s * (HEAD**-0.5 * LOG2E))
            dp = lax.dot_general(v, u, across, preferred_element_type=WIDE)
            ds = (p * dp).astype(LOW)
            dv = dv + jnp.dot(p.astype(LOW), u, preferred_element_type=WIDE)
            dk = dk + jnp.dot(ds, q, preferred_element_type=WIDE)
            dqt = jnp.dot(kt, ds, preferred_element_type=WIDE)
            qh[h, rows, :] = (dqt.T * HEAD**-0.5).astype(LOW)
        kh[h] = (dk * HEAD**-0.5).astype(LOW)
        vh[h] = dv.astype(LOW)
        for at, task in tasks.items():

            @pl.when(h == at)
            def _(task=task):
                task()

        return carry

    lax.fori_loop(0, HEADS, head, 0)

    def store(i, side):
        rows = pl.ds(pl.multiple_of(i * CHUNK, CHUNK), CHUNK)
        return pltpu.make_async_copy(
            leave.at[side], out_ref.at[side, rows], leave_sems.at[side]
        )

    def drain(i, carry):
        rows = pl.ds(pl.multiple_of(i * CHUNK, CHUNK), CHUNK)
        parts = [g[h, rows, :][:, :HEAD] for g in (qh, kh, vh) for h in range(HEADS)]
        for side in range(2):

            @pl.when(i > 0)
            def _(side=side):
                store(i - 1, side).wait()

            own = parts[side * len(parts) // 2 : (side + 1) * len(parts) // 2]
            leave[side] = jnp.concatenate(own, axis=1)
            store(i, side).start()
        return carry

    lax.fori_loop(0, chunks, drain, 0)
    run(fc1, "total")
    for side in range(2):
        store(chunks - 1, side).wait()
    for part in fc2:
        part.final(fc2_out)
    for part in proj:
        part.final(proj_out)


def attend_back(upstream, heads, fc1_sums, proj_totals, joints, bases):
    tokens = upstream.shape[0]
    count, rows, columns = fc1_sums.shape[2:]
    totals = total_shapes(count, rows, columns)

    def shard(parts):
        return jax.ShapeDtypeStruct((sum(part.shape[1] for part in parts), parts[0].shape[2]), WIDE)

    out = pl.pallas_call(
        partial(attend_back_kernel, counts=(len(proj_totals), len(joints), len(totals))),
        out_shape=(
            jax.ShapeDtypeStruct((2, tokens, 3 * HEADS * HEAD // 2), LOW),
            shard(bases),
            shard(proj_totals),
        )
        + tuple(totals),
        in_specs=[VMEM] + [ANY] * 5 + [VMEM] * len(proj_totals) + [ANY] * (2 * len(joints)),
        out_specs=(ANY, VMEM, VMEM) + (VMEM,) * len(totals),
        scratch_shapes=[pltpu.VMEM((HEADS, tokens, LANES), LOW)] * 5
        + [pltpu.SemaphoreType.DMA((4,))]
        + [pltpu.VMEM((2, CHUNK, 3 * HEADS * HEAD // 2), LOW), pltpu.SemaphoreType.DMA((2,))]
        + loaded_scratch(fc1_sums.shape, False)
        + far_scratch(proj_totals)
        + late_scratch(bases),
        compiler_params=pltpu.CompilerParams(
            collective_id=2, has_side_effects=True, vmem_limit_bytes=63 * 2**20
        ),
        name="attend_back",
    )(upstream, *heads, fc1_sums, *proj_totals, *joints, *bases)
    return out[0], out[1], out[2], out[3:]


def normed(values):
    centre = values - jnp.mean(values, axis=-1, keepdims=True)
    inverse = lax.rsqrt(jnp.mean(centre * centre, axis=-1, keepdims=True) + EPS)
    return centre * inverse, inverse


def row_of(table, slot, group):
    return table[pl.ds(slot, 1), group * D : (group + 1) * D]


def column_sums(values):
    return jnp.sum(values, axis=0, keepdims=True)


def times_across(left, right):
    return lax.dot_general(left, right, (((1,), (1,)), ((), ())), preferred_element_type=WIDE)


def fixed(*shape):
    return pl.BlockSpec(
        shape, lambda i, slots: (0,) * len(shape), pipeline_mode=pl.Buffered(1)
    )


GELU = 0.7978845608028654
CUBIC = 0.044715
SPAN = 768
BLOCK = 512


def middle_kernel(
    slots, x_ref, g_ref, mixed_ref, table, bias, bias1, proj, fc1, fc2,
    block_ref, mlp_turned, hidden_turned, dpre_ref, dbranch_ref, dattn_ref, dmixed_ref, dx1_ref, sums_ref, dpre_sums,
    attn_out, mlp, branch,
):
    step = pl.program_id(0)
    tokens = x_ref.shape[0]

    @pl.when(step == 0)
    def _():
        def enter(tile_at, carry):
            rows = pl.ds(pl.multiple_of(tile_at * CHUNK, CHUNK), CHUNK)
            slot = slots[tile_at]
            gate1, shift2, scale2, gate2 = (row_of(table, slot, group) for group in (2, 3, 4, 5))
            mixed = mixed_ref[rows, :]
            out = jnp.concatenate([times(mixed, proj[0]), times(mixed, proj[1])], axis=1)
            out = out + bias[:, 2 * D : 3 * D]
            attn_out[rows, :] = out
            h2, _ = normed(x_ref[rows, :].astype(WIDE) + gate1 * out)
            mlp_in = (h2 * (1.0 + scale2) + shift2).astype(LOW)
            mlp[rows, :] = mlp_in
            mlp_turned[:, rows] = mlp_in.T
            dbranch = (gate2 * g_ref[rows, :].astype(WIDE)).astype(LOW)
            sums_ref[tile_at, 5:6, :] = column_sums(dbranch.astype(WIDE))
            dbranch_ref[0, rows, :] = dbranch[:, : D // 2]
            dbranch_ref[1, rows, :] = dbranch[:, D // 2 :]
            return carry

        lax.fori_loop(0, tokens // CHUNK, enter, 0)
        branch[...] = jnp.zeros_like(branch)
        dx1_ref[...] = jnp.zeros_like(dx1_ref)

    total = None
    for first in range(0, tokens, BLOCK):
        rows = slice(first, first + BLOCK)
        pre = times(mlp[rows, :], fc1[0]) + bias1[0]
        square = pre * pre
        bend = jnp.tanh(GELU * pre * (1.0 + CUBIC * square))
        rise = 0.5 * (1.0 + bend)
        hidden = (pre * rise).astype(LOW)
        hidden_turned[:, rows] = hidden.T
        for side in range(2):
            branch[side, rows] += times(hidden, fc2[side])
        slope = rise + 0.5 * GELU * pre * (1.0 - bend * bend) * (1.0 + 3.0 * CUBIC * square)
        dhidden = times_across(dbranch_ref[0, rows], fc2[0]) + times_across(dbranch_ref[1, rows], fc2[1])
        dpre = (dhidden * slope).astype(LOW)
        dpre_ref[0, rows] = dpre
        part = column_sums(dpre.astype(WIDE))
        total = part if total is None else total + part
        dx1_ref[rows, :] += times_across(dpre, fc1[0])
    dpre_sums[...] = total

    @pl.when(step == pl.num_programs(0) - 1)
    def _():
        def leave(tile_at, carry):
            rows = pl.ds(pl.multiple_of(tile_at * CHUNK, CHUNK), CHUNK)
            slot = slots[tile_at]
            gate1, scale2, gate2 = (row_of(table, slot, group) for group in (2, 4, 5))
            out = attn_out[rows, :]
            x1 = x_ref[rows, :].astype(WIDE) + gate1 * out
            h2, inverse = normed(x1)
            whole = jnp.concatenate([branch[0, rows, :], branch[1, rows, :]], axis=1) + bias[:, 3 * D + FF :]
            block_ref[rows, :] = (x1 + gate2 * whole).astype(LOW)
            g = g_ref[rows, :].astype(WIDE)
            sums_ref[tile_at, 3:4, :] = column_sums(g * whole)
            dmlp = dx1_ref[rows, :]
            sums_ref[tile_at, 1:2, :] = column_sums(dmlp)
            sums_ref[tile_at, 2:3, :] = column_sums(dmlp * h2)
            dh2 = dmlp * (1.0 + scale2)
            dx1 = g + inverse * (
                dh2
                - jnp.mean(dh2, axis=-1, keepdims=True)
                - h2 * jnp.mean(dh2 * h2, axis=-1, keepdims=True)
            )
            dx1_ref[rows, :] = dx1
            sums_ref[tile_at, 0:1, :] = column_sums(dx1 * out)
            dattn = (gate1 * dx1).astype(LOW)
            sums_ref[tile_at, 4:5, :] = column_sums(dattn.astype(WIDE))
            sums_ref[tile_at, 6:8, :] = jnp.zeros((2, D), WIDE)
            left, right = dattn[:, : D // 2], dattn[:, D // 2 :]
            dattn_ref[0, rows, :] = left
            dattn_ref[1, rows, :] = right
            dmixed_ref[rows, :] = (times_across(left, proj[0]) + times_across(right, proj[1])).astype(LOW)
            return carry

        lax.fori_loop(0, tokens // CHUNK, leave, 0)


def middle(slots, x_in, out_grad, mixed, table, bias, proj, fc1, fc2):
    tokens = x_in.shape[0]
    tiles = tokens // CHUNK
    steps = FF // SPAN
    per_side = steps // 2
    bias1 = bias[:, 3 * D : 3 * D + FF].reshape(steps, 1, SPAN)

    def by_unit(shape, place):
        return pl.BlockSpec(shape, lambda j, slots: place(j))

    outs = (
        ((tokens, D), LOW),
        ((D, tokens), LOW),
        ((FF, tokens), LOW),
        ((2, tokens, FF // 2), LOW),
        ((2, tokens, D // 2), LOW),
        ((2, tokens, D // 2), LOW),
        ((tokens, D), LOW),
        ((tokens, D), WIDE),
        ((tiles, 8, D), WIDE),
        ((1, FF), WIDE),
    )
    out_specs = [fixed(*shape) for shape, _ in outs]
    out_specs[2] = by_unit((SPAN, tokens), lambda j: (j, 0))
    out_specs[3] = by_unit((1, tokens, SPAN), lambda j: (j // per_side, 0, j % per_side))
    out_specs[9] = by_unit((1, SPAN), lambda j: (0, j))
    return pl.pallas_call(
        middle_kernel,
        out_shape=tuple(jax.ShapeDtypeStruct(shape, dtype) for shape, dtype in outs),
        grid_spec=pltpu.PrefetchScalarGridSpec(
            num_scalar_prefetch=1,
            grid=(steps,),
            in_specs=[
                fixed(tokens, D),
                fixed(tokens, D),
                fixed(tokens, D),
                fixed(*table.shape),
                fixed(*bias.shape),
                by_unit((1, 1, SPAN), lambda j: (j, 0, 0)),
                fixed(*proj.shape),
                by_unit((1, D, SPAN), lambda j: (j // per_side, 0, j % per_side)),
                by_unit((2, SPAN, D // 2), lambda j: (0, j, 0)),
            ],
            out_specs=tuple(out_specs),
            scratch_shapes=[
                pltpu.VMEM((tokens, D), WIDE),
                pltpu.VMEM((tokens, D), LOW),
                pltpu.VMEM((2, tokens, D // 2), WIDE),
            ],
        ),
        compiler_params=pltpu.CompilerParams(
            dimension_semantics=("arbitrary",), vmem_limit_bytes=63 * 2**20
        ),
        cost_estimate=pl.CostEstimate(
            flops=4 * tokens * (D * D + 2 * D * FF),
            bytes_accessed=(D * D + 2 * D * FF) * 2 + tokens * D * 40,
            transcendentals=0,
        ),
        name="middle",
    )(slots, x_in, out_grad, mixed, table, bias, bias1, proj, fc1, fc2)


def times(left, right):
    return jnp.dot(left, right, preferred_element_type=WIDE)


def times_back(left, right):
    return lax.dot_general(left, right, (((1,), (1,)), ((), ())), preferred_element_type=WIDE)


def body(
    x_in,
    cond,
    segments,
    out_grad,
    qkv_weight,
    qkv_moment,
    qkv_average,
    proj_weight,
    proj_moment,
    proj_average,
    fc1_weight,
    fc1_moment,
    fc1_average,
    fc2_weight,
    fc2_moment,
    fc2_average,
    bias_weight,
    bias_moment,
    bias_average,
    ada_weight,
    ada_moment,
    ada_average,
    adab_weight,
    adab_moment,
    adab_average,
):
    tokens, width = x_in.shape
    row_devices = lax.axis_size(ROWS)
    devices = lax.axis_size(ALL)
    row_index = lax.axis_index(ROWS)
    images = cond.shape[0] // 2

    cond_silu, silu_back = jax.vjp(jax.nn.silu, cond.astype(WIDE))
    half_silu = lax.dynamic_index_in_dim(
        cond_silu.astype(LOW).reshape(-1, 2, width // 2), lax.axis_index("mod"), 1, False
    )
    own_bias = bias_weight.shape[0]
    bias_block = jnp.pad(bias_weight.astype(LOW), (0, 8 * LANES - own_bias)).reshape(8, LANES)
    blank = jnp.zeros((8, LANES // 2), LOW)
    ada_low = ada_weight.astype(LOW)
    adab_row = lax.dynamic_update_slice_in_dim(
        jnp.zeros((1, ada_weight.shape[1]), LOW),
        adab_weight.astype(LOW),
        row_index * adab_weight.shape[1],
        1,
    )
    ada_rows = jnp.concatenate([ada_low, adab_row])
    small_w, qkv_w, proj_w, fc1_w, table = first_gather(
        jnp.pad(ada_rows, ((0, LANES - ada_rows.shape[0]), (0, 0))),
        jnp.concatenate([half_silu, bias_block, blank], axis=1),
        qkv_weight.astype(LOW),
        proj_weight.astype(LOW),
        fc1_weight.astype(LOW),
    )
    small = small_w.reshape(2, row_devices * 8, -1)
    silu_all = jnp.concatenate([small[0, :, : width // 2], small[1, :, : width // 2]], axis=1)
    bias_all = small[:, :, width // 2 : width // 2 + LANES].reshape(2, row_devices, -1)
    bias_full = jnp.swapaxes(bias_all[:, :, :own_bias], 0, 1).reshape(1, -1).astype(WIDE)
    table = lax.dynamic_slice_in_dim(table, lax.axis_index("mod") * images, images, 1)
    table = jnp.swapaxes(table, 0, 1).reshape(images, -1)

    def joined(whole):
        return whole.reshape(2, -1, whole.shape[-1])

    qkv_low = joined(qkv_w)
    slots = segments[::CHUNK]
    joint_bias = jnp.concatenate(
        [bias_full[:, 0:width], jnp.zeros((1, width), WIDE), bias_full[:, width : 2 * width]], axis=1
    )
    def blocked(turned):
        return turned.reshape(row_devices // 4, 2, 2, -1, tokens)

    act_turned, mixture, mixture_turned, heads, (proj_w, fc1_w, fc2_w) = attend(
        slots,
        x_in,
        table,
        joint_bias,
        qkv_low,
        segments,
        fc2_weight.astype(LOW),
        proj_w,
        fc1_w,
    )
    (
        block_out, mlp_turned, hidden_turned, pre_halves, branch_halves, attn_halves, mixture_grad, middle_grad, sums, pre_sums,
    ) = middle(
        slots, x_in, out_grad, mixture, table, bias_full, joined(proj_w), joined(fc1_w), joined(fc2_w)
    )
    proj_totals, fc2_joints, fc2_bases, fc1_sums = weight_grads(
        blocked(hidden_turned),
        branch_halves,
        blocked(mlp_turned),
        pre_halves,
        blocked(mixture_turned),
        attn_halves,
    )
    joint_halves, fc2_shard, proj_shard, fc1_totals = attend_back(
        mixture_grad, heads, fc1_sums, proj_totals, fc2_joints, fc2_bases
    )
    chooser = (slots[None, :] == (jnp.arange(2 * images, dtype=jnp.int32) % images)[:, None]).astype(WIDE)
    qkv_shard, fc1_shard, small_grads, x_grad = last_scatter(
        slots,
        blocked(act_turned),
        joint_halves,
        x_in,
        middle_grad,
        table,
        qkv_low,
        sums,
        pre_sums,
        chooser,
        fc1_totals,
    )
    small_grads = small_grads.reshape(2, row_devices, 16, -1)
    mod_grads = lax.dynamic_slice_in_dim(small_grads, lax.axis_index("mod") * images, images, 2)
    mod_grad_all = jnp.swapaxes(mod_grads, 0, 1).reshape(2 * row_devices * images, -1)
    bias_grads = small_grads[:, :, 8:11].reshape(devices, -1)
    own_biases = lax.dynamic_slice_in_dim(bias_grads, lax.axis_index(ALL) * own_bias, own_bias, 1)
    bias_shard = jnp.sum(own_biases.astype(WIDE), axis=0)
    own_rows = ada_weight.shape[0]
    own_silu = lax.dynamic_slice_in_dim(silu_all, row_index * own_rows, own_rows, 1)
    ada_shard = jnp.einsum("ic,io->co", own_silu, mod_grad_all, preferred_element_type=WIDE)
    own_columns = adab_weight.shape[1]
    adab_shard = jnp.sum(
        lax.dynamic_slice_in_dim(mod_grad_all, row_index * own_columns, own_columns, 1).astype(WIDE),
        axis=0,
    )
    silu_part = times_back(mod_grad_all, ada_low)
    row_images = 2 * images
    silu_part = jnp.broadcast_to(
        silu_part.reshape(row_devices, 1, row_images, -1), (row_devices, 2, row_images, own_rows)
    ).reshape(devices * row_images, own_rows)
    silu_part = lax.all_to_all(silu_part, ALL, split_axis=0, concat_axis=1, tiled=True)
    silu_grad = jnp.sum(silu_part.reshape(row_images, row_devices, 2, own_rows), axis=2)
    cond_grad = silu_back(silu_grad.reshape(row_images, -1))[0]

    rates = step_rates(tokens * devices)
    states_out = []
    states_out.extend(nesterov(qkv_weight, qkv_moment, qkv_average, qkv_shard, rates[0]))
    states_out.extend(nesterov(proj_weight, proj_moment, proj_average, proj_shard, rates[1]))
    states_out.extend(nesterov(fc1_weight, fc1_moment, fc1_average, fc1_shard, rates[2]))
    states_out.extend(nesterov(fc2_weight, fc2_moment, fc2_average, fc2_shard, rates[3]))
    states_out.extend(nesterov(bias_weight, bias_moment, bias_average, bias_shard, rates[4]))
    states_out.extend(nesterov(ada_weight, ada_moment, ada_average, ada_shard, rates[5]))
    states_out.extend(
        nesterov(adab_weight, adab_moment, adab_average, adab_shard.reshape(1, -1), rates[6])
    )
    return (block_out, x_grad, cond_grad) + tuple(states_out)


def solution(mesh):
    far = mesh.shape["dp"] // 4
    fine = Mesh(mesh.devices.reshape(far, 2, 2, mesh.shape["mod"]), ALL)
    tokens = P(ALL, None)
    images = P(ROWS, None)
    trunk = P(ROWS, "mod")
    bias = P(ALL)
    adab = P("mod", ROWS)
    states = (trunk,) * 12 + (bias,) * 3 + (trunk,) * 3 + (adab,) * 3
    return jax.shard_map(
        body,
        mesh=fine,
        in_specs=(tokens, images, bias, tokens) + states,
        out_specs=(tokens, tokens, images) + states,
        check_vma=False,
    )
```

```python
from functools import partial

import jax
import jax.numpy as jnp
from jax import lax
from jax.experimental import pallas as pl
from jax.experimental.pallas import tpu as pltpu
from jax.sharding import Mesh
from jax.sharding import PartitionSpec as P

D = 1152
HEADS = 16
HEAD = 72
FF = 4608
LANES = 128
CHUNK = 256

ROWS = ("far", "near", "core")
ALL = ("far", "near", "core", "mod")
LOW = jnp.bfloat16
WIDE = jnp.float32
LOG2E = 1.4426950408889634
NEG = -1e30
MESH = pl.DeviceIdType.MESH
VMEM = pl.BlockSpec(memory_space=pltpu.VMEM)
ANY = pl.BlockSpec(memory_space=pl.ANY)

EPS = 1e-06
MOMENTUM = 0.9
DECAY = 0.5


def step_rates(tokens_all):
    base_rate = tokens_all ** (-0.5)
    return (
        2.5 * D ** (-0.5) * base_rate,
        3.0 * D ** (-0.5) * base_rate,
        3.3 * D ** (-0.5) * base_rate,
        2.8 * FF ** (-0.5) * base_rate,
        0.5 * base_rate,
        2.0 * D ** (-0.5) * base_rate,
        0.3 * base_rate,
    )


def nesterov(weight, moment, average, gradient, rate):
    moment = MOMENTUM * moment + gradient
    weight = weight - rate * (gradient + MOMENTUM * moment)
    average = DECAY * average + (1.0 - DECAY) * weight
    return (weight, moment, average)


def places():
    return {name: lax.axis_index(name) for name in ALL}


def greet():
    here = places()
    count = lax.axis_size("far")
    others = [dict(far=lax.rem(here["far"] + d, count)) for d in range(1, count)]
    others += [{name: 1 - here[name]} for name in ("near", "core", "mod")]
    barrier = pltpu.get_barrier_semaphore()
    for other in others:
        pl.semaphore_signal(barrier, inc=1, device_id=other, device_id_type=MESH)
    pl.semaphore_wait(barrier, len(others))


def fetches(pairs, sems):
    return [
        pltpu.make_async_copy(source, target, sems.at[number])
        for number, (source, target) in enumerate(pairs)
    ]


def remote(source, target, sends, receives, slot, other):
    return pltpu.make_async_remote_copy(
        src_ref=source,
        dst_ref=target,
        send_sem=sends.at[slot],
        recv_sem=receives.at[slot],
        device_id=other,
        device_id_type=MESH,
    )


def messages(count):
    return count - 1 + 8


class Gather:
    def __init__(self, whole, sends, receives):
        self.whole, self.sends, self.receives = whole, sends, receives
        self.here = places()
        self.count = lax.axis_size("far")
        rows = whole.shape[4]
        self.rows = rows
        self.split = rows if rows % 8 else 8 * ((rows // 8 + 1) // 2)

    def _block(self, far):
        return self.whole.at[self.here["mod"], far, self.here["near"], self.here["core"]]

    def _far(self, shard, distance):
        far = self.here["far"]
        other = dict(far=lax.rem(far + distance, self.count))
        return remote(shard, self._block(far), self.sends, self.receives, distance - 1, other)

    def _far_came(self, shard, distance):
        origin = lax.rem(self.here["far"] + self.count - distance, self.count)
        return remote(
            shard, self._block(origin), self.sends, self.receives, distance - 1, dict(far=origin)
        )

    def start_far(self, shard, local):
        pltpu.make_async_copy(shard, self._block(self.here["far"]), local).start()
        for distance in range(1, self.count):
            self._far(shard, distance).start()

    def finish_far(self, shard, local):
        pltpu.make_async_copy(shard, self._block(self.here["far"]), local).wait()
        for distance in range(1, self.count):
            self._far(shard, distance).wait_send()
            self._far_came(shard, distance).wait_recv()

    def _quad(self, flips, first, size):
        near, core, mod = (
            1 - self.here[name] if name in flips else self.here[name] for name in ("near", "core", "mod")
        )
        return self.whole.at[mod, :, near, core, pl.ds(first, size)]

    def _step(self, name):
        head, rest = (0, self.split), (self.split, self.rows - self.split)
        full = (0, self.rows)
        return {
            "near": ((), "near", full, 0),
            "mod": ((), "mod", full, 1),
            "near_mod": (("near",), "mod", head, 2),
            "mod_near": (("mod",), "near", rest, 3),
            "core": ((), "core", full, 4),
            "near_core": (("near",), "core", full, 5),
            "mod_core": (("mod",), "core", full, 6),
            "both_core": (("near", "mod"), "core", full, 7),
        }[name]

    def _copy(self, name, incoming):
        flips, axis, span, slot = self._step(name)
        if span[1] == 0:
            return None
        quad = self._quad(flips + (axis,) if incoming else flips, *span)
        other = {axis: 1 - self.here[axis]}
        return remote(quad, quad, self.sends, self.receives, self.count - 1 + slot, other)

    def start(self, *names):
        for name in names:
            copy = self._copy(name, False)
            if copy is not None:
                copy.start()

    def receive(self, *names):
        for name in names:
            copy = self._copy(name, True)
            if copy is not None:
                copy.wait_recv()

    def spread(self):
        self.start("near", "mod", "core")

    def cross(self):
        self.receive("near")
        self.start("near_mod", "near_core")
        self.receive("mod")
        self.start("mod_near", "mod_core")

    def close(self):
        self.receive("near_mod", "mod_near")
        self.start("both_core")

    def end(self):
        self.receive("core", "near_core", "mod_core", "both_core")
        for name in (
            "near", "mod", "near_mod", "mod_near", "core", "near_core", "mod_core", "both_core",
        ):
            copy = self._copy(name, False)
            if copy is not None:
                copy.wait_send()


def gather_scratch(weights, locals_):
    count = lax.axis_size("far")
    shapes = [pltpu.SemaphoreType.DMA((messages(count),))] * (2 * weights)
    return shapes + [pltpu.SemaphoreType.DMA((locals_,))]


def whole_shape(shard):
    return jax.ShapeDtypeStruct((2, lax.axis_size("far"), 2, 2) + shard.shape, LOW)


def modulate(small_w, ada, table, local, small, partials, came_core, came_near, came_far, own, sends, receives):
    here = places()
    count = lax.axis_size("far")
    far, near, core, mod = (here[name] for name in ALL)
    row_devices = 4 * count
    rows = D // row_devices
    fetch = pltpu.make_async_copy(small_w, small, local)
    fetch.start()
    fetch.wait()
    device = (far * 2 + near) * 2 + core
    half = lax.div(device, row_devices // 2)
    first = lax.rem(device, row_devices // 2) * rows
    width = small.shape[-1]
    images = small.shape[-2]
    row = lax.broadcasted_iota(jnp.int32, (width, LANES), 0)
    column = lax.broadcasted_iota(jnp.int32, (width, LANES), 1)
    select = jnp.where(jnp.logical_and(row == first + column, column < rows), 1.0, 0.0).astype(LOW)
    for at in range(count):
        silu = small[half, at].reshape(4 * images, width).astype(WIDE).astype(LOW)
        mine = times(silu, select)
        mine = jnp.where(lanes(mine.shape) == rows, 1.0, mine).astype(LOW)
        partials[at] = times(mine, ada[...]).reshape(2, 2, images, -1)

    def move(source, target, slot, other):
        return remote(source, target, sends, receives, slot, other)

    to_core = move(partials.at[:, :, 1 - core], came_core, 0, dict(core=1 - core))
    to_core.start()
    to_core.wait()
    for at in range(count):
        partials[at, :, core] = partials[at, :, core] + came_core[at]
    to_near = move(partials.at[:, 1 - near, core], came_near, 1, dict(near=1 - near))
    to_near.start()
    yield
    to_near.wait()
    for at in range(count):
        partials[at, near, core] = partials[at, near, core] + came_near[at]
    copies = []
    for distance in range(1, count):
        target = lax.rem(far + distance, count)
        copies.append(
            move(partials.at[target, near, core], came_far.at[distance - 1], 2 + distance, dict(far=target))
        )
        copies[-1].start()
    yield
    total = partials[far, near, core]
    for distance, copy in enumerate(copies):
        copy.wait()
        total = total + came_far[distance]
    own[...] = total.astype(LOW).astype(WIDE)
    keep = pltpu.make_async_copy(own, table.at[mod], local)
    keep.start()
    to_mod = move(own, table.at[mod], 2, dict(mod=1 - mod))
    to_mod.start()
    yield
    keep.wait()
    to_mod.wait_send()
    move(own, table.at[1 - mod], 2, dict(mod=1 - mod)).wait_recv()


def first_kernel(*refs):
    small_s, *wide, ada = refs[:5]
    table = refs[9]
    rounded, gather_sems, (local, *parts) = refs[10:13], refs[13:21], refs[21:]
    qkv_s, proj_s, fc1_s = rounded
    for source, target in zip(wide, rounded):
        target[...] = source[...].astype(LOW)
    small, qkv, proj, fc1 = (
        Gather(w, s, r) for w, s, r in zip(refs[5:9], gather_sems[0::2], gather_sems[1::2])
    )
    greet()
    small.start_far(small_s, local.at[3])
    qkv.start_far(qkv_s, local.at[0])
    proj.start_far(proj_s, local.at[1])
    small.finish_far(small_s, local.at[3])
    small.spread()
    small.cross()
    small.close()
    small.end()
    stages = modulate(small.whole, ada, table, local.at[3], *parts)
    next(stages)
    qkv.finish_far(qkv_s, local.at[0])
    qkv.spread()
    next(stages)
    fc1.start_far(fc1_s, local.at[2])
    next(stages)
    qkv.cross()
    qkv.close()
    qkv.end()
    next(stages, None)
    proj.finish_far(proj_s, local.at[1])
    fc1.finish_far(fc1_s, local.at[2])


def first_gather(ada, *shards):
    count = lax.axis_size("far")
    small = whole_shape(shards[0])
    images = small.shape[4]
    columns = ada.shape[1]
    return pl.pallas_call(
        first_kernel,
        out_shape=tuple(whole_shape(shard) for shard in shards)
        + (jax.ShapeDtypeStruct((2, images, columns), WIDE),),
        in_specs=[VMEM] * 5,
        out_specs=(ANY,) * 5,
        scratch_shapes=[pltpu.VMEM(shard.shape, LOW) for shard in shards[1:]]
        + gather_scratch(4, 4)
        + [
            pltpu.VMEM(small.shape, LOW),
            pltpu.VMEM((count, 2, 2, images, columns), WIDE),
            pltpu.VMEM((count, 2, images, columns), WIDE),
            pltpu.VMEM((count, images, columns), WIDE),
            pltpu.VMEM((count - 1, images, columns), WIDE),
            pltpu.VMEM((images, columns), WIDE),
            pltpu.SemaphoreType.DMA((count + 2,)),
            pltpu.SemaphoreType.DMA((count + 2,)),
        ],
        compiler_params=pltpu.CompilerParams(
            collective_id=0, has_side_effects=True, vmem_limit_bytes=60 * 2**20
        ),
        name="first_gather",
    )(*shards, ada)


def lanes(shape): return lax.broadcasted_iota(jnp.int32, shape, 1)

def seg_codes(seg, n):
    lane = lanes((n, LANES))
    code = lane - HEAD
    inside = jnp.logical_and(code >= 0, code < 4)
    same = code == seg
    q = jnp.where(jnp.logical_and(inside, same), 1.0, 0.0)
    k = jnp.where(jnp.logical_and(inside, jnp.logical_not(same)), NEG, 0.0)
    return q, k

def head_of(wide_rows, start):
    return wide_rows[:, start:start+HEAD]

def pad_head(part, aug):
    n = part.shape[0]
    full = jnp.concatenate([part, jnp.zeros((n, LANES-HEAD), part.dtype)], axis=1)
    return jnp.where(lanes((n,LANES)) < HEAD, full, aug)

def split3(v):
    hi = v.astype(LOW).astype(WIDE)
    mid = (v - hi).astype(LOW).astype(WIDE)
    lo = v - hi - mid
    return hi, mid, lo


def attend_kernel(*refs):
    slots, x_hbm, table, bias, weight_hbm, seg_ref, fc2_s = refs[:7]
    act_turned, mixed_ref, turned_ref = refs[9:12]
    saved, (proj_w, fc1_w, fc2_w) = refs[12:16], refs[16:19]
    heads, (x_ref, weight, fetch_sems, *sems, local, save_sems) = refs[19:23], refs[23:]
    qh, kh, vh, oh = heads
    proj, fc1, fc2 = (
        Gather(w, s, r) for w, s, r in zip((proj_w, fc1_w, fc2_w), sems[0::2], sems[1::2])
    )
    greet()
    fc2.start_far(fc2_s, local.at[0])
    proj.spread()
    fc1.spread()
    loads = fetches(((x_hbm, x_ref), (weight_hbm, weight)), fetch_sems)
    for load in loads:
        load.start()
    for load in loads:
        load.wait()

    T = x_ref.shape[0]

    def fill(i, carry):
        rows = pl.ds(pl.multiple_of(i * CHUNK, CHUNK), CHUNK)
        slot = slots[i]
        h1, _ = normed(x_ref[rows, :].astype(WIDE))
        act = (h1 * (1.0 + row_of(table, slot, 1)) + row_of(table, slot, 0)).astype(LOW)
        act_turned[:, rows] = act.T
        joint = jnp.concatenate([times(act, weight[0]), times(act, weight[1])], axis=1)
        joint = (joint + bias[...]).astype(LOW)
        lane = lanes((CHUNK, LANES))
        qc, kc = seg_codes(seg_ref[rows, :], CHUNK)
        qc = qc.astype(LOW)
        kc = jnp.where(jnp.logical_and(lane >= HEAD + 4, lane < HEAD + 7), 1.0, kc).astype(LOW)
        ones = jnp.where(jnp.logical_and(lane >= HEAD, lane < HEAD+3), 1.0, 0.0).astype(LOW)
        for h in range(HEADS):
            qh[h, rows, :] = pad_head(joint[:, h*HEAD:(h+1)*HEAD], qc)
            kh[h, rows, :] = pad_head(joint[:, D+h*HEAD:D+(h+1)*HEAD], kc)
            vh[h, rows, :] = pad_head(joint[:, 2*D+h*HEAD:2*D+(h+1)*HEAD], ones)
        pl.when(i == 2)(proj.cross)
        return carry
    lax.fori_loop(0, T//CHUNK, fill, 0)

    def save(number):
        return pltpu.make_async_copy(heads[number], saved[number], save_sems.at[number])

    save(1).start()
    save(2).start()
    def head(h, carry):
        k = kh[h]; v = vh[h]
        for i in range(T//CHUNK):
            rows = pl.ds(i*CHUNK, CHUNK)
            q = qh[h, rows, :]
            s = lax.dot_general(q, k, (((1,),(1,)),((),())), preferred_element_type=WIDE)
            m = jnp.max(s, axis=1, keepdims=True)
            p = jnp.exp2((s - m)*(HEAD**-0.5*LOG2E)).astype(LOW)
            o = jnp.dot(p, v, preferred_element_type=WIDE)
            l = o[:, HEAD:HEAD+1]
            oh[h, rows, :] = (o / l).astype(LOW)
            hi, mid, lo = split3(-(m + jnp.log(l) * HEAD**0.5))
            lane = lanes((CHUNK, LANES))
            q = jnp.where(lane == HEAD + 4, hi.astype(LOW), q)
            q = jnp.where(lane == HEAD + 5, mid.astype(LOW), q)
            qh[h, rows, :] = jnp.where(lane == HEAD + 6, lo.astype(LOW), q)
        tasks = {
            3: lambda: (fc2.finish_far(fc2_s, local.at[0]), fc2.spread()),
            6: fc1.cross,
            8: proj.close,
            10: proj.end,
        }
        for at, task in tasks.items():

            @pl.when(h == at)
            def _(task=task):
                task()

        return carry
    lax.fori_loop(0, HEADS, head, 0)
    save(0).start()
    save(3).start()

    def drain(i, carry):
        rows = pl.ds(pl.multiple_of(i*CHUNK, CHUNK), CHUNK)
        mixed = jnp.concatenate([oh[h, rows, :][:, :HEAD] for h in range(HEADS)], axis=1)
        mixed_ref[rows, :] = mixed
        turned_ref[:, rows] = mixed.T
        return carry
    lax.fori_loop(0, T//CHUNK, drain, 0)
    fc2.cross()
    fc1.close()
    fc1.end()
    fc2.close()
    fc2.end()
    for number in range(4):
        save(number).wait()


def attend(slots, x_in, table, bias, weight, segments, fc2_s, proj_w, fc1_w):
    tokens = x_in.shape[0]
    wide = HEADS * HEAD
    heads = (HEADS, tokens, LANES)
    out = pl.pallas_call(
        attend_kernel,
        out_shape=(
            jax.ShapeDtypeStruct((wide, tokens), LOW),
            jax.ShapeDtypeStruct((tokens, wide), LOW),
            jax.ShapeDtypeStruct((wide, tokens), LOW),
        )
        + (jax.ShapeDtypeStruct(heads, LOW),) * 4
        + (
            jax.ShapeDtypeStruct(proj_w.shape, LOW),
            jax.ShapeDtypeStruct(fc1_w.shape, LOW),
            whole_shape(fc2_s),
        ),
        in_specs=[pl.BlockSpec(memory_space=pltpu.SMEM), ANY, VMEM, VMEM, ANY, VMEM, VMEM, ANY, ANY],
        out_specs=(VMEM,) * 3 + (ANY,) * 7,
        scratch_shapes=[pltpu.VMEM(heads, LOW)] * 4
        + [pltpu.VMEM(x_in.shape, LOW), pltpu.VMEM(weight.shape, LOW), pltpu.SemaphoreType.DMA((2,))]
        + gather_scratch(3, 1)
        + [pltpu.SemaphoreType.DMA((4,))],
        input_output_aliases={7: 7, 8: 8},
        compiler_params=pltpu.CompilerParams(
            collective_id=1, has_side_effects=True, vmem_limit_bytes=60 * 2**20
        ),
        name="attend",
    )(slots, x_in, table, bias, weight, segments.reshape(tokens, 1), fc2_s, proj_w, fc1_w)
    return out[0], out[1], out[2], out[3:7], out[7:]


def row_spans(rows):
    first = rows if rows % 8 else 8 * ((rows // 8 + 1) // 2)
    return [(0, first)] + ([(first, rows - first)] if first < rows else [])


class Reduce:
    def __init__(self, part, span, first, came, joint, total, base, sems, loads=False):
        self.part, self.span, self.first = part, span, first
        self.second = "near" if first == "mod" else "mod"
        self.came_both, self.came_first, self.came_second, self.came_far = came
        self.joint, self.total_, self.base = joint, total, base
        self.sends, self.receives, self.locals_ = sems
        self.loads = loads
        self.here = places()
        self.count = lax.axis_size("far")

    def _swap(self, source, target, slot, axis):
        return remote(source, target, self.sends, self.receives, slot, {axis: 1 - self.here[axis]})

    def _both(self):
        return self._swap(self.part("near", "mod"), self.came_both, 0, self.first)

    def _first(self):
        return self._swap(self.part(self.first), self.came_first, 1, self.first)

    def _second(self):
        return self._swap(self.joint, self.came_second, 2, self.second)

    def _load(self, number):
        source, target = ((self.part(self.second), self.joint), (self.part(), self.total_))[number]
        return pltpu.make_async_copy(source, target, self.locals_.at[number])

    def _far(self, distance):
        target = lax.rem(self.here["far"] + distance, self.count)
        return remote(
            self.total_.at[target],
            self.came_far.at[distance - 1],
            self.sends,
            self.receives,
            2 + distance,
            dict(far=target),
        )

    def start_ahead(self):
        self._both().start()
        if self.first == "near":
            self._first().start()

    def start_rest(self):
        if self.first == "mod":
            self._first().start()

    def start(self):
        self._both().start()
        self._first().start()
        if self.loads:
            self._load(0).start()
            self._load(1).start()

    def merge(self):
        if self.loads:
            self._load(0).wait()
        self._both().wait_recv()

        def add(at, carry):
            self.joint[at] = (self.joint[at].astype(WIDE) + self.came_both[at].astype(WIDE)).astype(LOW)
            return carry

        lax.fori_loop(0, self.count, add, 0)
        self._second().start()

    def total(self):
        if self.loads:
            self._load(1).wait()
        self._first().wait_recv()
        self._second().wait_recv()

        def add(at, carry):
            self.total_[at] = (
                self.base[at].astype(WIDE)
                + self.came_first[at].astype(WIDE)
                + self.came_second[at].astype(WIDE)
            ).astype(LOW)
            return carry

        lax.fori_loop(0, self.count, add, 0)
        self._both().wait_send()
        self._first().wait_send()
        self._second().wait_send()

    def early(self):
        second = self.part(self.second)
        self._both().wait_recv()
        self._first().wait_recv()

        def add(at, carry):
            self.joint[at] = (second[at].astype(WIDE) + self.came_both[at].astype(WIDE)).astype(LOW)
            self.total_[at] = (self.base[at].astype(WIDE) + self.came_first[at].astype(WIDE)).astype(LOW)
            return carry

        lax.fori_loop(0, self.count, add, 0)
        self._both().wait_send()
        self._first().wait_send()

    def _load_base(self):
        return pltpu.make_async_copy(self.base, self.total_, self.locals_.at[1])

    def late_start(self):
        self._load_base().start()
        self._second().start()

    def late_total(self):
        self._load_base().wait()
        self._second().wait_recv()

        def add(at, carry):
            self.total_[at] = (self.total_[at].astype(WIDE) + self.came_second[at].astype(WIDE)).astype(LOW)
            return carry

        lax.fori_loop(0, self.count, add, 0)
        self._second().wait_send()

    def start_far(self):
        for distance in range(1, self.count):
            self._far(distance).start()

    def final(self, out):
        value = self.total_[self.here["far"]].astype(WIDE)
        for distance in range(1, self.count):
            self._far(distance).wait_recv()
            value = value + self.came_far[distance - 1].astype(WIDE)
        out[pl.ds(*self.span), :] = value
        for distance in range(1, self.count):
            self._far(distance).wait_send()


ORDERS = ("mod", "near")


def run(parts, *names):
    for part in parts:
        for name in names:
            getattr(part, name)()


def span_part(sums, span):
    def part(*flips):
        near, mod = (
            1 - lax.axis_index(name) if name in flips else lax.axis_index(name) for name in ("near", "mod")
        )
        return sums.at[mod, near, :, pl.ds(*span)]

    return part


def take(scratch, number):
    return scratch[:number], scratch[number:]


def came_scratch(count, span, columns, far=True):
    block = (count, span[1], columns)
    shapes = [pltpu.VMEM(block, LOW)] * 3
    return shapes + ([pltpu.VMEM((count - 1,) + block[1:], LOW)] if far else [])


def sem_scratch(count):
    return [pltpu.SemaphoreType.DMA((count + 2,))] * 2 + [pltpu.SemaphoreType.DMA((2,))]


def loaded_scratch(shape, total=True):
    count, rows, columns = shape[2:]
    shapes = []
    for span in row_spans(rows):
        shapes += came_scratch(count, span, columns, total)
        shapes += [pltpu.VMEM((count, span[1], columns), LOW)] * (2 if total else 1)
        shapes += sem_scratch(count)
    return shapes


def loaded_reduces(sums, scratch, totals=None):
    reduces = []
    for number, span in enumerate(row_spans(sums.shape[3])):
        came, scratch = take(scratch, 4 if totals is None else 3)
        came = list(came) + [None] * (4 - len(came))
        (joint,), scratch = take(scratch, 1)
        if totals is None:
            (total,), scratch = take(scratch, 1)
        else:
            total = totals[number]
        sems, scratch = take(scratch, 3)
        reduces.append(
            Reduce(span_part(sums, span), span, ORDERS[number], came, joint, total, total, sems, True)
        )
    return reduces, scratch


def resident_scratch(shape, far=True):
    count, rows, columns = shape[2:]
    shapes = []
    for span in row_spans(rows):
        shapes += came_scratch(count, span, columns, far) + sem_scratch(count)
    return shapes


def resident_reduces(sums, scratch, totals=None, joints=None):
    reduces = []
    for number, span in enumerate(row_spans(sums.shape[3])):
        came, scratch = take(scratch, 4 if totals is None else 3 if joints is None else 2)
        sems, scratch = take(scratch, 3)
        part = span_part(sums, span)
        order = ORDERS[number]
        own = part()
        total = own if totals is None else totals[number]
        came = list(came) + [None] * (4 - len(came))
        joint = part("near" if order == "mod" else "mod") if joints is None else joints[number]
        reduces.append(Reduce(part, span, order, came, joint, total, own, sems))
    return reduces, scratch


def early_scratch(shape):
    count, rows, columns = shape[2:]
    shapes = []
    for span in row_spans(rows):
        shapes += [pltpu.VMEM((count, span[1], columns), LOW)] * 2 + sem_scratch(count)
    return shapes


def late_scratch(bases):
    shapes = []
    for base in bases:
        far = pltpu.VMEM((base.shape[0] - 1,) + base.shape[1:], LOW)
        shapes += [pltpu.VMEM(base.shape, LOW)] * 2 + [far] + sem_scratch(base.shape[0])
    return shapes


def late_reduces(joints, bases, rows, scratch):
    reduces = []
    for number, span in enumerate(row_spans(rows)):
        (came, total, came_far), scratch = take(scratch, 3)
        sems, scratch = take(scratch, 3)
        came = (None, None, came, came_far)
        reduces.append(
            Reduce(None, span, ORDERS[number], came, joints[number], total, bases[number], sems)
        )
    return reduces, scratch


def far_scratch(totals):
    shapes = []
    for total in totals:
        count = total.shape[0]
        shapes += [pltpu.VMEM((count - 1,) + total.shape[1:], LOW)] + sem_scratch(count)[:2]
    return shapes


def far_reduces(totals, rows, scratch):
    reduces = []
    for total, span in zip(totals, row_spans(rows)):
        (came, sends, receives), scratch = take(scratch, 3)
        came = (None, None, None, came)
        reduces.append(Reduce(None, span, "mod", came, None, total, total, (sends, receives, None)))
    return reduces, scratch


class Product:
    def __init__(self, left, right, scratch):
        self.left, self.right = left, right
        self.rows_, self.sums, self.came, self.loads, self.sends, self.receives = scratch
        self.core = lax.axis_index("core")
        near = lax.axis_index("near")
        self.nears = (1 - near, near)

    @staticmethod
    def scratch(count, rows, tokens, columns):
        sums = pltpu.VMEM((2, 2, count, rows, columns), LOW)
        sems = [pltpu.SemaphoreType.DMA((4,))] * 3
        return [pltpu.VMEM((2, count, rows, tokens), LOW), sums, sums] + sems

    def _load(self, near, own):
        core = self.core if own else 1 - self.core
        return pltpu.make_async_copy(
            self.left.at[:, near, core], self.rows_.at[near], self.loads.at[2 * own + near]
        )

    def load(self):
        for near in self.nears:
            self._load(near, 0).start()

    def _copy(self, mod, near):
        return remote(
            self.sums.at[mod, near],
            self.came.at[mod, near],
            self.sends,
            self.receives,
            2 * mod + near,
            dict(core=1 - self.core),
        )

    def _blocks(self, near, own, store):
        count, rows, tokens = self.rows_.shape[1:]
        columns = self.right.shape[2]
        self._load(near, own).wait()
        left = self.rows_[near].reshape(count * rows, tokens)
        width = columns if columns <= 1024 else columns // 2
        width = width if width % LANES == 0 else columns
        for mod in (0, 1):
            for at in range(0, columns, width):
                product = times(left, self.right[mod, :, at : at + width])
                store(mod, at, width, product.reshape(count, rows, width))

    def send(self):
        for near in self.nears:

            def store(mod, at, width, product, near=near):
                self.sums[mod, near, :, :, at : at + width] = product.astype(LOW)

            self._blocks(near, 0, store)
            self._load(near, 1).start()
            for mod in (0, 1):
                self._copy(mod, near).start()

    def sum(self, reduces=()):
        for near, names in zip(self.nears, ("start_ahead", "start_rest")):
            for mod in (0, 1):
                self._copy(mod, near).wait_send()
                self._copy(mod, near).wait_recv()

            def store(mod, at, width, product, near=near):
                came = self.came[mod, near, :, :, at : at + width]
                self.sums[mod, near, :, :, at : at + width] = (product + came.astype(WIDE)).astype(LOW)

            self._blocks(near, 1, store)
            run(reduces, names)


def total_shapes(count, rows, columns):
    return [jax.ShapeDtypeStruct((count, span[1], columns), LOW) for span in row_spans(rows)]


def weight_kernel(*refs, modes, spans):
    sides, refs = take(refs, 2 * len(modes))
    outs = []
    for mode, count in zip(modes, spans):
        used, refs = take(refs, {"whole": count, "early": 2 * count, "chip": 1}[mode])
        outs.append(used)
    fetch_sems, *scratch = refs
    rights, scratch = take(scratch, len(modes) - 1)
    products, reduces = [], []
    for number in range(len(modes)):
        used, scratch = take(scratch, 6)
        right = rights[number - 1] if number else sides[1]
        products.append(Product(sides[2 * number], right, used))
    loads = fetches(list(zip(sides[3::2], rights)), fetch_sems)
    for mode, count, product, out in zip(modes, spans, products, outs):
        parts = []
        if mode == "whole":
            parts, scratch = resident_reduces(product.sums, scratch, out)
        elif mode == "early":
            parts, scratch = resident_reduces(product.sums, scratch, out[count:], out[:count])
        reduces.append(parts)
    (out_sem,) = scratch
    products[0].load()
    for load in loads:
        load.start()
    greet()
    copies = []
    for number, product in enumerate(products):
        before = number and modes[number - 1] == "whole"
        if number:
            loads[number - 1].wait()
        product.send()
        if before:
            run(reduces[number - 1], "merge")
        if number + 1 < len(products):
            products[number + 1].load()
        product.sum(reduces[number])
        if before:
            run(reduces[number - 1], "total")
        if modes[number] == "chip":
            copies.append(pltpu.make_async_copy(product.sums, outs[number][0], out_sem.at[0]))
            copies[-1].start()
    for number, mode in enumerate(modes):
        if mode == "early":
            run(reduces[number], "early")
    for copy in copies:
        copy.wait()


def weight_call(pairs, modes, number):
    count = pairs[0][0].shape[0]
    tokens = pairs[0][0].shape[4]
    products, sums, shapes, specs, spans = [], [], [], [], []
    for (left, right), mode in zip(pairs, modes):
        rows, columns = left.shape[3], right.shape[2]
        shape = (2, 2, count, rows, columns)
        products += Product.scratch(count, rows, tokens, columns)
        totals = total_shapes(count, rows, columns)
        spans.append(len(totals))
        if mode == "chip":
            shapes.append(jax.ShapeDtypeStruct(shape, LOW))
            specs.append(ANY)
        else:
            sums += resident_scratch(shape, False) if mode == "whole" else early_scratch(shape)
            outs = totals * (1 if mode == "whole" else 2)
            shapes += outs
            specs += [VMEM] * len(outs)
    out = pl.pallas_call(
        partial(weight_kernel, modes=modes, spans=tuple(spans)),
        out_shape=tuple(shapes),
        in_specs=[ANY, VMEM] + [ANY, ANY] * (len(pairs) - 1),
        out_specs=tuple(specs),
        scratch_shapes=[pltpu.SemaphoreType.DMA((len(pairs),))]
        + [pltpu.VMEM(right.shape, LOW) for _, right in pairs[1:]]
        + products
        + sums
        + [pltpu.SemaphoreType.DMA((1,))],
        compiler_params=pltpu.CompilerParams(
            collective_id=number, has_side_effects=True, vmem_limit_bytes=63 * 2**20
        ),
        name="weight_grads",
    )(*[side for pair in pairs for side in pair])
    return out, spans


def weight_grads(hidden, branch, mlp, pre, mixed, attn):
    proj, fc2, fc1 = (mixed, attn), (hidden, branch), (mlp, pre)
    if mlp.shape[3] % 8 == 0:
        out, spans = weight_call([proj, fc2, fc1], ("whole", "early", "chip"), 4)
        first, second = spans[0], spans[0] + spans[1]
        return out[:first], out[first:second], out[second:-1], out[-1]
    early, spans = weight_call([fc2], ("early",), 4)
    rest, _ = weight_call([proj, fc1], ("whole", "chip"), 5)
    return rest[:-1], early[: spans[0]], early[spans[0] :], rest[-1]


def tile_sums_by_slot(chooser, sums):
    total = None
    for at, row in enumerate(sums):
        part = chooser[:, at : at + 1] * row
        total = part if total is None else total + part
    return total


def last_kernel(*refs, spans):
    slots, act, joint, x_hbm, dx1_hbm, weight_hbm, table, mid_sums, pre_sums, chooser = refs[:10]
    totals, refs = take(refs[10:], spans)
    qkv_out, fc1_out, small_w, x_grad_ref, *scratch = refs
    qkv_scratch, scratch = take(scratch, 6)
    qkv = Product(act, joint, qkv_scratch)
    qkv_sum, scratch = resident_reduces(qkv.sums, scratch)
    fc1_sum, scratch = far_reduces(totals, fc1_out.shape[0], scratch)
    small_sends, small_receives, local, first_sums, joint_sums, small_s, *scratch = scratch
    x_ref, dx1_ref, weight, fetch_sems = scratch
    loads = fetches(((x_hbm, x_ref), (dx1_hbm, dx1_ref), (weight_hbm, weight)), fetch_sems)
    small = Gather(small_w, small_sends, small_receives)
    tiles = x_ref.shape[0] // CHUNK
    qkv.load()
    greet()
    run(fc1_sum, "start_far")
    for load in loads:
        load.start()
    qkv.send()
    qkv.sum(qkv_sum)
    for load in loads:
        load.wait()

    def back(at, carry):
        rows = pl.ds(pl.multiple_of(at * CHUNK, CHUNK), CHUNK)
        dact = times_across(joint[0, rows, :], weight[0]) + times_across(joint[1, rows, :], weight[1])
        h1, inverse = normed(x_ref[rows, :].astype(WIDE))
        first_sums[at, 0:1, :] = column_sums(dact)
        first_sums[at, 1:2, :] = column_sums(dact * h1)
        dh1 = dact * (1.0 + row_of(table, slots[at], 1))
        x_grad_ref[rows, :] = dx1_ref[rows, :] + inverse * (
            dh1
            - jnp.mean(dh1, axis=-1, keepdims=True)
            - h1 * jnp.mean(dh1 * h1, axis=-1, keepdims=True)
        )
        for side in range(2):
            joint_sums[side : side + 1, :] += column_sums(joint[side, rows, :].astype(WIDE))

        @pl.when(at == tiles // 2 - 1)
        def _():
            run(qkv_sum, "merge")

        return carry

    joint_sums[...] = jnp.zeros_like(joint_sums)
    lax.fori_loop(0, tiles, back, 0)
    choose = chooser[...]
    upper = lax.broadcasted_iota(jnp.int32, (choose.shape[0], D), 0) < choose.shape[0] // 2
    groups = (
        [first_sums[at, 0:1, :] for at in range(tiles)],
        [first_sums[at, 1:2, :] for at in range(tiles)],
    ) + tuple([mid_sums[at, row : row + 1, :] for at in range(tiles)] for row in range(4))
    for group in range(3):
        value = jnp.where(
            upper, tile_sums_by_slot(choose, groups[group]), tile_sums_by_slot(choose, groups[group + 3])
        )
        small_s[0:8, group * D : (group + 1) * D] = value.astype(LOW)
    pre = pre_sums[...]
    tile_rows = [column_sums(mid_sums[:, row, :]) for row in (4, 5)]
    biases = (
        (joint_sums[0:1, :D], joint_sums[1:2, D // 2 :], tile_rows[0]),
        tuple(pre[:, at * D : (at + 1) * D] for at in range(3)),
        (pre[:, 3 * D :], tile_rows[1], jnp.zeros((1, D), WIDE)),
    )
    blank = jnp.zeros((5, D), WIDE)
    for group in range(3):
        rows = jnp.concatenate([biases[row][group] for row in range(3)] + [blank], axis=0)
        small_s[8:16, group * D : (group + 1) * D] = rows.astype(LOW)
    small.start_far(small_s, local.at[0])
    small.finish_far(small_s, local.at[0])
    small.spread()
    run(qkv_sum, "total", "start_far")
    small.cross()
    small.close()
    small.end()
    for part in fc1_sum:
        part.final(fc1_out)
    for part in qkv_sum:
        part.final(qkv_out)


def last_scatter(slots, act, joint, x_in, dx1, table, weight, mid_sums, pre_sums, chooser, totals):
    count, _, _, rows, tokens = act.shape
    fc1_columns = totals[0].shape[2]
    columns = joint.shape[2]
    small_s = jax.ShapeDtypeStruct((16, 3 * D), LOW)
    return pl.pallas_call(
        partial(last_kernel, spans=len(totals)),
        out_shape=(
            jax.ShapeDtypeStruct((rows, columns), WIDE),
            jax.ShapeDtypeStruct((sum(total.shape[1] for total in totals), fc1_columns), WIDE),
            whole_shape(small_s),
            jax.ShapeDtypeStruct((tokens, D), WIDE),
        ),
        in_specs=[pl.BlockSpec(memory_space=pltpu.SMEM), ANY, VMEM, ANY, ANY, ANY]
        + [VMEM] * (4 + len(totals)),
        out_specs=(VMEM, VMEM, ANY, VMEM),
        scratch_shapes=Product.scratch(count, rows, tokens, columns)
        + resident_scratch((2, 2, count, rows, columns))
        + far_scratch(totals)
        + gather_scratch(1, 1)
        + [
            pltpu.VMEM((tokens // CHUNK, 8, D), WIDE),
            pltpu.VMEM((2, columns), WIDE),
            pltpu.VMEM(small_s.shape, LOW),
            pltpu.VMEM(x_in.shape, LOW),
            pltpu.VMEM(dx1.shape, WIDE),
            pltpu.VMEM(weight.shape, LOW),
            pltpu.SemaphoreType.DMA((3,)),
        ],
        compiler_params=pltpu.CompilerParams(
            collective_id=3, has_side_effects=True, vmem_limit_bytes=63 * 2**20
        ),
        name="last_scatter",
    )(slots, act, joint, x_in, dx1, weight, table, mid_sums, pre_sums, chooser, *totals)


def attend_back_kernel(*refs, counts):
    up_ref, heads, fc1_sums = refs[0], refs[1:5], refs[5]
    proj_totals, refs = take(refs[6:], counts[0])
    joints, refs = take(refs, counts[1])
    bases, refs = take(refs, counts[1])
    out_ref, fc2_out, proj_out, *refs = refs
    fc1_totals, refs = take(refs, counts[2])
    qh, kh, vh, uh, oh, load_sems, leave, leave_sems, *scratch = refs
    fc1, scratch = loaded_reduces(fc1_sums, scratch, fc1_totals)
    proj, scratch = far_reduces(proj_totals, proj_out.shape[0], scratch)
    fc2, scratch = late_reduces(joints, bases, fc2_out.shape[0], scratch)
    T = up_ref.shape[0]
    chunks = T // CHUNK

    def load(number):
        return pltpu.make_async_copy(heads[number], (qh, kh, vh, oh)[number], load_sems.at[number])

    for number in (3, 0, 1, 2):
        load(number).start()
    greet()
    run(fc2, "late_start")
    run(proj, "start_far")
    run(fc1, "start")
    load(3).wait()

    def fill(i, carry):
        rows = pl.ds(pl.multiple_of(i * CHUNK, CHUNK), CHUNK)
        lane = lanes((CHUNK, LANES))
        for h in range(HEADS):
            u = pad_head(up_ref[rows, h * HEAD : (h + 1) * HEAD], jnp.zeros((CHUNK, LANES), LOW))
            delta = jnp.sum(u.astype(WIDE) * oh[h, rows, :].astype(WIDE), axis=1, keepdims=True)
            hi, mid, lo = split3(-delta)
            u = jnp.where(lane == HEAD, hi.astype(LOW), u)
            u = jnp.where(lane == HEAD + 1, mid.astype(LOW), u)
            uh[h, rows, :] = jnp.where(lane == HEAD + 2, lo.astype(LOW), u)
        return carry

    lax.fori_loop(0, chunks, fill, 0)
    for number in range(3):
        load(number).wait()
    across = (((1,), (1,)), ((), ()))
    tasks = {
        4: lambda: run(fc2, "late_total", "start_far"),
        9: lambda: run(fc1, "merge"),
    }

    def head(h, carry):
        k = kh[h]
        v = vh[h]
        kt = k.T
        dk = jnp.zeros((T, LANES), WIDE)
        dv = jnp.zeros((T, LANES), WIDE)
        for i in range(chunks):
            rows = pl.ds(i * CHUNK, CHUNK)
            q = qh[h, rows, :]
            u = uh[h, rows, :]
            s = lax.dot_general(k, q, across, preferred_element_type=WIDE)
            p = jnp.exp2(s * (HEAD**-0.5 * LOG2E))
            dp = lax.dot_general(v, u, across, preferred_element_type=WIDE)
            ds = (p * dp).astype(LOW)
            dv = dv + jnp.dot(p.astype(LOW), u, preferred_element_type=WIDE)
            dk = dk + jnp.dot(ds, q, preferred_element_type=WIDE)
            dqt = jnp.dot(kt, ds, preferred_element_type=WIDE)
            qh[h, rows, :] = (dqt.T * HEAD**-0.5).astype(LOW)
        kh[h] = (dk * HEAD**-0.5).astype(LOW)
        vh[h] = dv.astype(LOW)
        for at, task in tasks.items():

            @pl.when(h == at)
            def _(task=task):
                task()

        return carry

    lax.fori_loop(0, HEADS, head, 0)

    def store(i, side):
        rows = pl.ds(pl.multiple_of(i * CHUNK, CHUNK), CHUNK)
        return pltpu.make_async_copy(
            leave.at[side], out_ref.at[side, rows], leave_sems.at[side]
        )

    def drain(i, carry):
        rows = pl.ds(pl.multiple_of(i * CHUNK, CHUNK), CHUNK)
        parts = [g[h, rows, :][:, :HEAD] for g in (qh, kh, vh) for h in range(HEADS)]
        for side in range(2):

            @pl.when(i > 0)
            def _(side=side):
                store(i - 1, side).wait()

            own = parts[side * len(parts) // 2 : (side + 1) * len(parts) // 2]
            leave[side] = jnp.concatenate(own, axis=1)
            store(i, side).start()
        return carry

    lax.fori_loop(0, chunks, drain, 0)
    run(fc1, "total")
    for side in range(2):
        store(chunks - 1, side).wait()
    for part in fc2:
        part.final(fc2_out)
    for part in proj:
        part.final(proj_out)


def attend_back(upstream, heads, fc1_sums, proj_totals, joints, bases):
    tokens = upstream.shape[0]
    count, rows, columns = fc1_sums.shape[2:]
    totals = total_shapes(count, rows, columns)

    def shard(parts):
        return jax.ShapeDtypeStruct((sum(part.shape[1] for part in parts), parts[0].shape[2]), WIDE)

    out = pl.pallas_call(
        partial(attend_back_kernel, counts=(len(proj_totals), len(joints), len(totals))),
        out_shape=(
            jax.ShapeDtypeStruct((2, tokens, 3 * HEADS * HEAD // 2), LOW),
            shard(bases),
            shard(proj_totals),
        )
        + tuple(totals),
        in_specs=[VMEM] + [ANY] * 5 + [VMEM] * len(proj_totals) + [ANY] * (2 * len(joints)),
        out_specs=(ANY, VMEM, VMEM) + (VMEM,) * len(totals),
        scratch_shapes=[pltpu.VMEM((HEADS, tokens, LANES), LOW)] * 5
        + [pltpu.SemaphoreType.DMA((4,))]
        + [pltpu.VMEM((2, CHUNK, 3 * HEADS * HEAD // 2), LOW), pltpu.SemaphoreType.DMA((2,))]
        + loaded_scratch(fc1_sums.shape, False)
        + far_scratch(proj_totals)
        + late_scratch(bases),
        compiler_params=pltpu.CompilerParams(
            collective_id=2, has_side_effects=True, vmem_limit_bytes=63 * 2**20
        ),
        name="attend_back",
    )(upstream, *heads, fc1_sums, *proj_totals, *joints, *bases)
    return out[0], out[1], out[2], out[3:]


def normed(values):
    centre = values - jnp.mean(values, axis=-1, keepdims=True)
    inverse = lax.rsqrt(jnp.mean(centre * centre, axis=-1, keepdims=True) + EPS)
    return centre * inverse, inverse


def row_of(table, slot, group):
    return table[pl.ds(slot, 1), group * D : (group + 1) * D]


def column_sums(values):
    return jnp.sum(values, axis=0, keepdims=True)


def times_across(left, right):
    return lax.dot_general(left, right, (((1,), (1,)), ((), ())), preferred_element_type=WIDE)


def fixed(*shape):
    return pl.BlockSpec(
        shape, lambda i, slots: (0,) * len(shape), pipeline_mode=pl.Buffered(1)
    )


GELU = 0.7978845608028654
CUBIC = 0.044715
SPAN = 768
BLOCK = 512


def middle_kernel(
    slots, x_ref, g_ref, mixed_ref, table, bias, bias1, proj, fc1, fc2,
    block_ref, mlp_turned, hidden_turned, dpre_ref, dbranch_ref, dattn_ref, dmixed_ref, dx1_ref, sums_ref, dpre_sums,
    attn_out, mlp, branch,
):
    step = pl.program_id(0)
    tokens = x_ref.shape[0]

    @pl.when(step == 0)
    def _():
        def enter(tile_at, carry):
            rows = pl.ds(pl.multiple_of(tile_at * CHUNK, CHUNK), CHUNK)
            slot = slots[tile_at]
            gate1, shift2, scale2, gate2 = (row_of(table, slot, group) for group in (2, 3, 4, 5))
            mixed = mixed_ref[rows, :]
            out = jnp.concatenate([times(mixed, proj[0]), times(mixed, proj[1])], axis=1)
            out = out + bias[:, 2 * D : 3 * D]
            attn_out[rows, :] = out
            h2, _ = normed(x_ref[rows, :].astype(WIDE) + gate1 * out)
            mlp_in = (h2 * (1.0 + scale2) + shift2).astype(LOW)
            mlp[rows, :] = mlp_in
            mlp_turned[:, rows] = mlp_in.T
            dbranch = (gate2 * g_ref[rows, :].astype(WIDE)).astype(LOW)
            sums_ref[tile_at, 5:6, :] = column_sums(dbranch.astype(WIDE))
            dbranch_ref[0, rows, :] = dbranch[:, : D // 2]
            dbranch_ref[1, rows, :] = dbranch[:, D // 2 :]
            return carry

        lax.fori_loop(0, tokens // CHUNK, enter, 0)
        branch[...] = jnp.zeros_like(branch)
        dx1_ref[...] = jnp.zeros_like(dx1_ref)

    total = None
    for first in range(0, tokens, BLOCK):
        rows = slice(first, first + BLOCK)
        pre = times(mlp[rows, :], fc1[0]) + bias1[0]
        square = pre * pre
        bend = jnp.tanh(GELU * pre * (1.0 + CUBIC * square))
        rise = 0.5 * (1.0 + bend)
        hidden = (pre * rise).astype(LOW)
        hidden_turned[:, rows] = hidden.T
        for side in range(2):
            branch[side, rows] += times(hidden, fc2[side])
        slope = rise + 0.5 * GELU * pre * (1.0 - bend * bend) * (1.0 + 3.0 * CUBIC * square)
        dhidden = times_across(dbranch_ref[0, rows], fc2[0]) + times_across(dbranch_ref[1, rows], fc2[1])
        dpre = (dhidden * slope).astype(LOW)
        dpre_ref[0, rows] = dpre
        part = column_sums(dpre.astype(WIDE))
        total = part if total is None else total + part
        dx1_ref[rows, :] += times_across(dpre, fc1[0])
    dpre_sums[...] = total

    @pl.when(step == pl.num_programs(0) - 1)
    def _():
        def leave(tile_at, carry):
            rows = pl.ds(pl.multiple_of(tile_at * CHUNK, CHUNK), CHUNK)
            slot = slots[tile_at]
            gate1, scale2, gate2 = (row_of(table, slot, group) for group in (2, 4, 5))
            out = attn_out[rows, :]
            x1 = x_ref[rows, :].astype(WIDE) + gate1 * out
            h2, inverse = normed(x1)
            whole = jnp.concatenate([branch[0, rows, :], branch[1, rows, :]], axis=1) + bias[:, 3 * D + FF :]
            block_ref[rows, :] = (x1 + gate2 * whole).astype(LOW)
            g = g_ref[rows, :].astype(WIDE)
            sums_ref[tile_at, 3:4, :] = column_sums(g * whole)
            dmlp = dx1_ref[rows, :]
            sums_ref[tile_at, 1:2, :] = column_sums(dmlp)
            sums_ref[tile_at, 2:3, :] = column_sums(dmlp * h2)
            dh2 = dmlp * (1.0 + scale2)
            dx1 = g + inverse * (
                dh2
                - jnp.mean(dh2, axis=-1, keepdims=True)
                - h2 * jnp.mean(dh2 * h2, axis=-1, keepdims=True)
            )
            dx1_ref[rows, :] = dx1
            sums_ref[tile_at, 0:1, :] = column_sums(dx1 * out)
            dattn = (gate1 * dx1).astype(LOW)
            sums_ref[tile_at, 4:5, :] = column_sums(dattn.astype(WIDE))
            sums_ref[tile_at, 6:8, :] = jnp.zeros((2, D), WIDE)
            left, right = dattn[:, : D // 2], dattn[:, D // 2 :]
            dattn_ref[0, rows, :] = left
            dattn_ref[1, rows, :] = right
            dmixed_ref[rows, :] = (times_across(left, proj[0]) + times_across(right, proj[1])).astype(LOW)
            return carry

        lax.fori_loop(0, tokens // CHUNK, leave, 0)


def middle(slots, x_in, out_grad, mixed, table, bias, proj, fc1, fc2):
    tokens = x_in.shape[0]
    tiles = tokens // CHUNK
    steps = FF // SPAN
    per_side = steps // 2
    bias1 = bias[:, 3 * D : 3 * D + FF].reshape(steps, 1, SPAN)

    def by_unit(shape, place):
        return pl.BlockSpec(shape, lambda j, slots: place(j))

    outs = (
        ((tokens, D), LOW),
        ((D, tokens), LOW),
        ((FF, tokens), LOW),
        ((2, tokens, FF // 2), LOW),
        ((2, tokens, D // 2), LOW),
        ((2, tokens, D // 2), LOW),
        ((tokens, D), LOW),
        ((tokens, D), WIDE),
        ((tiles, 8, D), WIDE),
        ((1, FF), WIDE),
    )
    out_specs = [fixed(*shape) for shape, _ in outs]
    out_specs[2] = by_unit((SPAN, tokens), lambda j: (j, 0))
    out_specs[3] = by_unit((1, tokens, SPAN), lambda j: (j // per_side, 0, j % per_side))
    out_specs[9] = by_unit((1, SPAN), lambda j: (0, j))
    return pl.pallas_call(
        middle_kernel,
        out_shape=tuple(jax.ShapeDtypeStruct(shape, dtype) for shape, dtype in outs),
        grid_spec=pltpu.PrefetchScalarGridSpec(
            num_scalar_prefetch=1,
            grid=(steps,),
            in_specs=[
                fixed(tokens, D),
                fixed(tokens, D),
                fixed(tokens, D),
                fixed(*table.shape),
                fixed(*bias.shape),
                by_unit((1, 1, SPAN), lambda j: (j, 0, 0)),
                fixed(*proj.shape),
                by_unit((1, D, SPAN), lambda j: (j // per_side, 0, j % per_side)),
                by_unit((2, SPAN, D // 2), lambda j: (0, j, 0)),
            ],
            out_specs=tuple(out_specs),
            scratch_shapes=[
                pltpu.VMEM((tokens, D), WIDE),
                pltpu.VMEM((tokens, D), LOW),
                pltpu.VMEM((2, tokens, D // 2), WIDE),
            ],
        ),
        compiler_params=pltpu.CompilerParams(
            dimension_semantics=("arbitrary",), vmem_limit_bytes=63 * 2**20
        ),
        cost_estimate=pl.CostEstimate(
            flops=4 * tokens * (D * D + 2 * D * FF),
            bytes_accessed=(D * D + 2 * D * FF) * 2 + tokens * D * 40,
            transcendentals=0,
        ),
        name="middle",
    )(slots, x_in, out_grad, mixed, table, bias, bias1, proj, fc1, fc2)


def times(left, right):
    return jnp.dot(left, right, preferred_element_type=WIDE)


def times_back(left, right):
    return lax.dot_general(left, right, (((1,), (1,)), ((), ())), preferred_element_type=WIDE)


def body(
    x_in,
    cond,
    segments,
    out_grad,
    qkv_weight,
    qkv_moment,
    qkv_average,
    proj_weight,
    proj_moment,
    proj_average,
    fc1_weight,
    fc1_moment,
    fc1_average,
    fc2_weight,
    fc2_moment,
    fc2_average,
    bias_weight,
    bias_moment,
    bias_average,
    ada_weight,
    ada_moment,
    ada_average,
    adab_weight,
    adab_moment,
    adab_average,
):
    tokens, width = x_in.shape
    row_devices = lax.axis_size(ROWS)
    devices = lax.axis_size(ALL)
    row_index = lax.axis_index(ROWS)
    images = cond.shape[0] // 2

    cond_silu, silu_back = jax.vjp(jax.nn.silu, cond.astype(WIDE))
    half_silu = lax.dynamic_index_in_dim(
        cond_silu.astype(LOW).reshape(-1, 2, width // 2), lax.axis_index("mod"), 1, False
    )
    own_bias = bias_weight.shape[0]
    bias_block = jnp.pad(bias_weight.astype(LOW), (0, 8 * LANES - own_bias)).reshape(8, LANES)
    blank = jnp.zeros((8, LANES // 2), LOW)
    ada_low = ada_weight.astype(LOW)
    adab_row = lax.dynamic_update_slice_in_dim(
        jnp.zeros((1, ada_weight.shape[1]), LOW),
        adab_weight.astype(LOW),
        row_index * adab_weight.shape[1],
        1,
    )
    ada_rows = jnp.concatenate([ada_low, adab_row])
    small_w, qkv_w, proj_w, fc1_w, table = first_gather(
        jnp.pad(ada_rows, ((0, LANES - ada_rows.shape[0]), (0, 0))),
        jnp.concatenate([half_silu, bias_block, blank], axis=1),
        qkv_weight,
        proj_weight,
        fc1_weight,
    )
    small = small_w.reshape(2, row_devices * 8, -1)
    silu_all = jnp.concatenate([small[0, :, : width // 2], small[1, :, : width // 2]], axis=1)
    bias_all = small[:, :, width // 2 : width // 2 + LANES].reshape(2, row_devices, -1)
    bias_full = jnp.swapaxes(bias_all[:, :, :own_bias], 0, 1).reshape(1, -1).astype(WIDE)
    table = lax.dynamic_slice_in_dim(table, lax.axis_index("mod") * images, images, 1)
    table = jnp.swapaxes(table, 0, 1).reshape(images, -1)

    def joined(whole):
        return whole.reshape(2, -1, whole.shape[-1])

    qkv_low = joined(qkv_w)
    slots = segments[::CHUNK]
    joint_bias = jnp.concatenate(
        [bias_full[:, 0:width], jnp.zeros((1, width), WIDE), bias_full[:, width : 2 * width]], axis=1
    )
    def blocked(turned):
        return turned.reshape(row_devices // 4, 2, 2, -1, tokens)

    act_turned, mixture, mixture_turned, heads, (proj_w, fc1_w, fc2_w) = attend(
        slots,
        x_in,
        table,
        joint_bias,
        qkv_low,
        segments,
        fc2_weight.astype(LOW),
        proj_w,
        fc1_w,
    )
    (
        block_out, mlp_turned, hidden_turned, pre_halves, branch_halves, attn_halves, mixture_grad, middle_grad, sums, pre_sums,
    ) = middle(
        slots, x_in, out_grad, mixture, table, bias_full, joined(proj_w), joined(fc1_w), joined(fc2_w)
    )
    proj_totals, fc2_joints, fc2_bases, fc1_sums = weight_grads(
        blocked(hidden_turned),
        branch_halves,
        blocked(mlp_turned),
        pre_halves,
        blocked(mixture_turned),
        attn_halves,
    )
    joint_halves, fc2_shard, proj_shard, fc1_totals = attend_back(
        mixture_grad, heads, fc1_sums, proj_totals, fc2_joints, fc2_bases
    )
    chooser = (slots[None, :] == (jnp.arange(2 * images, dtype=jnp.int32) % images)[:, None]).astype(WIDE)
    qkv_shard, fc1_shard, small_grads, x_grad = last_scatter(
        slots,
        blocked(act_turned),
        joint_halves,
        x_in,
        middle_grad,
        table,
        qkv_low,
        sums,
        pre_sums,
        chooser,
        fc1_totals,
    )
    small_grads = small_grads.reshape(2, row_devices, 16, -1)
    mod_grads = lax.dynamic_slice_in_dim(small_grads, lax.axis_index("mod") * images, images, 2)
    mod_grad_all = jnp.swapaxes(mod_grads, 0, 1).reshape(2 * row_devices * images, -1)
    bias_grads = small_grads[:, :, 8:11].reshape(devices, -1)
    own_biases = lax.dynamic_slice_in_dim(bias_grads, lax.axis_index(ALL) * own_bias, own_bias, 1)
    bias_shard = jnp.sum(own_biases.astype(WIDE), axis=0)
    own_rows = ada_weight.shape[0]
    own_silu = lax.dynamic_slice_in_dim(silu_all, row_index * own_rows, own_rows, 1)
    ada_shard = jnp.einsum("ic,io->co", own_silu, mod_grad_all, preferred_element_type=WIDE)
    own_columns = adab_weight.shape[1]
    adab_shard = jnp.sum(
        lax.dynamic_slice_in_dim(mod_grad_all, row_index * own_columns, own_columns, 1).astype(WIDE),
        axis=0,
    )
    silu_part = times_back(mod_grad_all, ada_low)
    row_images = 2 * images
    silu_part = jnp.broadcast_to(
        silu_part.reshape(row_devices, 1, row_images, -1), (row_devices, 2, row_images, own_rows)
    ).reshape(devices * row_images, own_rows)
    silu_part = lax.all_to_all(silu_part, ALL, split_axis=0, concat_axis=1, tiled=True)
    silu_grad = jnp.sum(silu_part.reshape(row_images, row_devices, 2, own_rows), axis=2)
    cond_grad = silu_back(silu_grad.reshape(row_images, -1))[0]

    rates = step_rates(tokens * devices)
    states_out = []
    states_out.extend(nesterov(qkv_weight, qkv_moment, qkv_average, qkv_shard, rates[0]))
    states_out.extend(nesterov(proj_weight, proj_moment, proj_average, proj_shard, rates[1]))
    states_out.extend(nesterov(fc1_weight, fc1_moment, fc1_average, fc1_shard, rates[2]))
    states_out.extend(nesterov(fc2_weight, fc2_moment, fc2_average, fc2_shard, rates[3]))
    states_out.extend(nesterov(bias_weight, bias_moment, bias_average, bias_shard, rates[4]))
    states_out.extend(nesterov(ada_weight, ada_moment, ada_average, ada_shard, rates[5]))
    states_out.extend(
        nesterov(adab_weight, adab_moment, adab_average, adab_shard.reshape(1, -1), rates[6])
    )
    return (block_out, x_grad, cond_grad) + tuple(states_out)


def solution(mesh):
    far = mesh.shape["dp"] // 4
    fine = Mesh(mesh.devices.reshape(far, 2, 2, mesh.shape["mod"]), ALL)
    tokens = P(ALL, None)
    images = P(ROWS, None)
    trunk = P(ROWS, "mod")
    bias = P(ALL)
    adab = P("mod", ROWS)
    states = (trunk,) * 12 + (bias,) * 3 + (trunk,) * 3 + (adab,) * 3
    return jax.shard_map(
        body,
        mesh=fine,
        in_specs=(tokens, images, bias, tokens) + states,
        out_specs=(tokens, tokens, images) + states,
        check_vma=False,
    )
```

```python
from functools import partial

import jax
import jax.numpy as jnp
from jax import lax
from jax.experimental import pallas as pl
from jax.experimental.pallas import tpu as pltpu
from jax.sharding import Mesh
from jax.sharding import PartitionSpec as P

D = 1152
HEADS = 16
HEAD = 72
FF = 4608
LANES = 128
CHUNK = 256

ROWS = ("far", "near", "core")
ALL = ("far", "near", "core", "mod")
LOW = jnp.bfloat16
WIDE = jnp.float32
LOG2E = 1.4426950408889634
NEG = -1e30
MESH = pl.DeviceIdType.MESH
VMEM = pl.BlockSpec(memory_space=pltpu.VMEM)
ANY = pl.BlockSpec(memory_space=pl.ANY)

EPS = 1e-06
MOMENTUM = 0.9
DECAY = 0.5


def step_rates(tokens_all):
    base_rate = tokens_all ** (-0.5)
    return (
        2.5 * D ** (-0.5) * base_rate,
        3.0 * D ** (-0.5) * base_rate,
        3.3 * D ** (-0.5) * base_rate,
        2.8 * FF ** (-0.5) * base_rate,
        0.5 * base_rate,
        2.0 * D ** (-0.5) * base_rate,
        0.3 * base_rate,
    )


def nesterov(weight, moment, average, gradient, rate):
    moment = MOMENTUM * moment + gradient
    weight = weight - rate * (gradient + MOMENTUM * moment)
    average = DECAY * average + (1.0 - DECAY) * weight
    return (weight, moment, average)


def places():
    return {name: lax.axis_index(name) for name in ALL}


def greet():
    here = places()
    count = lax.axis_size("far")
    others = [dict(far=lax.rem(here["far"] + d, count)) for d in range(1, count)]
    others += [{name: 1 - here[name]} for name in ("near", "core", "mod")]
    barrier = pltpu.get_barrier_semaphore()
    for other in others:
        pl.semaphore_signal(barrier, inc=1, device_id=other, device_id_type=MESH)
    pl.semaphore_wait(barrier, len(others))


def fetches(pairs, sems):
    return [
        pltpu.make_async_copy(source, target, sems.at[number])
        for number, (source, target) in enumerate(pairs)
    ]


def remote(source, target, sends, receives, slot, other):
    return pltpu.make_async_remote_copy(
        src_ref=source,
        dst_ref=target,
        send_sem=sends.at[slot],
        recv_sem=receives.at[slot],
        device_id=other,
        device_id_type=MESH,
    )


def messages(count):
    return count - 1 + 8


class Gather:
    def __init__(self, whole, sends, receives):
        self.whole, self.sends, self.receives = whole, sends, receives
        self.here = places()
        self.count = lax.axis_size("far")
        rows = whole.shape[4]
        self.rows = rows
        self.split = rows if rows % 8 else 8 * ((rows // 8 + 1) // 2)

    def _block(self, far):
        return self.whole.at[self.here["mod"], far, self.here["near"], self.here["core"]]

    def _far(self, shard, distance):
        far = self.here["far"]
        other = dict(far=lax.rem(far + distance, self.count))
        return remote(shard, self._block(far), self.sends, self.receives, distance - 1, other)

    def _far_came(self, shard, distance):
        origin = lax.rem(self.here["far"] + self.count - distance, self.count)
        return remote(
            shard, self._block(origin), self.sends, self.receives, distance - 1, dict(far=origin)
        )

    def start_far(self, shard, local):
        pltpu.make_async_copy(shard, self._block(self.here["far"]), local).start()
        for distance in range(1, self.count):
            self._far(shard, distance).start()

    def finish_far(self, shard, local):
        pltpu.make_async_copy(shard, self._block(self.here["far"]), local).wait()
        for distance in range(1, self.count):
            self._far(shard, distance).wait_send()
            self._far_came(shard, distance).wait_recv()

    def _quad(self, flips, first, size):
        near, core, mod = (
            1 - self.here[name] if name in flips else self.here[name] for name in ("near", "core", "mod")
        )
        return self.whole.at[mod, :, near, core, pl.ds(first, size)]

    def _step(self, name):
        head, rest = (0, self.split), (self.split, self.rows - self.split)
        full = (0, self.rows)
        return {
            "near": ((), "near", full, 0),
            "mod": ((), "mod", full, 1),
            "near_mod": (("near",), "mod", head, 2),
            "mod_near": (("mod",), "near", rest, 3),
            "core": ((), "core", full, 4),
            "near_core": (("near",), "core", full, 5),
            "mod_core": (("mod",), "core", full, 6),
            "both_core": (("near", "mod"), "core", full, 7),
        }[name]

    def _copy(self, name, incoming):
        flips, axis, span, slot = self._step(name)
        if span[1] == 0:
            return None
        quad = self._quad(flips + (axis,) if incoming else flips, *span)
        other = {axis: 1 - self.here[axis]}
        return remote(quad, quad, self.sends, self.receives, self.count - 1 + slot, other)

    def start(self, *names):
        for name in names:
            copy = self._copy(name, False)
            if copy is not None:
                copy.start()

    def receive(self, *names):
        for name in names:
            copy = self._copy(name, True)
            if copy is not None:
                copy.wait_recv()

    def spread(self):
        self.start("near", "mod", "core")

    def cross(self):
        self.receive("near")
        self.start("near_mod", "near_core")
        self.receive("mod")
        self.start("mod_near", "mod_core")

    def close(self):
        self.receive("near_mod", "mod_near")
        self.start("both_core")

    def end(self):
        self.receive("core", "near_core", "mod_core", "both_core")
        for name in (
            "near", "mod", "near_mod", "mod_near", "core", "near_core", "mod_core", "both_core",
        ):
            copy = self._copy(name, False)
            if copy is not None:
                copy.wait_send()


def gather_scratch(weights, locals_):
    count = lax.axis_size("far")
    shapes = [pltpu.SemaphoreType.DMA((messages(count),))] * (2 * weights)
    return shapes + [pltpu.SemaphoreType.DMA((locals_,))]


def whole_shape(shard):
    return jax.ShapeDtypeStruct((2, lax.axis_size("far"), 2, 2) + shard.shape, LOW)


def modulate(small_w, ada, table, local, small, partials, came_core, came_near, came_far, own, sends, receives):
    here = places()
    count = lax.axis_size("far")
    far, near, core, mod = (here[name] for name in ALL)
    row_devices = 4 * count
    rows = D // row_devices
    fetch = pltpu.make_async_copy(small_w, small, local)
    fetch.start()
    fetch.wait()
    device = (far * 2 + near) * 2 + core
    half = lax.div(device, row_devices // 2)
    first = lax.rem(device, row_devices // 2) * rows
    width = small.shape[-1]
    images = small.shape[-2]
    row = lax.broadcasted_iota(jnp.int32, (width, LANES), 0)
    column = lax.broadcasted_iota(jnp.int32, (width, LANES), 1)
    select = jnp.where(jnp.logical_and(row == first + column, column < rows), 1.0, 0.0).astype(LOW)
    for at in range(count):
        silu = small[half, at].reshape(4 * images, width).astype(WIDE).astype(LOW)
        mine = times(silu, select)
        mine = jnp.where(lanes(mine.shape) == rows, 1.0, mine).astype(LOW)
        partials[at] = times(mine, ada[...]).reshape(2, 2, images, -1)

    def move(source, target, slot, other):
        return remote(source, target, sends, receives, slot, other)

    to_core = move(partials.at[:, :, 1 - core], came_core, 0, dict(core=1 - core))
    to_core.start()
    to_core.wait()
    for at in range(count):
        partials[at, :, core] = partials[at, :, core] + came_core[at]
    to_near = move(partials.at[:, 1 - near, core], came_near, 1, dict(near=1 - near))
    to_near.start()
    yield
    to_near.wait()
    for at in range(count):
        partials[at, near, core] = partials[at, near, core] + came_near[at]
    copies = []
    for distance in range(1, count):
        target = lax.rem(far + distance, count)
        copies.append(
            move(partials.at[target, near, core], came_far.at[distance - 1], 2 + distance, dict(far=target))
        )
        copies[-1].start()
    yield
    total = partials[far, near, core]
    for distance, copy in enumerate(copies):
        copy.wait()
        total = total + came_far[distance]
    own[...] = total.astype(LOW).astype(WIDE)
    keep = pltpu.make_async_copy(own, table.at[mod], local)
    keep.start()
    to_mod = move(own, table.at[mod], 2, dict(mod=1 - mod))
    to_mod.start()
    yield
    keep.wait()
    to_mod.wait_send()
    move(own, table.at[1 - mod], 2, dict(mod=1 - mod)).wait_recv()


def first_kernel(*refs):
    small_s, *wide, ada = refs[:5]
    table = refs[9]
    rounded, gather_sems, (local, *parts) = refs[10:13], refs[13:21], refs[21:]
    qkv_s, proj_s, fc1_s = rounded
    for source, target in zip(wide, rounded):
        target[...] = source[...].astype(LOW)
    small, qkv, proj, fc1 = (
        Gather(w, s, r) for w, s, r in zip(refs[5:9], gather_sems[0::2], gather_sems[1::2])
    )
    greet()
    small.start_far(small_s, local.at[3])
    qkv.start_far(qkv_s, local.at[0])
    proj.start_far(proj_s, local.at[1])
    small.finish_far(small_s, local.at[3])
    small.spread()
    small.cross()
    small.close()
    small.end()
    stages = modulate(small.whole, ada, table, local.at[3], *parts)
    next(stages)
    qkv.finish_far(qkv_s, local.at[0])
    qkv.spread()
    next(stages)
    fc1.start_far(fc1_s, local.at[2])
    next(stages)
    qkv.cross()
    qkv.close()
    qkv.end()
    next(stages, None)
    proj.finish_far(proj_s, local.at[1])
    fc1.finish_far(fc1_s, local.at[2])


def first_gather(ada, *shards):
    count = lax.axis_size("far")
    small = whole_shape(shards[0])
    images = small.shape[4]
    columns = ada.shape[1]
    return pl.pallas_call(
        first_kernel,
        out_shape=tuple(whole_shape(shard) for shard in shards)
        + (jax.ShapeDtypeStruct((2, images, columns), WIDE),),
        in_specs=[VMEM] * 5,
        out_specs=(ANY,) * 5,
        scratch_shapes=[pltpu.VMEM(shard.shape, LOW) for shard in shards[1:]]
        + gather_scratch(4, 4)
        + [
            pltpu.VMEM(small.shape, LOW),
            pltpu.VMEM((count, 2, 2, images, columns), WIDE),
            pltpu.VMEM((count, 2, images, columns), WIDE),
            pltpu.VMEM((count, images, columns), WIDE),
            pltpu.VMEM((count - 1, images, columns), WIDE),
            pltpu.VMEM((images, columns), WIDE),
            pltpu.SemaphoreType.DMA((count + 2,)),
            pltpu.SemaphoreType.DMA((count + 2,)),
        ],
        compiler_params=pltpu.CompilerParams(
            collective_id=0, has_side_effects=True, vmem_limit_bytes=60 * 2**20
        ),
        name="first_gather",
    )(*shards, ada)


def lanes(shape): return lax.broadcasted_iota(jnp.int32, shape, 1)

def seg_codes(seg, n):
    lane = lanes((n, LANES))
    code = lane - HEAD
    inside = jnp.logical_and(code >= 0, code < 4)
    same = code == seg
    q = jnp.where(jnp.logical_and(inside, same), 1.0, 0.0)
    k = jnp.where(jnp.logical_and(inside, jnp.logical_not(same)), NEG, 0.0)
    return q, k

def head_of(wide_rows, start):
    return wide_rows[:, start:start+HEAD]

def pad_head(part, aug):
    n = part.shape[0]
    full = jnp.concatenate([part, jnp.zeros((n, LANES-HEAD), part.dtype)], axis=1)
    return jnp.where(lanes((n,LANES)) < HEAD, full, aug)

def split3(v):
    hi = v.astype(LOW).astype(WIDE)
    mid = (v - hi).astype(LOW).astype(WIDE)
    lo = v - hi - mid
    return hi, mid, lo


def attend_kernel(*refs):
    slots, x_hbm, table, bias, weight_hbm, seg_ref, fc2_s = refs[:7]
    act_turned, mixed_ref, turned_ref = refs[9:12]
    saved, (proj_w, fc1_w, fc2_w) = refs[12:16], refs[16:19]
    heads, (x_ref, weight, fetch_sems, *sems, local, save_sems) = refs[19:23], refs[23:]
    qh, kh, vh, oh = heads
    proj, fc1, fc2 = (
        Gather(w, s, r) for w, s, r in zip((proj_w, fc1_w, fc2_w), sems[0::2], sems[1::2])
    )
    greet()
    fc2.start_far(fc2_s, local.at[0])
    proj.spread()
    fc1.spread()
    loads = fetches(((x_hbm, x_ref), (weight_hbm, weight)), fetch_sems)
    for load in loads:
        load.start()
    for load in loads:
        load.wait()

    T = x_ref.shape[0]

    def fill(i, carry):
        rows = pl.ds(pl.multiple_of(i * CHUNK, CHUNK), CHUNK)
        slot = slots[i]
        h1, _ = normed(x_ref[rows, :].astype(WIDE))
        act = (h1 * (1.0 + row_of(table, slot, 1)) + row_of(table, slot, 0)).astype(LOW)
        act_turned[:, rows] = act.T
        joint = jnp.concatenate([times(act, weight[0]), times(act, weight[1])], axis=1)
        joint = (joint + bias[...]).astype(LOW)
        lane = lanes((CHUNK, LANES))
        qc, kc = seg_codes(seg_ref[rows, :], CHUNK)
        qc = qc.astype(LOW)
        kc = jnp.where(jnp.logical_and(lane >= HEAD + 4, lane < HEAD + 7), 1.0, kc).astype(LOW)
        ones = jnp.where(jnp.logical_and(lane >= HEAD, lane < HEAD+3), 1.0, 0.0).astype(LOW)
        for h in range(HEADS):
            qh[h, rows, :] = pad_head(joint[:, h*HEAD:(h+1)*HEAD], qc)
            kh[h, rows, :] = pad_head(joint[:, D+h*HEAD:D+(h+1)*HEAD], kc)
            vh[h, rows, :] = pad_head(joint[:, 2*D+h*HEAD:2*D+(h+1)*HEAD], ones)
        pl.when(i == 2)(proj.cross)
        return carry
    lax.fori_loop(0, T//CHUNK, fill, 0)

    def save(number):
        return pltpu.make_async_copy(heads[number], saved[number], save_sems.at[number])

    save(1).start()
    save(2).start()
    def head(h, carry):
        k = kh[h]; v = vh[h]
        for i in range(T//CHUNK):
            rows = pl.ds(i*CHUNK, CHUNK)
            q = qh[h, rows, :]
            s = lax.dot_general(q, k, (((1,),(1,)),((),())), preferred_element_type=WIDE)
            m = jnp.max(s, axis=1, keepdims=True)
            p = jnp.exp2((s - m)*(HEAD**-0.5*LOG2E)).astype(LOW)
            o = jnp.dot(p, v, preferred_element_type=WIDE)
            l = o[:, HEAD:HEAD+1]
            oh[h, rows, :] = (o / l).astype(LOW)
            hi, mid, lo = split3(-(m + jnp.log(l) * HEAD**0.5))
            lane = lanes((CHUNK, LANES))
            q = jnp.where(lane == HEAD + 4, hi.astype(LOW), q)
            q = jnp.where(lane == HEAD + 5, mid.astype(LOW), q)
            qh[h, rows, :] = jnp.where(lane == HEAD + 6, lo.astype(LOW), q)
        tasks = {
            3: lambda: (fc2.finish_far(fc2_s, local.at[0]), fc2.spread()),
            6: fc1.cross,
            8: proj.close,
            10: proj.end,
        }
        for at, task in tasks.items():

            @pl.when(h == at)
            def _(task=task):
                task()

        return carry
    lax.fori_loop(0, HEADS, head, 0)
    save(0).start()
    save(3).start()

    def drain(i, carry):
        rows = pl.ds(pl.multiple_of(i*CHUNK, CHUNK), CHUNK)
        mixed = jnp.concatenate([oh[h, rows, :][:, :HEAD] for h in range(HEADS)], axis=1)
        mixed_ref[rows, :] = mixed
        turned_ref[:, rows] = mixed.T
        return carry
    lax.fori_loop(0, T//CHUNK, drain, 0)
    fc2.cross()
    fc1.close()
    fc1.end()
    fc2.close()
    fc2.end()
    for number in range(4):
        save(number).wait()


def attend(slots, x_in, table, bias, weight, segments, fc2_s, proj_w, fc1_w):
    tokens = x_in.shape[0]
    wide = HEADS * HEAD
    heads = (HEADS, tokens, LANES)
    out = pl.pallas_call(
        attend_kernel,
        out_shape=(
            jax.ShapeDtypeStruct((wide, tokens), LOW),
            jax.ShapeDtypeStruct((tokens, wide), LOW),
            jax.ShapeDtypeStruct((wide, tokens), LOW),
        )
        + (jax.ShapeDtypeStruct(heads, LOW),) * 4
        + (
            jax.ShapeDtypeStruct(proj_w.shape, LOW),
            jax.ShapeDtypeStruct(fc1_w.shape, LOW),
            whole_shape(fc2_s),
        ),
        in_specs=[pl.BlockSpec(memory_space=pltpu.SMEM), ANY, VMEM, VMEM, ANY, VMEM, VMEM, ANY, ANY],
        out_specs=(VMEM,) * 3 + (ANY,) * 7,
        scratch_shapes=[pltpu.VMEM(heads, LOW)] * 4
        + [pltpu.VMEM(x_in.shape, LOW), pltpu.VMEM(weight.shape, LOW), pltpu.SemaphoreType.DMA((2,))]
        + gather_scratch(3, 1)
        + [pltpu.SemaphoreType.DMA((4,))],
        input_output_aliases={7: 7, 8: 8},
        compiler_params=pltpu.CompilerParams(
            collective_id=1, has_side_effects=True, vmem_limit_bytes=60 * 2**20
        ),
        name="attend",
    )(slots, x_in, table, bias, weight, segments.reshape(tokens, 1), fc2_s, proj_w, fc1_w)
    return out[0], out[1], out[2], out[3:7], out[7:]


def row_spans(rows):
    first = rows if rows % 8 else 8 * ((rows // 8 + 1) // 2)
    return [(0, first)] + ([(first, rows - first)] if first < rows else [])


class Reduce:
    def __init__(self, part, span, first, came, joint, total, base, sems, loads=False):
        self.part, self.span, self.first = part, span, first
        self.second = "near" if first == "mod" else "mod"
        self.came_both, self.came_first, self.came_second, self.came_far = came
        self.joint, self.total_, self.base = joint, total, base
        self.sends, self.receives, self.locals_ = sems
        self.loads = loads
        self.here = places()
        self.count = lax.axis_size("far")

    def _swap(self, source, target, slot, axis):
        return remote(source, target, self.sends, self.receives, slot, {axis: 1 - self.here[axis]})

    def _both(self):
        return self._swap(self.part("near", "mod"), self.came_both, 0, self.first)

    def _first(self):
        return self._swap(self.part(self.first), self.came_first, 1, self.first)

    def _second(self):
        return self._swap(self.joint, self.came_second, 2, self.second)

    def _load(self, number):
        source, target = ((self.part(self.second), self.joint), (self.part(), self.total_))[number]
        return pltpu.make_async_copy(source, target, self.locals_.at[number])

    def _far(self, distance):
        target = lax.rem(self.here["far"] + distance, self.count)
        return remote(
            self.total_.at[target],
            self.came_far.at[distance - 1],
            self.sends,
            self.receives,
            2 + distance,
            dict(far=target),
        )

    def start_ahead(self):
        self._both().start()
        if self.first == "near":
            self._first().start()

    def start_rest(self):
        if self.first == "mod":
            self._first().start()

    def start(self):
        self._both().start()
        self._first().start()
        if self.loads:
            self._load(0).start()
            self._load(1).start()

    def merge(self):
        if self.loads:
            self._load(0).wait()
        self._both().wait_recv()

        def add(at, carry):
            self.joint[at] = (self.joint[at].astype(WIDE) + self.came_both[at].astype(WIDE)).astype(LOW)
            return carry

        lax.fori_loop(0, self.count, add, 0)
        self._second().start()

    def total(self):
        if self.loads:
            self._load(1).wait()
        self._first().wait_recv()
        self._second().wait_recv()

        def add(at, carry):
            self.total_[at] = (
                self.base[at].astype(WIDE)
                + self.came_first[at].astype(WIDE)
                + self.came_second[at].astype(WIDE)
            ).astype(LOW)
            return carry

        lax.fori_loop(0, self.count, add, 0)
        self._both().wait_send()
        self._first().wait_send()
        self._second().wait_send()

    def early(self):
        second = self.part(self.second)
        self._both().wait_recv()
        self._first().wait_recv()

        def add(at, carry):
            self.joint[at] = (second[at].astype(WIDE) + self.came_both[at].astype(WIDE)).astype(LOW)
            self.total_[at] = (self.base[at].astype(WIDE) + self.came_first[at].astype(WIDE)).astype(LOW)
            return carry

        lax.fori_loop(0, self.count, add, 0)
        self._both().wait_send()
        self._first().wait_send()

    def _load_base(self):
        return pltpu.make_async_copy(self.base, self.total_, self.locals_.at[1])

    def late_start(self):
        self._load_base().start()
        self._second().start()

    def late_total(self):
        self._load_base().wait()
        self._second().wait_recv()

        def add(at, carry):
            self.total_[at] = (self.total_[at].astype(WIDE) + self.came_second[at].astype(WIDE)).astype(LOW)
            return carry

        lax.fori_loop(0, self.count, add, 0)
        self._second().wait_send()

    def start_far(self):
        for distance in range(1, self.count):
            self._far(distance).start()

    def final(self, out):
        value = self.total_[self.here["far"]].astype(WIDE)
        for distance in range(1, self.count):
            self._far(distance).wait_recv()
            value = value + self.came_far[distance - 1].astype(WIDE)
        out[pl.ds(*self.span), :] = value
        for distance in range(1, self.count):
            self._far(distance).wait_send()


ORDERS = ("mod", "near")


def run(parts, *names):
    for part in parts:
        for name in names:
            getattr(part, name)()


def span_part(sums, span):
    def part(*flips):
        near, mod = (
            1 - lax.axis_index(name) if name in flips else lax.axis_index(name) for name in ("near", "mod")
        )
        return sums.at[mod, near, :, pl.ds(*span)]

    return part


def take(scratch, number):
    return scratch[:number], scratch[number:]


def came_scratch(count, span, columns, far=True):
    block = (count, span[1], columns)
    shapes = [pltpu.VMEM(block, LOW)] * 3
    return shapes + ([pltpu.VMEM((count - 1,) + block[1:], LOW)] if far else [])


def sem_scratch(count):
    return [pltpu.SemaphoreType.DMA((count + 2,))] * 2 + [pltpu.SemaphoreType.DMA((2,))]


def loaded_scratch(shape, total=True):
    count, rows, columns = shape[2:]
    shapes = []
    for span in row_spans(rows):
        shapes += came_scratch(count, span, columns, total)
        shapes += [pltpu.VMEM((count, span[1], columns), LOW)] * (2 if total else 1)
        shapes += sem_scratch(count)
    return shapes


def loaded_reduces(sums, scratch, totals=None):
    reduces = []
    for number, span in enumerate(row_spans(sums.shape[3])):
        came, scratch = take(scratch, 4 if totals is None else 3)
        came = list(came) + [None] * (4 - len(came))
        (joint,), scratch = take(scratch, 1)
        if totals is None:
            (total,), scratch = take(scratch, 1)
        else:
            total = totals[number]
        sems, scratch = take(scratch, 3)
        reduces.append(
            Reduce(span_part(sums, span), span, ORDERS[number], came, joint, total, total, sems, True)
        )
    return reduces, scratch


def resident_scratch(shape, far=True):
    count, rows, columns = shape[2:]
    shapes = []
    for span in row_spans(rows):
        shapes += came_scratch(count, span, columns, far) + sem_scratch(count)
    return shapes


def resident_reduces(sums, scratch, totals=None, joints=None):
    reduces = []
    for number, span in enumerate(row_spans(sums.shape[3])):
        came, scratch = take(scratch, 4 if totals is None else 3 if joints is None else 2)
        sems, scratch = take(scratch, 3)
        part = span_part(sums, span)
        order = ORDERS[number]
        own = part()
        total = own if totals is None else totals[number]
        came = list(came) + [None] * (4 - len(came))
        joint = part("near" if order == "mod" else "mod") if joints is None else joints[number]
        reduces.append(Reduce(part, span, order, came, joint, total, own, sems))
    return reduces, scratch


def early_scratch(shape):
    count, rows, columns = shape[2:]
    shapes = []
    for span in row_spans(rows):
        shapes += [pltpu.VMEM((count, span[1], columns), LOW)] * 2 + sem_scratch(count)
    return shapes


def late_scratch(bases):
    shapes = []
    for base in bases:
        far = pltpu.VMEM((base.shape[0] - 1,) + base.shape[1:], LOW)
        shapes += [pltpu.VMEM(base.shape, LOW)] * 2 + [far] + sem_scratch(base.shape[0])
    return shapes


def late_reduces(joints, bases, rows, scratch):
    reduces = []
    for number, span in enumerate(row_spans(rows)):
        (came, total, came_far), scratch = take(scratch, 3)
        sems, scratch = take(scratch, 3)
        came = (None, None, came, came_far)
        reduces.append(
            Reduce(None, span, ORDERS[number], came, joints[number], total, bases[number], sems)
        )
    return reduces, scratch


def far_scratch(totals):
    shapes = []
    for total in totals:
        count = total.shape[0]
        shapes += [pltpu.VMEM((count - 1,) + total.shape[1:], LOW)] + sem_scratch(count)[:2]
    return shapes


def far_reduces(totals, rows, scratch):
    reduces = []
    for total, span in zip(totals, row_spans(rows)):
        (came, sends, receives), scratch = take(scratch, 3)
        came = (None, None, None, came)
        reduces.append(Reduce(None, span, "mod", came, None, total, total, (sends, receives, None)))
    return reduces, scratch


class Product:
    def __init__(self, left, right, scratch):
        self.left, self.right = left, right
        self.rows_, self.sums, self.came, self.loads, self.sends, self.receives = scratch
        self.core = lax.axis_index("core")
        near = lax.axis_index("near")
        self.nears = (1 - near, near)

    @staticmethod
    def scratch(count, rows, tokens, columns):
        sums = pltpu.VMEM((2, 2, count, rows, columns), LOW)
        sems = [pltpu.SemaphoreType.DMA((4,))] * 3
        return [pltpu.VMEM((2, count, rows, tokens), LOW), sums, sums] + sems

    def _load(self, near, own):
        core = self.core if own else 1 - self.core
        return pltpu.make_async_copy(
            self.left.at[:, near, core], self.rows_.at[near], self.loads.at[2 * own + near]
        )

    def load(self):
        for near in self.nears:
            self._load(near, 0).start()

    def _copy(self, mod, near):
        return remote(
            self.sums.at[mod, near],
            self.came.at[mod, near],
            self.sends,
            self.receives,
            2 * mod + near,
            dict(core=1 - self.core),
        )

    def _blocks(self, near, own, store):
        count, rows, tokens = self.rows_.shape[1:]
        columns = self.right.shape[2]
        self._load(near, own).wait()
        left = self.rows_[near].reshape(count * rows, tokens)
        width = columns if columns <= 1024 else columns // 2
        width = width if width % LANES == 0 else columns
        for mod in (0, 1):
            for at in range(0, columns, width):
                product = times(left, self.right[mod, :, at : at + width])
                store(mod, at, width, product.reshape(count, rows, width))

    def send(self):
        for near in self.nears:

            def store(mod, at, width, product, near=near):
                self.sums[mod, near, :, :, at : at + width] = product.astype(LOW)

            self._blocks(near, 0, store)
            self._load(near, 1).start()
            for mod in (0, 1):
                self._copy(mod, near).start()

    def sum(self, reduces=()):
        for near, names in zip(self.nears, ("start_ahead", "start_rest")):
            for mod in (0, 1):
                self._copy(mod, near).wait_send()
                self._copy(mod, near).wait_recv()

            def store(mod, at, width, product, near=near):
                came = self.came[mod, near, :, :, at : at + width]
                self.sums[mod, near, :, :, at : at + width] = (product + came.astype(WIDE)).astype(LOW)

            self._blocks(near, 1, store)
            run(reduces, names)


def total_shapes(count, rows, columns):
    return [jax.ShapeDtypeStruct((count, span[1], columns), LOW) for span in row_spans(rows)]


def weight_kernel(*refs, modes, spans):
    sides, refs = take(refs, 2 * len(modes))
    outs = []
    for mode, count in zip(modes, spans):
        used, refs = take(refs, {"whole": count, "early": 2 * count, "chip": 1}[mode])
        outs.append(used)
    fetch_sems, *scratch = refs
    rights, scratch = take(scratch, len(modes) - 1)
    products, reduces = [], []
    for number in range(len(modes)):
        used, scratch = take(scratch, 6)
        right = rights[number - 1] if number else sides[1]
        products.append(Product(sides[2 * number], right, used))
    loads = fetches(list(zip(sides[3::2], rights)), fetch_sems)
    for mode, count, product, out in zip(modes, spans, products, outs):
        parts = []
        if mode == "whole":
            parts, scratch = resident_reduces(product.sums, scratch, out)
        elif mode == "early":
            parts, scratch = resident_reduces(product.sums, scratch, out[count:], out[:count])
        reduces.append(parts)
    (out_sem,) = scratch
    products[0].load()
    for load in loads:
        load.start()
    greet()
    copies = []
    for number, product in enumerate(products):
        before = number and modes[number - 1] == "whole"
        if number:
            loads[number - 1].wait()
        product.send()
        if before:
            run(reduces[number - 1], "merge")
        if number + 1 < len(products):
            products[number + 1].load()
        product.sum(reduces[number])
        if before:
            run(reduces[number - 1], "total")
        if modes[number] == "chip":
            copies.append(pltpu.make_async_copy(product.sums, outs[number][0], out_sem.at[0]))
            copies[-1].start()
    for number, mode in enumerate(modes):
        if mode == "early":
            run(reduces[number], "early")
    for copy in copies:
        copy.wait()


def weight_call(pairs, modes, number):
    count = pairs[0][0].shape[0]
    tokens = pairs[0][0].shape[4]
    products, sums, shapes, specs, spans = [], [], [], [], []
    for (left, right), mode in zip(pairs, modes):
        rows, columns = left.shape[3], right.shape[2]
        shape = (2, 2, count, rows, columns)
        products += Product.scratch(count, rows, tokens, columns)
        totals = total_shapes(count, rows, columns)
        spans.append(len(totals))
        if mode == "chip":
            shapes.append(jax.ShapeDtypeStruct(shape, LOW))
            specs.append(ANY)
        else:
            sums += resident_scratch(shape, False) if mode == "whole" else early_scratch(shape)
            outs = totals * (1 if mode == "whole" else 2)
            shapes += outs
            specs += [VMEM] * len(outs)
    out = pl.pallas_call(
        partial(weight_kernel, modes=modes, spans=tuple(spans)),
        out_shape=tuple(shapes),
        in_specs=[ANY, VMEM] + [ANY, ANY] * (len(pairs) - 1),
        out_specs=tuple(specs),
        scratch_shapes=[pltpu.SemaphoreType.DMA((len(pairs),))]
        + [pltpu.VMEM(right.shape, LOW) for _, right in pairs[1:]]
        + products
        + sums
        + [pltpu.SemaphoreType.DMA((1,))],
        compiler_params=pltpu.CompilerParams(
            collective_id=number, has_side_effects=True, vmem_limit_bytes=63 * 2**20
        ),
        name="weight_grads",
    )(*[side for pair in pairs for side in pair])
    return out, spans


def weight_grads(hidden, branch, mlp, pre, mixed, attn):
    proj, fc2, fc1 = (mixed, attn), (hidden, branch), (mlp, pre)
    if mlp.shape[3] % 8 == 0:
        out, spans = weight_call([proj, fc2, fc1], ("whole", "early", "chip"), 4)
        first, second = spans[0], spans[0] + spans[1]
        return out[:first], out[first:second], out[second:-1], out[-1]
    early, spans = weight_call([fc2], ("early",), 4)
    rest, _ = weight_call([proj, fc1], ("whole", "chip"), 5)
    return rest[:-1], early[: spans[0]], early[spans[0] :], rest[-1]


def tile_sums_by_slot(chooser, sums):
    total = None
    for at, row in enumerate(sums):
        part = chooser[:, at : at + 1] * row
        total = part if total is None else total + part
    return total


def last_kernel(*refs, spans):
    slots, act, joint, x_hbm, dx1_hbm, weight_hbm, table, mid_sums, pre_sums, chooser = refs[:10]
    totals, refs = take(refs[10:], spans)
    qkv_out, fc1_out, small_w, x_grad_ref, *scratch = refs
    qkv_scratch, scratch = take(scratch, 6)
    qkv = Product(act, joint, qkv_scratch)
    qkv_sum, scratch = resident_reduces(qkv.sums, scratch)
    fc1_sum, scratch = far_reduces(totals, fc1_out.shape[0], scratch)
    small_sends, small_receives, local, first_sums, joint_sums, small_s, *scratch = scratch
    x_ref, dx1_ref, weight, fetch_sems = scratch
    loads = fetches(((x_hbm, x_ref), (dx1_hbm, dx1_ref), (weight_hbm, weight)), fetch_sems)
    small = Gather(small_w, small_sends, small_receives)
    tiles = x_ref.shape[0] // CHUNK
    qkv.load()
    greet()
    run(fc1_sum, "start_far")
    for load in loads:
        load.start()
    qkv.send()
    qkv.sum(qkv_sum)
    for load in loads:
        load.wait()

    def back(at, carry):
        rows = pl.ds(pl.multiple_of(at * CHUNK, CHUNK), CHUNK)
        dact = times_across(joint[0, rows, :], weight[0]) + times_across(joint[1, rows, :], weight[1])
        h1, inverse = normed(x_ref[rows, :].astype(WIDE))
        first_sums[at, 0:1, :] = column_sums(dact)
        first_sums[at, 1:2, :] = column_sums(dact * h1)
        dh1 = dact * (1.0 + row_of(table, slots[at], 1))
        x_grad_ref[rows, :] = dx1_ref[rows, :] + inverse * (
            dh1
            - jnp.mean(dh1, axis=-1, keepdims=True)
            - h1 * jnp.mean(dh1 * h1, axis=-1, keepdims=True)
        )
        for side in range(2):
            joint_sums[side : side + 1, :] += column_sums(joint[side, rows, :].astype(WIDE))

        @pl.when(at == tiles // 2 - 1)
        def _():
            run(qkv_sum, "merge")

        return carry

    joint_sums[...] = jnp.zeros_like(joint_sums)
    lax.fori_loop(0, tiles, back, 0)
    choose = chooser[...]
    upper = lax.broadcasted_iota(jnp.int32, (choose.shape[0], D), 0) < choose.shape[0] // 2
    groups = (
        [first_sums[at, 0:1, :] for at in range(tiles)],
        [first_sums[at, 1:2, :] for at in range(tiles)],
    ) + tuple([mid_sums[at, row : row + 1, :] for at in range(tiles)] for row in range(4))
    for group in range(3):
        value = jnp.where(
            upper, tile_sums_by_slot(choose, groups[group]), tile_sums_by_slot(choose, groups[group + 3])
        )
        small_s[0:8, group * D : (group + 1) * D] = value.astype(LOW)
    pre = pre_sums[...]
    tile_rows = [column_sums(mid_sums[:, row, :]) for row in (4, 5)]
    biases = (
        (joint_sums[0:1, :D], joint_sums[1:2, D // 2 :], tile_rows[0]),
        tuple(pre[:, at * D : (at + 1) * D] for at in range(3)),
        (pre[:, 3 * D :], tile_rows[1], jnp.zeros((1, D), WIDE)),
    )
    blank = jnp.zeros((5, D), WIDE)
    for group in range(3):
        rows = jnp.concatenate([biases[row][group] for row in range(3)] + [blank], axis=0)
        small_s[8:16, group * D : (group + 1) * D] = rows.astype(LOW)
    small.start_far(small_s, local.at[0])
    small.finish_far(small_s, local.at[0])
    small.spread()
    run(qkv_sum, "total", "start_far")
    small.cross()
    small.close()
    small.end()
    for part in fc1_sum:
        part.final(fc1_out)
    for part in qkv_sum:
        part.final(qkv_out)


def last_scatter(slots, act, joint, x_in, dx1, table, weight, mid_sums, pre_sums, chooser, totals):
    count, _, _, rows, tokens = act.shape
    fc1_columns = totals[0].shape[2]
    columns = joint.shape[2]
    small_s = jax.ShapeDtypeStruct((16, 3 * D), LOW)
    return pl.pallas_call(
        partial(last_kernel, spans=len(totals)),
        out_shape=(
            jax.ShapeDtypeStruct((rows, columns), WIDE),
            jax.ShapeDtypeStruct((sum(total.shape[1] for total in totals), fc1_columns), WIDE),
            whole_shape(small_s),
            jax.ShapeDtypeStruct((tokens, D), WIDE),
        ),
        in_specs=[pl.BlockSpec(memory_space=pltpu.SMEM), ANY, VMEM, ANY, ANY, ANY]
        + [VMEM] * (4 + len(totals)),
        out_specs=(VMEM, VMEM, ANY, VMEM),
        scratch_shapes=Product.scratch(count, rows, tokens, columns)
        + resident_scratch((2, 2, count, rows, columns))
        + far_scratch(totals)
        + gather_scratch(1, 1)
        + [
            pltpu.VMEM((tokens // CHUNK, 8, D), WIDE),
            pltpu.VMEM((2, columns), WIDE),
            pltpu.VMEM(small_s.shape, LOW),
            pltpu.VMEM(x_in.shape, LOW),
            pltpu.VMEM(dx1.shape, WIDE),
            pltpu.VMEM(weight.shape, LOW),
            pltpu.SemaphoreType.DMA((3,)),
        ],
        compiler_params=pltpu.CompilerParams(
            collective_id=3, has_side_effects=True, vmem_limit_bytes=63 * 2**20
        ),
        name="last_scatter",
    )(slots, act, joint, x_in, dx1, weight, table, mid_sums, pre_sums, chooser, *totals)


def attend_back_kernel(*refs, counts):
    up_ref, heads, fc1_sums = refs[0], refs[1:5], refs[5]
    proj_totals, refs = take(refs[6:], counts[0])
    joints, refs = take(refs, counts[1])
    bases, refs = take(refs, counts[1])
    out_ref, fc2_out, proj_out, *refs = refs
    fc1_totals, refs = take(refs, counts[2])
    qh, kh, vh, uh, oh, load_sems, leave, leave_sems, *scratch = refs
    fc1, scratch = loaded_reduces(fc1_sums, scratch, fc1_totals)
    proj, scratch = far_reduces(proj_totals, proj_out.shape[0], scratch)
    fc2, scratch = late_reduces(joints, bases, fc2_out.shape[0], scratch)
    T = up_ref.shape[0]
    chunks = T // CHUNK

    def load(number):
        return pltpu.make_async_copy(heads[number], (qh, kh, vh, oh)[number], load_sems.at[number])

    for number in (3, 0, 1, 2):
        load(number).start()
    greet()
    run(fc2, "late_start")
    run(proj, "start_far")
    run(fc1, "start")
    load(3).wait()

    def fill(i, carry):
        rows = pl.ds(pl.multiple_of(i * CHUNK, CHUNK), CHUNK)
        lane = lanes((CHUNK, LANES))
        for h in range(HEADS):
            u = pad_head(up_ref[rows, h * HEAD : (h + 1) * HEAD], jnp.zeros((CHUNK, LANES), LOW))
            delta = jnp.sum(u.astype(WIDE) * oh[h, rows, :].astype(WIDE), axis=1, keepdims=True)
            hi, mid, lo = split3(-delta)
            u = jnp.where(lane == HEAD, hi.astype(LOW), u)
            u = jnp.where(lane == HEAD + 1, mid.astype(LOW), u)
            uh[h, rows, :] = jnp.where(lane == HEAD + 2, lo.astype(LOW), u)
        return carry

    lax.fori_loop(0, chunks, fill, 0)
    for number in range(3):
        load(number).wait()
    across = (((1,), (1,)), ((), ()))
    tasks = {
        4: lambda: run(fc2, "late_total", "start_far"),
        9: lambda: run(fc1, "merge"),
    }

    def head(h, carry):
        k = kh[h]
        v = vh[h]
        kt = k.T
        dk = jnp.zeros((T, LANES), WIDE)
        dv = jnp.zeros((T, LANES), WIDE)
        for i in range(chunks):
            rows = pl.ds(i * CHUNK, CHUNK)
            q = qh[h, rows, :]
            u = uh[h, rows, :]
            s = lax.dot_general(k, q, across, preferred_element_type=WIDE)
            p = jnp.exp2(s * (HEAD**-0.5 * LOG2E))
            dp = lax.dot_general(v, u, across, preferred_element_type=WIDE)
            ds = (p * dp).astype(LOW)
            dv = dv + jnp.dot(p.astype(LOW), u, preferred_element_type=WIDE)
            dk = dk + jnp.dot(ds, q, preferred_element_type=WIDE)
            dqt = jnp.dot(kt, ds, preferred_element_type=WIDE)
            qh[h, rows, :] = (dqt.T * HEAD**-0.5).astype(LOW)
        kh[h] = (dk * HEAD**-0.5).astype(LOW)
        vh[h] = dv.astype(LOW)
        for at, task in tasks.items():

            @pl.when(h == at)
            def _(task=task):
                task()

        return carry

    lax.fori_loop(0, HEADS, head, 0)

    def store(i, side):
        rows = pl.ds(pl.multiple_of(i * CHUNK, CHUNK), CHUNK)
        return pltpu.make_async_copy(
            leave.at[side], out_ref.at[side, rows], leave_sems.at[side]
        )

    def drain(i, carry):
        rows = pl.ds(pl.multiple_of(i * CHUNK, CHUNK), CHUNK)
        parts = [g[h, rows, :][:, :HEAD] for g in (qh, kh, vh) for h in range(HEADS)]
        for side in range(2):

            @pl.when(i > 0)
            def _(side=side):
                store(i - 1, side).wait()

            own = parts[side * len(parts) // 2 : (side + 1) * len(parts) // 2]
            leave[side] = jnp.concatenate(own, axis=1)
            store(i, side).start()
        return carry

    lax.fori_loop(0, chunks, drain, 0)
    run(fc1, "total")
    for side in range(2):
        store(chunks - 1, side).wait()
    for part in fc2:
        part.final(fc2_out)
    for part in proj:
        part.final(proj_out)


def attend_back(upstream, heads, fc1_sums, proj_totals, joints, bases):
    tokens = upstream.shape[0]
    count, rows, columns = fc1_sums.shape[2:]
    totals = total_shapes(count, rows, columns)

    def shard(parts):
        return jax.ShapeDtypeStruct((sum(part.shape[1] for part in parts), parts[0].shape[2]), WIDE)

    out = pl.pallas_call(
        partial(attend_back_kernel, counts=(len(proj_totals), len(joints), len(totals))),
        out_shape=(
            jax.ShapeDtypeStruct((2, tokens, 3 * HEADS * HEAD // 2), LOW),
            shard(bases),
            shard(proj_totals),
        )
        + tuple(totals),
        in_specs=[VMEM] + [ANY] * 5 + [VMEM] * len(proj_totals) + [ANY] * (2 * len(joints)),
        out_specs=(ANY, VMEM, VMEM) + (VMEM,) * len(totals),
        scratch_shapes=[pltpu.VMEM((HEADS, tokens, LANES), LOW)] * 5
        + [pltpu.SemaphoreType.DMA((4,))]
        + [pltpu.VMEM((2, CHUNK, 3 * HEADS * HEAD // 2), LOW), pltpu.SemaphoreType.DMA((2,))]
        + loaded_scratch(fc1_sums.shape, False)
        + far_scratch(proj_totals)
        + late_scratch(bases),
        compiler_params=pltpu.CompilerParams(
            collective_id=2, has_side_effects=True, vmem_limit_bytes=63 * 2**20
        ),
        name="attend_back",
    )(upstream, *heads, fc1_sums, *proj_totals, *joints, *bases)
    return out[0], out[1], out[2], out[3:]


def normed(values):
    centre = values - jnp.mean(values, axis=-1, keepdims=True)
    inverse = lax.rsqrt(jnp.mean(centre * centre, axis=-1, keepdims=True) + EPS)
    return centre * inverse, inverse


def row_of(table, slot, group):
    return table[group // 3, pl.ds(slot, 1), group % 3 * D : (group % 3 + 1) * D]


def column_sums(values):
    return jnp.sum(values, axis=0, keepdims=True)


def times_across(left, right):
    return lax.dot_general(left, right, (((1,), (1,)), ((), ())), preferred_element_type=WIDE)


def fixed(*shape):
    return pl.BlockSpec(
        shape, lambda i, slots: (0,) * len(shape), pipeline_mode=pl.Buffered(1)
    )


GELU = 0.7978845608028654
CUBIC = 0.044715
SPAN = 768
BLOCK = 512


def middle_kernel(
    slots, x_ref, g_ref, mixed_ref, table, bias, bias1, proj, fc1, fc2,
    block_ref, mlp_turned, hidden_turned, dpre_ref, dbranch_ref, dattn_ref, dmixed_ref, dx1_ref, sums_ref, dpre_sums,
    attn_out, mlp, branch,
):
    step = pl.program_id(0)
    tokens = x_ref.shape[0]

    @pl.when(step == 0)
    def _():
        def enter(tile_at, carry):
            rows = pl.ds(pl.multiple_of(tile_at * CHUNK, CHUNK), CHUNK)
            slot = slots[tile_at]
            gate1, shift2, scale2, gate2 = (row_of(table, slot, group) for group in (2, 3, 4, 5))
            mixed = mixed_ref[rows, :]
            out = jnp.concatenate([times(mixed, proj[0]), times(mixed, proj[1])], axis=1)
            out = out + bias[:, 2 * D : 3 * D]
            attn_out[rows, :] = out
            h2, _ = normed(x_ref[rows, :].astype(WIDE) + gate1 * out)
            mlp_in = (h2 * (1.0 + scale2) + shift2).astype(LOW)
            mlp[rows, :] = mlp_in
            mlp_turned[:, rows] = mlp_in.T
            dbranch = (gate2 * g_ref[rows, :].astype(WIDE)).astype(LOW)
            sums_ref[tile_at, 5:6, :] = column_sums(dbranch.astype(WIDE))
            dbranch_ref[0, rows, :] = dbranch[:, : D // 2]
            dbranch_ref[1, rows, :] = dbranch[:, D // 2 :]
            return carry

        lax.fori_loop(0, tokens // CHUNK, enter, 0)
        branch[...] = jnp.zeros_like(branch)
        dx1_ref[...] = jnp.zeros_like(dx1_ref)

    total = None
    for first in range(0, tokens, BLOCK):
        rows = slice(first, first + BLOCK)
        pre = times(mlp[rows, :], fc1[0]) + bias1[0]
        square = pre * pre
        bend = jnp.tanh(GELU * pre * (1.0 + CUBIC * square))
        rise = 0.5 * (1.0 + bend)
        hidden = (pre * rise).astype(LOW)
        hidden_turned[:, rows] = hidden.T
        for side in range(2):
            branch[side, rows] += times(hidden, fc2[side])
        slope = rise + 0.5 * GELU * pre * (1.0 - bend * bend) * (1.0 + 3.0 * CUBIC * square)
        dhidden = times_across(dbranch_ref[0, rows], fc2[0]) + times_across(dbranch_ref[1, rows], fc2[1])
        dpre = (dhidden * slope).astype(LOW)
        dpre_ref[0, rows] = dpre
        part = column_sums(dpre.astype(WIDE))
        total = part if total is None else total + part
        dx1_ref[rows, :] += times_across(dpre, fc1[0])
    dpre_sums[...] = total

    @pl.when(step == pl.num_programs(0) - 1)
    def _():
        def leave(tile_at, carry):
            rows = pl.ds(pl.multiple_of(tile_at * CHUNK, CHUNK), CHUNK)
            slot = slots[tile_at]
            gate1, scale2, gate2 = (row_of(table, slot, group) for group in (2, 4, 5))
            out = attn_out[rows, :]
            x1 = x_ref[rows, :].astype(WIDE) + gate1 * out
            h2, inverse = normed(x1)
            whole = jnp.concatenate([branch[0, rows, :], branch[1, rows, :]], axis=1) + bias[:, 3 * D + FF :]
            block_ref[rows, :] = (x1 + gate2 * whole).astype(LOW)
            g = g_ref[rows, :].astype(WIDE)
            sums_ref[tile_at, 3:4, :] = column_sums(g * whole)
            dmlp = dx1_ref[rows, :]
            sums_ref[tile_at, 1:2, :] = column_sums(dmlp)
            sums_ref[tile_at, 2:3, :] = column_sums(dmlp * h2)
            dh2 = dmlp * (1.0 + scale2)
            dx1 = g + inverse * (
                dh2
                - jnp.mean(dh2, axis=-1, keepdims=True)
                - h2 * jnp.mean(dh2 * h2, axis=-1, keepdims=True)
            )
            dx1_ref[rows, :] = dx1
            sums_ref[tile_at, 0:1, :] = column_sums(dx1 * out)
            dattn = (gate1 * dx1).astype(LOW)
            sums_ref[tile_at, 4:5, :] = column_sums(dattn.astype(WIDE))
            sums_ref[tile_at, 6:8, :] = jnp.zeros((2, D), WIDE)
            left, right = dattn[:, : D // 2], dattn[:, D // 2 :]
            dattn_ref[0, rows, :] = left
            dattn_ref[1, rows, :] = right
            dmixed_ref[rows, :] = (times_across(left, proj[0]) + times_across(right, proj[1])).astype(LOW)
            return carry

        lax.fori_loop(0, tokens // CHUNK, leave, 0)


def middle(slots, x_in, out_grad, mixed, table, bias, proj, fc1, fc2):
    tokens = x_in.shape[0]
    tiles = tokens // CHUNK
    steps = FF // SPAN
    per_side = steps // 2
    bias1 = bias[:, 3 * D : 3 * D + FF].reshape(steps, 1, SPAN)

    def by_unit(shape, place):
        return pl.BlockSpec(shape, lambda j, slots: place(j))

    outs = (
        ((tokens, D), LOW),
        ((D, tokens), LOW),
        ((FF, tokens), LOW),
        ((2, tokens, FF // 2), LOW),
        ((2, tokens, D // 2), LOW),
        ((2, tokens, D // 2), LOW),
        ((tokens, D), LOW),
        ((tokens, D), WIDE),
        ((tiles, 8, D), WIDE),
        ((1, FF), WIDE),
    )
    out_specs = [fixed(*shape) for shape, _ in outs]
    out_specs[2] = by_unit((SPAN, tokens), lambda j: (j, 0))
    out_specs[3] = by_unit((1, tokens, SPAN), lambda j: (j // per_side, 0, j % per_side))
    out_specs[9] = by_unit((1, SPAN), lambda j: (0, j))
    return pl.pallas_call(
        middle_kernel,
        out_shape=tuple(jax.ShapeDtypeStruct(shape, dtype) for shape, dtype in outs),
        grid_spec=pltpu.PrefetchScalarGridSpec(
            num_scalar_prefetch=1,
            grid=(steps,),
            in_specs=[
                fixed(tokens, D),
                fixed(tokens, D),
                fixed(tokens, D),
                fixed(*table.shape),
                fixed(*bias.shape),
                by_unit((1, 1, SPAN), lambda j: (j, 0, 0)),
                fixed(*proj.shape),
                by_unit((1, D, SPAN), lambda j: (j // per_side, 0, j % per_side)),
                by_unit((2, SPAN, D // 2), lambda j: (0, j, 0)),
            ],
            out_specs=tuple(out_specs),
            scratch_shapes=[
                pltpu.VMEM((tokens, D), WIDE),
                pltpu.VMEM((tokens, D), LOW),
                pltpu.VMEM((2, tokens, D // 2), WIDE),
            ],
        ),
        compiler_params=pltpu.CompilerParams(
            dimension_semantics=("arbitrary",), vmem_limit_bytes=63 * 2**20
        ),
        cost_estimate=pl.CostEstimate(
            flops=4 * tokens * (D * D + 2 * D * FF),
            bytes_accessed=(D * D + 2 * D * FF) * 2 + tokens * D * 40,
            transcendentals=0,
        ),
        name="middle",
    )(slots, x_in, out_grad, mixed, table, bias, bias1, proj, fc1, fc2)


def times(left, right):
    return jnp.dot(left, right, preferred_element_type=WIDE)


def times_back(left, right):
    return lax.dot_general(left, right, (((1,), (1,)), ((), ())), preferred_element_type=WIDE)


def body(
    x_in,
    cond,
    segments,
    out_grad,
    qkv_weight,
    qkv_moment,
    qkv_average,
    proj_weight,
    proj_moment,
    proj_average,
    fc1_weight,
    fc1_moment,
    fc1_average,
    fc2_weight,
    fc2_moment,
    fc2_average,
    bias_weight,
    bias_moment,
    bias_average,
    ada_weight,
    ada_moment,
    ada_average,
    adab_weight,
    adab_moment,
    adab_average,
):
    tokens, width = x_in.shape
    row_devices = lax.axis_size(ROWS)
    devices = lax.axis_size(ALL)
    row_index = lax.axis_index(ROWS)
    images = cond.shape[0] // 2

    cond_silu, silu_back = jax.vjp(jax.nn.silu, cond.astype(WIDE))
    half_silu = lax.dynamic_index_in_dim(
        cond_silu.astype(LOW).reshape(-1, 2, width // 2), lax.axis_index("mod"), 1, False
    )
    own_bias = bias_weight.shape[0]
    bias_block = jnp.pad(bias_weight.astype(LOW), (0, 8 * LANES - own_bias)).reshape(8, LANES)
    blank = jnp.zeros((8, LANES // 2), LOW)
    ada_low = ada_weight.astype(LOW)
    adab_row = lax.dynamic_update_slice_in_dim(
        jnp.zeros((1, ada_weight.shape[1]), LOW),
        adab_weight.astype(LOW),
        row_index * adab_weight.shape[1],
        1,
    )
    ada_rows = jnp.concatenate([ada_low, adab_row])
    small_w, qkv_w, proj_w, fc1_w, table = first_gather(
        jnp.pad(ada_rows, ((0, LANES - ada_rows.shape[0]), (0, 0))),
        jnp.concatenate([half_silu, bias_block, blank], axis=1),
        qkv_weight,
        proj_weight,
        fc1_weight,
    )
    small = small_w.reshape(2, row_devices * 8, -1)
    silu_all = jnp.concatenate([small[0, :, : width // 2], small[1, :, : width // 2]], axis=1)
    bias_all = small[:, :, width // 2 : width // 2 + LANES].reshape(2, row_devices, -1)
    bias_full = jnp.swapaxes(bias_all[:, :, :own_bias], 0, 1).reshape(1, -1).astype(WIDE)
    def joined(whole):
        return whole.reshape(2, -1, whole.shape[-1])

    qkv_low = joined(qkv_w)
    slots = segments[::CHUNK]
    table_rows = slots + lax.axis_index("mod") * images
    joint_bias = jnp.concatenate(
        [bias_full[:, 0:width], jnp.zeros((1, width), WIDE), bias_full[:, width : 2 * width]], axis=1
    )
    def blocked(turned):
        return turned.reshape(row_devices // 4, 2, 2, -1, tokens)

    act_turned, mixture, mixture_turned, heads, (proj_w, fc1_w, fc2_w) = attend(
        table_rows,
        x_in,
        table,
        joint_bias,
        qkv_low,
        segments,
        fc2_weight.astype(LOW),
        proj_w,
        fc1_w,
    )
    (
        block_out, mlp_turned, hidden_turned, pre_halves, branch_halves, attn_halves, mixture_grad, middle_grad, sums, pre_sums,
    ) = middle(
        table_rows, x_in, out_grad, mixture, table, bias_full, joined(proj_w), joined(fc1_w), joined(fc2_w)
    )
    proj_totals, fc2_joints, fc2_bases, fc1_sums = weight_grads(
        blocked(hidden_turned),
        branch_halves,
        blocked(mlp_turned),
        pre_halves,
        blocked(mixture_turned),
        attn_halves,
    )
    joint_halves, fc2_shard, proj_shard, fc1_totals = attend_back(
        mixture_grad, heads, fc1_sums, proj_totals, fc2_joints, fc2_bases
    )
    chooser = (slots[None, :] == (jnp.arange(2 * images, dtype=jnp.int32) % images)[:, None]).astype(WIDE)
    qkv_shard, fc1_shard, small_grads, x_grad = last_scatter(
        table_rows,
        blocked(act_turned),
        joint_halves,
        x_in,
        middle_grad,
        table,
        qkv_low,
        sums,
        pre_sums,
        chooser,
        fc1_totals,
    )
    small_grads = small_grads.reshape(2, row_devices, 16, -1)
    mod_grads = lax.dynamic_slice_in_dim(small_grads, lax.axis_index("mod") * images, images, 2)
    mod_grad_all = jnp.swapaxes(mod_grads, 0, 1).reshape(2 * row_devices * images, -1)
    bias_grads = small_grads[:, :, 8:11].reshape(devices, -1)
    own_biases = lax.dynamic_slice_in_dim(bias_grads, lax.axis_index(ALL) * own_bias, own_bias, 1)
    bias_shard = jnp.sum(own_biases.astype(WIDE), axis=0)
    own_rows = ada_weight.shape[0]
    own_silu = lax.dynamic_slice_in_dim(silu_all, row_index * own_rows, own_rows, 1)
    ada_shard = jnp.einsum("ic,io->co", own_silu, mod_grad_all, preferred_element_type=WIDE)
    own_columns = adab_weight.shape[1]
    adab_shard = jnp.sum(
        lax.dynamic_slice_in_dim(mod_grad_all, row_index * own_columns, own_columns, 1).astype(WIDE),
        axis=0,
    )
    silu_part = times_back(mod_grad_all, ada_low)
    row_images = 2 * images
    silu_part = jnp.broadcast_to(
        silu_part.reshape(row_devices, 1, row_images, -1), (row_devices, 2, row_images, own_rows)
    ).reshape(devices * row_images, own_rows)
    silu_part = lax.all_to_all(silu_part, ALL, split_axis=0, concat_axis=1, tiled=True)
    silu_grad = jnp.sum(silu_part.reshape(row_images, row_devices, 2, own_rows), axis=2)
    cond_grad = silu_back(silu_grad.reshape(row_images, -1))[0]

    rates = step_rates(tokens * devices)
    states_out = []
    states_out.extend(nesterov(qkv_weight, qkv_moment, qkv_average, qkv_shard, rates[0]))
    states_out.extend(nesterov(proj_weight, proj_moment, proj_average, proj_shard, rates[1]))
    states_out.extend(nesterov(fc1_weight, fc1_moment, fc1_average, fc1_shard, rates[2]))
    states_out.extend(nesterov(fc2_weight, fc2_moment, fc2_average, fc2_shard, rates[3]))
    states_out.extend(nesterov(bias_weight, bias_moment, bias_average, bias_shard, rates[4]))
    states_out.extend(nesterov(ada_weight, ada_moment, ada_average, ada_shard, rates[5]))
    states_out.extend(
        nesterov(adab_weight, adab_moment, adab_average, adab_shard.reshape(1, -1), rates[6])
    )
    return (block_out, x_grad, cond_grad) + tuple(states_out)


def solution(mesh):
    far = mesh.shape["dp"] // 4
    fine = Mesh(mesh.devices.reshape(far, 2, 2, mesh.shape["mod"]), ALL)
    tokens = P(ALL, None)
    images = P(ROWS, None)
    trunk = P(ROWS, "mod")
    bias = P(ALL)
    adab = P("mod", ROWS)
    states = (trunk,) * 12 + (bias,) * 3 + (trunk,) * 3 + (adab,) * 3
    return jax.shard_map(
        body,
        mesh=fine,
        in_specs=(tokens, images, bias, tokens) + states,
        out_specs=(tokens, tokens, images) + states,
        check_vma=False,
    )
```
